32 devices in a mesh: dp: 8 (over z, x), tensor: 4 (over y, core).
Axes of the slice: x: 2, y: 2, z: 4, core: 2. Of those that a mesh axis runs over, the one named last changes fastest.
Arguments:
- inputs: bfloat16 [16, 512, 2048], P('dp'), may hold values from -6 to 6
- attention_gain: bfloat16 [2048], P('dp'), may hold values from 0.099609375 to 1.8984375
- query_weight: bfloat16 [2048, 2048], P('dp', 'tensor'), may hold values from -0.1875 to 0.1875
- key_matrix: bfloat16 [2048, 512], P('dp', 'tensor'), may hold values from -0.1875 to 0.1875
- value_matrix: bfloat16 [2048, 512], P('dp', 'tensor'), may hold values from -0.125 to 0.125
- out_weight: bfloat16 [2048, 2048], P('tensor', 'dp'), may hold values from -1 to 1
- feedforward_gain: bfloat16 [2048], P('dp'), may hold values from 0.099609375 to 1.8984375
- gate_weight: bfloat16 [2048, 5632], P('dp', 'tensor'), may hold values from -0.125 to 0.125
- up_weight: bfloat16 [2048, 5632], P('dp', 'tensor'), may hold values from -0.125 to 0.125
- down_weight: bfloat16 [5632, 2048], P('tensor', 'dp'), may hold values from -0.109375 to 0.109375
- cotangent: bfloat16 [16, 512, 2048], P('dp'), may hold values from -6 to 6
- layer_keep: int32 [16], P('dp'), may hold values 0 or 1
- prefix_length: int32 [16], P('dp'), may hold values from 51 to 256
Outputs:
- output: bfloat16 [16, 512, 2048], P('dp')
- input_grad: bfloat16 [16, 512, 2048], P('dp')
- grad_attention_gain: float32 [2048], P('dp')
- grad_query: float32 [2048, 2048], P('dp', 'tensor')
- grad_key: float32 [2048, 512], P('dp', 'tensor')
- grad_value: float32 [2048, 512], P('dp', 'tensor')
- grad_out: float32 [2048, 2048], P('tensor', 'dp')
- grad_feedforward_gain: float32 [2048], P('dp')
- grad_gate: float32 [2048, 5632], P('dp', 'tensor')
- grad_up: float32 [2048, 5632], P('dp', 'tensor')
- grad_down: float32 [5632, 2048], P('tensor', 'dp')
The draws below stay inside these ranges and needn't reach their ends.
All inputs are finite; a program needn't handle non-finite values. No bound on the sum of `layer_keep` on one device may be relied on, other than what follows from the above.
Results may differ from the reference program's by a relative error of at most 0.015.
The reference program's roundings to bfloat16 on the way count: a program that leaves them out, or rounds other values in their place, can miss the bound.
Values may be sent and summed in bfloat16 or wider, within the bound.
A program may use at most 256 MiB of HBM per device.

```python
import math
import jax
import jax.numpy as jnp
from jax import lax

MODEL_WIDTH = 2048
QUERY_HEADS = 16
KEY_VALUE_HEADS = 4
HEAD_SIZE = 128
FF = 5632
SEQ = 512
SEQS = 16


def with_ends(drawn, rng, smallest, high):
    extent = drawn.shape
    spot = [jax.random.randint(jax.random.fold_in(rng, axis), (), 0, extent[axis]) for axis in range(len(extent))]
    drawn = drawn.at[tuple(spot)].set(smallest)
    longest = extent.index(max(extent))
    spot[longest] = (spot[longest] + 1) % extent[longest]
    return drawn.at[tuple(spot)].set(high)


def block_scale(stream_key, extent, pieces, smallest, largest):
    factor_of, own = 1.0, jax.random.fold_in(stream_key, 6)
    for dim, blocks in pieces:
        heights = jnp.exp(jax.random.uniform(jax.random.fold_in(own, dim), (blocks,), jnp.float32, smallest / len(pieces), largest / len(pieces)))
        factor_of = factor_of * jnp.repeat(heights, extent[dim] // blocks).reshape([-1 if axis == dim else 1 for axis in range(len(extent))])
    return factor_of


def noise(own_key, dims, deviation, bound, pieces=(), kind=jnp.bfloat16):
    factor_of = block_scale(own_key, dims, pieces, -0.22, 0.18) if pieces else 1.0
    values = jax.random.normal(own_key, dims, jnp.float32) * deviation * factor_of
    return jnp.minimum(jnp.maximum(values, -bound), bound).astype(kind)


def setup_inputs(seed: int = 0) -> dict:
    key_of = jax.random.split(jax.random.key(seed), 14)
    return {
        "inputs": noise(key_of[0], (SEQS, SEQ, MODEL_WIDTH), 1.0, 6.0, ((0, 8),)),
        "attention_gain": jnp.clip(1.0 + 0.18 * jax.random.normal(key_of[1], (MODEL_WIDTH,), jnp.float32), 0.099609375, 1.8984375).astype(jnp.bfloat16),
        "query_weight": noise(key_of[2], (MODEL_WIDTH, QUERY_HEADS * HEAD_SIZE), (MODEL_WIDTH // 2) ** -0.5, 0.1875, ((0, 8), (1, 4))),
        "key_matrix": noise(key_of[3], (MODEL_WIDTH, KEY_VALUE_HEADS * HEAD_SIZE), (MODEL_WIDTH // 2) ** -0.5, 0.1875, ((0, 8), (1, 4))),
        "value_matrix": noise(key_of[4], (MODEL_WIDTH, KEY_VALUE_HEADS * HEAD_SIZE), MODEL_WIDTH ** -0.5, 0.125, ((0, 8), (1, 4))),
        "out_weight": noise(key_of[5], (QUERY_HEADS * HEAD_SIZE, MODEL_WIDTH), (QUERY_HEADS * HEAD_SIZE // 64) ** -0.5, 1.0, ((0, 4), (1, 8))),
        "feedforward_gain": jnp.clip(1.0 + 0.18 * jax.random.normal(key_of[6], (MODEL_WIDTH,), jnp.float32), 0.099609375, 1.8984375).astype(jnp.bfloat16),
        "gate_weight": noise(key_of[7], (MODEL_WIDTH, FF), MODEL_WIDTH ** -0.5, 0.125, ((0, 8), (1, 4))),
        "up_weight": noise(key_of[8], (MODEL_WIDTH, FF), MODEL_WIDTH ** -0.5, 0.125, ((0, 8), (1, 4))),
        "down_weight": noise(key_of[9], (FF, MODEL_WIDTH), (FF // 2) ** -0.5, 0.109375, ((0, 4), (1, 8))),
        "cotangent": noise(key_of[10], (SEQS, SEQ, MODEL_WIDTH), 1.0, 6.0, ((0, 8),)),
        "layer_keep": with_ends((jax.random.randint(key_of[11], (SEQS,), 0, 4) < 3).astype(jnp.int32), jax.random.fold_in(key_of[11], 1), 0, 1),
        "prefix_length": with_ends(jax.random.randint(key_of[12], (SEQS,), SEQ // 10, SEQ // 2 + 1), jax.random.fold_in(key_of[12], 1), SEQ // 10, (SEQ // 2 + 1) - 1).astype(jnp.int32),
    }


epsilon = 1e-05
negative = -1e+30

@jax.custom_vjp
def lowered_cast(v):
    return lax.optimization_barrier(v.astype(jnp.bfloat16)).astype(jnp.float32)

@jax.custom_vjp
def lowered_cast_back(v):
    return v

def low_keep(v):
    return (lowered_cast(v), None)

def low_pass(kept, grad):
    return (grad,)

def back_keep(v):
    return (v, None)

def back_low(kept, grad):
    return (lowered_cast(grad),)
lowered_cast.defvjp(low_keep, low_pass)
lowered_cast_back.defvjp(back_keep, back_low)

def exact_product(left_rows, right_rows):
    return jnp.dot(left_rows, right_rows, precision=lax.Precision.HIGHEST, preferred_element_type=jnp.float32)

def rotary_tables(length_total, head_width):
    half_width = head_width // 2
    frequency = 10000.0 ** (-(jnp.arange(half_width, dtype=jnp.float32) * 2.0) / head_width)
    angles = jnp.arange(length_total, dtype=jnp.float32)[:, None] * frequency[None, :]
    return (jnp.cos(angles), jnp.sin(angles))

def rotate(head_values, cosine_table, sine_table):
    half_width = head_values.shape[-1] // 2
    first_half = head_values[..., :half_width]
    second_half = head_values[..., half_width:]
    cos_part = cosine_table[:, None, :]
    sin_part = sine_table[:, None, :]
    return jnp.concatenate([first_half * cos_part - second_half * sin_part, first_half * sin_part + second_half * cos_part], axis=-1)

def rms_scale(token_rows, gain_vec):
    inv_rms = lax.rsqrt(lax.optimization_barrier(jnp.mean(token_rows * token_rows, axis=-1, keepdims=True)) + epsilon)
    return token_rows * inv_rms * gain_vec

def layer_forward(inputs, attention_gain, query_weight, key_matrix, value_matrix, out_weight, feedforward_gain, gate_weight, up_weight, down_weight, keep_flag, prefix_length):
    query_group_total, length_total, width_model = inputs.shape
    token_rows = inputs.reshape(query_group_total * length_total, width_model)
    attention_normed = lowered_cast(rms_scale(token_rows, attention_gain))
    queries = lowered_cast_back(exact_product(attention_normed, query_weight)).reshape(query_group_total, length_total, QUERY_HEADS, HEAD_SIZE)
    key_projected = lowered_cast_back(exact_product(attention_normed, key_matrix)).reshape(query_group_total, length_total, KEY_VALUE_HEADS, HEAD_SIZE)
    value_projected = lowered_cast(lowered_cast_back(exact_product(attention_normed, value_matrix))).reshape(query_group_total, length_total, KEY_VALUE_HEADS, HEAD_SIZE)
    cosine_table, sine_table = rotary_tables(length_total, HEAD_SIZE)
    position = jnp.arange(length_total, dtype=jnp.int32)
    score_scale = 1.0 / math.sqrt(HEAD_SIZE)

    def attend(seq_block):
        query_seq, key_seq, value_sequence, prefix_end = seq_block
        query_rot = lowered_cast(rotate(query_seq, cosine_table, sine_table))
        key_rotated = lowered_cast(rotate(key_seq, cosine_table, sine_table))
        key_repeated = jnp.repeat(key_rotated, QUERY_HEADS // KEY_VALUE_HEADS, axis=1)
        value_repeated = jnp.repeat(value_sequence, QUERY_HEADS // KEY_VALUE_HEADS, axis=1)
        scores = lowered_cast_back(jnp.einsum('qhd,khd->hqk', query_rot, key_repeated, precision=lax.Precision.HIGHEST) * score_scale)
        allowed = (position[None, :] <= position[:, None]) | (position[None, :] < prefix_end)
        scores = jnp.where(allowed[None], scores, negative)
        attn_probs = jax.nn.softmax(scores, axis=-1)
        return jnp.einsum('hqk,khd->qhd', lowered_cast(attn_probs), value_repeated, precision=lax.Precision.HIGHEST)
    mixed_heads = lax.map(jax.checkpoint(attend), (queries, key_projected, value_projected, prefix_length))
    mixed_rows = lowered_cast(lowered_cast_back(mixed_heads.reshape(query_group_total * length_total, QUERY_HEADS * HEAD_SIZE)))
    keep_rows = jnp.repeat(keep_flag, length_total)[:, None]
    hidden = token_rows + keep_rows * lowered_cast_back(exact_product(mixed_rows, out_weight))
    normed_m = lowered_cast(rms_scale(hidden, feedforward_gain))
    gate_proj = lowered_cast_back(exact_product(normed_m, gate_weight))
    up_proj = lowered_cast_back(exact_product(normed_m, up_weight))
    act_rows = lowered_cast(jax.nn.silu(gate_proj) * up_proj)
    result = hidden + keep_rows * lowered_cast_back(exact_product(act_rows, down_weight))
    return result.reshape(query_group_total, length_total, width_model)

def reference(inputs, attention_gain, query_weight, key_matrix, value_matrix, out_weight, feedforward_gain, gate_weight, up_weight, down_weight, cotangent, layer_keep, prefix_length):
    group_size = math.gcd(SEQS, 8)
    weights = tuple((weight_arg.astype(jnp.float32) for weight_arg in (attention_gain, query_weight, key_matrix, value_matrix, out_weight, feedforward_gain, gate_weight, up_weight, down_weight)))

    def shaped(array_in):
        return array_in.reshape((SEQS // group_size, group_size) + array_in.shape[1:])

    def accumulate(totals, seq_block):
        in_block, cot_block, keep_block, prefix_block = seq_block

        def forward(block_in, *params):
            return layer_forward(block_in, *params, keep_block.astype(jnp.float32), prefix_block)
        result, pullback = jax.vjp(forward, in_block.astype(jnp.float32), *weights)
        grad_all = pullback(cot_block.astype(jnp.float32))
        totals = tuple((running + addend for running, addend in zip(totals, grad_all[1:])))
        return (totals, (result.astype(jnp.bfloat16), grad_all[0].astype(jnp.bfloat16)))
    zeros_init = tuple((jnp.zeros(weight_arg.shape, jnp.float32) for weight_arg in weights))
    totals, (out_blocks, grad_blocks) = lax.scan(accumulate, zeros_init, (shaped(inputs), shaped(cotangent), shaped(layer_keep), shaped(prefix_length)))
    return (out_blocks.reshape(inputs.shape), grad_blocks.reshape(inputs.shape), totals[0], totals[1], totals[2], totals[3], totals[4], totals[5], totals[6], totals[7], totals[8])
```

```python
import math

import jax
import jax.numpy as jnp
import numpy as np
from jax import lax
from jax.sharding import PartitionSpec as P

HEAD_SIZE = 128
EPSILON = 1e-05
NEGATIVE = -1e30
BF16 = jnp.bfloat16
F32 = jnp.float32


def rotary_tables(length_total):
    half_width = HEAD_SIZE // 2
    frequency = (10000.0 ** (-(np.arange(half_width, dtype=np.float32) * 2.0) / HEAD_SIZE)).astype(np.float32)
    angles = np.arange(length_total, dtype=np.float32)[:, None] * frequency[None, :]
    return (jnp.asarray(np.cos(angles)), jnp.asarray(np.sin(angles)))


def rotate(values, cos_part, sin_part):
    first, second = jnp.split(values, 2, axis=-1)
    return jnp.concatenate(
        [first * cos_part - second * sin_part, first * sin_part + second * cos_part], axis=-1
    )


def dot(a, b):
    return jnp.dot(a, b, preferred_element_type=F32)


def dot_ta(a, b):
    return lax.dot_general(a, b, (((0,), (0,)), ((), ())), preferred_element_type=F32)


def dot_tb(a, b):
    return lax.dot_general(a, b, (((1,), (1,)), ((), ())), preferred_element_type=F32)


class Ring:
    def __init__(self, size):
        self.size = size
        self.half = size // 2
        self.order = [2 * p if p < self.half else 2 * (size - 1 - p) + 1 for p in range(size)]
        self.right = [(self.order[p], self.order[(p + 1) % size]) for p in range(size)]
        self.left = [(b, a) for a, b in self.right]

    def place(self):
        me = lax.axis_index("dp")
        odd = me % 2
        return (1 - odd) * (me // 2) + odd * (self.size - 1 - me // 2)

    def owners(self):
        return jnp.asarray(np.array(self.order, np.int32))[(self.place() + np.arange(self.size)) % self.size]

    def gather(self, shard):
        n, m = self.size, self.half
        pieces = [None] * n
        pieces[0] = shard
        from_left, from_right = shard, shard
        for hop in range(1, m):
            from_left = lax.ppermute(from_left, "dp", self.right)
            from_right = lax.ppermute(from_right, "dp", self.left)
            pieces[n - hop] = from_left
            pieces[hop] = from_right
        rows = shard.shape[0] // 2
        top = lax.ppermute(from_left[:rows], "dp", self.right)
        low = lax.ppermute(from_right[rows:], "dp", self.left)
        pieces[m] = jnp.concatenate([top, low], axis=0)
        return pieces

    def scatter(self, parts):
        n, m = self.size, self.half
        rows = parts[0].shape[0] // 2
        kind = BF16
        up = lax.ppermute(parts[m][:rows].astype(kind), "dp", self.right)
        down = lax.ppermute(parts[m][rows:].astype(kind), "dp", self.left)
        for hop in range(m - 1, 0, -1):
            mine_up, mine_down = parts[hop], parts[n - hop]
            if hop == m - 1:
                mine_up = jnp.concatenate([mine_up[:rows] + up.astype(F32), mine_up[rows:]], axis=0)
                mine_down = jnp.concatenate([mine_down[:rows], mine_down[rows:] + down.astype(F32)], axis=0)
            else:
                mine_up = mine_up + up.astype(F32)
                mine_down = mine_down + down.astype(F32)
            up = lax.ppermute(mine_up.astype(kind), "dp", self.right)
            down = lax.ppermute(mine_down.astype(kind), "dp", self.left)
        if m == 1:
            return jnp.concatenate([parts[0][:rows] + up.astype(F32), parts[0][rows:] + down.astype(F32)], axis=0)
        return parts[0] + up.astype(F32) + down.astype(F32)


CORE_PAIRS = [(0, 1), (1, 0), (2, 3), (3, 2)]
CHIP_PAIRS = [(0, 2), (2, 0), (1, 3), (3, 1)]


def swap_core(value):
    return lax.ppermute(value, "tensor", CORE_PAIRS)


def swap_chip(value):
    return lax.ppermute(value, "tensor", CHIP_PAIRS)


def tensor_sum(part):
    near = part[0] + swap_core(part[1].astype(BF16)).astype(F32)
    near = near.astype(BF16)
    return near.astype(F32) + swap_chip(near).astype(F32)


def local(ring, inputs, attention_gain, query_weight, key_matrix, value_matrix, out_weight, feedforward_gain,
          gate_weight, up_weight, down_weight, cotangent, layer_keep, prefix_length):
    n = ring.size
    seqs, length, width = inputs.shape
    block = width // n
    q_cols, kv_cols = query_weight.shape[1], key_matrix.shape[1]
    heads = q_cols // HEAD_SIZE
    kv_heads = kv_cols // HEAD_SIZE
    repeat = heads // kv_heads
    scale = 1.0 / math.sqrt(HEAD_SIZE)
    core = lax.axis_index("tensor") % 2
    owners = ring.owners()

    def arrange(array):
        array = jnp.where(core == 0, array, array[::-1])
        return jnp.concatenate(
            [lax.dynamic_slice_in_dim(array, owners[j] * block, block, axis=2) for j in range(n)], axis=2
        )

    def restore(own, other):
        array = jnp.stack([jnp.where(core == 0, own, other), jnp.where(core == 0, other, own)])
        places = jnp.asarray(np.argsort(np.array(ring.order)).astype(np.int32))
        where = (places - ring.place()) % n
        return jnp.concatenate(
            [lax.dynamic_slice_in_dim(array, where[j] * block, block, axis=2) for j in range(n)], axis=2
        )

    gains = jnp.concatenate([attention_gain, feedforward_gain])
    fill = jnp.zeros((8, q_cols + 2 * kv_cols), BF16)
    fill = lax.dynamic_update_slice(fill, gains[None, :], (0, 0))
    first = jnp.concatenate(
        [jnp.concatenate([query_weight, key_matrix, value_matrix], axis=1), fill], axis=0
    )
    first_pieces = ring.gather(first)
    qkv_w = jnp.concatenate([p[:block] for p in first_pieces], axis=0)
    gain_a = jnp.concatenate([p[block, :block] for p in first_pieces]).astype(F32)
    gain_f = jnp.concatenate([p[block, block : 2 * block] for p in first_pieces]).astype(F32)
    out_w = jnp.concatenate(ring.gather(out_weight), axis=1)
    gate_w = jnp.concatenate(ring.gather(gate_weight), axis=0)
    up_w = jnp.concatenate(ring.gather(up_weight), axis=0)
    down_w = jnp.concatenate(ring.gather(down_weight), axis=1)

    keep = layer_keep.astype(F32)
    keep = jnp.where(core == 0, keep, keep[::-1])
    prefix = jnp.where(core == 0, prefix_length, prefix_length[::-1])
    x = arrange(inputs)
    dy = arrange(cotangent)

    cos_part, sin_part = rotary_tables(length)
    cos_part, sin_part = cos_part[None, :, None, :], sin_part[None, :, None, :]
    position = jnp.arange(length, dtype=jnp.int32)

    rows = x.reshape(seqs * length, width).astype(F32)
    r1 = lax.rsqrt(jnp.mean(rows * rows, axis=-1, keepdims=True) + EPSILON)
    n1 = (rows * r1 * gain_a).astype(BF16)
    qkv = dot(n1, qkv_w)
    q = rotate(qkv[:, :q_cols].reshape(seqs, length, heads, HEAD_SIZE), cos_part, sin_part).astype(BF16)
    k = rotate(qkv[:, q_cols : q_cols + kv_cols].reshape(seqs, length, kv_heads, HEAD_SIZE), cos_part, sin_part).astype(BF16)
    v = qkv[:, q_cols + kv_cols :].astype(BF16).reshape(seqs, length, kv_heads, HEAD_SIZE)
    q = q.reshape(seqs, length, kv_heads, repeat, HEAD_SIZE)
    scores = jnp.einsum("bqgrd,bkgd->bgrqk", q, k, preferred_element_type=F32) * scale
    allowed = (position[None, None, :] <= position[None, :, None]) | (position[None, None, :] < prefix[:, None, None])
    scores = jnp.where(allowed[:, None, None], scores, NEGATIVE)
    exps = jnp.exp(scores - jnp.max(scores, axis=-1, keepdims=True))
    probs = exps / jnp.sum(exps, axis=-1, keepdims=True)
    probs_low = probs.astype(BF16)
    mixed = jnp.einsum("bgrqk,bkgd->bqgrd", probs_low, v, preferred_element_type=F32)
    mixed = mixed.reshape(seqs * length, q_cols).astype(BF16)
    a_own = tensor_sum(dot(mixed, out_w).reshape(seqs, length, width))
    x_own = x[0].astype(F32)
    hid = x_own + keep[0] * a_own
    r2 = lax.rsqrt(jnp.mean(hid * hid, axis=-1, keepdims=True) + EPSILON)
    n2_own = (hid * r2 * gain_f).astype(BF16)
    n2 = jnp.concatenate([n2_own, swap_core(n2_own)], axis=0)

    g = dot(n2, gate_w)
    u = dot(n2, up_w)
    sig = jax.nn.sigmoid(g)
    swish = g * sig
    m = (swish * u).astype(BF16)
    f_own = tensor_sum(dot(m, down_w).reshape(seqs, length, width))
    out_own = (hid + keep[0] * f_own).astype(BF16)
    output = restore(out_own, swap_core(out_own))

    df = (keep[:, None, None] * dy.astype(F32)).astype(BF16).reshape(seqs * length, width)
    grad_down = dot_ta(m, df)
    dm = dot_tb(df, down_w)
    dg = (dm * u * sig * (1.0 + g * (1.0 - sig))).astype(BF16)
    du = (dm * swish).astype(BF16)
    grad_down = ring.scatter([grad_down[:, j * block : (j + 1) * block] for j in range(n)])
    grad_gate = dot_ta(n2, dg)
    grad_gate = ring.scatter([grad_gate[j * block : (j + 1) * block] for j in range(n)])
    grad_up = dot_ta(n2, du)
    grad_up = ring.scatter([grad_up[j * block : (j + 1) * block] for j in range(n)])
    dn2 = tensor_sum((dot_tb(dg, gate_w) + dot_tb(du, up_w)).reshape(seqs, length, width))
    gain_f_sum = jnp.sum(dn2 * hid * r2, axis=0)
    scaled = dn2 * gain_f
    dh = dy[0].astype(F32) + r2 * scaled - hid * (r2 * r2 * r2) * jnp.mean(scaled * hid, axis=-1, keepdims=True)
    da_own = (keep[0] * dh).astype(BF16)
    da = jnp.concatenate([da_own, swap_core(da_own)], axis=0)

    grad_out = dot_ta(mixed, da)
    grad_out = ring.scatter([grad_out[:, j * block : (j + 1) * block] for j in range(n)])
    dmixed = dot_tb(da, out_w).astype(BF16).reshape(seqs, length, kv_heads, repeat, HEAD_SIZE)
    dprobs = jnp.einsum("bqgrd,bkgd->bgrqk", dmixed, v, preferred_element_type=F32)
    dv = jnp.einsum("bgrqk,bqgrd->bkgd", probs_low, dmixed, preferred_element_type=F32).astype(BF16)
    inner = jnp.sum(probs * dprobs, axis=-1, keepdims=True)
    dscores = (probs * (dprobs - inner)).astype(BF16)
    dq = jnp.einsum("bgrqk,bkgd->bqgrd", dscores, k, preferred_element_type=F32) * scale
    dk = jnp.einsum("bgrqk,bqgrd->bkgd", dscores, q, preferred_element_type=F32) * scale
    dq = rotate(dq.reshape(seqs, length, heads, HEAD_SIZE), cos_part, -sin_part).astype(BF16)
    dk = rotate(dk, cos_part, -sin_part).astype(BF16)
    dqkv = jnp.concatenate(
        [d.reshape(seqs * length, -1) for d in (dq, dk, dv)], axis=1
    )
    grad_qkv = dot_ta(n1, dqkv)
    grad_qkv = ring.scatter([grad_qkv[j * block : (j + 1) * block] for j in range(n)])
    dn1 = tensor_sum(dot_tb(dqkv, qkv_w).reshape(seqs, length, width))
    r1_own = r1[:length]
    gain_a_sum = jnp.sum(dn1 * x_own * r1_own, axis=0)
    scaled = dn1 * gain_a
    dx = dh + r1_own * scaled - x_own * (r1_own * r1_own * r1_own) * jnp.mean(scaled * x_own, axis=-1, keepdims=True)
    dx = dx.astype(BF16)
    input_grad = restore(dx, swap_core(dx))

    sums = jnp.stack([gain_a_sum, gain_f_sum]).reshape(2, n, block)
    sums = sums + swap_core(sums)
    up = sums[:, ring.half]
    down = None
    for hop in range(ring.half - 1, -1, -1):
        up = lax.ppermute(up, "dp", ring.right)
        up = up + sums[:, hop]
    if n > 2:
        down = sums[:, ring.half + 1]
        for hop in range(ring.half - 2, -1, -1):
            down = lax.ppermute(down, "dp", ring.left)
            if hop:
                down = down + sums[:, n - hop]
        up = up + down
    return (
        output,
        input_grad,
        up[0],
        grad_qkv[:, :q_cols],
        grad_qkv[:, q_cols : q_cols + kv_cols],
        grad_qkv[:, q_cols + kv_cols :],
        grad_out,
        up[1],
        grad_gate,
        grad_up,
        grad_down,
    )


def solution(mesh):
    ring = Ring(mesh.shape["dp"])
    if mesh.shape["tensor"] != 4:
        raise ValueError("tensor axis")
    row, col = P("dp", "tensor"), P("tensor", "dp")
    data = P("dp", None, None)
    return jax.shard_map(
        lambda *args: local(ring, *args),
        mesh=mesh,
        in_specs=(data, P("dp"), row, row, row, col, P("dp"), row, row, col, data, P("dp"), P("dp")),
        out_specs=(data, data, P("dp"), row, row, row, col, P("dp"), row, row, col),
        check_vma=False,
    )
```

```python
import functools
import math

import jax
import jax.numpy as jnp
import numpy as np
from jax import lax
from jax.experimental import pallas as pl
from jax.experimental.pallas import tpu as pltpu
from jax.sharding import PartitionSpec as P

HEAD_SIZE = 128
EPSILON = 1e-05
NEGATIVE = -1e30
BF16 = jnp.bfloat16
F32 = jnp.float32
MESH = pl.DeviceIdType.MESH
HBM = pl.BlockSpec(memory_space=pltpu.HBM)
SMEM = pl.BlockSpec(memory_space=pltpu.SMEM)
ROWS = 256


def dot(a, b):
    return jnp.dot(a, b, preferred_element_type=F32)


def dot_ta(a, b):
    return lax.dot_general(a, b, (((0,), (0,)), ((), ())), preferred_element_type=F32)


def dot_tb(a, b):
    return lax.dot_general(a, b, (((1,), (1,)), ((), ())), preferred_element_type=F32)


def spec(rows, cols):
    return pl.BlockSpec((rows, cols), lambda i: (i, 0))


def fixed(*shape):
    return pl.BlockSpec(shape, lambda i: (0,) * len(shape))


def tiles(total, step=256):
    return [(at, min(step, total - at)) for at in range(0, total, step)]


def gain_row(gains_ref, which):
    n = gains_ref.shape[0]
    return jnp.concatenate([gains_ref[j, which : which + 1, :] for j in range(n)], axis=1).astype(F32)


def turn(values, cos, sin):
    return values * cos + pltpu.roll(values, HEAD_SIZE // 2, axis=1) * sin


class Place:
    def __init__(self, n):
        self.n = n
        self.me = lax.axis_index("dp")
        odd = self.me % 2
        self.p = (1 - odd) * (self.me // 2) + odd * (n - 1 - self.me // 2)
        tensor = lax.axis_index("tensor")
        self.core = tensor % 2
        self.core_peer = tensor + 1 - 2 * self.core
        self.chip_peer = (tensor + 2) % 4
        self.right = self.at(1)
        self.left = self.at(-1)

    def at(self, j):
        p = (self.p + j + 2 * self.n) % self.n
        low = p // (self.n // 2)
        return (1 - low) * 2 * p + low * (2 * (self.n - 1 - p) + 1)

    def greet(self):
        barrier = pltpu.get_barrier_semaphore()
        for peer in (self.left, self.right):
            pl.semaphore_signal(barrier, inc=1, device_id={"dp": peer}, device_id_type=MESH)
        for peer in (self.core_peer, self.chip_peer):
            pl.semaphore_signal(barrier, inc=1, device_id={"tensor": peer}, device_id_type=MESH)
        pl.semaphore_wait(barrier, 4)


class Gather:
    def __init__(self, place, shard, whole, where, local_sem, send_sems, recv_sems):
        self.place, self.shard, self.whole, self.where = place, shard, whole, where
        self.send_sems, self.recv_sems = send_sems, recv_sems
        self.hops = place.n // 2
        self.copies = {}
        self.local = pltpu.make_async_copy(shard, where(whole, place.me, None), local_sem)
        self.local.start()

    def send(self, way, hop):
        place = self.place
        sign = 1 - 2 * way
        owner = place.at(-sign * (hop - 1))
        half = way if hop == self.hops else None
        target = self.where(self.whole, owner, half)
        if hop > 1:
            self.copies[way, hop - 1].wait_recv()
            source = target
        elif half is None:
            source = self.shard
        else:
            rows = self.shard.shape[0] // 2
            source = self.shard.at[pl.ds(half * rows, rows)]
        copy = pltpu.make_async_remote_copy(
            src_ref=source,
            dst_ref=target,
            send_sem=self.send_sems.at[way, hop - 1],
            recv_sem=self.recv_sems.at[way, hop - 1],
            device_id={"dp": place.right if way == 0 else place.left},
            device_id_type=MESH,
        )
        copy.start()
        self.copies[way, hop] = copy

    def step(self, hop):
        self.send(0, hop)
        self.send(1, hop)

    def arrived(self):
        self.local.wait()
        self.copies[0, self.hops].wait_recv()
        self.copies[1, self.hops].wait_recv()

    def drain(self):
        for copy in self.copies.values():
            copy.wait_send()


def by_rows(rows):
    def where(whole, owner, half):
        if half is None:
            return whole.at[pl.ds(pl.multiple_of(owner * rows, rows), rows)]
        return whole.at[pl.ds(pl.multiple_of(owner * rows + half * (rows // 2), rows // 2), rows // 2)]

    return where


def by_cols(rows, cols):
    def where(whole, owner, half):
        at = pl.ds(pl.multiple_of(owner * cols, cols), cols)
        if half is None:
            return whole.at[:, at]
        return whole.at[pl.ds(half * (rows // 2), rows // 2), at]

    return where


def by_slot(whole, owner, half):
    if half is None:
        return whole.at[owner]
    rows = whole.shape[1] // 2
    return whole.at[owner, pl.ds(half * rows, rows)]


class Swap:
    def __init__(self, source, target, peer, send_sem, recv_sem):
        self.copy = pltpu.make_async_remote_copy(
            src_ref=source, dst_ref=target, send_sem=send_sem, recv_sem=recv_sem,
            device_id={"tensor": peer}, device_id_type=MESH,
        )
        self.copy.start()


def forward_kernel(
    n, length, x_hbm, dy_hbm, gains_in, wq_in, wk_in, wv_in, wo_in, wg_in, wu_in, wd_in, cos_hbm, sin_hbm, keep_ref, prefix_ref,
    gains_w, wq, wk, wv, wo, wg, wu, wd, n1_hbm, q_hbm, k_hbm, v_hbm, ob_hbm, hid_hbm, n2_hbm, m_hbm, fa_hbm, fb_hbm, gd_hbm,
    own_hbm, other_hbm, peer_hbm, near_hbm, far_hbm,
    local_sems, send_sems, recv_sems, swap_send, swap_recv,
):
    place = Place(n)
    core = place.core
    place.greet()
    tokens, width = x_hbm.shape
    scale = 1.0 / math.sqrt(HEAD_SIZE)
    arrays = (
        (gains_in, gains_w, by_slot),
        (wq_in, wq, by_rows(wq_in.shape[0])),
        (wk_in, wk, by_rows(wk_in.shape[0])),
        (wv_in, wv, by_rows(wv_in.shape[0])),
        (wo_in, wo, by_cols(*wo_in.shape)),
        (wg_in, wg, by_rows(wg_in.shape[0])),
        (wu_in, wu, by_rows(wu_in.shape[0])),
        (wd_in, wd, by_cols(*wd_in.shape)),
    )
    rings = [
        Gather(place, shard, whole, where, local_sems.at[i], send_sems.at[i], recv_sems.at[i])
        for i, (shard, whole, where) in enumerate(arrays)
    ]
    hops = n // 2
    starts = (0, 0, 0, 0, 1, 3, 6, 9)
    todo = sorted((starts[i] + hop, i, hop) for i in range(len(rings)) for hop in range(1, hops + 1))

    def pump(slot):
        while todo and todo[0][0] <= slot:
            _, i, hop = todo.pop(0)
            rings[i].step(hop)

    own_rows = pl.ds(pl.multiple_of(core * length, length), length)
    other_rows = pl.ds(pl.multiple_of((1 - core) * length, length), length)

    pump(5)
    for i in range(4):
        rings[i].arrived()

    def project(x_ref, gains_ref, wq_ref, wk_ref, wv_ref, cos_ref, sin_ref, n1_ref, q_ref, k_ref, v_ref):
        gain = gain_row(gains_ref, 0)

        @pl.loop(0, ROWS, step=32)
        def _(at):
            part = pl.ds(pl.multiple_of(at, 32), 32)
            xf = x_ref[part, :].astype(F32)
            r1 = lax.rsqrt(jnp.mean(xf * xf, axis=-1, keepdims=True) + EPSILON)
            n1_ref[part, :] = (xf * r1 * gain).astype(BF16)

        rows = n1_ref[...]
        cos, sin = cos_ref[...], sin_ref[...]
        for w_ref, o_ref in ((wq_ref, q_ref), (wk_ref, k_ref)):
            for at in range(0, w_ref.shape[1], HEAD_SIZE):
                head = slice(at, at + HEAD_SIZE)
                o_ref[:, head] = turn(dot(rows, w_ref[:, head]), cos, sin).astype(BF16)
        v_ref[...] = dot(rows, wv_ref[...]).astype(BF16)

    q_cols, kv_cols = wq.shape[1], wk.shape[1]
    per = length // ROWS
    turns = pl.BlockSpec((ROWS, HEAD_SIZE), lambda i: (i % per, 0))
    pltpu.emit_pipeline(
        project,
        grid=(tokens // ROWS,),
        in_specs=[spec(ROWS, width), fixed(*gains_w.shape), fixed(*wq.shape), fixed(*wk.shape), fixed(*wv.shape), turns, turns],
        out_specs=[spec(ROWS, width), spec(ROWS, q_cols), spec(ROWS, kv_cols), spec(ROWS, kv_cols)],
    )(x_hbm, gains_w, wq, wk, wv, cos_hbm, sin_hbm, n1_hbm, q_hbm, k_hbm, v_hbm)
    pump(6)

    repeat = q_cols // kv_cols

    def attend(which, q_ref, k_ref, v_ref, o_ref):
        prefix = prefix_ref[which]
        keys, values = k_ref[...], v_ref[...]

        @pl.loop(0, length, step=128)
        def _(at):
            part = pl.ds(pl.multiple_of(at, 128), 128)
            s = dot_tb(q_ref[part, :], keys) * scale
            row = lax.broadcasted_iota(jnp.int32, s.shape, 0) + at
            col = lax.broadcasted_iota(jnp.int32, s.shape, 1)
            s = jnp.where((col <= row) | (col < prefix), s, NEGATIVE)
            e = jnp.exp(s - jnp.max(s, axis=-1, keepdims=True))
            p = e / jnp.sum(e, axis=-1, keepdims=True)
            o_ref[part, :] = dot(p.astype(BF16), values).astype(BF16)

    for which in range(2):
        seq = pl.ds(which * length, length)
        pltpu.emit_pipeline(
            functools.partial(attend, which),
            grid=(q_cols // HEAD_SIZE,),
            in_specs=[
                pl.BlockSpec((length, HEAD_SIZE), lambda h: (0, h)),
                pl.BlockSpec((length, HEAD_SIZE), lambda h: (0, h // repeat)),
                pl.BlockSpec((length, HEAD_SIZE), lambda h: (0, h // repeat)),
            ],
            out_specs=[pl.BlockSpec((length, HEAD_SIZE), lambda h: (0, h))],
        )(q_hbm.at[seq], k_hbm.at[seq], v_hbm.at[seq], ob_hbm.at[seq])
        pump(7 + which)

    rings[4].arrived()

    def mix(ob_ref, wo_ref, o_ref):
        o_ref[...] = dot(ob_ref[...], wo_ref[...]).astype(o_ref.dtype)

    def project_out(rows, target):
        pltpu.emit_pipeline(
            mix, grid=(length // ROWS,), in_specs=[spec(ROWS, q_cols), fixed(*wo.shape)], out_specs=[spec(ROWS, width)]
        )(ob_hbm.at[rows], wo, target)

    project_out(other_rows, other_hbm)
    to_core = Swap(other_hbm, peer_hbm, place.core_peer, swap_send.at[0], swap_recv.at[0])
    project_out(own_rows, own_hbm)
    to_core.copy.wait_recv()

    def nearby(own_ref, peer_ref, near_ref):
        near_ref[...] = (own_ref[...] + peer_ref[...].astype(F32)).astype(BF16)

    pltpu.emit_pipeline(
        nearby, grid=(length // 64,), in_specs=[spec(64, width)] * 2, out_specs=[spec(64, width)]
    )(own_hbm, peer_hbm, near_hbm)
    to_chip = Swap(near_hbm, far_hbm, place.chip_peer, swap_send.at[1], swap_recv.at[1])
    pump(10)
    to_chip.copy.wait_recv()

    def residual(near_ref, far_ref, x_ref, gains_ref, hid_ref, n2_ref):
        gain = gain_row(gains_ref, 1)
        a = near_ref[...].astype(F32) + far_ref[...].astype(F32)
        h = x_ref[...].astype(F32) + keep_ref[core] * a
        hid_ref[...] = h
        r2 = lax.rsqrt(jnp.mean(h * h, axis=-1, keepdims=True) + EPSILON)
        n2_ref[...] = (h * r2 * gain).astype(BF16)

    pltpu.emit_pipeline(
        residual,
        grid=(length // 32,),
        in_specs=[spec(32, width)] * 3 + [fixed(*gains_w.shape)],
        out_specs=[spec(32, width)] * 2,
    )(near_hbm, far_hbm, x_hbm.at[own_rows], gains_w, hid_hbm, n2_hbm.at[own_rows])
    share = Swap(n2_hbm.at[own_rows], n2_hbm.at[own_rows], place.core_peer, swap_send.at[2], swap_recv.at[2])
    pump(11)
    share.copy.wait_recv()
    rings[5].arrived()
    rings[6].arrived()

    hidden = wg.shape[1]

    def feed(n2_ref, wg_ref, wu_ref, m_ref, fa_ref, fb_ref):
        rows = n2_ref[...]
        for at, size in tiles(hidden):
            cols = slice(at, at + size)
            g = dot(rows, wg_ref[:, cols])
            u = dot(rows, wu_ref[:, cols])
            sig = 1.0 / (1.0 + jnp.exp(-g))
            swish = g * sig
            m_ref[:, cols] = (swish * u).astype(BF16)
            fa_ref[:, cols] = u * sig * (1.0 + g * (1.0 - sig))
            fb_ref[:, cols] = swish

    pltpu.emit_pipeline(
        feed,
        grid=(tokens // ROWS,),
        in_specs=[spec(ROWS, width), fixed(*wg.shape), fixed(*wu.shape)],
        out_specs=[spec(ROWS, hidden)] * 3,
    )(n2_hbm, wg, wu, m_hbm, fa_hbm, fb_hbm)
    pump(12)

    def down_grad(m_ref, dy_ref, o_ref):
        total = None
        for which in range(2):
            seq = slice(which * length, (which + 1) * length)
            df = (dy_ref[seq, :].astype(F32) * keep_ref[which]).astype(BF16)
            term = dot_ta(m_ref[seq, :], df)
            total = term if total is None else total + term
        o_ref[...] = total.astype(BF16)

    cols = pl.BlockSpec((tokens, 256), lambda i: (0, i))
    pltpu.emit_pipeline(
        down_grad,
        grid=(width // 256,),
        in_specs=[fixed(tokens, hidden), cols],
        out_specs=[pl.BlockSpec((hidden, 256), lambda i: (0, i))],
    )(m_hbm, dy_hbm, gd_hbm)
    pump(100)
    rings[7].arrived()
    for ring in rings:
        ring.drain()
    for swap in (to_core, to_chip, share):
        swap.copy.wait_send()


def forward(n, x, dy, gains, wq, wk, wv, wo, wg, wu, wd, cos, sin, keep, prefix, length):
    tokens, width = x.shape
    shape = jax.ShapeDtypeStruct
    ff = wg.shape[1]
    outs = [
        shape((n,) + gains.shape, BF16),
        shape((width, wq.shape[1]), BF16),
        shape((width, wk.shape[1]), BF16),
        shape((width, wv.shape[1]), BF16),
        shape((wo.shape[0], width), BF16),
        shape((width, ff), BF16),
        shape((width, ff), BF16),
        shape((ff, width), BF16),
        shape((tokens, width), BF16),
        shape((tokens, wq.shape[1]), BF16),
        shape((tokens, wk.shape[1]), BF16),
        shape((tokens, wv.shape[1]), BF16),
        shape((tokens, wq.shape[1]), BF16),
        shape((length, width), F32),
        shape((tokens, width), BF16),
        shape((tokens, ff), BF16),
        shape((tokens, ff), F32),
        shape((tokens, ff), F32),
        shape((ff, width), BF16),
        shape((length, width), F32),
        shape((length, width), BF16),
        shape((length, width), BF16),
        shape((length, width), BF16),
        shape((length, width), BF16),
    ]
    return pl.pallas_call(
        functools.partial(forward_kernel, n, length),
        out_shape=outs,
        in_specs=[HBM] * 12 + [SMEM] * 2,
        out_specs=[HBM] * len(outs),
        scratch_shapes=[
            pltpu.SemaphoreType.DMA((8,)),
            pltpu.SemaphoreType.DMA((8, 2, n // 2)),
            pltpu.SemaphoreType.DMA((8, 2, n // 2)),
            pltpu.SemaphoreType.DMA((3,)),
            pltpu.SemaphoreType.DMA((3,)),
        ],
        compiler_params=pltpu.CompilerParams(collective_id=0, has_side_effects=True, vmem_limit_bytes=60 * 1024 * 1024),
    )(x, dy, gains, wq, wk, wv, wo, wg, wu, wd, cos, sin, keep, prefix)


def rotary_tables(length_total):
    half_width = HEAD_SIZE // 2
    frequency = (10000.0 ** (-(np.arange(half_width, dtype=np.float32) * 2.0) / HEAD_SIZE)).astype(np.float32)
    angles = np.arange(length_total, dtype=np.float32)[:, None] * frequency[None, :]
    return (jnp.asarray(np.cos(angles)), jnp.asarray(np.sin(angles)))


def rotate(values, cos_part, sin_part):
    first, second = jnp.split(values, 2, axis=-1)
    return jnp.concatenate(
        [first * cos_part - second * sin_part, first * sin_part + second * cos_part], axis=-1
    )


class Ring:
    def __init__(self, size):
        self.size = size
        self.half = size // 2
        self.order = [2 * p if p < self.half else 2 * (size - 1 - p) + 1 for p in range(size)]
        self.right = [(self.order[p], self.order[(p + 1) % size]) for p in range(size)]
        self.left = [(b, a) for a, b in self.right]

    def place(self):
        me = lax.axis_index("dp")
        odd = me % 2
        return (1 - odd) * (me // 2) + odd * (self.size - 1 - me // 2)

    def owners(self):
        return jnp.asarray(np.array(self.order, np.int32))[(self.place() + np.arange(self.size)) % self.size]

    def gather(self, shard):
        n, m = self.size, self.half
        pieces = [None] * n
        pieces[0] = shard
        from_left, from_right = shard, shard
        for hop in range(1, m):
            from_left = lax.ppermute(from_left, "dp", self.right)
            from_right = lax.ppermute(from_right, "dp", self.left)
            pieces[n - hop] = from_left
            pieces[hop] = from_right
        rows = shard.shape[0] // 2
        top = lax.ppermute(from_left[:rows], "dp", self.right)
        low = lax.ppermute(from_right[rows:], "dp", self.left)
        pieces[m] = jnp.concatenate([top, low], axis=0)
        return pieces

    def scatter(self, parts):
        n, m = self.size, self.half
        rows = parts[0].shape[0] // 2
        kind = BF16
        up = lax.ppermute(parts[m][:rows].astype(kind), "dp", self.right)
        down = lax.ppermute(parts[m][rows:].astype(kind), "dp", self.left)
        for hop in range(m - 1, 0, -1):
            mine_up, mine_down = parts[hop], parts[n - hop]
            if hop == m - 1:
                mine_up = jnp.concatenate([mine_up[:rows] + up.astype(F32), mine_up[rows:]], axis=0)
                mine_down = jnp.concatenate([mine_down[:rows], mine_down[rows:] + down.astype(F32)], axis=0)
            else:
                mine_up = mine_up + up.astype(F32)
                mine_down = mine_down + down.astype(F32)
            up = lax.ppermute(mine_up.astype(kind), "dp", self.right)
            down = lax.ppermute(mine_down.astype(kind), "dp", self.left)
        if m == 1:
            return jnp.concatenate([parts[0][:rows] + up.astype(F32), parts[0][rows:] + down.astype(F32)], axis=0)
        return parts[0] + up.astype(F32) + down.astype(F32)


    def small_scatter(self, sums):
        up = sums[:, self.half]
        for hop in range(self.half - 1, -1, -1):
            up = lax.ppermute(up, "dp", self.right)
            up = up + sums[:, hop]
        if self.size > 2:
            down = sums[:, self.half + 1]
            for hop in range(self.half - 2, -1, -1):
                down = lax.ppermute(down, "dp", self.left)
                if hop:
                    down = down + sums[:, self.size - hop]
            up = up + down
        return up


CORE_PAIRS = [(0, 1), (1, 0), (2, 3), (3, 2)]
CHIP_PAIRS = [(0, 2), (2, 0), (1, 3), (3, 1)]


def swap_core(value):
    return lax.ppermute(value, "tensor", CORE_PAIRS)


def swap_chip(value):
    return lax.ppermute(value, "tensor", CHIP_PAIRS)


def tensor_sum(part):
    near = part[0] + swap_core(part[1].astype(BF16)).astype(F32)
    near = near.astype(BF16)
    return near.astype(F32) + swap_chip(near).astype(F32)


def ring_local(ring, inputs, attention_gain, query_weight, key_matrix, value_matrix, out_weight, feedforward_gain,
          gate_weight, up_weight, down_weight, cotangent, layer_keep, prefix_length):
    n = ring.size
    seqs, length, width = inputs.shape
    block = width // n
    q_cols, kv_cols = query_weight.shape[1], key_matrix.shape[1]
    heads = q_cols // HEAD_SIZE
    kv_heads = kv_cols // HEAD_SIZE
    repeat = heads // kv_heads
    scale = 1.0 / math.sqrt(HEAD_SIZE)
    core = lax.axis_index("tensor") % 2
    owners = ring.owners()

    def arrange(array):
        array = jnp.where(core == 0, array, array[::-1])
        return jnp.concatenate(
            [lax.dynamic_slice_in_dim(array, owners[j] * block, block, axis=2) for j in range(n)], axis=2
        )

    def restore(own, other):
        array = jnp.stack([jnp.where(core == 0, own, other), jnp.where(core == 0, other, own)])
        places = jnp.asarray(np.argsort(np.array(ring.order)).astype(np.int32))
        where = (places - ring.place()) % n
        return jnp.concatenate(
            [lax.dynamic_slice_in_dim(array, where[j] * block, block, axis=2) for j in range(n)], axis=2
        )

    gains = jnp.concatenate([attention_gain, feedforward_gain])
    fill = jnp.zeros((8, q_cols + 2 * kv_cols), BF16)
    fill = lax.dynamic_update_slice(fill, gains[None, :], (0, 0))
    first = jnp.concatenate(
        [jnp.concatenate([query_weight, key_matrix, value_matrix], axis=1), fill], axis=0
    )
    first_pieces = ring.gather(first)
    qkv_w = jnp.concatenate([p[:block] for p in first_pieces], axis=0)
    gain_a = jnp.concatenate([p[block, :block] for p in first_pieces]).astype(F32)
    gain_f = jnp.concatenate([p[block, block : 2 * block] for p in first_pieces]).astype(F32)
    out_w = jnp.concatenate(ring.gather(out_weight), axis=1)
    gate_w = jnp.concatenate(ring.gather(gate_weight), axis=0)
    up_w = jnp.concatenate(ring.gather(up_weight), axis=0)
    down_w = jnp.concatenate(ring.gather(down_weight), axis=1)

    keep = layer_keep.astype(F32)
    keep = jnp.where(core == 0, keep, keep[::-1])
    prefix = jnp.where(core == 0, prefix_length, prefix_length[::-1])
    x = arrange(inputs)
    dy = arrange(cotangent)

    cos_part, sin_part = rotary_tables(length)
    cos_part, sin_part = cos_part[None, :, None, :], sin_part[None, :, None, :]
    position = jnp.arange(length, dtype=jnp.int32)

    rows = x.reshape(seqs * length, width).astype(F32)
    r1 = lax.rsqrt(jnp.mean(rows * rows, axis=-1, keepdims=True) + EPSILON)
    n1 = (rows * r1 * gain_a).astype(BF16)
    qkv = dot(n1, qkv_w)
    q = rotate(qkv[:, :q_cols].reshape(seqs, length, heads, HEAD_SIZE), cos_part, sin_part).astype(BF16)
    k = rotate(qkv[:, q_cols : q_cols + kv_cols].reshape(seqs, length, kv_heads, HEAD_SIZE), cos_part, sin_part).astype(BF16)
    v = qkv[:, q_cols + kv_cols :].astype(BF16).reshape(seqs, length, kv_heads, HEAD_SIZE)
    q = q.reshape(seqs, length, kv_heads, repeat, HEAD_SIZE)
    scores = jnp.einsum("bqgrd,bkgd->bgrqk", q, k, preferred_element_type=F32) * scale
    allowed = (position[None, None, :] <= position[None, :, None]) | (position[None, None, :] < prefix[:, None, None])
    scores = jnp.where(allowed[:, None, None], scores, NEGATIVE)
    exps = jnp.exp(scores - jnp.max(scores, axis=-1, keepdims=True))
    probs = exps / jnp.sum(exps, axis=-1, keepdims=True)
    probs_low = probs.astype(BF16)
    mixed = jnp.einsum("bgrqk,bkgd->bqgrd", probs_low, v, preferred_element_type=F32)
    mixed = mixed.reshape(seqs * length, q_cols).astype(BF16)
    a_own = tensor_sum(dot(mixed, out_w).reshape(seqs, length, width))
    x_own = x[0].astype(F32)
    hid = x_own + keep[0] * a_own
    r2 = lax.rsqrt(jnp.mean(hid * hid, axis=-1, keepdims=True) + EPSILON)
    n2_own = (hid * r2 * gain_f).astype(BF16)
    n2 = jnp.concatenate([n2_own, swap_core(n2_own)], axis=0)

    g = dot(n2, gate_w)
    u = dot(n2, up_w)
    sig = jax.nn.sigmoid(g)
    swish = g * sig
    m = (swish * u).astype(BF16)
    f_own = tensor_sum(dot(m, down_w).reshape(seqs, length, width))
    out_own = (hid + keep[0] * f_own).astype(BF16)
    output = restore(out_own, swap_core(out_own))

    df = (keep[:, None, None] * dy.astype(F32)).astype(BF16).reshape(seqs * length, width)
    grad_down = dot_ta(m, df)
    dm = dot_tb(df, down_w)
    dg = (dm * u * sig * (1.0 + g * (1.0 - sig))).astype(BF16)
    du = (dm * swish).astype(BF16)
    grad_down = ring.scatter([grad_down[:, j * block : (j + 1) * block] for j in range(n)])
    grad_gate = dot_ta(n2, dg)
    grad_gate = ring.scatter([grad_gate[j * block : (j + 1) * block] for j in range(n)])
    grad_up = dot_ta(n2, du)
    grad_up = ring.scatter([grad_up[j * block : (j + 1) * block] for j in range(n)])
    dn2 = tensor_sum((dot_tb(dg, gate_w) + dot_tb(du, up_w)).reshape(seqs, length, width))
    gain_f_sum = jnp.sum(dn2 * hid * r2, axis=0)
    scaled = dn2 * gain_f
    dh = dy[0].astype(F32) + r2 * scaled - hid * (r2 * r2 * r2) * jnp.mean(scaled * hid, axis=-1, keepdims=True)
    da_own = (keep[0] * dh).astype(BF16)
    da = jnp.concatenate([da_own, swap_core(da_own)], axis=0)

    grad_out = dot_ta(mixed, da)
    grad_out = ring.scatter([grad_out[:, j * block : (j + 1) * block] for j in range(n)])
    dmixed = dot_tb(da, out_w).astype(BF16).reshape(seqs, length, kv_heads, repeat, HEAD_SIZE)
    dprobs = jnp.einsum("bqgrd,bkgd->bgrqk", dmixed, v, preferred_element_type=F32)
    dv = jnp.einsum("bgrqk,bqgrd->bkgd", probs_low, dmixed, preferred_element_type=F32).astype(BF16)
    inner = jnp.sum(probs * dprobs, axis=-1, keepdims=True)
    dscores = (probs * (dprobs - inner)).astype(BF16)
    dq = jnp.einsum("bgrqk,bkgd->bqgrd", dscores, k, preferred_element_type=F32) * scale
    dk = jnp.einsum("bgrqk,bqgrd->bkgd", dscores, q, preferred_element_type=F32) * scale
    dq = rotate(dq.reshape(seqs, length, heads, HEAD_SIZE), cos_part, -sin_part).astype(BF16)
    dk = rotate(dk, cos_part, -sin_part).astype(BF16)
    dqkv = jnp.concatenate(
        [d.reshape(seqs * length, -1) for d in (dq, dk, dv)], axis=1
    )
    grad_qkv = dot_ta(n1, dqkv)
    grad_qkv = ring.scatter([grad_qkv[j * block : (j + 1) * block] for j in range(n)])
    dn1 = tensor_sum(dot_tb(dqkv, qkv_w).reshape(seqs, length, width))
    r1_own = r1[:length]
    gain_a_sum = jnp.sum(dn1 * x_own * r1_own, axis=0)
    scaled = dn1 * gain_a
    dx = dh + r1_own * scaled - x_own * (r1_own * r1_own * r1_own) * jnp.mean(scaled * x_own, axis=-1, keepdims=True)
    dx = dx.astype(BF16)
    input_grad = restore(dx, swap_core(dx))

    sums = jnp.stack([gain_a_sum, gain_f_sum]).reshape(2, n, block)
    sums = sums + swap_core(sums)
    gain_grads = ring.small_scatter(sums)
    return (
        output,
        input_grad,
        gain_grads[0],
        grad_qkv[:, :q_cols],
        grad_qkv[:, q_cols : q_cols + kv_cols],
        grad_qkv[:, q_cols + kv_cols :],
        grad_out,
        gain_grads[1],
        grad_gate,
        grad_up,
        grad_down,
    )


def local(ring, inputs, attention_gain, query_weight, key_matrix, value_matrix, out_weight, feedforward_gain,
          gate_weight, up_weight, down_weight, cotangent, layer_keep, prefix_length):
    n = ring.size
    seqs, length, width = inputs.shape
    tokens = seqs * length
    block = width // n
    q_cols, kv_cols = query_weight.shape[1], key_matrix.shape[1]
    heads = q_cols // HEAD_SIZE
    kv_heads = kv_cols // HEAD_SIZE
    repeat = heads // kv_heads
    scale = 1.0 / math.sqrt(HEAD_SIZE)
    core = lax.axis_index("tensor") % 2
    owners = ring.owners()
    cos_part, sin_part = rotary_tables(length)
    cos_full = jnp.concatenate([cos_part, cos_part], axis=1)
    sin_full = jnp.concatenate([-sin_part, sin_part], axis=1)
    keep = layer_keep.astype(F32)
    gains = jnp.concatenate([attention_gain[None], feedforward_gain[None], jnp.zeros((14, block), BF16)], axis=0)
    x2 = inputs.reshape(tokens, width)
    dy2 = cotangent.reshape(tokens, width)
    (gains_w, wq, wk, wv, out_w, gate_w, up_w, down_w, n1, q, k, v, mixed, hid, n2, m, fa, fb, grad_down) = forward(
        n, x2, dy2, gains, query_weight, key_matrix, value_matrix, out_weight, gate_weight, up_weight, down_weight,
        cos_full, sin_full, keep, prefix_length, length,
    )[:19]
    gain_a = gains_w[:, 0].reshape(width).astype(F32)
    gain_f = gains_w[:, 1].reshape(width).astype(F32)
    qkv_w = jnp.concatenate([wq, wk, wv], axis=1)

    def rows_of(grad):
        return ring.scatter([lax.dynamic_slice_in_dim(grad, owners[j] * block, block, axis=0).astype(F32) for j in range(n)])

    def cols_of(grad):
        return ring.scatter([lax.dynamic_slice_in_dim(grad, owners[j] * block, block, axis=1).astype(F32) for j in range(n)])

    def mine(array):
        return lax.dynamic_index_in_dim(array.reshape(seqs, length, -1), core, 0, keepdims=False)

    def total(part):
        part = part.reshape(seqs, length, width)
        part = jnp.where(core == 0, part, part[::-1])
        return tensor_sum(part)

    def both(own):
        other = swap_core(own)
        return jnp.stack([jnp.where(core == 0, own, other), jnp.where(core == 0, other, own)])

    grad_down = cols_of(grad_down)
    df = (keep[:, None, None] * cotangent.astype(F32)).astype(BF16).reshape(tokens, width)
    dm = dot_tb(df, down_w)
    dg = (dm * fa).astype(BF16)
    du = (dm * fb).astype(BF16)
    grad_gate = rows_of(dot_ta(n2, dg))
    grad_up = rows_of(dot_ta(n2, du))
    dn2 = total(dot_tb(dg, gate_w) + dot_tb(du, up_w))
    f_own = total(dot(m, down_w))
    keep_own = keep[core]
    output = both((hid + keep_own * f_own).astype(BF16))
    r2 = lax.rsqrt(jnp.mean(hid * hid, axis=-1, keepdims=True) + EPSILON)
    gain_f_sum = jnp.sum(dn2 * hid * r2, axis=0)
    scaled = dn2 * gain_f
    dh = mine(dy2).astype(F32) + r2 * scaled - hid * (r2 * r2 * r2) * jnp.mean(scaled * hid, axis=-1, keepdims=True)
    da = both((keep_own * dh).astype(BF16)).reshape(tokens, width)
    grad_out = cols_of(dot_ta(mixed, da))
    q = q.reshape(seqs, length, kv_heads, repeat, HEAD_SIZE)
    k = k.reshape(seqs, length, kv_heads, HEAD_SIZE)
    v = v.reshape(seqs, length, kv_heads, HEAD_SIZE)
    position = jnp.arange(length, dtype=jnp.int32)
    scores = jnp.einsum("bqgrd,bkgd->bgrqk", q, k, preferred_element_type=F32) * scale
    allowed = (position[None, None, :] <= position[None, :, None]) | (position[None, None, :] < prefix_length[:, None, None])
    scores = jnp.where(allowed[:, None, None], scores, NEGATIVE)
    exps = jnp.exp(scores - jnp.max(scores, axis=-1, keepdims=True))
    probs = exps / jnp.sum(exps, axis=-1, keepdims=True)
    probs_low = probs.astype(BF16)
    dmixed = dot_tb(da, out_w).astype(BF16).reshape(seqs, length, kv_heads, repeat, HEAD_SIZE)
    dprobs = jnp.einsum("bqgrd,bkgd->bgrqk", dmixed, v, preferred_element_type=F32)
    dv = jnp.einsum("bgrqk,bqgrd->bkgd", probs_low, dmixed, preferred_element_type=F32).astype(BF16)
    inner = jnp.sum(probs * dprobs, axis=-1, keepdims=True)
    dscores = (probs * (dprobs - inner)).astype(BF16)
    dq = jnp.einsum("bgrqk,bkgd->bqgrd", dscores, k, preferred_element_type=F32) * scale
    dk = jnp.einsum("bgrqk,bqgrd->bkgd", dscores, q, preferred_element_type=F32) * scale
    cp, sp = cos_part[None, :, None, :], sin_part[None, :, None, :]
    dq = rotate(dq.reshape(seqs, length, heads, HEAD_SIZE), cp, -sp).astype(BF16)
    dk = rotate(dk, cp, -sp).astype(BF16)
    dqkv = jnp.concatenate([d.reshape(tokens, -1) for d in (dq, dk, dv)], axis=1)
    grad_qkv = rows_of(dot_ta(n1, dqkv))
    dn1 = total(dot_tb(dqkv, qkv_w))
    x_own = mine(x2).astype(F32)
    r1 = lax.rsqrt(jnp.mean(x_own * x_own, axis=-1, keepdims=True) + EPSILON)
    gain_a_sum = jnp.sum(dn1 * x_own * r1, axis=0)
    scaled = dn1 * gain_a
    dx = dh + r1 * scaled - x_own * (r1 * r1 * r1) * jnp.mean(scaled * x_own, axis=-1, keepdims=True)
    input_grad = both(dx.astype(BF16))
    sums = jnp.stack([gain_a_sum, gain_f_sum]).reshape(2, n, block)
    sums = sums + swap_core(sums)
    sums = sums[:, owners]
    gain_grads = ring.small_scatter(sums)
    return (
        output,
        input_grad,
        gain_grads[0],
        grad_qkv[:, :q_cols],
        grad_qkv[:, q_cols : q_cols + kv_cols],
        grad_qkv[:, q_cols + kv_cols :],
        grad_out,
        gain_grads[1],
        grad_gate,
        grad_up,
        grad_down,
    )


def solution(mesh):
    ring = Ring(mesh.shape["dp"])
    if mesh.shape["tensor"] != 4:
        raise ValueError("tensor axis")
    row, col = P("dp", "tensor"), P("tensor", "dp")
    data = P("dp", None, None)

    def layer(*args):
        block = args[0].shape[2] // ring.size
        return (local if block % 256 == 0 else ring_local)(ring, *args)

    return jax.shard_map(
        layer,
        mesh=mesh,
        in_specs=(data, P("dp"), row, row, row, col, P("dp"), row, row, col, data, P("dp"), P("dp")),
        out_specs=(data, data, P("dp"), row, row, row, col, P("dp"), row, row, col),
        check_vma=False,
    )
```

```python
import functools
import math

import jax
import jax.numpy as jnp
import numpy as np
from jax import lax
from jax.experimental import pallas as pl
from jax.experimental.pallas import tpu as pltpu
from jax.sharding import PartitionSpec as P

HEAD_SIZE = 128
EPSILON = 1e-05
NEGATIVE = -1e30
BF16 = jnp.bfloat16
F32 = jnp.float32
MESH = pl.DeviceIdType.MESH
HBM = pl.BlockSpec(memory_space=pltpu.HBM)
SMEM = pl.BlockSpec(memory_space=pltpu.SMEM)
ROWS = 256


def dot(a, b):
    return jnp.dot(a, b, preferred_element_type=F32)


def dot_ta(a, b):
    return lax.dot_general(a, b, (((0,), (0,)), ((), ())), preferred_element_type=F32)


def dot_tb(a, b):
    return lax.dot_general(a, b, (((1,), (1,)), ((), ())), preferred_element_type=F32)


def spec(rows, cols):
    return pl.BlockSpec((rows, cols), lambda i: (i, 0))


def fixed(*shape):
    return pl.BlockSpec(shape, lambda i: (0,) * len(shape))


def tiles(total, step=256):
    return [(at, min(step, total - at)) for at in range(0, total, step)]


def gain_row(gains_ref, which):
    n = gains_ref.shape[0]
    return jnp.concatenate([gains_ref[j, which : which + 1, :] for j in range(n)], axis=1).astype(F32)


def turn(values, cos, sin):
    return values * cos + pltpu.roll(values, HEAD_SIZE // 2, axis=1) * sin


class Place:
    def __init__(self, n):
        self.n = n
        self.me = lax.axis_index("dp")
        odd = self.me % 2
        self.p = (1 - odd) * (self.me // 2) + odd * (n - 1 - self.me // 2)
        tensor = lax.axis_index("tensor")
        self.core = tensor % 2
        self.core_peer = tensor + 1 - 2 * self.core
        self.chip_peer = (tensor + 2) % 4
        self.right = self.at(1)
        self.left = self.at(-1)

    def at(self, j):
        p = (self.p + j + 2 * self.n) % self.n
        low = p // (self.n // 2)
        return (1 - low) * 2 * p + low * (2 * (self.n - 1 - p) + 1)

    def greet(self):
        barrier = pltpu.get_barrier_semaphore()
        for peer in (self.left, self.right):
            pl.semaphore_signal(barrier, inc=1, device_id={"dp": peer}, device_id_type=MESH)
        for peer in (self.core_peer, self.chip_peer):
            pl.semaphore_signal(barrier, inc=1, device_id={"tensor": peer}, device_id_type=MESH)
        pl.semaphore_wait(barrier, 4)


class Gather:
    def __init__(self, place, shard, whole, where, local_sem, send_sems, recv_sems):
        self.place, self.shard, self.whole, self.where = place, shard, whole, where
        self.send_sems, self.recv_sems = send_sems, recv_sems
        self.hops = place.n // 2
        self.copies = {}
        self.local = pltpu.make_async_copy(shard, where(whole, place.me, None), local_sem)
        self.local.start()

    def send(self, way, hop):
        place = self.place
        sign = 1 - 2 * way
        owner = place.at(-sign * (hop - 1))
        half = way if hop == self.hops else None
        target = self.where(self.whole, owner, half)
        if hop > 1:
            self.copies[way, hop - 1].wait_recv()
            source = target
        elif half is None:
            source = self.shard
        else:
            rows = self.shard.shape[0] // 2
            source = self.shard.at[pl.ds(half * rows, rows)]
        copy = pltpu.make_async_remote_copy(
            src_ref=source,
            dst_ref=target,
            send_sem=self.send_sems.at[way, hop - 1],
            recv_sem=self.recv_sems.at[way, hop - 1],
            device_id={"dp": place.right if way == 0 else place.left},
            device_id_type=MESH,
        )
        copy.start()
        self.copies[way, hop] = copy

    def step(self, hop):
        self.send(0, hop)
        self.send(1, hop)

    def arrived(self):
        self.local.wait()
        self.copies[0, self.hops].wait_recv()
        self.copies[1, self.hops].wait_recv()

    def drain(self):
        for copy in self.copies.values():
            copy.wait_send()


def by_rows(rows):
    def where(whole, owner, half):
        if half is None:
            return whole.at[pl.ds(pl.multiple_of(owner * rows, rows), rows)]
        return whole.at[pl.ds(pl.multiple_of(owner * rows + half * (rows // 2), rows // 2), rows // 2)]

    return where


def by_cols(rows, cols):
    def where(whole, owner, half):
        at = pl.ds(pl.multiple_of(owner * cols, cols), cols)
        if half is None:
            return whole.at[:, at]
        return whole.at[pl.ds(half * (rows // 2), rows // 2), at]

    return where


def by_slot(whole, owner, half):
    if half is None:
        return whole.at[owner]
    rows = whole.shape[1] // 2
    return whole.at[owner, pl.ds(half * rows, rows)]


class Swap:
    def __init__(self, source, target, peer, send_sem, recv_sem):
        self.copy = pltpu.make_async_remote_copy(
            src_ref=source, dst_ref=target, send_sem=send_sem, recv_sem=recv_sem,
            device_id={"tensor": peer}, device_id_type=MESH,
        )
        self.copy.start()


def forward_kernel(
    n, length, x_hbm, dy_hbm, gains_in, wq_in, wk_in, wv_in, wo_in, wg_in, wu_in, wd_in, cos_hbm, sin_hbm, keep_ref, prefix_ref,
    gains_w, wq, wk, wv, wo, wg, wu, wd, n1_hbm, q_hbm, k_hbm, v_hbm, ob_hbm, hid_hbm, n2_hbm, m_hbm, fa_hbm, fb_hbm, gd_hbm,
    own_hbm, other_hbm, peer_hbm, near_hbm, far_hbm,
    local_sems, send_sems, recv_sems, swap_send, swap_recv,
):
    place = Place(n)
    core = place.core
    place.greet()
    tokens, width = x_hbm.shape
    scale = 1.0 / math.sqrt(HEAD_SIZE)
    arrays = (
        (gains_in, gains_w, by_slot),
        (wq_in, wq, by_rows(wq_in.shape[0])),
        (wk_in, wk, by_rows(wk_in.shape[0])),
        (wv_in, wv, by_rows(wv_in.shape[0])),
        (wo_in, wo, by_cols(*wo_in.shape)),
        (wg_in, wg, by_rows(wg_in.shape[0])),
        (wu_in, wu, by_rows(wu_in.shape[0])),
        (wd_in, wd, by_cols(*wd_in.shape)),
    )
    rings = [
        Gather(place, shard, whole, where, local_sems.at[i], send_sems.at[i], recv_sems.at[i])
        for i, (shard, whole, where) in enumerate(arrays)
    ]
    hops = n // 2
    starts = (0, 0, 0, 0, 1, 3, 6, 9)
    todo = sorted((starts[i] + hop, i, hop) for i in range(len(rings)) for hop in range(1, hops + 1))

    def pump(slot):
        while todo and todo[0][0] <= slot:
            _, i, hop = todo.pop(0)
            rings[i].step(hop)

    own_rows = pl.ds(pl.multiple_of(core * length, length), length)
    other_rows = pl.ds(pl.multiple_of((1 - core) * length, length), length)

    pump(5)
    for i in range(4):
        rings[i].arrived()

    def project(x_ref, gains_ref, wq_ref, wk_ref, wv_ref, cos_ref, sin_ref, n1_ref, q_ref, k_ref, v_ref):
        gain = gain_row(gains_ref, 0)

        @pl.loop(0, ROWS, step=32)
        def _(at):
            part = pl.ds(pl.multiple_of(at, 32), 32)
            xf = x_ref[part, :].astype(F32)
            r1 = lax.rsqrt(jnp.mean(xf * xf, axis=-1, keepdims=True) + EPSILON)
            n1_ref[part, :] = (xf * r1 * gain).astype(BF16)

        rows = n1_ref[...]
        cos, sin = cos_ref[...], sin_ref[...]
        for w_ref, o_ref in ((wq_ref, q_ref), (wk_ref, k_ref)):
            for at in range(0, w_ref.shape[1], HEAD_SIZE):
                head = slice(at, at + HEAD_SIZE)
                o_ref[:, head] = turn(dot(rows, w_ref[:, head]), cos, sin).astype(BF16)
        v_ref[...] = dot(rows, wv_ref[...]).astype(BF16)

    q_cols, kv_cols = wq.shape[1], wk.shape[1]
    per = length // ROWS
    turns = pl.BlockSpec((ROWS, HEAD_SIZE), lambda i: (i % per, 0))
    pltpu.emit_pipeline(
        project,
        grid=(tokens // ROWS,),
        in_specs=[spec(ROWS, width), fixed(*gains_w.shape), fixed(*wq.shape), fixed(*wk.shape), fixed(*wv.shape), turns, turns],
        out_specs=[spec(ROWS, width), spec(ROWS, q_cols), spec(ROWS, kv_cols), spec(ROWS, kv_cols)],
    )(x_hbm, gains_w, wq, wk, wv, cos_hbm, sin_hbm, n1_hbm, q_hbm, k_hbm, v_hbm)
    pump(6)

    repeat = q_cols // kv_cols

    def attend(which, q_ref, k_ref, v_ref, o_ref):
        prefix = prefix_ref[which]
        keys, values = k_ref[...], v_ref[...]

        @pl.loop(0, length, step=128)
        def _(at):
            part = pl.ds(pl.multiple_of(at, 128), 128)
            s = dot_tb(q_ref[part, :], keys) * scale
            row = lax.broadcasted_iota(jnp.int32, s.shape, 0) + at
            col = lax.broadcasted_iota(jnp.int32, s.shape, 1)
            s = jnp.where((col <= row) | (col < prefix), s, NEGATIVE)
            e = jnp.exp(s - jnp.max(s, axis=-1, keepdims=True))
            p = e / jnp.sum(e, axis=-1, keepdims=True)
            o_ref[part, :] = dot(p.astype(BF16), values).astype(BF16)

    for which in range(2):
        seq = pl.ds(which * length, length)
        pltpu.emit_pipeline(
            functools.partial(attend, which),
            grid=(q_cols // HEAD_SIZE,),
            in_specs=[
                pl.BlockSpec((length, HEAD_SIZE), lambda h: (0, h)),
                pl.BlockSpec((length, HEAD_SIZE), lambda h: (0, h // repeat)),
                pl.BlockSpec((length, HEAD_SIZE), lambda h: (0, h // repeat)),
            ],
            out_specs=[pl.BlockSpec((length, HEAD_SIZE), lambda h: (0, h))],
        )(q_hbm.at[seq], k_hbm.at[seq], v_hbm.at[seq], ob_hbm.at[seq])
        pump(7 + which)

    rings[4].arrived()

    def mix(ob_ref, wo_ref, o_ref):
        o_ref[...] = dot(ob_ref[...], wo_ref[...]).astype(o_ref.dtype)

    def project_out(rows, target):
        pltpu.emit_pipeline(
            mix, grid=(length // ROWS,), in_specs=[spec(ROWS, q_cols), fixed(*wo.shape)], out_specs=[spec(ROWS, width)]
        )(ob_hbm.at[rows], wo, target)

    project_out(other_rows, other_hbm)
    to_core = Swap(other_hbm, peer_hbm, place.core_peer, swap_send.at[0], swap_recv.at[0])
    project_out(own_rows, own_hbm)
    to_core.copy.wait_recv()

    def nearby(own_ref, peer_ref, near_ref):
        near_ref[...] = (own_ref[...] + peer_ref[...].astype(F32)).astype(BF16)

    pltpu.emit_pipeline(
        nearby, grid=(length // 64,), in_specs=[spec(64, width)] * 2, out_specs=[spec(64, width)]
    )(own_hbm, peer_hbm, near_hbm)
    to_chip = Swap(near_hbm, far_hbm, place.chip_peer, swap_send.at[1], swap_recv.at[1])
    pump(10)
    to_chip.copy.wait_recv()

    def residual(near_ref, far_ref, x_ref, gains_ref, hid_ref, n2_ref):
        gain = gain_row(gains_ref, 1)
        a = near_ref[...].astype(F32) + far_ref[...].astype(F32)
        h = x_ref[...].astype(F32) + keep_ref[core] * a
        hid_ref[...] = h
        r2 = lax.rsqrt(jnp.mean(h * h, axis=-1, keepdims=True) + EPSILON)
        n2_ref[...] = (h * r2 * gain).astype(BF16)

    pltpu.emit_pipeline(
        residual,
        grid=(length // 32,),
        in_specs=[spec(32, width)] * 3 + [fixed(*gains_w.shape)],
        out_specs=[spec(32, width)] * 2,
    )(near_hbm, far_hbm, x_hbm.at[own_rows], gains_w, hid_hbm, n2_hbm.at[own_rows])
    share = Swap(n2_hbm.at[own_rows], n2_hbm.at[own_rows], place.core_peer, swap_send.at[2], swap_recv.at[2])
    pump(11)
    share.copy.wait_recv()
    rings[5].arrived()
    rings[6].arrived()

    hidden = wg.shape[1]

    def feed(n2_ref, wg_ref, wu_ref, m_ref, fa_ref, fb_ref):
        rows = n2_ref[...]
        for at, size in tiles(hidden):
            cols = slice(at, at + size)
            g = dot(rows, wg_ref[:, cols])
            u = dot(rows, wu_ref[:, cols])
            sig = 1.0 / (1.0 + jnp.exp(-g))
            swish = g * sig
            m_ref[:, cols] = (swish * u).astype(BF16)
            fa_ref[:, cols] = u * sig * (1.0 + g * (1.0 - sig))
            fb_ref[:, cols] = swish

    pltpu.emit_pipeline(
        feed,
        grid=(tokens // ROWS,),
        in_specs=[spec(ROWS, width), fixed(*wg.shape), fixed(*wu.shape)],
        out_specs=[spec(ROWS, hidden)] * 3,
    )(n2_hbm, wg, wu, m_hbm, fa_hbm, fb_hbm)
    pump(12)

    def down_grad(m_ref, dy_ref, o_ref):
        total = None
        for which in range(2):
            seq = slice(which * length, (which + 1) * length)
            df = (dy_ref[seq, :].astype(F32) * keep_ref[which]).astype(BF16)
            term = dot_ta(m_ref[seq, :], df)
            total = term if total is None else total + term
        o_ref[...] = total.astype(BF16)

    cols = pl.BlockSpec((tokens, 256), lambda i: (0, i))
    pltpu.emit_pipeline(
        down_grad,
        grid=(width // 256,),
        in_specs=[fixed(tokens, hidden), cols],
        out_specs=[pl.BlockSpec((hidden, 256), lambda i: (0, i))],
    )(m_hbm, dy_hbm, gd_hbm)
    pump(100)
    rings[7].arrived()
    for ring in rings:
        ring.drain()
    for swap in (to_core, to_chip, share):
        swap.copy.wait_send()


def forward(n, x, dy, gains, wq, wk, wv, wo, wg, wu, wd, cos, sin, keep, prefix, length):
    tokens, width = x.shape
    shape = jax.ShapeDtypeStruct
    ff = wg.shape[1]
    outs = [
        shape((n,) + gains.shape, BF16),
        shape((width, wq.shape[1]), BF16),
        shape((width, wk.shape[1]), BF16),
        shape((width, wv.shape[1]), BF16),
        shape((wo.shape[0], width), BF16),
        shape((width, ff), BF16),
        shape((width, ff), BF16),
        shape((ff, width), BF16),
        shape((tokens, width), BF16),
        shape((tokens, wq.shape[1]), BF16),
        shape((tokens, wk.shape[1]), BF16),
        shape((tokens, wv.shape[1]), BF16),
        shape((tokens, wq.shape[1]), BF16),
        shape((length, width), F32),
        shape((tokens, width), BF16),
        shape((tokens, ff), BF16),
        shape((tokens, ff), F32),
        shape((tokens, ff), F32),
        shape((ff, width), BF16),
        shape((length, width), F32),
        shape((length, width), BF16),
        shape((length, width), BF16),
        shape((length, width), BF16),
        shape((length, width), BF16),
    ]
    return pl.pallas_call(
        functools.partial(forward_kernel, n, length),
        out_shape=outs,
        in_specs=[HBM] * 12 + [SMEM] * 2,
        out_specs=[HBM] * len(outs),
        scratch_shapes=[
            pltpu.SemaphoreType.DMA((8,)),
            pltpu.SemaphoreType.DMA((8, 2, n // 2)),
            pltpu.SemaphoreType.DMA((8, 2, n // 2)),
            pltpu.SemaphoreType.DMA((3,)),
            pltpu.SemaphoreType.DMA((3,)),
        ],
        compiler_params=pltpu.CompilerParams(collective_id=0, has_side_effects=True, vmem_limit_bytes=60 * 1024 * 1024),
    )(x, dy, gains, wq, wk, wv, wo, wg, wu, wd, cos, sin, keep, prefix)


class Scatter:
    def __init__(self, place, whole, where, slots, send_sems, recv_sems):
        self.place, self.whole, self.where, self.slots = place, whole, where, slots
        self.send_sems, self.recv_sems = send_sems, recv_sems
        self.hops = place.n // 2
        self.copies = {}

    def view(self, way, hop):
        sign = 1 - 2 * way
        owner = self.place.at(sign * (self.hops + 1 - hop))
        return self.where(self.whole, owner, way if hop == 1 else None)

    def slot(self, way, hop):
        first, rest = self.slots[way]
        return first if hop == 1 else rest.at[hop - 2]

    def add(self, hop):
        terms, views = [], []
        for way in range(2):
            self.copies[way, hop - 1].wait_recv()
            sign = 1 - 2 * way
            owner = self.place.at(sign * (self.hops + 1 - hop))
            views.append(self.where(self.whole, owner, way if hop == 2 else None))
            terms.append(self.slot(way, hop - 1))
        rows, cols = views[0].shape
        count = 2 if hop == 2 else 4

        def body(a_ref, b_ref, c_ref, d_ref, o_ref, p_ref):
            o_ref[...] = (a_ref[...].astype(F32) + b_ref[...].astype(F32)).astype(BF16)
            p_ref[...] = (c_ref[...].astype(F32) + d_ref[...].astype(F32)).astype(BF16)

        pltpu.emit_pipeline(
            body, grid=(count,), in_specs=[spec(rows // count, cols)] * 4, out_specs=[spec(rows // count, cols)] * 2
        )(views[0], terms[0], views[1], terms[1], views[0], views[1])

    def step(self, hop):
        if hop > 1:
            self.add(hop)
        for way in range(2):
            copy = pltpu.make_async_remote_copy(
                src_ref=self.view(way, hop),
                dst_ref=self.slot(way, hop),
                send_sem=self.send_sems.at[way, hop - 1],
                recv_sem=self.recv_sems.at[way, hop - 1],
                device_id={"dp": self.place.right if way == 0 else self.place.left},
                device_id_type=MESH,
            )
            copy.start()
            self.copies[way, hop] = copy

    def drain(self):
        for way in range(2):
            self.copies[way, self.hops].wait_recv()
        for copy in self.copies.values():
            copy.wait_send()


def backward_kernel(n, length, names_in, names_out, *refs):
    ins = dict(zip(names_in, refs))
    outs = dict(zip(names_out, refs[len(names_in) :]))
    (gsum, gpieces, local_sems, send_sems, recv_sems, swap_send, swap_recv, gain_send, gain_recv) = refs[
        len(names_in) + len(names_out) :
    ]
    keep_ref, prefix_ref = ins["keep"], ins["prefix"]
    dy, x, gains_w = ins["dy"], ins["x"], ins["gains"]
    wq, wk, wv, wo, wg, wu, wd = (ins[name] for name in ("wq", "wk", "wv", "wo", "wg", "wu", "wd"))
    tokens, width = x.shape
    q_cols, kv_cols, hidden = wq.shape[1], wk.shape[1], wg.shape[1]
    block = width // n
    per = length // ROWS
    repeat = q_cols // kv_cols
    scale = 1.0 / math.sqrt(HEAD_SIZE)
    place = Place(n)
    core = place.core
    barrier = pltpu.get_barrier_semaphore()
    for j in range(1, n):
        pl.semaphore_signal(barrier, inc=1, device_id={"dp": place.at(j)}, device_id_type=MESH)
    for peer in (place.core_peer, place.chip_peer):
        pl.semaphore_signal(barrier, inc=1, device_id={"tensor": peer}, device_id_type=MESH)
    pl.semaphore_wait(barrier, n + 1)

    own_rows = pl.ds(pl.multiple_of(core * length, length), length)
    other_rows = pl.ds(pl.multiple_of((1 - core) * length, length), length)
    wheres = {
        "down": by_cols(hidden, block),
        "gate": by_rows(block),
        "up": by_rows(block),
        "out": by_cols(q_cols, block),
        "qkv": by_rows(block),
    }
    rings = {
        name: Scatter(
            place,
            outs["g_" + name],
            wheres[name],
            [(outs[f"r_{name}_{way}_first"], outs[f"r_{name}_{way}"]) for way in range(2)],
            send_sems.at[i],
            recv_sems.at[i],
        )
        for i, name in enumerate(wheres)
    }
    swaps = []

    def swap(source, target, peer):
        i = len(swaps)
        swaps.append(Swap(source, target, peer, swap_send.at[i], swap_recv.at[i]))
        return swaps[-1].copy

    def act_grads():
        def body(dy_ref, wd_ref, fa_ref, fb_ref, dg_ref, du_ref):
            which = pl.program_id(0) // per
            df = (dy_ref[...].astype(F32) * keep_ref[which]).astype(BF16)
            for at, size in tiles(hidden):
                cols = slice(at, at + size)
                dm = dot_tb(df, wd_ref[cols, :])
                dg_ref[:, cols] = (dm * fa_ref[:, cols]).astype(BF16)
                du_ref[:, cols] = (dm * fb_ref[:, cols]).astype(BF16)

        pltpu.emit_pipeline(
            body,
            grid=(tokens // ROWS,),
            in_specs=[spec(ROWS, width), fixed(hidden, width), spec(ROWS, hidden), spec(ROWS, hidden)],
            out_specs=[spec(ROWS, hidden)] * 2,
        )(dy, wd, ins["fa"], ins["fb"], outs["dg"], outs["du"])

    def outer(left, right, target):
        def body(l_ref, r_ref, o_ref):
            o_ref[...] = dot_ta(l_ref[...], r_ref[...]).astype(BF16)

        cols = right.shape[1]
        pltpu.emit_pipeline(
            body,
            grid=(width // 256,),
            in_specs=[pl.BlockSpec((tokens, 256), lambda i: (0, i)), fixed(tokens, cols)],
            out_specs=[spec(256, cols)],
        )(left, right, target)

    def back(rows, target, *pairs):
        def body(*refs):
            o_ref = refs[-1]
            for at, size in tiles(width):
                cols = slice(at, at + size)
                total = None
                for d_ref, w_ref in zip(refs[: len(pairs)], refs[len(pairs) : -1]):
                    term = dot_tb(d_ref[...], w_ref[cols, :])
                    total = term if total is None else total + term
                o_ref[:, cols] = total.astype(o_ref.dtype)

        pltpu.emit_pipeline(
            body,
            grid=(length // ROWS,),
            in_specs=[spec(ROWS, w.shape[1]) for _, w in pairs] + [fixed(*w.shape) for _, w in pairs],
            out_specs=[spec(ROWS, width)],
        )(*[d.at[rows] for d, _ in pairs], *[w for _, w in pairs], target)

    def nearby(name):
        def body(own_ref, peer_ref, near_ref):
            near_ref[...] = (own_ref[...] + peer_ref[...].astype(F32)).astype(BF16)

        pltpu.emit_pipeline(
            body, grid=(length // 64,), in_specs=[spec(64, width)] * 2, out_specs=[spec(64, width)]
        )(outs["own_" + name], outs["peer_" + name], outs["near_" + name])
        return swap(outs["near_" + name], outs["far_" + name], place.chip_peer)

    def add_gain(which, terms):
        gsum[which] += sum(terms[i * 8 : (i + 1) * 8] for i in range(terms.shape[0] // 8))

    def norm_back(d, h, gain, which):
        r = lax.rsqrt(jnp.mean(h * h, axis=-1, keepdims=True) + EPSILON)
        add_gain(which, d * h * r)
        scaled = d * gain
        return r * scaled - h * (r * r * r) * jnp.mean(scaled * h, axis=-1, keepdims=True)

    def hid_grads():
        def body(near_ref, far_ref, hid_ref, dy_ref, gains_ref, dh_ref, da_ref):
            d = near_ref[...].astype(F32) + far_ref[...].astype(F32)
            dh = dy_ref[...].astype(F32) + norm_back(d, hid_ref[...], gain_row(gains_ref, 1), 1)
            dh_ref[...] = dh
            da_ref[...] = (keep_ref[core] * dh).astype(BF16)

        pltpu.emit_pipeline(
            body,
            grid=(length // 32,),
            in_specs=[spec(32, width)] * 4 + [fixed(*gains_w.shape)],
            out_specs=[spec(32, width)] * 2,
        )(outs["near_n2"], outs["far_n2"], ins["hid"], dy.at[own_rows], gains_w, outs["dh"], outs["da"].at[own_rows])
        return swap(outs["da"].at[own_rows], outs["da"].at[own_rows], place.core_peer)

    def input_grads():
        def body(near_ref, far_ref, x_ref, dh_ref, gains_ref, dx_ref):
            d = near_ref[...].astype(F32) + far_ref[...].astype(F32)
            xf = x_ref[...].astype(F32)
            dx_ref[...] = (dh_ref[...] + norm_back(d, xf, gain_row(gains_ref, 0), 0)).astype(BF16)

        pltpu.emit_pipeline(
            body,
            grid=(length // 32,),
            in_specs=[spec(32, width)] * 4 + [fixed(*gains_w.shape)],
            out_specs=[spec(32, width)],
        )(outs["near_n1"], outs["far_n1"], x.at[own_rows], outs["dh"], gains_w, outs["dx"].at[own_rows])
        return swap(outs["dx"].at[own_rows], outs["dx"].at[own_rows], place.core_peer)

    def results():
        def body(near_ref, far_ref, hid_ref, o_ref):
            f = near_ref[...].astype(F32) + far_ref[...].astype(F32)
            o_ref[...] = (hid_ref[...] + keep_ref[core] * f).astype(BF16)

        pltpu.emit_pipeline(
            body, grid=(length // 64,), in_specs=[spec(64, width)] * 3, out_specs=[spec(64, width)]
        )(outs["near_f"], outs["far_f"], ins["hid"], outs["output"].at[own_rows])
        return swap(outs["output"].at[own_rows], outs["output"].at[own_rows], place.core_peer)

    def forth(rows, target):
        def body(m_ref, wd_ref, o_ref):
            for at, size in tiles(width, 512):
                cols = slice(at, at + size)
                o_ref[:, cols] = dot(m_ref[...], wd_ref[:, cols]).astype(o_ref.dtype)

        pltpu.emit_pipeline(
            body, grid=(length // ROWS,), in_specs=[spec(ROWS, hidden), fixed(hidden, width)], out_specs=[spec(ROWS, width)]
        )(ins["m"].at[rows], wd, target)

    def out_grad():
        def body(ob_ref, da_ref, o_ref):
            o_ref[...] = dot_ta(ob_ref[...], da_ref[...]).astype(BF16)

        pltpu.emit_pipeline(
            body,
            grid=(width // 256,),
            in_specs=[fixed(tokens, q_cols), pl.BlockSpec((tokens, 256), lambda i: (0, i))],
            out_specs=[pl.BlockSpec((q_cols, 256), lambda i: (0, i))],
        )(ins["ob"], outs["da"], outs["g_out"])

    def mixed_grad():
        def body(da_ref, wo_ref, o_ref):
            o_ref[...] = dot_tb(da_ref[...], wo_ref[...]).astype(BF16)

        pltpu.emit_pipeline(
            body, grid=(tokens // ROWS,), in_specs=[spec(ROWS, width), fixed(q_cols, width)], out_specs=[spec(ROWS, q_cols)]
        )(outs["da"], wo, outs["dob"])

    def attend_back(which):
        seq = pl.ds(which * length, length)

        def heads(dk_sum, dv_sum):
            def body(q_ref, k_ref, v_ref, d_ref, cos_ref, sin_ref, dq_ref, dk_ref, dv_ref):
                head = pl.program_id(0) % repeat
                prefix = prefix_ref[which]
                keys, values = k_ref[...], v_ref[...]

                @pl.when(head == 0)
                def _():
                    dk_sum[...] = jnp.zeros_like(dk_sum)
                    dv_sum[...] = jnp.zeros_like(dv_sum)

                @pl.loop(0, length, step=128)
                def _(at):
                    part = pl.ds(pl.multiple_of(at, 128), 128)
                    queries, grads = q_ref[part, :], d_ref[part, :]
                    s = dot_tb(keys, queries) * scale
                    col = lax.broadcasted_iota(jnp.int32, s.shape, 0)
                    row = lax.broadcasted_iota(jnp.int32, s.shape, 1) + at
                    s = jnp.where((col <= row) | (col < prefix), s, NEGATIVE)
                    e = jnp.exp(s - jnp.max(s, axis=0, keepdims=True))
                    p = e / jnp.sum(e, axis=0, keepdims=True)
                    dp = dot_tb(values, grads)
                    inner = jnp.sum(p * dp, axis=0, keepdims=True)
                    dz = (p * (dp - inner)).astype(BF16)
                    dv_sum[...] += dot(p.astype(BF16), grads)
                    dk_sum[...] += dot(dz, queries)
                    dq = dot_ta(dz, keys) * scale
                    dq_ref[part, :] = turn(dq, cos_ref[part, :], -sin_ref[part, :]).astype(BF16)

                @pl.when(head == repeat - 1)
                def _():
                    dk_ref[...] = turn(dk_sum[...] * scale, cos_ref[...], -sin_ref[...]).astype(BF16)
                    dv_ref[...] = dv_sum[...].astype(BF16)

            one = pl.BlockSpec((length, HEAD_SIZE), lambda h: (0, h))
            shared = pl.BlockSpec((length, HEAD_SIZE), lambda h: (0, h // repeat))
            table = pl.BlockSpec((length, HEAD_SIZE), lambda h: (0, 0))
            dqkv = outs["dqkv"].at[seq]
            pltpu.emit_pipeline(
                body,
                grid=(q_cols // HEAD_SIZE,),
                in_specs=[one, shared, shared, one, table, table],
                out_specs=[one, shared, shared],
            )(
                ins["q"].at[seq],
                ins["k"].at[seq],
                ins["v"].at[seq],
                outs["dob"].at[seq],
                ins["cos"],
                ins["sin"],
                dqkv.at[:, pl.ds(0, q_cols)],
                dqkv.at[:, pl.ds(q_cols, kv_cols)],
                dqkv.at[:, pl.ds(q_cols + kv_cols, kv_cols)],
            )

        pl.run_scoped(heads, pltpu.VMEM((length, HEAD_SIZE), F32), pltpu.VMEM((length, HEAD_SIZE), F32))

    def back_qkv(rows, target):
        def body(d_ref, wq_ref, wk_ref, wv_ref, o_ref):
            dq, dk, dv = d_ref[:, :q_cols], d_ref[:, q_cols : q_cols + kv_cols], d_ref[:, q_cols + kv_cols :]
            for at, size in tiles(width):
                cols = slice(at, at + size)
                total = dot_tb(dq, wq_ref[cols, :]) + dot_tb(dk, wk_ref[cols, :]) + dot_tb(dv, wv_ref[cols, :])
                o_ref[:, cols] = total.astype(o_ref.dtype)

        pltpu.emit_pipeline(
            body,
            grid=(length // ROWS,),
            in_specs=[spec(ROWS, q_cols + 2 * kv_cols), fixed(*wq.shape), fixed(*wk.shape), fixed(*wv.shape)],
            out_specs=[spec(ROWS, width)],
        )(outs["dqkv"].at[rows], wq, wk, wv, target)

    def gain_grads():
        for which in range(2):
            row = jnp.sum(gsum[which], axis=0, keepdims=True)
            for j in range(n):
                gpieces[j, which : which + 1, :] = row[:, j * block : (j + 1) * block]
        copy = pltpu.make_async_copy(gpieces, outs["gain_terms"], local_sems.at[0])
        copy.start()
        copy.wait()
        mine = pltpu.make_async_copy(outs["gain_terms"].at[place.me], outs["gain_slots"].at[0], local_sems.at[1])
        mine.start()
        copies = []
        for j in range(1, n):
            copy = pltpu.make_async_remote_copy(
                src_ref=outs["gain_terms"].at[place.at(j)],
                dst_ref=outs["gain_slots"].at[j],
                send_sem=gain_send.at[j],
                recv_sem=gain_recv.at[j],
                device_id={"dp": place.at(j)},
                device_id_type=MESH,
            )
            copy.start()
            copies.append(copy)
        return mine, copies

    gsum[...] = jnp.zeros_like(gsum)
    gpieces[...] = jnp.zeros_like(gpieces)
    rings["down"].step(1)
    act_grads()
    back(other_rows, outs["other_n2"], (outs["dg"], wg), (outs["du"], wu))
    core_n2 = swap(outs["other_n2"], outs["peer_n2"], place.core_peer)
    rings["down"].step(2)
    back(own_rows, outs["own_n2"], (outs["dg"], wg), (outs["du"], wu))
    core_n2.wait_recv()
    chip_n2 = nearby("n2")
    outer(ins["n2"], outs["dg"], outs["g_gate"])
    rings["gate"].step(1)
    rings["down"].step(3)
    outer(ins["n2"], outs["du"], outs["g_up"])
    rings["gate"].step(2)
    rings["down"].step(4)
    forth(other_rows, outs["other_f"])
    core_f = swap(outs["other_f"], outs["peer_f"], place.core_peer)
    rings["gate"].step(3)
    rings["up"].step(1)
    forth(own_rows, outs["own_f"])
    core_f.wait_recv()
    chip_n2.wait_recv()
    share_da = hid_grads()
    chip_f = nearby("f")
    rings["gate"].step(4)
    rings["up"].step(2)
    share_da.wait_recv()
    mixed_grad()
    attend_back(0)
    rings["up"].step(3)
    out_grad()
    rings["out"].step(1)
    attend_back(1)
    rings["up"].step(4)
    back_qkv(other_rows, outs["other_n1"])
    core_n1 = swap(outs["other_n1"], outs["peer_n1"], place.core_peer)
    back_qkv(own_rows, outs["own_n1"])
    core_n1.wait_recv()
    chip_f.wait_recv()
    chip_n1 = nearby("n1")
    outer(ins["n1"], outs["dqkv"], outs["g_qkv"])
    rings["qkv"].step(1)
    rings["out"].step(2)
    rings["qkv"].step(2)
    rings["out"].step(3)
    share_out = results()
    rings["qkv"].step(3)
    rings["out"].step(4)
    chip_n1.wait_recv()
    share_dx = input_grads()
    mine, copies = gain_grads()
    rings["qkv"].step(4)
    share_out.wait_recv()
    share_dx.wait_recv()
    mine.wait()
    for copy in copies:
        copy.wait_recv()
    for ring in rings.values():
        ring.drain()
    for copy in copies:
        copy.wait_send()
    for item in swaps:
        item.copy.wait_send()


def backward(n, length, values):
    shape = jax.ShapeDtypeStruct
    tokens, width = values["x"].shape
    q_cols, kv_cols, hidden = values["wq"].shape[1], values["wk"].shape[1], values["wg"].shape[1]
    block = width // n
    outs = {}
    sizes = {
        "down": ((hidden, width), (hidden, block)),
        "gate": ((width, hidden), (block, hidden)),
        "up": ((width, hidden), (block, hidden)),
        "out": ((q_cols, width), (q_cols, block)),
        "qkv": ((width, q_cols + 2 * kv_cols), (block, q_cols + 2 * kv_cols)),
    }
    for name, (whole, piece) in sizes.items():
        outs["g_" + name] = shape(whole, BF16)
        for way in range(2):
            outs[f"r_{name}_{way}_first"] = shape((piece[0] // 2, piece[1]), BF16)
            outs[f"r_{name}_{way}"] = shape((n // 2 - 1,) + piece, BF16)
    for name in ("n2", "f", "n1"):
        outs["own_" + name] = shape((length, width), F32)
        for kind in ("other", "peer", "near", "far"):
            outs[f"{kind}_{name}"] = shape((length, width), BF16)
    outs["dg"] = outs["du"] = shape((tokens, hidden), BF16)
    outs["dh"] = shape((length, width), F32)
    outs["da"] = outs["dx"] = outs["output"] = shape((tokens, width), BF16)
    outs["dob"] = shape((tokens, q_cols), BF16)
    outs["dqkv"] = shape((tokens, q_cols + 2 * kv_cols), BF16)
    outs["gain_terms"] = outs["gain_slots"] = shape((n, 8, block), F32)
    names_in, names_out = list(values), list(outs)
    results = pl.pallas_call(
        functools.partial(backward_kernel, n, length, names_in, names_out),
        out_shape=list(outs.values()),
        in_specs=[SMEM if name in ("keep", "prefix") else HBM for name in names_in],
        out_specs=[HBM] * len(outs),
        input_output_aliases={names_in.index("g_down"): names_out.index("g_down")},
        scratch_shapes=[
            pltpu.VMEM((2, 8, width), F32),
            pltpu.VMEM((n, 8, block), F32),
            pltpu.SemaphoreType.DMA((2,)),
            pltpu.SemaphoreType.DMA((5, 2, n // 2)),
            pltpu.SemaphoreType.DMA((5, 2, n // 2)),
            pltpu.SemaphoreType.DMA((9,)),
            pltpu.SemaphoreType.DMA((9,)),
            pltpu.SemaphoreType.DMA((n,)),
            pltpu.SemaphoreType.DMA((n,)),
        ],
        compiler_params=pltpu.CompilerParams(collective_id=1, has_side_effects=True, vmem_limit_bytes=60 * 1024 * 1024),
    )(*values.values())
    return dict(zip(names_out, results))


def rotary_tables(length_total):
    half_width = HEAD_SIZE // 2
    frequency = (10000.0 ** (-(np.arange(half_width, dtype=np.float32) * 2.0) / HEAD_SIZE)).astype(np.float32)
    angles = np.arange(length_total, dtype=np.float32)[:, None] * frequency[None, :]
    return (jnp.asarray(np.cos(angles)), jnp.asarray(np.sin(angles)))


def rotate(values, cos_part, sin_part):
    first, second = jnp.split(values, 2, axis=-1)
    return jnp.concatenate(
        [first * cos_part - second * sin_part, first * sin_part + second * cos_part], axis=-1
    )


class Ring:
    def __init__(self, size):
        self.size = size
        self.half = size // 2
        self.order = [2 * p if p < self.half else 2 * (size - 1 - p) + 1 for p in range(size)]
        self.right = [(self.order[p], self.order[(p + 1) % size]) for p in range(size)]
        self.left = [(b, a) for a, b in self.right]

    def place(self):
        me = lax.axis_index("dp")
        odd = me % 2
        return (1 - odd) * (me // 2) + odd * (self.size - 1 - me // 2)

    def owners(self):
        return jnp.asarray(np.array(self.order, np.int32))[(self.place() + np.arange(self.size)) % self.size]

    def gather(self, shard):
        n, m = self.size, self.half
        pieces = [None] * n
        pieces[0] = shard
        from_left, from_right = shard, shard
        for hop in range(1, m):
            from_left = lax.ppermute(from_left, "dp", self.right)
            from_right = lax.ppermute(from_right, "dp", self.left)
            pieces[n - hop] = from_left
            pieces[hop] = from_right
        rows = shard.shape[0] // 2
        top = lax.ppermute(from_left[:rows], "dp", self.right)
        low = lax.ppermute(from_right[rows:], "dp", self.left)
        pieces[m] = jnp.concatenate([top, low], axis=0)
        return pieces

    def scatter(self, parts):
        n, m = self.size, self.half
        rows = parts[0].shape[0] // 2
        kind = BF16
        up = lax.ppermute(parts[m][:rows].astype(kind), "dp", self.right)
        down = lax.ppermute(parts[m][rows:].astype(kind), "dp", self.left)
        for hop in range(m - 1, 0, -1):
            mine_up, mine_down = parts[hop], parts[n - hop]
            if hop == m - 1:
                mine_up = jnp.concatenate([mine_up[:rows] + up.astype(F32), mine_up[rows:]], axis=0)
                mine_down = jnp.concatenate([mine_down[:rows], mine_down[rows:] + down.astype(F32)], axis=0)
            else:
                mine_up = mine_up + up.astype(F32)
                mine_down = mine_down + down.astype(F32)
            up = lax.ppermute(mine_up.astype(kind), "dp", self.right)
            down = lax.ppermute(mine_down.astype(kind), "dp", self.left)
        if m == 1:
            return jnp.concatenate([parts[0][:rows] + up.astype(F32), parts[0][rows:] + down.astype(F32)], axis=0)
        return parts[0] + up.astype(F32) + down.astype(F32)


    def small_scatter(self, sums):
        up = sums[:, self.half]
        for hop in range(self.half - 1, -1, -1):
            up = lax.ppermute(up, "dp", self.right)
            up = up + sums[:, hop]
        if self.size > 2:
            down = sums[:, self.half + 1]
            for hop in range(self.half - 2, -1, -1):
                down = lax.ppermute(down, "dp", self.left)
                if hop:
                    down = down + sums[:, self.size - hop]
            up = up + down
        return up


CORE_PAIRS = [(0, 1), (1, 0), (2, 3), (3, 2)]
CHIP_PAIRS = [(0, 2), (2, 0), (1, 3), (3, 1)]


def swap_core(value):
    return lax.ppermute(value, "tensor", CORE_PAIRS)


def swap_chip(value):
    return lax.ppermute(value, "tensor", CHIP_PAIRS)


def tensor_sum(part):
    near = part[0] + swap_core(part[1].astype(BF16)).astype(F32)
    near = near.astype(BF16)
    return near.astype(F32) + swap_chip(near).astype(F32)


def ring_local(ring, inputs, attention_gain, query_weight, key_matrix, value_matrix, out_weight, feedforward_gain,
          gate_weight, up_weight, down_weight, cotangent, layer_keep, prefix_length):
    n = ring.size
    seqs, length, width = inputs.shape
    block = width // n
    q_cols, kv_cols = query_weight.shape[1], key_matrix.shape[1]
    heads = q_cols // HEAD_SIZE
    kv_heads = kv_cols // HEAD_SIZE
    repeat = heads // kv_heads
    scale = 1.0 / math.sqrt(HEAD_SIZE)
    core = lax.axis_index("tensor") % 2
    owners = ring.owners()

    def arrange(array):
        array = jnp.where(core == 0, array, array[::-1])
        return jnp.concatenate(
            [lax.dynamic_slice_in_dim(array, owners[j] * block, block, axis=2) for j in range(n)], axis=2
        )

    def restore(own, other):
        array = jnp.stack([jnp.where(core == 0, own, other), jnp.where(core == 0, other, own)])
        places = jnp.asarray(np.argsort(np.array(ring.order)).astype(np.int32))
        where = (places - ring.place()) % n
        return jnp.concatenate(
            [lax.dynamic_slice_in_dim(array, where[j] * block, block, axis=2) for j in range(n)], axis=2
        )

    gains = jnp.concatenate([attention_gain, feedforward_gain])
    fill = jnp.zeros((8, q_cols + 2 * kv_cols), BF16)
    fill = lax.dynamic_update_slice(fill, gains[None, :], (0, 0))
    first = jnp.concatenate(
        [jnp.concatenate([query_weight, key_matrix, value_matrix], axis=1), fill], axis=0
    )
    first_pieces = ring.gather(first)
    qkv_w = jnp.concatenate([p[:block] for p in first_pieces], axis=0)
    gain_a = jnp.concatenate([p[block, :block] for p in first_pieces]).astype(F32)
    gain_f = jnp.concatenate([p[block, block : 2 * block] for p in first_pieces]).astype(F32)
    out_w = jnp.concatenate(ring.gather(out_weight), axis=1)
    gate_w = jnp.concatenate(ring.gather(gate_weight), axis=0)
    up_w = jnp.concatenate(ring.gather(up_weight), axis=0)
    down_w = jnp.concatenate(ring.gather(down_weight), axis=1)

    keep = layer_keep.astype(F32)
    keep = jnp.where(core == 0, keep, keep[::-1])
    prefix = jnp.where(core == 0, prefix_length, prefix_length[::-1])
    x = arrange(inputs)
    dy = arrange(cotangent)

    cos_part, sin_part = rotary_tables(length)
    cos_part, sin_part = cos_part[None, :, None, :], sin_part[None, :, None, :]
    position = jnp.arange(length, dtype=jnp.int32)

    rows = x.reshape(seqs * length, width).astype(F32)
    r1 = lax.rsqrt(jnp.mean(rows * rows, axis=-1, keepdims=True) + EPSILON)
    n1 = (rows * r1 * gain_a).astype(BF16)
    qkv = dot(n1, qkv_w)
    q = rotate(qkv[:, :q_cols].reshape(seqs, length, heads, HEAD_SIZE), cos_part, sin_part).astype(BF16)
    k = rotate(qkv[:, q_cols : q_cols + kv_cols].reshape(seqs, length, kv_heads, HEAD_SIZE), cos_part, sin_part).astype(BF16)
    v = qkv[:, q_cols + kv_cols :].astype(BF16).reshape(seqs, length, kv_heads, HEAD_SIZE)
    q = q.reshape(seqs, length, kv_heads, repeat, HEAD_SIZE)
    scores = jnp.einsum("bqgrd,bkgd->bgrqk", q, k, preferred_element_type=F32) * scale
    allowed = (position[None, None, :] <= position[None, :, None]) | (position[None, None, :] < prefix[:, None, None])
    scores = jnp.where(allowed[:, None, None], scores, NEGATIVE)
    exps = jnp.exp(scores - jnp.max(scores, axis=-1, keepdims=True))
    probs = exps / jnp.sum(exps, axis=-1, keepdims=True)
    probs_low = probs.astype(BF16)
    mixed = jnp.einsum("bgrqk,bkgd->bqgrd", probs_low, v, preferred_element_type=F32)
    mixed = mixed.reshape(seqs * length, q_cols).astype(BF16)
    a_own = tensor_sum(dot(mixed, out_w).reshape(seqs, length, width))
    x_own = x[0].astype(F32)
    hid = x_own + keep[0] * a_own
    r2 = lax.rsqrt(jnp.mean(hid * hid, axis=-1, keepdims=True) + EPSILON)
    n2_own = (hid * r2 * gain_f).astype(BF16)
    n2 = jnp.concatenate([n2_own, swap_core(n2_own)], axis=0)

    g = dot(n2, gate_w)
    u = dot(n2, up_w)
    sig = jax.nn.sigmoid(g)
    swish = g * sig
    m = (swish * u).astype(BF16)
    f_own = tensor_sum(dot(m, down_w).reshape(seqs, length, width))
    out_own = (hid + keep[0] * f_own).astype(BF16)
    output = restore(out_own, swap_core(out_own))

    df = (keep[:, None, None] * dy.astype(F32)).astype(BF16).reshape(seqs * length, width)
    grad_down = dot_ta(m, df)
    dm = dot_tb(df, down_w)
    dg = (dm * u * sig * (1.0 + g * (1.0 - sig))).astype(BF16)
    du = (dm * swish).astype(BF16)
    grad_down = ring.scatter([grad_down[:, j * block : (j + 1) * block] for j in range(n)])
    grad_gate = dot_ta(n2, dg)
    grad_gate = ring.scatter([grad_gate[j * block : (j + 1) * block] for j in range(n)])
    grad_up = dot_ta(n2, du)
    grad_up = ring.scatter([grad_up[j * block : (j + 1) * block] for j in range(n)])
    dn2 = tensor_sum((dot_tb(dg, gate_w) + dot_tb(du, up_w)).reshape(seqs, length, width))
    gain_f_sum = jnp.sum(dn2 * hid * r2, axis=0)
    scaled = dn2 * gain_f
    dh = dy[0].astype(F32) + r2 * scaled - hid * (r2 * r2 * r2) * jnp.mean(scaled * hid, axis=-1, keepdims=True)
    da_own = (keep[0] * dh).astype(BF16)
    da = jnp.concatenate([da_own, swap_core(da_own)], axis=0)

    grad_out = dot_ta(mixed, da)
    grad_out = ring.scatter([grad_out[:, j * block : (j + 1) * block] for j in range(n)])
    dmixed = dot_tb(da, out_w).astype(BF16).reshape(seqs, length, kv_heads, repeat, HEAD_SIZE)
    dprobs = jnp.einsum("bqgrd,bkgd->bgrqk", dmixed, v, preferred_element_type=F32)
    dv = jnp.einsum("bgrqk,bqgrd->bkgd", probs_low, dmixed, preferred_element_type=F32).astype(BF16)
    inner = jnp.sum(probs * dprobs, axis=-1, keepdims=True)
    dscores = (probs * (dprobs - inner)).astype(BF16)
    dq = jnp.einsum("bgrqk,bkgd->bqgrd", dscores, k, preferred_element_type=F32) * scale
    dk = jnp.einsum("bgrqk,bqgrd->bkgd", dscores, q, preferred_element_type=F32) * scale
    dq = rotate(dq.reshape(seqs, length, heads, HEAD_SIZE), cos_part, -sin_part).astype(BF16)
    dk = rotate(dk, cos_part, -sin_part).astype(BF16)
    dqkv = jnp.concatenate(
        [d.reshape(seqs * length, -1) for d in (dq, dk, dv)], axis=1
    )
    grad_qkv = dot_ta(n1, dqkv)
    grad_qkv = ring.scatter([grad_qkv[j * block : (j + 1) * block] for j in range(n)])
    dn1 = tensor_sum(dot_tb(dqkv, qkv_w).reshape(seqs, length, width))
    r1_own = r1[:length]
    gain_a_sum = jnp.sum(dn1 * x_own * r1_own, axis=0)
    scaled = dn1 * gain_a
    dx = dh + r1_own * scaled - x_own * (r1_own * r1_own * r1_own) * jnp.mean(scaled * x_own, axis=-1, keepdims=True)
    dx = dx.astype(BF16)
    input_grad = restore(dx, swap_core(dx))

    sums = jnp.stack([gain_a_sum, gain_f_sum]).reshape(2, n, block)
    sums = sums + swap_core(sums)
    gain_grads = ring.small_scatter(sums)
    return (
        output,
        input_grad,
        gain_grads[0],
        grad_qkv[:, :q_cols],
        grad_qkv[:, q_cols : q_cols + kv_cols],
        grad_qkv[:, q_cols + kv_cols :],
        grad_out,
        gain_grads[1],
        grad_gate,
        grad_up,
        grad_down,
    )


def local(ring, inputs, attention_gain, query_weight, key_matrix, value_matrix, out_weight, feedforward_gain,
          gate_weight, up_weight, down_weight, cotangent, layer_keep, prefix_length):
    n = ring.size
    seqs, length, width = inputs.shape
    tokens = seqs * length
    block = width // n
    q_cols, kv_cols = query_weight.shape[1], key_matrix.shape[1]
    cos_part, sin_part = rotary_tables(length)
    cos = jnp.concatenate([cos_part, cos_part], axis=1)
    sin = jnp.concatenate([-sin_part, sin_part], axis=1)
    keep = layer_keep.astype(F32)
    gains = jnp.concatenate([attention_gain[None], feedforward_gain[None], jnp.zeros((14, block), BF16)], axis=0)
    x = inputs.reshape(tokens, width)
    dy = cotangent.reshape(tokens, width)
    names = "gains wq wk wv wo wg wu wd n1 q k v ob hid n2 m fa fb g_down".split()
    values = dict(
        zip(
            names,
            forward(
                n, x, dy, gains, query_weight, key_matrix, value_matrix, out_weight, gate_weight, up_weight, down_weight,
                cos, sin, keep, prefix_length, length,
            ),
        )
    )
    values |= {"x": x, "dy": dy, "cos": cos, "sin": sin, "keep": keep, "prefix": prefix_length}
    outs = backward(n, length, values)
    me = lax.axis_index("dp")

    def total(name, axis):
        own = lax.dynamic_slice_in_dim(outs["g_" + name], me * block, block, axis=axis)
        return own.astype(F32) + outs[f"r_{name}_0"][-1].astype(F32) + outs[f"r_{name}_1"][-1].astype(F32)

    qkv = total("qkv", 0)
    gain_sums = jnp.sum(outs["gain_slots"], axis=0)[:2]
    gain_sums = gain_sums + swap_core(gain_sums)
    return (
        outs["output"].reshape(inputs.shape),
        outs["dx"].reshape(inputs.shape),
        gain_sums[0],
        qkv[:, :q_cols],
        qkv[:, q_cols : q_cols + kv_cols],
        qkv[:, q_cols + kv_cols :],
        total("out", 1),
        gain_sums[1],
        total("gate", 0),
        total("up", 0),
        total("down", 1),
    )


def solution(mesh):
    ring = Ring(mesh.shape["dp"])
    if mesh.shape["tensor"] != 4:
        raise ValueError("tensor axis")
    row, col = P("dp", "tensor"), P("tensor", "dp")
    data = P("dp", None, None)

    def layer(*args):
        block = args[0].shape[2] // ring.size
        return (local if block % 256 == 0 else ring_local)(ring, *args)

    return jax.shard_map(
        layer,
        mesh=mesh,
        in_specs=(data, P("dp"), row, row, row, col, P("dp"), row, row, col, data, P("dp"), P("dp")),
        out_specs=(data, data, P("dp"), row, row, row, col, P("dp"), row, row, col),
        check_vma=False,
    )
```

```python
import functools
import math

import jax
import jax.numpy as jnp
import numpy as np
from jax import lax
from jax.experimental import pallas as pl
from jax.experimental.pallas import tpu as pltpu
from jax.sharding import PartitionSpec as P

HEAD_SIZE = 128
EPSILON = 1e-05
NEGATIVE = -1e30
BF16 = jnp.bfloat16
F32 = jnp.float32
MESH = pl.DeviceIdType.MESH
HBM = pl.BlockSpec(memory_space=pltpu.HBM)
SMEM = pl.BlockSpec(memory_space=pltpu.SMEM)
ROWS = 256


def dot(a, b):
    return jnp.dot(a, b, preferred_element_type=F32)


def dot_ta(a, b):
    return lax.dot_general(a, b, (((0,), (0,)), ((), ())), preferred_element_type=F32)


def dot_tb(a, b):
    return lax.dot_general(a, b, (((1,), (1,)), ((), ())), preferred_element_type=F32)


def spec(rows, cols):
    return pl.BlockSpec((rows, cols), lambda i: (i, 0))


def fixed(*shape):
    return pl.BlockSpec(shape, lambda i: (0,) * len(shape))


def tiles(total, step=256):
    return [(at, min(step, total - at)) for at in range(0, total, step)]


def gain_row(gains_ref, which):
    n = gains_ref.shape[0]
    return jnp.concatenate([gains_ref[j, which : which + 1, :] for j in range(n)], axis=1).astype(F32)


def turn(values, cos, sin):
    return values * cos + pltpu.roll(values, HEAD_SIZE // 2, axis=1) * sin


class Place:
    def __init__(self, n):
        self.n = n
        self.me = lax.axis_index("dp")
        odd = self.me % 2
        self.p = (1 - odd) * (self.me // 2) + odd * (n - 1 - self.me // 2)
        tensor = lax.axis_index("tensor")
        self.core = tensor % 2
        self.core_peer = tensor + 1 - 2 * self.core
        self.chip_peer = (tensor + 2) % 4
        self.right = self.at(1)
        self.left = self.at(-1)

    def at(self, j):
        p = (self.p + j + 2 * self.n) % self.n
        low = p // (self.n // 2)
        return (1 - low) * 2 * p + low * (2 * (self.n - 1 - p) + 1)

    def greet(self):
        barrier = pltpu.get_barrier_semaphore()
        for peer in (self.left, self.right):
            pl.semaphore_signal(barrier, inc=1, device_id={"dp": peer}, device_id_type=MESH)
        for peer in (self.core_peer, self.chip_peer):
            pl.semaphore_signal(barrier, inc=1, device_id={"tensor": peer}, device_id_type=MESH)
        pl.semaphore_wait(barrier, 4)


class Gather:
    def __init__(self, place, shard, whole, where, local_sem, send_sems, recv_sems):
        self.place, self.shard, self.whole, self.where = place, shard, whole, where
        self.send_sems, self.recv_sems = send_sems, recv_sems
        self.hops = place.n // 2
        self.local = pltpu.make_async_copy(shard, where(whole, place.me, None), local_sem)

    def copy(self, way, hop):
        place = self.place
        sign = 1 - 2 * way
        owner = place.at(-sign * (hop - 1))
        half = way if hop == self.hops else None
        target = self.where(self.whole, owner, half)
        if hop > 1:
            source = target
        elif half is None:
            source = self.shard
        else:
            rows = self.shard.shape[0] // 2
            source = self.shard.at[pl.ds(half * rows, rows)]
        return pltpu.make_async_remote_copy(
            src_ref=source,
            dst_ref=target,
            send_sem=self.send_sems.at[way, hop - 1],
            recv_sem=self.recv_sems.at[way, hop - 1],
            device_id={"dp": place.right if way == 0 else place.left},
            device_id_type=MESH,
        )

    def step(self, hop):
        for way in range(2):
            if hop > 1:
                self.copy(way, hop - 1).wait_recv()
            self.copy(way, hop).start()

    def arrived(self):
        self.local.wait()
        for way in range(2):
            self.copy(way, self.hops).wait_recv()

    def drain(self):
        for way in range(2):
            for hop in range(1, self.hops + 1):
                self.copy(way, hop).wait_send()


def by_rows(rows):
    def where(whole, owner, half):
        if half is None:
            return whole.at[pl.ds(pl.multiple_of(owner * rows, rows), rows)]
        return whole.at[pl.ds(pl.multiple_of(owner * rows + half * (rows // 2), rows // 2), rows // 2)]

    return where


def by_cols(rows, cols):
    def where(whole, owner, half):
        at = pl.ds(pl.multiple_of(owner * cols, cols), cols)
        if half is None:
            return whole.at[:, at]
        return whole.at[pl.ds(half * (rows // 2), rows // 2), at]

    return where


def by_slot(whole, owner, half):
    if half is None:
        return whole.at[owner]
    rows = whole.shape[1] // 2
    return whole.at[owner, pl.ds(half * rows, rows)]


class Swap:
    def __init__(self, source, target, peer, send_sem, recv_sem):
        self.copy = pltpu.make_async_remote_copy(
            src_ref=source, dst_ref=target, send_sem=send_sem, recv_sem=recv_sem,
            device_id={"tensor": peer}, device_id_type=MESH,
        )
        self.copy.start()


class Exchange:
    def __init__(self, place, other, peer, near, far, sems):
        self.place, self.other, self.peer, self.near, self.far, self.sems = place, other, peer, near, far, sems
        self.per, self.rows = other.shape[0], other.shape[1]

    def core(self, i):
        return pltpu.make_async_remote_copy(
            src_ref=self.other.at[i], dst_ref=self.peer.at[i], send_sem=self.sems.at[0, i], recv_sem=self.sems.at[1, i],
            device_id={"tensor": self.place.core_peer}, device_id_type=MESH,
        )

    def chip(self, i):
        return pltpu.make_async_remote_copy(
            src_ref=self.near.at[i], dst_ref=self.far.at[i], send_sem=self.sems.at[2, i], recv_sem=self.sems.at[3, i],
            device_id={"tensor": self.place.chip_peer}, device_id_type=MESH,
        )

    def run(self, term, width, step, row_cols, row_args, fixed_args):
        per, core = self.per, self.place.core
        count = len(row_args) + len(fixed_args)

        def body(*refs):
            s = pl.program_id(0)
            for i in range(per):
                if i:
                    @pl.when(s == i)
                    def _():
                        self.core(i - 1).start()

                @pl.when(s == per + i)
                def _():
                    if i == 0:
                        self.core(per - 1).start()
                    else:
                        self.chip(i - 1).start()
                    self.core(i).wait_recv()

            @pl.when(s < per)
            def _():
                for at, size in tiles(width, step):
                    cols = slice(at, at + size)
                    self.other[s, :, cols] = term(refs, cols).astype(BF16)

            @pl.when(s >= per)
            def _():
                for at, size in tiles(width, step):
                    cols = slice(at, at + size)
                    self.near[s - per, :, cols] = (term(refs, cols) + self.peer[s - per, :, cols].astype(F32)).astype(BF16)

        def block(s):
            return ((1 - core) + (s // per) * (2 * core - 1)) * per + s % per

        pltpu.emit_pipeline(
            body,
            grid=(2 * per,),
            in_specs=[pl.BlockSpec((self.rows, cols), lambda s: (block(s), 0)) for cols in row_cols]
            + [fixed(*w.shape) for w in fixed_args],
        )(*row_args, *fixed_args)
        self.chip(per - 1).start()
        for i in range(per):
            self.core(i).wait_send()

    def arrived(self):
        for i in range(self.per):
            self.chip(i).wait_recv()

    def drain(self):
        for i in range(self.per):
            self.chip(i).wait_send()

    def total(self, at, rows):
        i, part = at // self.rows, pl.ds(pl.multiple_of(at % self.rows, rows), rows)
        return self.near[i, part, :].astype(F32) + self.far[i, part, :].astype(F32)


CHUNK = 16
BLOCK = 128


def by_chunks(step, body):
    @pl.loop(0, BLOCK, step=CHUNK)
    def _(at):
        at = pl.multiple_of(at, CHUNK)
        body(pl.ds(at, CHUNK), step * BLOCK + at)


def forward_kernel(
    n, length, x_hbm, dy_hbm, gains_in, wq_in, wk_in, wv_in, wo_in, wg_in, wu_in, wd_in, cos_hbm, sin_hbm, keep_ref, prefix_ref,
    gains_w, wq, wk, wv, wo, wg, wu, wd, n1_hbm, q_hbm, k_hbm, v_hbm, ob_hbm, hid_hbm, n2_hbm, m_hbm, fa_hbm, fb_hbm, gd_hbm,
    other, peer, near, far, local_sems, send_sems, recv_sems, swap_sems, share_sems,
):
    place = Place(n)
    core = place.core
    place.greet()
    tokens, width = x_hbm.shape
    scale = 1.0 / math.sqrt(HEAD_SIZE)
    half = wd_in.shape[0] // 2
    upper, lower = pl.ds(0, half), pl.ds(half, half)
    arrays = {
        "n": (gains_in, gains_w, by_slot),
        "q": (wq_in, wq, by_rows(wq_in.shape[0])),
        "k": (wk_in, wk, by_rows(wk_in.shape[0])),
        "v": (wv_in, wv, by_rows(wv_in.shape[0])),
        "o": (wo_in, wo, by_cols(*wo_in.shape)),
        "g": (wg_in, wg, by_rows(wg_in.shape[0])),
        "u": (wu_in, wu, by_rows(wu_in.shape[0])),
        "a": (wd_in.at[upper], wd.at[upper], by_cols(half, wd_in.shape[1])),
        "b": (wd_in.at[lower], wd.at[lower], by_cols(half, wd_in.shape[1])),
    }
    rings = {
        name: Gather(place, shard, whole, where, local_sems.at[i], send_sems.at[i], recv_sems.at[i])
        for i, (name, (shard, whole, where)) in enumerate(arrays.items())
    }
    hops = n // 2
    done = {name: 0 for name in rings}

    def go(names):
        for name in names:
            if done[name] < hops:
                done[name] += 1
                rings[name].step(done[name])

    own_rows = pl.ds(pl.multiple_of(core * length, length), length)
    other_rows = pl.ds(pl.multiple_of((1 - core) * length, length), length)

    go("nqkv")
    for name in "nqkvogu":
        rings[name].local.start()
    go("nqkvo")
    go("nqkvo")
    go("nqkvog")
    for name in "nqkv":
        go(name * hops)
        rings[name].arrived()

    def project(x_ref, gains_ref, wq_ref, wk_ref, wv_ref, cos_ref, sin_ref, n1_ref, q_ref, k_ref, v_ref):
        gain = gain_row(gains_ref, 0)

        @pl.loop(0, ROWS, step=32)
        def _(at):
            part = pl.ds(pl.multiple_of(at, 32), 32)
            xf = x_ref[part, :].astype(F32)
            r1 = lax.rsqrt(jnp.mean(xf * xf, axis=-1, keepdims=True) + EPSILON)
            n1_ref[part, :] = (xf * r1 * gain).astype(BF16)

        rows = n1_ref[...]
        cos, sin = cos_ref[...], sin_ref[...]
        for w_ref, o_ref in ((wq_ref, q_ref), (wk_ref, k_ref)):
            for at in range(0, w_ref.shape[1], HEAD_SIZE):
                head = slice(at, at + HEAD_SIZE)
                o_ref[:, head] = turn(dot(rows, w_ref[:, head]), cos, sin).astype(BF16)
        v_ref[...] = dot(rows, wv_ref[...]).astype(BF16)

    q_cols, kv_cols = wq.shape[1], wk.shape[1]
    per = length // ROWS
    turns = pl.BlockSpec((ROWS, HEAD_SIZE), lambda i: (i % per, 0))
    pltpu.emit_pipeline(
        project,
        grid=(tokens // ROWS,),
        in_specs=[spec(ROWS, width), fixed(*gains_w.shape), fixed(*wq.shape), fixed(*wk.shape), fixed(*wv.shape), turns, turns],
        out_specs=[spec(ROWS, width), spec(ROWS, q_cols), spec(ROWS, kv_cols), spec(ROWS, kv_cols)],
    )(x_hbm, gains_w, wq, wk, wv, cos_hbm, sin_hbm, n1_hbm, q_hbm, k_hbm, v_hbm)
    go("ogu")

    repeat = q_cols // kv_cols

    def attend(which, q_ref, k_ref, v_ref, o_ref):
        prefix = prefix_ref[which]
        keys, values = k_ref[...], v_ref[...]

        @pl.loop(0, length, step=128)
        def _(at):
            part = pl.ds(pl.multiple_of(at, 128), 128)
            s = dot_tb(q_ref[part, :], keys) * scale
            row = lax.broadcasted_iota(jnp.int32, s.shape, 0) + at
            col = lax.broadcasted_iota(jnp.int32, s.shape, 1)
            s = jnp.where((col <= row) | (col < prefix), s, NEGATIVE)
            e = jnp.exp(s - jnp.max(s, axis=-1, keepdims=True))
            p = e / jnp.sum(e, axis=-1, keepdims=True)
            o_ref[part, :] = dot(p.astype(BF16), values).astype(BF16)

    for which in range(2):
        seq = pl.ds(which * length, length)
        pltpu.emit_pipeline(
            functools.partial(attend, which),
            grid=(q_cols // HEAD_SIZE,),
            in_specs=[
                pl.BlockSpec((length, HEAD_SIZE), lambda h: (0, h)),
                pl.BlockSpec((length, HEAD_SIZE), lambda h: (0, h // repeat)),
                pl.BlockSpec((length, HEAD_SIZE), lambda h: (0, h // repeat)),
            ],
            out_specs=[pl.BlockSpec((length, HEAD_SIZE), lambda h: (0, h))],
        )(q_hbm.at[seq], k_hbm.at[seq], v_hbm.at[seq], ob_hbm.at[seq])

    go("o" * hops)
    rings["o"].arrived()
    go("g")
    mixed = Exchange(place, other, peer, near, far, swap_sems)
    mixed.run(lambda refs, cols: dot(refs[0][...], refs[1][:, cols]), width, 512, [q_cols], [ob_hbm], [wo])
    for name in "ab":
        rings[name].local.start()
    go("u")
    go("g")
    go("u")
    mixed.arrived()

    def residual(x_ref, gains_ref, hid_ref, n2_ref):
        gain = gain_row(gains_ref, 1)
        keep = keep_ref[core]

        def chunk(part, row):
            h = x_ref[part, :].astype(F32) + keep * mixed.total(row, CHUNK)
            hid_ref[part, :] = h
            r2 = lax.rsqrt(jnp.mean(h * h, axis=-1, keepdims=True) + EPSILON)
            n2_ref[part, :] = (h * r2 * gain).astype(BF16)

        by_chunks(pl.program_id(0), chunk)

    pltpu.emit_pipeline(
        residual,
        grid=(length // BLOCK,),
        in_specs=[spec(BLOCK, width), fixed(*gains_w.shape)],
        out_specs=[spec(BLOCK, width)] * 2,
    )(x_hbm.at[own_rows], gains_w, hid_hbm, n2_hbm.at[own_rows])
    share = Swap(n2_hbm.at[own_rows], n2_hbm.at[own_rows], place.core_peer, share_sems.at[0], share_sems.at[1])
    share.copy.wait_recv()
    go("g" * hops + "u" * hops + "ab")
    rings["g"].arrived()
    rings["u"].arrived()

    hidden = wg.shape[1]

    def during(at, name, hop):
        pl.when(pl.program_id(0) == at)(lambda: rings[name].step(hop))
        done[name] = hop

    def feed(n2_ref, wg_ref, wu_ref, m_ref, fa_ref, fb_ref):
        during(tokens // ROWS - 2, "a", 2)
        during(tokens // ROWS - 1, "b", 2)
        rows = n2_ref[...]
        for at, size in tiles(hidden):
            cols = slice(at, at + size)
            g = dot(rows, wg_ref[:, cols])
            u = dot(rows, wu_ref[:, cols])
            sig = 1.0 / (1.0 + jnp.exp(-g))
            swish = g * sig
            m_ref[:, cols] = (swish * u).astype(BF16)
            fa_ref[:, cols] = u * sig * (1.0 + g * (1.0 - sig))
            fb_ref[:, cols] = swish

    pltpu.emit_pipeline(
        feed,
        grid=(tokens // ROWS,),
        in_specs=[spec(ROWS, width), fixed(*wg.shape), fixed(*wu.shape)],
        out_specs=[spec(ROWS, hidden)] * 3,
    )(n2_hbm, wg, wu, m_hbm, fa_hbm, fb_hbm)

    def down_grad(m_ref, dy_ref, o_ref):
        during(1, "a", 3)
        during(5, "b", 3)
        total = None
        for which in range(2):
            seq = slice(which * length, (which + 1) * length)
            df = (dy_ref[seq, :].astype(F32) * keep_ref[which]).astype(BF16)
            term = dot_ta(m_ref[seq, :], df)
            total = term if total is None else total + term
        o_ref[...] = total.astype(BF16)

    cols = pl.BlockSpec((tokens, 256), lambda i: (0, i))
    pltpu.emit_pipeline(
        down_grad,
        grid=(width // 256,),
        in_specs=[fixed(tokens, hidden), cols],
        out_specs=[pl.BlockSpec((hidden, 256), lambda i: (0, i))],
    )(m_hbm, dy_hbm, gd_hbm)
    for _ in range(hops):
        go("ab")
    rings["a"].arrived()
    rings["b"].arrived()
    for ring in rings.values():
        ring.drain()
    mixed.drain()
    share.copy.wait_send()


def forward(n, x, dy, gains, wq, wk, wv, wo, wg, wu, wd, cos, sin, keep, prefix, length):
    tokens, width = x.shape
    shape = jax.ShapeDtypeStruct
    ff = wg.shape[1]
    outs = [
        shape((n,) + gains.shape, BF16),
        shape((width, wq.shape[1]), BF16),
        shape((width, wk.shape[1]), BF16),
        shape((width, wv.shape[1]), BF16),
        shape((wo.shape[0], width), BF16),
        shape((width, ff), BF16),
        shape((width, ff), BF16),
        shape((ff, width), BF16),
        shape((tokens, width), BF16),
        shape((tokens, wq.shape[1]), BF16),
        shape((tokens, wk.shape[1]), BF16),
        shape((tokens, wv.shape[1]), BF16),
        shape((tokens, wq.shape[1]), BF16),
        shape((length, width), F32),
        shape((tokens, width), BF16),
        shape((tokens, ff), BF16),
        shape((tokens, ff), F32),
        shape((tokens, ff), F32),
        shape((ff, width), BF16),
    ]
    blocks = pltpu.VMEM((length // ROWS, ROWS, width), BF16)
    return pl.pallas_call(
        functools.partial(forward_kernel, n, length),
        out_shape=outs,
        in_specs=[HBM] * 12 + [SMEM] * 2,
        out_specs=[HBM] * len(outs),
        scratch_shapes=[
            blocks,
            blocks,
            blocks,
            blocks,
            pltpu.SemaphoreType.DMA((9,)),
            pltpu.SemaphoreType.DMA((9, 2, n // 2)),
            pltpu.SemaphoreType.DMA((9, 2, n // 2)),
            pltpu.SemaphoreType.DMA((4, length // ROWS)),
            pltpu.SemaphoreType.DMA((2,)),
        ],
        compiler_params=pltpu.CompilerParams(collective_id=0, has_side_effects=True, vmem_limit_bytes=60 * 1024 * 1024),
    )(x, dy, gains, wq, wk, wv, wo, wg, wu, wd, cos, sin, keep, prefix)


class Scatter:
    def __init__(self, place, whole, where, slots, send_sems, recv_sems):
        self.place, self.whole, self.where, self.slots = place, whole, where, slots
        self.send_sems, self.recv_sems = send_sems, recv_sems
        self.hops = place.n // 2
        self.copies = {}

    def view(self, way, hop):
        sign = 1 - 2 * way
        owner = self.place.at(sign * (self.hops + 1 - hop))
        return self.where(self.whole, owner, way if hop == 1 else None)

    def slot(self, way, hop):
        first, rest = self.slots[way]
        return first if hop == 1 else rest.at[hop - 2]

    def add(self, hop):
        terms, views = [], []
        for way in range(2):
            self.copies[way, hop - 1].wait_recv()
            sign = 1 - 2 * way
            owner = self.place.at(sign * (self.hops + 1 - hop))
            views.append(self.where(self.whole, owner, way if hop == 2 else None))
            terms.append(self.slot(way, hop - 1))
        rows, cols = views[0].shape
        count = 2 if hop == 2 else 4

        def body(a_ref, b_ref, c_ref, d_ref, o_ref, p_ref):
            o_ref[...] = (a_ref[...].astype(F32) + b_ref[...].astype(F32)).astype(BF16)
            p_ref[...] = (c_ref[...].astype(F32) + d_ref[...].astype(F32)).astype(BF16)

        pltpu.emit_pipeline(
            body, grid=(count,), in_specs=[spec(rows // count, cols)] * 4, out_specs=[spec(rows // count, cols)] * 2
        )(views[0], terms[0], views[1], terms[1], views[0], views[1])

    def step(self, hop):
        if hop > 1:
            self.add(hop)
        for way in range(2):
            copy = pltpu.make_async_remote_copy(
                src_ref=self.view(way, hop),
                dst_ref=self.slot(way, hop),
                send_sem=self.send_sems.at[way, hop - 1],
                recv_sem=self.recv_sems.at[way, hop - 1],
                device_id={"dp": self.place.right if way == 0 else self.place.left},
                device_id_type=MESH,
            )
            copy.start()
            self.copies[way, hop] = copy

    def drain(self):
        for way in range(2):
            self.copies[way, self.hops].wait_recv()
        for copy in self.copies.values():
            copy.wait_send()


def backward_kernel(n, length, names_in, names_out, *refs):
    ins = dict(zip(names_in, refs))
    outs = dict(zip(names_out, refs[len(names_in) :]))
    (gsum, gpieces, dh, other, peers, nears, fars, local_sems, send_sems, recv_sems, swap_sems, swap_send, swap_recv, gain_send, gain_recv) = refs[
        len(names_in) + len(names_out) :
    ]
    keep_ref, prefix_ref = ins["keep"], ins["prefix"]
    dy, x, gains_w = ins["dy"], ins["x"], ins["gains"]
    wq, wk, wv, wo, wg, wu, wd = (ins[name] for name in ("wq", "wk", "wv", "wo", "wg", "wu", "wd"))
    tokens, width = x.shape
    q_cols, kv_cols, hidden = wq.shape[1], wk.shape[1], wg.shape[1]
    block = width // n
    per = length // ROWS
    repeat = q_cols // kv_cols
    scale = 1.0 / math.sqrt(HEAD_SIZE)
    place = Place(n)
    core = place.core
    barrier = pltpu.get_barrier_semaphore()
    for j in range(1, n):
        pl.semaphore_signal(barrier, inc=1, device_id={"dp": place.at(j)}, device_id_type=MESH)
    for peer in (place.core_peer, place.chip_peer):
        pl.semaphore_signal(barrier, inc=1, device_id={"tensor": peer}, device_id_type=MESH)
    pl.semaphore_wait(barrier, n + 1)

    own_rows = pl.ds(pl.multiple_of(core * length, length), length)
    wheres = {
        "down": by_cols(hidden, block),
        "gate": by_rows(block),
        "up": by_rows(block),
        "out": by_cols(q_cols, block),
        "qkv": by_rows(block),
    }
    rings = {
        name: Scatter(
            place,
            outs["g_" + name],
            wheres[name],
            [(outs[f"r_{name}_{way}_first"], outs[f"r_{name}_{way}"]) for way in range(2)],
            send_sems.at[i],
            recv_sems.at[i],
        )
        for i, name in enumerate(wheres)
    }
    swaps = []

    def swap(source, target, peer):
        i = len(swaps)
        swaps.append(Swap(source, target, peer, swap_send.at[i], swap_recv.at[i]))
        return swaps[-1].copy

    def act_grads():
        def body(dy_ref, wd_ref, fa_ref, fb_ref, dg_ref, du_ref):
            which = pl.program_id(0) // per
            df = (dy_ref[...].astype(F32) * keep_ref[which]).astype(BF16)
            for at, size in tiles(hidden):
                cols = slice(at, at + size)
                dm = dot_tb(df, wd_ref[cols, :])
                dg_ref[:, cols] = (dm * fa_ref[:, cols]).astype(BF16)
                du_ref[:, cols] = (dm * fb_ref[:, cols]).astype(BF16)

        pltpu.emit_pipeline(
            body,
            grid=(tokens // ROWS,),
            in_specs=[spec(ROWS, width), fixed(hidden, width), spec(ROWS, hidden), spec(ROWS, hidden)],
            out_specs=[spec(ROWS, hidden)] * 2,
        )(dy, wd, ins["fa"], ins["fb"], outs["dg"], outs["du"])

    def outer(left, right, target):
        def body(l_ref, r_ref, o_ref):
            o_ref[...] = dot_ta(l_ref[...], r_ref[...]).astype(BF16)

        cols = right.shape[1]
        pltpu.emit_pipeline(
            body,
            grid=(width // 256,),
            in_specs=[pl.BlockSpec((tokens, 256), lambda i: (0, i)), fixed(tokens, cols)],
            out_specs=[spec(256, cols)],
        )(left, right, target)

    def exchange(i):
        return Exchange(place, other, peers.at[i], nears.at[i], fars.at[i], swap_sems.at[i])

    in_n2, in_f, in_n1 = exchange(0), exchange(1), exchange(2)

    def back():
        in_n2.run(
            lambda refs, cols: dot_tb(refs[0][...], refs[2][cols, :]) + dot_tb(refs[1][...], refs[3][cols, :]),
            width, 256, [hidden, hidden], [outs["dg"], outs["du"]], [wg, wu],
        )

    def add_gain(which, terms):
        gsum[which] += sum(terms[i * 8 : (i + 1) * 8] for i in range(terms.shape[0] // 8))

    def norm_back(d, h, gain, which):
        r = lax.rsqrt(jnp.mean(h * h, axis=-1, keepdims=True) + EPSILON)
        add_gain(which, d * h * r)
        scaled = d * gain
        return r * scaled - h * (r * r * r) * jnp.mean(scaled * h, axis=-1, keepdims=True)

    def hid_grads():
        def body(hid_ref, dy_ref, gains_ref, da_ref):
            gain = gain_row(gains_ref, 1)
            keep = keep_ref[core]

            def chunk(part, row):
                d = in_n2.total(row, CHUNK)
                value = dy_ref[part, :].astype(F32) + norm_back(d, hid_ref[part, :], gain, 1)
                dh[pl.ds(pl.multiple_of(row, CHUNK), CHUNK), :] = value
                da_ref[part, :] = (keep * value).astype(BF16)

            by_chunks(pl.program_id(0), chunk)

        pltpu.emit_pipeline(
            body,
            grid=(length // BLOCK,),
            in_specs=[spec(BLOCK, width)] * 2 + [fixed(*gains_w.shape)],
            out_specs=[spec(BLOCK, width)],
        )(ins["hid"], dy.at[own_rows], gains_w, outs["da"].at[own_rows])
        return swap(outs["da"].at[own_rows], outs["da"].at[own_rows], place.core_peer)

    def input_grads():
        def body(x_ref, gains_ref, dx_ref):
            gain = gain_row(gains_ref, 0)

            def chunk(part, row):
                d = in_n1.total(row, CHUNK)
                value = norm_back(d, x_ref[part, :].astype(F32), gain, 0)
                dx_ref[part, :] = (dh[pl.ds(pl.multiple_of(row, CHUNK), CHUNK), :] + value).astype(BF16)

            by_chunks(pl.program_id(0), chunk)

        pltpu.emit_pipeline(
            body,
            grid=(length // BLOCK,),
            in_specs=[spec(BLOCK, width), fixed(*gains_w.shape)],
            out_specs=[spec(BLOCK, width)],
        )(x.at[own_rows], gains_w, outs["dx"].at[own_rows])
        return swap(outs["dx"].at[own_rows], outs["dx"].at[own_rows], place.core_peer)

    def results():
        def body(hid_ref, o_ref):
            keep = keep_ref[core]

            def chunk(part, row):
                o_ref[part, :] = (hid_ref[part, :] + keep * in_f.total(row, CHUNK)).astype(BF16)

            by_chunks(pl.program_id(0), chunk)

        pltpu.emit_pipeline(
            body, grid=(length // BLOCK,), in_specs=[spec(BLOCK, width)], out_specs=[spec(BLOCK, width)]
        )(ins["hid"], outs["output"].at[own_rows])
        return swap(outs["output"].at[own_rows], outs["output"].at[own_rows], place.core_peer)

    def forth():
        in_f.run(lambda refs, cols: dot(refs[0][...], refs[1][:, cols]), width, 512, [hidden], [ins["m"]], [wd])

    def out_grad():
        def body(ob_ref, da_ref, o_ref):
            o_ref[...] = dot_ta(ob_ref[...], da_ref[...]).astype(BF16)

        pltpu.emit_pipeline(
            body,
            grid=(width // 256,),
            in_specs=[fixed(tokens, q_cols), pl.BlockSpec((tokens, 256), lambda i: (0, i))],
            out_specs=[pl.BlockSpec((q_cols, 256), lambda i: (0, i))],
        )(ins["ob"], outs["da"], outs["g_out"])

    def mixed_grad():
        def body(da_ref, wo_ref, o_ref):
            o_ref[...] = dot_tb(da_ref[...], wo_ref[...]).astype(BF16)

        pltpu.emit_pipeline(
            body, grid=(tokens // ROWS,), in_specs=[spec(ROWS, width), fixed(q_cols, width)], out_specs=[spec(ROWS, q_cols)]
        )(outs["da"], wo, outs["dob"])

    def attend_back(which):
        seq = pl.ds(which * length, length)

        def heads(dk_sum, dv_sum):
            def body(q_ref, k_ref, v_ref, d_ref, cos_ref, sin_ref, dq_ref, dk_ref, dv_ref):
                head = pl.program_id(0) % repeat
                prefix = prefix_ref[which]
                keys, values = k_ref[...], v_ref[...]

                @pl.when(head == 0)
                def _():
                    dk_sum[...] = jnp.zeros_like(dk_sum)
                    dv_sum[...] = jnp.zeros_like(dv_sum)

                @pl.loop(0, length, step=128)
                def _(at):
                    part = pl.ds(pl.multiple_of(at, 128), 128)
                    queries, grads = q_ref[part, :], d_ref[part, :]
                    s = dot_tb(keys, queries) * scale
                    col = lax.broadcasted_iota(jnp.int32, s.shape, 0)
                    row = lax.broadcasted_iota(jnp.int32, s.shape, 1) + at
                    s = jnp.where((col <= row) | (col < prefix), s, NEGATIVE)
                    e = jnp.exp(s - jnp.max(s, axis=0, keepdims=True))
                    p = e / jnp.sum(e, axis=0, keepdims=True)
                    dp = dot_tb(values, grads)
                    inner = jnp.sum(p * dp, axis=0, keepdims=True)
                    dz = (p * (dp - inner)).astype(BF16)
                    dv_sum[...] += dot(p.astype(BF16), grads)
                    dk_sum[...] += dot(dz, queries)
                    dq = dot_ta(dz, keys) * scale
                    dq_ref[part, :] = turn(dq, cos_ref[part, :], -sin_ref[part, :]).astype(BF16)

                @pl.when(head == repeat - 1)
                def _():
                    dk_ref[...] = turn(dk_sum[...] * scale, cos_ref[...], -sin_ref[...]).astype(BF16)
                    dv_ref[...] = dv_sum[...].astype(BF16)

            one = pl.BlockSpec((length, HEAD_SIZE), lambda h: (0, h))
            shared = pl.BlockSpec((length, HEAD_SIZE), lambda h: (0, h // repeat))
            table = pl.BlockSpec((length, HEAD_SIZE), lambda h: (0, 0))
            dqkv = outs["dqkv"].at[seq]
            pltpu.emit_pipeline(
                body,
                grid=(q_cols // HEAD_SIZE,),
                in_specs=[one, shared, shared, one, table, table],
                out_specs=[one, shared, shared],
            )(
                ins["q"].at[seq],
                ins["k"].at[seq],
                ins["v"].at[seq],
                outs["dob"].at[seq],
                ins["cos"],
                ins["sin"],
                dqkv.at[:, pl.ds(0, q_cols)],
                dqkv.at[:, pl.ds(q_cols, kv_cols)],
                dqkv.at[:, pl.ds(q_cols + kv_cols, kv_cols)],
            )

        pl.run_scoped(heads, pltpu.VMEM((length, HEAD_SIZE), F32), pltpu.VMEM((length, HEAD_SIZE), F32))

    def back_qkv():
        def term(refs, cols):
            d_ref, wq_ref, wk_ref, wv_ref = refs
            dq, dk, dv = d_ref[:, :q_cols], d_ref[:, q_cols : q_cols + kv_cols], d_ref[:, q_cols + kv_cols :]
            return dot_tb(dq, wq_ref[cols, :]) + dot_tb(dk, wk_ref[cols, :]) + dot_tb(dv, wv_ref[cols, :])

        in_n1.run(term, width, 256, [q_cols + 2 * kv_cols], [outs["dqkv"]], [wq, wk, wv])

    def gain_grads():
        for which in range(2):
            row = jnp.sum(gsum[which], axis=0, keepdims=True)
            for j in range(n):
                gpieces[j, which : which + 1, :] = row[:, j * block : (j + 1) * block]
        copy = pltpu.make_async_copy(gpieces, outs["gain_terms"], local_sems.at[0])
        copy.start()
        copy.wait()
        mine = pltpu.make_async_copy(outs["gain_terms"].at[place.me], outs["gain_slots"].at[0], local_sems.at[1])
        mine.start()
        copies = []
        for j in range(1, n):
            copy = pltpu.make_async_remote_copy(
                src_ref=outs["gain_terms"].at[place.at(j)],
                dst_ref=outs["gain_slots"].at[j],
                send_sem=gain_send.at[j],
                recv_sem=gain_recv.at[j],
                device_id={"dp": place.at(j)},
                device_id_type=MESH,
            )
            copy.start()
            copies.append(copy)
        return mine, copies

    gsum[...] = jnp.zeros_like(gsum)
    gpieces[...] = jnp.zeros_like(gpieces)
    rings["down"].step(1)
    act_grads()
    rings["down"].step(2)
    back()
    rings["down"].step(3)
    outer(ins["n2"], outs["dg"], outs["g_gate"])
    rings["gate"].step(1)
    rings["down"].step(4)
    outer(ins["n2"], outs["du"], outs["g_up"])
    rings["gate"].step(2)
    rings["up"].step(1)
    forth()
    rings["gate"].step(3)
    in_n2.arrived()
    share_da = hid_grads()
    rings["up"].step(2)
    rings["gate"].step(4)
    share_da.wait_recv()
    mixed_grad()
    attend_back(0)
    rings["up"].step(3)
    out_grad()
    rings["out"].step(1)
    attend_back(1)
    rings["up"].step(4)
    back_qkv()
    outer(ins["n1"], outs["dqkv"], outs["g_qkv"])
    rings["qkv"].step(1)
    rings["out"].step(2)
    in_f.arrived()
    share_out = results()
    rings["qkv"].step(2)
    rings["out"].step(3)
    rings["qkv"].step(3)
    rings["out"].step(4)
    in_n1.arrived()
    share_dx = input_grads()
    rings["qkv"].step(4)
    mine, copies = gain_grads()
    share_out.wait_recv()
    share_dx.wait_recv()
    mine.wait()
    for copy in copies:
        copy.wait_recv()
    for ring in rings.values():
        ring.drain()
    for copy in copies:
        copy.wait_send()
    for item in swaps:
        item.copy.wait_send()
    for item in (in_n2, in_f, in_n1):
        item.drain()


def backward(n, length, values):
    shape = jax.ShapeDtypeStruct
    tokens, width = values["x"].shape
    q_cols, kv_cols, hidden = values["wq"].shape[1], values["wk"].shape[1], values["wg"].shape[1]
    block = width // n
    outs = {}
    sizes = {
        "down": ((hidden, width), (hidden, block)),
        "gate": ((width, hidden), (block, hidden)),
        "up": ((width, hidden), (block, hidden)),
        "out": ((q_cols, width), (q_cols, block)),
        "qkv": ((width, q_cols + 2 * kv_cols), (block, q_cols + 2 * kv_cols)),
    }
    for name, (whole, piece) in sizes.items():
        outs["g_" + name] = shape(whole, BF16)
        for way in range(2):
            outs[f"r_{name}_{way}_first"] = shape((piece[0] // 2, piece[1]), BF16)
            outs[f"r_{name}_{way}"] = shape((n // 2 - 1,) + piece, BF16)
    outs["dg"] = outs["du"] = shape((tokens, hidden), BF16)
    outs["da"] = outs["dx"] = outs["output"] = shape((tokens, width), BF16)
    outs["dob"] = shape((tokens, q_cols), BF16)
    outs["dqkv"] = shape((tokens, q_cols + 2 * kv_cols), BF16)
    outs["gain_terms"] = outs["gain_slots"] = shape((n, 8, block), F32)
    names_in, names_out = list(values), list(outs)
    results = pl.pallas_call(
        functools.partial(backward_kernel, n, length, names_in, names_out),
        out_shape=list(outs.values()),
        in_specs=[SMEM if name in ("keep", "prefix") else HBM for name in names_in],
        out_specs=[HBM] * len(outs),
        input_output_aliases={names_in.index("g_down"): names_out.index("g_down")},
        scratch_shapes=[
            pltpu.VMEM((2, 8, width), F32),
            pltpu.VMEM((n, 8, block), F32),
            pltpu.VMEM((length, width), F32),
            pltpu.VMEM((length // ROWS, ROWS, width), BF16),
            pltpu.VMEM((3, length // ROWS, ROWS, width), BF16),
            pltpu.VMEM((3, length // ROWS, ROWS, width), BF16),
            pltpu.VMEM((3, length // ROWS, ROWS, width), BF16),
            pltpu.SemaphoreType.DMA((2,)),
            pltpu.SemaphoreType.DMA((5, 2, n // 2)),
            pltpu.SemaphoreType.DMA((5, 2, n // 2)),
            pltpu.SemaphoreType.DMA((3, 4, length // ROWS)),
            pltpu.SemaphoreType.DMA((3,)),
            pltpu.SemaphoreType.DMA((3,)),
            pltpu.SemaphoreType.DMA((n,)),
            pltpu.SemaphoreType.DMA((n,)),
        ],
        compiler_params=pltpu.CompilerParams(collective_id=1, has_side_effects=True, vmem_limit_bytes=60 * 1024 * 1024),
    )(*values.values())
    return dict(zip(names_out, results))


def rotary_tables(length_total):
    half_width = HEAD_SIZE // 2
    frequency = (10000.0 ** (-(np.arange(half_width, dtype=np.float32) * 2.0) / HEAD_SIZE)).astype(np.float32)
    angles = np.arange(length_total, dtype=np.float32)[:, None] * frequency[None, :]
    return (jnp.asarray(np.cos(angles)), jnp.asarray(np.sin(angles)))


def rotate(values, cos_part, sin_part):
    first, second = jnp.split(values, 2, axis=-1)
    return jnp.concatenate(
        [first * cos_part - second * sin_part, first * sin_part + second * cos_part], axis=-1
    )


class Ring:
    def __init__(self, size):
        self.size = size
        self.half = size // 2
        self.order = [2 * p if p < self.half else 2 * (size - 1 - p) + 1 for p in range(size)]
        self.right = [(self.order[p], self.order[(p + 1) % size]) for p in range(size)]
        self.left = [(b, a) for a, b in self.right]

    def place(self):
        me = lax.axis_index("dp")
        odd = me % 2
        return (1 - odd) * (me // 2) + odd * (self.size - 1 - me // 2)

    def owners(self):
        return jnp.asarray(np.array(self.order, np.int32))[(self.place() + np.arange(self.size)) % self.size]

    def gather(self, shard):
        n, m = self.size, self.half
        pieces = [None] * n
        pieces[0] = shard
        from_left, from_right = shard, shard
        for hop in range(1, m):
            from_left = lax.ppermute(from_left, "dp", self.right)
            from_right = lax.ppermute(from_right, "dp", self.left)
            pieces[n - hop] = from_left
            pieces[hop] = from_right
        rows = shard.shape[0] // 2
        top = lax.ppermute(from_left[:rows], "dp", self.right)
        low = lax.ppermute(from_right[rows:], "dp", self.left)
        pieces[m] = jnp.concatenate([top, low], axis=0)
        return pieces

    def scatter(self, parts):
        n, m = self.size, self.half
        rows = parts[0].shape[0] // 2
        kind = BF16
        up = lax.ppermute(parts[m][:rows].astype(kind), "dp", self.right)
        down = lax.ppermute(parts[m][rows:].astype(kind), "dp", self.left)
        for hop in range(m - 1, 0, -1):
            mine_up, mine_down = parts[hop], parts[n - hop]
            if hop == m - 1:
                mine_up = jnp.concatenate([mine_up[:rows] + up.astype(F32), mine_up[rows:]], axis=0)
                mine_down = jnp.concatenate([mine_down[:rows], mine_down[rows:] + down.astype(F32)], axis=0)
            else:
                mine_up = mine_up + up.astype(F32)
                mine_down = mine_down + down.astype(F32)
            up = lax.ppermute(mine_up.astype(kind), "dp", self.right)
            down = lax.ppermute(mine_down.astype(kind), "dp", self.left)
        if m == 1:
            return jnp.concatenate([parts[0][:rows] + up.astype(F32), parts[0][rows:] + down.astype(F32)], axis=0)
        return parts[0] + up.astype(F32) + down.astype(F32)


    def small_scatter(self, sums):
        up = sums[:, self.half]
        for hop in range(self.half - 1, -1, -1):
            up = lax.ppermute(up, "dp", self.right)
            up = up + sums[:, hop]
        if self.size > 2:
            down = sums[:, self.half + 1]
            for hop in range(self.half - 2, -1, -1):
                down = lax.ppermute(down, "dp", self.left)
                if hop:
                    down = down + sums[:, self.size - hop]
            up = up + down
        return up


CORE_PAIRS = [(0, 1), (1, 0), (2, 3), (3, 2)]
CHIP_PAIRS = [(0, 2), (2, 0), (1, 3), (3, 1)]


def swap_core(value):
    return lax.ppermute(value, "tensor", CORE_PAIRS)


def swap_chip(value):
    return lax.ppermute(value, "tensor", CHIP_PAIRS)


def tensor_sum(part):
    near = part[0] + swap_core(part[1].astype(BF16)).astype(F32)
    near = near.astype(BF16)
    return near.astype(F32) + swap_chip(near).astype(F32)


def ring_local(ring, inputs, attention_gain, query_weight, key_matrix, value_matrix, out_weight, feedforward_gain,
          gate_weight, up_weight, down_weight, cotangent, layer_keep, prefix_length):
    n = ring.size
    seqs, length, width = inputs.shape
    block = width // n
    q_cols, kv_cols = query_weight.shape[1], key_matrix.shape[1]
    heads = q_cols // HEAD_SIZE
    kv_heads = kv_cols // HEAD_SIZE
    repeat = heads // kv_heads
    scale = 1.0 / math.sqrt(HEAD_SIZE)
    core = lax.axis_index("tensor") % 2
    owners = ring.owners()

    def arrange(array):
        array = jnp.where(core == 0, array, array[::-1])
        return jnp.concatenate(
            [lax.dynamic_slice_in_dim(array, owners[j] * block, block, axis=2) for j in range(n)], axis=2
        )

    def restore(own, other):
        array = jnp.stack([jnp.where(core == 0, own, other), jnp.where(core == 0, other, own)])
        places = jnp.asarray(np.argsort(np.array(ring.order)).astype(np.int32))
        where = (places - ring.place()) % n
        return jnp.concatenate(
            [lax.dynamic_slice_in_dim(array, where[j] * block, block, axis=2) for j in range(n)], axis=2
        )

    gains = jnp.concatenate([attention_gain, feedforward_gain])
    fill = jnp.zeros((8, q_cols + 2 * kv_cols), BF16)
    fill = lax.dynamic_update_slice(fill, gains[None, :], (0, 0))
    first = jnp.concatenate(
        [jnp.concatenate([query_weight, key_matrix, value_matrix], axis=1), fill], axis=0
    )
    first_pieces = ring.gather(first)
    qkv_w = jnp.concatenate([p[:block] for p in first_pieces], axis=0)
    gain_a = jnp.concatenate([p[block, :block] for p in first_pieces]).astype(F32)
    gain_f = jnp.concatenate([p[block, block : 2 * block] for p in first_pieces]).astype(F32)
    out_w = jnp.concatenate(ring.gather(out_weight), axis=1)
    gate_w = jnp.concatenate(ring.gather(gate_weight), axis=0)
    up_w = jnp.concatenate(ring.gather(up_weight), axis=0)
    down_w = jnp.concatenate(ring.gather(down_weight), axis=1)

    keep = layer_keep.astype(F32)
    keep = jnp.where(core == 0, keep, keep[::-1])
    prefix = jnp.where(core == 0, prefix_length, prefix_length[::-1])
    x = arrange(inputs)
    dy = arrange(cotangent)

    cos_part, sin_part = rotary_tables(length)
    cos_part, sin_part = cos_part[None, :, None, :], sin_part[None, :, None, :]
    position = jnp.arange(length, dtype=jnp.int32)

    rows = x.reshape(seqs * length, width).astype(F32)
    r1 = lax.rsqrt(jnp.mean(rows * rows, axis=-1, keepdims=True) + EPSILON)
    n1 = (rows * r1 * gain_a).astype(BF16)
    qkv = dot(n1, qkv_w)
    q = rotate(qkv[:, :q_cols].reshape(seqs, length, heads, HEAD_SIZE), cos_part, sin_part).astype(BF16)
    k = rotate(qkv[:, q_cols : q_cols + kv_cols].reshape(seqs, length, kv_heads, HEAD_SIZE), cos_part, sin_part).astype(BF16)
    v = qkv[:, q_cols + kv_cols :].astype(BF16).reshape(seqs, length, kv_heads, HEAD_SIZE)
    q = q.reshape(seqs, length, kv_heads, repeat, HEAD_SIZE)
    scores = jnp.einsum("bqgrd,bkgd->bgrqk", q, k, preferred_element_type=F32) * scale
    allowed = (position[None, None, :] <= position[None, :, None]) | (position[None, None, :] < prefix[:, None, None])
    scores = jnp.where(allowed[:, None, None], scores, NEGATIVE)
    exps = jnp.exp(scores - jnp.max(scores, axis=-1, keepdims=True))
    probs = exps / jnp.sum(exps, axis=-1, keepdims=True)
    probs_low = probs.astype(BF16)
    mixed = jnp.einsum("bgrqk,bkgd->bqgrd", probs_low, v, preferred_element_type=F32)
    mixed = mixed.reshape(seqs * length, q_cols).astype(BF16)
    a_own = tensor_sum(dot(mixed, out_w).reshape(seqs, length, width))
    x_own = x[0].astype(F32)
    hid = x_own + keep[0] * a_own
    r2 = lax.rsqrt(jnp.mean(hid * hid, axis=-1, keepdims=True) + EPSILON)
    n2_own = (hid * r2 * gain_f).astype(BF16)
    n2 = jnp.concatenate([n2_own, swap_core(n2_own)], axis=0)

    g = dot(n2, gate_w)
    u = dot(n2, up_w)
    sig = jax.nn.sigmoid(g)
    swish = g * sig
    m = (swish * u).astype(BF16)
    f_own = tensor_sum(dot(m, down_w).reshape(seqs, length, width))
    out_own = (hid + keep[0] * f_own).astype(BF16)
    output = restore(out_own, swap_core(out_own))

    df = (keep[:, None, None] * dy.astype(F32)).astype(BF16).reshape(seqs * length, width)
    grad_down = dot_ta(m, df)
    dm = dot_tb(df, down_w)
    dg = (dm * u * sig * (1.0 + g * (1.0 - sig))).astype(BF16)
    du = (dm * swish).astype(BF16)
    grad_down = ring.scatter([grad_down[:, j * block : (j + 1) * block] for j in range(n)])
    grad_gate = dot_ta(n2, dg)
    grad_gate = ring.scatter([grad_gate[j * block : (j + 1) * block] for j in range(n)])
    grad_up = dot_ta(n2, du)
    grad_up = ring.scatter([grad_up[j * block : (j + 1) * block] for j in range(n)])
    dn2 = tensor_sum((dot_tb(dg, gate_w) + dot_tb(du, up_w)).reshape(seqs, length, width))
    gain_f_sum = jnp.sum(dn2 * hid * r2, axis=0)
    scaled = dn2 * gain_f
    dh = dy[0].astype(F32) + r2 * scaled - hid * (r2 * r2 * r2) * jnp.mean(scaled * hid, axis=-1, keepdims=True)
    da_own = (keep[0] * dh).astype(BF16)
    da = jnp.concatenate([da_own, swap_core(da_own)], axis=0)

    grad_out = dot_ta(mixed, da)
    grad_out = ring.scatter([grad_out[:, j * block : (j + 1) * block] for j in range(n)])
    dmixed = dot_tb(da, out_w).astype(BF16).reshape(seqs, length, kv_heads, repeat, HEAD_SIZE)
    dprobs = jnp.einsum("bqgrd,bkgd->bgrqk", dmixed, v, preferred_element_type=F32)
    dv = jnp.einsum("bgrqk,bqgrd->bkgd", probs_low, dmixed, preferred_element_type=F32).astype(BF16)
    inner = jnp.sum(probs * dprobs, axis=-1, keepdims=True)
    dscores = (probs * (dprobs - inner)).astype(BF16)
    dq = jnp.einsum("bgrqk,bkgd->bqgrd", dscores, k, preferred_element_type=F32) * scale
    dk = jnp.einsum("bgrqk,bqgrd->bkgd", dscores, q, preferred_element_type=F32) * scale
    dq = rotate(dq.reshape(seqs, length, heads, HEAD_SIZE), cos_part, -sin_part).astype(BF16)
    dk = rotate(dk, cos_part, -sin_part).astype(BF16)
    dqkv = jnp.concatenate(
        [d.reshape(seqs * length, -1) for d in (dq, dk, dv)], axis=1
    )
    grad_qkv = dot_ta(n1, dqkv)
    grad_qkv = ring.scatter([grad_qkv[j * block : (j + 1) * block] for j in range(n)])
    dn1 = tensor_sum(dot_tb(dqkv, qkv_w).reshape(seqs, length, width))
    r1_own = r1[:length]
    gain_a_sum = jnp.sum(dn1 * x_own * r1_own, axis=0)
    scaled = dn1 * gain_a
    dx = dh + r1_own * scaled - x_own * (r1_own * r1_own * r1_own) * jnp.mean(scaled * x_own, axis=-1, keepdims=True)
    dx = dx.astype(BF16)
    input_grad = restore(dx, swap_core(dx))

    sums = jnp.stack([gain_a_sum, gain_f_sum]).reshape(2, n, block)
    sums = sums + swap_core(sums)
    gain_grads = ring.small_scatter(sums)
    return (
        output,
        input_grad,
        gain_grads[0],
        grad_qkv[:, :q_cols],
        grad_qkv[:, q_cols : q_cols + kv_cols],
        grad_qkv[:, q_cols + kv_cols :],
        grad_out,
        gain_grads[1],
        grad_gate,
        grad_up,
        grad_down,
    )


def local(ring, inputs, attention_gain, query_weight, key_matrix, value_matrix, out_weight, feedforward_gain,
          gate_weight, up_weight, down_weight, cotangent, layer_keep, prefix_length):
    n = ring.size
    seqs, length, width = inputs.shape
    tokens = seqs * length
    block = width // n
    q_cols, kv_cols = query_weight.shape[1], key_matrix.shape[1]
    cos_part, sin_part = rotary_tables(length)
    cos = jnp.concatenate([cos_part, cos_part], axis=1)
    sin = jnp.concatenate([-sin_part, sin_part], axis=1)
    keep = layer_keep.astype(F32)
    gains = jnp.concatenate([attention_gain[None], feedforward_gain[None], jnp.zeros((14, block), BF16)], axis=0)
    x = inputs.reshape(tokens, width)
    dy = cotangent.reshape(tokens, width)
    names = ("gains", "wq", "wk", "wv", "wo", "wg", "wu", "wd", "n1", "q", "k", "v", "ob", "hid", "n2", "m", "fa", "fb", "g_down")
    values = dict(
        zip(
            names,
            forward(
                n, x, dy, gains, query_weight, key_matrix, value_matrix, out_weight, gate_weight, up_weight, down_weight,
                cos, sin, keep, prefix_length, length,
            ),
        )
    )
    values |= {"x": x, "dy": dy, "cos": cos, "sin": sin, "keep": keep, "prefix": prefix_length}
    outs = backward(n, length, values)
    me = lax.axis_index("dp")

    def total(name, axis):
        own = lax.dynamic_slice_in_dim(outs["g_" + name], me * block, block, axis=axis)
        return own.astype(F32) + outs[f"r_{name}_0"][-1].astype(F32) + outs[f"r_{name}_1"][-1].astype(F32)

    qkv = total("qkv", 0)
    gain_sums = jnp.sum(outs["gain_slots"], axis=0)[:2]
    gain_sums = gain_sums + swap_core(gain_sums)
    return (
        outs["output"].reshape(inputs.shape),
        outs["dx"].reshape(inputs.shape),
        gain_sums[0],
        qkv[:, :q_cols],
        qkv[:, q_cols : q_cols + kv_cols],
        qkv[:, q_cols + kv_cols :],
        total("out", 1),
        gain_sums[1],
        total("gate", 0),
        total("up", 0),
        total("down", 1),
    )


def solution(mesh):
    ring = Ring(mesh.shape["dp"])
    if mesh.shape["tensor"] != 4:
        raise ValueError("tensor axis")
    row, col = P("dp", "tensor"), P("tensor", "dp")
    data = P("dp", None, None)

    def layer(*args):
        block = args[0].shape[2] // ring.size
        return (local if block % 256 == 0 else ring_local)(ring, *args)

    return jax.shard_map(
        layer,
        mesh=mesh,
        in_specs=(data, P("dp"), row, row, row, col, P("dp"), row, row, col, data, P("dp"), P("dp")),
        out_specs=(data, data, P("dp"), row, row, row, col, P("dp"), row, row, col),
        check_vma=False,
    )
```

```python
import functools
import math

import jax
import jax.numpy as jnp
import numpy as np
from jax import lax
from jax.experimental import pallas as pl
from jax.experimental.pallas import tpu as pltpu
from jax.sharding import PartitionSpec as P

HEAD_SIZE = 128
EPSILON = 1e-05
NEGATIVE = -1e30
BF16 = jnp.bfloat16
F32 = jnp.float32
MESH = pl.DeviceIdType.MESH
HBM = pl.BlockSpec(memory_space=pltpu.HBM)
SMEM = pl.BlockSpec(memory_space=pltpu.SMEM)
ROWS = 256


def dot(a, b):
    return jnp.dot(a, b, preferred_element_type=F32)


def dot_ta(a, b):
    return lax.dot_general(a, b, (((0,), (0,)), ((), ())), preferred_element_type=F32)


def dot_tb(a, b):
    return lax.dot_general(a, b, (((1,), (1,)), ((), ())), preferred_element_type=F32)


def spec(rows, cols):
    return pl.BlockSpec((rows, cols), lambda i: (i, 0))


def fixed(*shape):
    return pl.BlockSpec(shape, lambda i: (0,) * len(shape), pipeline_mode=pl.Buffered(1))


def tiles(total, step=256):
    return [(at, min(step, total - at)) for at in range(0, total, step)]


def gain_row(gains_ref, which):
    n = gains_ref.shape[0]
    return jnp.concatenate([gains_ref[j, which : which + 1, :] for j in range(n)], axis=1).astype(F32)


def turn(values, cos, sin):
    return values * cos + pltpu.roll(values, HEAD_SIZE // 2, axis=1) * sin


class Place:
    def __init__(self, n):
        self.n = n
        self.me = lax.axis_index("dp")
        odd = self.me % 2
        self.p = (1 - odd) * (self.me // 2) + odd * (n - 1 - self.me // 2)
        tensor = lax.axis_index("tensor")
        self.core = tensor % 2
        self.core_peer = tensor + 1 - 2 * self.core
        self.chip_peer = (tensor + 2) % 4
        self.right = self.at(1)
        self.left = self.at(-1)

    def at(self, j):
        p = (self.p + j + 2 * self.n) % self.n
        low = p // (self.n // 2)
        return (1 - low) * 2 * p + low * (2 * (self.n - 1 - p) + 1)

    def greet(self):
        barrier = pltpu.get_barrier_semaphore()
        for peer in (self.left, self.right):
            pl.semaphore_signal(barrier, inc=1, device_id={"dp": peer}, device_id_type=MESH)
        for peer in (self.core_peer, self.chip_peer):
            pl.semaphore_signal(barrier, inc=1, device_id={"tensor": peer}, device_id_type=MESH)
        pl.semaphore_wait(barrier, 4)


class Gather:
    def __init__(self, place, shard, whole, where, local_sem, send_sems, recv_sems):
        self.place, self.shard, self.whole, self.where = place, shard, whole, where
        self.send_sems, self.recv_sems = send_sems, recv_sems
        self.hops = place.n // 2
        self.local = pltpu.make_async_copy(shard, where(whole, place.me, None), local_sem)

    def copy(self, way, hop):
        place = self.place
        sign = 1 - 2 * way
        owner = place.at(-sign * (hop - 1))
        half = way if hop == self.hops else None
        target = self.where(self.whole, owner, half)
        if hop > 1:
            source = target
        elif half is None:
            source = self.shard
        else:
            rows = self.shard.shape[0] // 2
            source = self.shard.at[pl.ds(half * rows, rows)]
        return pltpu.make_async_remote_copy(
            src_ref=source,
            dst_ref=target,
            send_sem=self.send_sems.at[way, hop - 1],
            recv_sem=self.recv_sems.at[way, hop - 1],
            device_id={"dp": place.right if way == 0 else place.left},
            device_id_type=MESH,
        )

    def step(self, hop):
        for way in range(2):
            if hop > 1:
                self.copy(way, hop - 1).wait_recv()
            self.copy(way, hop).start()

    def arrived(self):
        self.local.wait()
        for way in range(2):
            self.copy(way, self.hops).wait_recv()

    def drain(self):
        for way in range(2):
            for hop in range(1, self.hops + 1):
                self.copy(way, hop).wait_send()


def by_rows(rows):
    def where(whole, owner, half):
        if half is None:
            return whole.at[pl.ds(pl.multiple_of(owner * rows, rows), rows)]
        return whole.at[pl.ds(pl.multiple_of(owner * rows + half * (rows // 2), rows // 2), rows // 2)]

    return where


def by_cols(rows, cols):
    def where(whole, owner, half):
        at = pl.ds(pl.multiple_of(owner * cols, cols), cols)
        if half is None:
            return whole.at[:, at]
        return whole.at[pl.ds(half * (rows // 2), rows // 2), at]

    return where


def by_slot(whole, owner, half):
    if half is None:
        return whole.at[owner]
    rows = whole.shape[1] // 2
    return whole.at[owner, pl.ds(half * rows, rows)]


class Swap:
    def __init__(self, source, target, peer, send_sem, recv_sem):
        self.copy = pltpu.make_async_remote_copy(
            src_ref=source, dst_ref=target, send_sem=send_sem, recv_sem=recv_sem,
            device_id={"tensor": peer}, device_id_type=MESH,
        )
        self.copy.start()


def with_jobs(jobs, body):
    def both(*refs):
        for step, job in jobs:
            pl.when(pl.program_id(0) == step)(job)
        body(*refs)

    return both


class Exchange:
    def __init__(self, place, other, peer, near, far, sems):
        self.place, self.other, self.peer, self.near, self.far, self.sems = place, other, peer, near, far, sems
        self.per, self.rows = other.shape[0], other.shape[1]

    def core(self, i):
        return pltpu.make_async_remote_copy(
            src_ref=self.other.at[i], dst_ref=self.peer.at[i], send_sem=self.sems.at[0, i], recv_sem=self.sems.at[1, i],
            device_id={"tensor": self.place.core_peer}, device_id_type=MESH,
        )

    def chip(self, i):
        return pltpu.make_async_remote_copy(
            src_ref=self.near.at[i], dst_ref=self.far.at[i], send_sem=self.sems.at[2, i], recv_sem=self.sems.at[3, i],
            device_id={"tensor": self.place.chip_peer}, device_id_type=MESH,
        )

    def run(self, term, width, step, row_cols, row_args, fixed_args, jobs=()):
        per, core = self.per, self.place.core

        def body(*refs):
            s = pl.program_id(0)
            for i in range(per):
                if i:
                    @pl.when(s == i)
                    def _():
                        self.core(i - 1).start()

                @pl.when(s == per + i)
                def _():
                    if i == 0:
                        self.core(per - 1).start()
                    else:
                        self.chip(i - 1).start()
                    self.core(i).wait_recv()

            @pl.when(s < per)
            def _():
                for at, size in tiles(width, step):
                    cols = slice(at, at + size)
                    self.other[s, :, cols] = term(refs, cols).astype(BF16)

            @pl.when(s >= per)
            def _():
                for at, size in tiles(width, step):
                    cols = slice(at, at + size)
                    self.near[s - per, :, cols] = (term(refs, cols) + self.peer[s - per, :, cols].astype(F32)).astype(BF16)

        def block(s):
            return ((1 - core) + (s // per) * (2 * core - 1)) * per + s % per

        pltpu.emit_pipeline(
            with_jobs(jobs, body),
            grid=(2 * per,),
            in_specs=[pl.BlockSpec((self.rows, cols), lambda s: (block(s), 0)) for cols in row_cols]
            + [fixed(*w.shape) for w in fixed_args],
        )(*row_args, *fixed_args)
        self.chip(per - 1).start()
        for i in range(per):
            self.core(i).wait_send()

    def arrivals(self):
        return [(i * (self.rows // BLOCK), self.chip(i).wait_recv) for i in range(self.per)]

    def drain(self):
        for i in range(self.per):
            self.chip(i).wait_send()

    def total(self, at, rows):
        i, part = at // self.rows, pl.ds(pl.multiple_of(at % self.rows, rows), rows)
        return self.near[i, part, :].astype(F32) + self.far[i, part, :].astype(F32)


CHUNK = 16
BLOCK = 128


def by_chunks(step, body):
    @pl.loop(0, BLOCK, step=CHUNK)
    def _(at):
        at = pl.multiple_of(at, CHUNK)
        body(pl.ds(at, CHUNK), step * BLOCK + at)


def forward_kernel(
    n, length, x_hbm, dy_hbm, gains_in, wq_in, wk_in, wv_in, wo_in, wg_in, wu_in, wd_in, cos_hbm, sin_hbm, keep_ref, prefix_ref,
    gains_w, wq, wk, wv, wo, wg, wu, wd, n1_hbm, q_hbm, k_hbm, v_hbm, ob_hbm, hid_hbm, n2_hbm, m_hbm, fa_hbm, fb_hbm, gd_hbm,
    other, peer, near, far, local_sems, send_sems, recv_sems, swap_sems, share_sems,
):
    place = Place(n)
    core = place.core
    place.greet()
    tokens, width = x_hbm.shape
    scale = 1.0 / math.sqrt(HEAD_SIZE)
    half = wd_in.shape[0] // 2
    upper, lower = pl.ds(0, half), pl.ds(half, half)
    arrays = {
        "n": (gains_in, gains_w, by_slot),
        "q": (wq_in, wq, by_rows(wq_in.shape[0])),
        "k": (wk_in, wk, by_rows(wk_in.shape[0])),
        "v": (wv_in, wv, by_rows(wv_in.shape[0])),
        "o": (wo_in, wo, by_cols(*wo_in.shape)),
        "g": (wg_in, wg, by_rows(wg_in.shape[0])),
        "u": (wu_in, wu, by_rows(wu_in.shape[0])),
        "a": (wd_in.at[upper], wd.at[upper], by_cols(half, wd_in.shape[1])),
        "b": (wd_in.at[lower], wd.at[lower], by_cols(half, wd_in.shape[1])),
    }
    rings = {
        name: Gather(place, shard, whole, where, local_sems.at[i], send_sems.at[i], recv_sems.at[i])
        for i, (name, (shard, whole, where)) in enumerate(arrays.items())
    }
    hops = n // 2
    done = {name: 0 for name in rings}

    def go(names):
        for name in names:
            if done[name] < hops:
                done[name] += 1
                rings[name].step(done[name])

    own_rows = pl.ds(pl.multiple_of(core * length, length), length)
    other_rows = pl.ds(pl.multiple_of((1 - core) * length, length), length)

    go("nqkv")
    for name in "nqkvogu":
        rings[name].local.start()
    go("nqkvo")
    go("nqkvo")
    go("nqkvog")
    for name in "nqkv":
        go(name * hops)
        rings[name].arrived()

    def project(x_ref, gains_ref, wq_ref, wk_ref, wv_ref, cos_ref, sin_ref, n1_ref, q_ref, k_ref, v_ref):
        gain = gain_row(gains_ref, 0)

        @pl.loop(0, ROWS, step=32)
        def _(at):
            part = pl.ds(pl.multiple_of(at, 32), 32)
            xf = x_ref[part, :].astype(F32)
            r1 = lax.rsqrt(jnp.mean(xf * xf, axis=-1, keepdims=True) + EPSILON)
            n1_ref[part, :] = (xf * r1 * gain).astype(BF16)

        rows = n1_ref[...]
        cos, sin = cos_ref[...], sin_ref[...]
        for w_ref, o_ref in ((wq_ref, q_ref), (wk_ref, k_ref)):
            for at in range(0, w_ref.shape[1], HEAD_SIZE):
                head = slice(at, at + HEAD_SIZE)
                o_ref[:, head] = turn(dot(rows, w_ref[:, head]), cos, sin).astype(BF16)
        v_ref[...] = dot(rows, wv_ref[...]).astype(BF16)

    q_cols, kv_cols = wq.shape[1], wk.shape[1]
    per = length // ROWS
    turns = pl.BlockSpec((ROWS, HEAD_SIZE), lambda i: (i % per, 0))
    pltpu.emit_pipeline(
        project,
        grid=(tokens // ROWS,),
        in_specs=[spec(ROWS, width), fixed(*gains_w.shape), fixed(*wq.shape), fixed(*wk.shape), fixed(*wv.shape), turns, turns],
        out_specs=[spec(ROWS, width), spec(ROWS, q_cols), spec(ROWS, kv_cols), spec(ROWS, kv_cols)],
    )(x_hbm, gains_w, wq, wk, wv, cos_hbm, sin_hbm, n1_hbm, q_hbm, k_hbm, v_hbm)
    go("ogu")

    repeat = q_cols // kv_cols

    def attend(which, q_ref, k_ref, v_ref, o_ref):
        prefix = prefix_ref[which]
        keys, values = k_ref[...], v_ref[...]

        @pl.loop(0, length, step=128)
        def _(at):
            part = pl.ds(pl.multiple_of(at, 128), 128)
            s = dot_tb(q_ref[part, :], keys) * scale
            row = lax.broadcasted_iota(jnp.int32, s.shape, 0) + at
            col = lax.broadcasted_iota(jnp.int32, s.shape, 1)
            s = jnp.where((col <= row) | (col < prefix), s, NEGATIVE)
            e = jnp.exp(s - jnp.max(s, axis=-1, keepdims=True))
            p = e / jnp.sum(e, axis=-1, keepdims=True)
            o_ref[part, :] = dot(p.astype(BF16), values).astype(BF16)

    for which in range(2):
        seq = pl.ds(which * length, length)
        pltpu.emit_pipeline(
            functools.partial(attend, which),
            grid=(q_cols // HEAD_SIZE,),
            in_specs=[
                pl.BlockSpec((length, HEAD_SIZE), lambda h: (0, h)),
                pl.BlockSpec((length, HEAD_SIZE), lambda h: (0, h // repeat)),
                pl.BlockSpec((length, HEAD_SIZE), lambda h: (0, h // repeat)),
            ],
            out_specs=[pl.BlockSpec((length, HEAD_SIZE), lambda h: (0, h))],
        )(q_hbm.at[seq], k_hbm.at[seq], v_hbm.at[seq], ob_hbm.at[seq])

    go("o" * hops)
    rings["o"].arrived()
    go("g")
    mixed = Exchange(place, other, peer, near, far, swap_sems)
    mixed.run(lambda refs, cols: dot(refs[0][...], refs[1][:, cols]), width, 512, [q_cols], [ob_hbm], [wo])
    for name in "ab":
        rings[name].local.start()
    go("u")
    go("g")
    go("u")

    def residual(x_ref, gains_ref, hid_ref, n2_ref):
        gain = gain_row(gains_ref, 1)
        keep = keep_ref[core]

        def chunk(part, row):
            h = x_ref[part, :].astype(F32) + keep * mixed.total(row, CHUNK)
            hid_ref[part, :] = h
            r2 = lax.rsqrt(jnp.mean(h * h, axis=-1, keepdims=True) + EPSILON)
            n2_ref[part, :] = (h * r2 * gain).astype(BF16)

        by_chunks(pl.program_id(0), chunk)

    pltpu.emit_pipeline(
        with_jobs(mixed.arrivals(), residual),
        grid=(length // BLOCK,),
        in_specs=[spec(BLOCK, width), fixed(*gains_w.shape)],
        out_specs=[spec(BLOCK, width)] * 2,
    )(x_hbm.at[own_rows], gains_w, hid_hbm, n2_hbm.at[own_rows])
    share = Swap(n2_hbm.at[own_rows], n2_hbm.at[own_rows], place.core_peer, share_sems.at[0], share_sems.at[1])
    share.copy.wait_recv()
    go("g" * hops + "u" * hops + "ab")
    rings["g"].arrived()
    rings["u"].arrived()

    hidden = wg.shape[1]

    def during(at, name, hop):
        pl.when(pl.program_id(0) == at)(lambda: rings[name].step(hop))
        done[name] = hop

    def feed(n2_ref, wg_ref, wu_ref, m_ref, fa_ref, fb_ref):
        during(tokens // ROWS - 2, "a", 2)
        during(tokens // ROWS - 1, "b", 2)
        rows = n2_ref[...]
        for at, size in tiles(hidden):
            cols = slice(at, at + size)
            g = dot(rows, wg_ref[:, cols])
            u = dot(rows, wu_ref[:, cols])
            sig = 1.0 / (1.0 + jnp.exp(-g))
            swish = g * sig
            m_ref[:, cols] = (swish * u).astype(BF16)
            fa_ref[:, cols] = u * sig * (1.0 + g * (1.0 - sig))
            fb_ref[:, cols] = swish

    pltpu.emit_pipeline(
        feed,
        grid=(tokens // ROWS,),
        in_specs=[spec(ROWS, width), fixed(*wg.shape), fixed(*wu.shape)],
        out_specs=[spec(ROWS, hidden)] * 3,
    )(n2_hbm, wg, wu, m_hbm, fa_hbm, fb_hbm)

    def down_grad(m_ref, dy_ref, o_ref):
        during(1, "a", 3)
        during(5, "b", 3)
        total = None
        for which in range(2):
            seq = slice(which * length, (which + 1) * length)
            df = (dy_ref[seq, :].astype(F32) * keep_ref[which]).astype(BF16)
            term = dot_ta(m_ref[seq, :], df)
            total = term if total is None else total + term
        o_ref[...] = total.astype(BF16)

    cols = pl.BlockSpec((tokens, 256), lambda i: (0, i))
    pltpu.emit_pipeline(
        down_grad,
        grid=(width // 256,),
        in_specs=[fixed(tokens, hidden), cols],
        out_specs=[pl.BlockSpec((hidden, 256), lambda i: (0, i))],
    )(m_hbm, dy_hbm, gd_hbm)
    for _ in range(hops):
        go("ab")
    rings["a"].arrived()
    rings["b"].arrived()
    for ring in rings.values():
        ring.drain()
    mixed.drain()
    share.copy.wait_send()


def forward(n, x, dy, gains, wq, wk, wv, wo, wg, wu, wd, cos, sin, keep, prefix, length):
    tokens, width = x.shape
    shape = jax.ShapeDtypeStruct
    ff = wg.shape[1]
    outs = [
        shape((n,) + gains.shape, BF16),
        shape((width, wq.shape[1]), BF16),
        shape((width, wk.shape[1]), BF16),
        shape((width, wv.shape[1]), BF16),
        shape((wo.shape[0], width), BF16),
        shape((width, ff), BF16),
        shape((width, ff), BF16),
        shape((ff, width), BF16),
        shape((tokens, width), BF16),
        shape((tokens, wq.shape[1]), BF16),
        shape((tokens, wk.shape[1]), BF16),
        shape((tokens, wv.shape[1]), BF16),
        shape((tokens, wq.shape[1]), BF16),
        shape((length, width), F32),
        shape((tokens, width), BF16),
        shape((tokens, ff), BF16),
        shape((tokens, ff), F32),
        shape((tokens, ff), F32),
        shape((ff, width), BF16),
    ]
    blocks = pltpu.VMEM((length // ROWS, ROWS, width), BF16)
    return pl.pallas_call(
        functools.partial(forward_kernel, n, length),
        out_shape=outs,
        in_specs=[HBM] * 12 + [SMEM] * 2,
        out_specs=[HBM] * len(outs),
        scratch_shapes=[
            blocks,
            blocks,
            blocks,
            blocks,
            pltpu.SemaphoreType.DMA((9,)),
            pltpu.SemaphoreType.DMA((9, 2, n // 2)),
            pltpu.SemaphoreType.DMA((9, 2, n // 2)),
            pltpu.SemaphoreType.DMA((4, length // ROWS)),
            pltpu.SemaphoreType.DMA((2,)),
        ],
        compiler_params=pltpu.CompilerParams(collective_id=0, has_side_effects=True, vmem_limit_bytes=60 * 1024 * 1024),
    )(x, dy, gains, wq, wk, wv, wo, wg, wu, wd, cos, sin, keep, prefix)


class Buffers:
    def __init__(self, arrived, sums, sems):
        self.arrived, self.sums, self.sems = arrived, sums, sems
        self.users = []


class Scatter:
    def __init__(self, place, whole, where, piece, slots, buffers, send_sems, recv_sems):
        self.place, self.whole, self.where, self.piece = place, whole, where, piece
        self.slots, self.buffers = slots, buffers
        self.send_sems, self.recv_sems = send_sems, recv_sems
        self.hops = place.n // 2
        self.turns = {}
        self.sent = set()

    def view(self, way, hop):
        sign = 1 - 2 * way
        owner = self.place.at(sign * (self.hops + 1 - hop))
        return self.where(self.whole, owner, way if hop == 1 else None)

    def slot(self, way, hop):
        first, rest = self.slots[way]
        return first if hop == 1 else rest.at[hop - 2]

    def going(self, way, hop):
        rows, cols = self.piece
        buffers = self.buffers
        return buffers.sums.at[self.turns[hop] % buffers.sums.shape[0], way, pl.ds(0, rows), pl.ds(0, cols)]

    def come(self, way, hop):
        rows, cols = self.piece
        buffers = self.buffers
        rows = rows // 2 if hop == 2 else rows
        return buffers.arrived.at[self.turns[hop] % buffers.arrived.shape[0], way, pl.ds(0, rows), pl.ds(0, cols)]

    def remote(self, way, hop):
        return pltpu.make_async_remote_copy(
            src_ref=self.view(way, hop) if hop == 1 else self.going(way, hop),
            dst_ref=self.slot(way, hop),
            send_sem=self.send_sems.at[way, hop - 1],
            recv_sem=self.recv_sems.at[way, hop - 1],
            device_id={"dp": self.place.right if way == 0 else self.place.left},
            device_id_type=MESH,
        )

    def locals(self, hop):
        sems = self.buffers.sems
        turn = self.turns[hop] % sems.shape[0]
        for way in range(2):
            yield pltpu.make_async_copy(self.slot(way, hop - 1), self.come(way, hop), sems.at[turn, way, 0])
            yield pltpu.make_async_copy(self.view(way, hop), self.going(way, hop), sems.at[turn, way, 1])

    def first(self):
        for way in range(2):
            self.remote(way, 1).start()

    def plan(self, hop):
        users = self.buffers.users
        self.turns[hop] = len(users)
        before = users[-self.buffers.sums.shape[0]] if len(users) >= self.buffers.sums.shape[0] else None
        users.append((self, hop))
        if before:
            before[0].sent.add(before[1])

        def fetch():
            for way in range(2):
                self.remote(way, hop - 1).wait_recv()
                if before:
                    before[0].remote(way, before[1]).wait_send()
            for copy in self.locals(hop):
                copy.start()

        def emit():
            for copy in self.locals(hop):
                copy.wait()
            rows = self.piece[0]
            for way in range(2):
                come, going = self.come(way, hop), self.going(way, hop)
                base = way * (rows // 2) if hop == 2 else 0

                @pl.loop(0, rows // 2 if hop == 2 else rows, step=CHUNK)
                def _(at):
                    at = pl.multiple_of(at, CHUNK)
                    part = pl.ds(pl.multiple_of(base + at, CHUNK), CHUNK)
                    going[part, :] = (going[part, :].astype(F32) + come[pl.ds(at, CHUNK), :].astype(F32)).astype(BF16)

                self.remote(way, hop).start()

        return fetch, emit

    def drain(self):
        for way in range(2):
            self.remote(way, self.hops).wait_recv()
            for hop in range(1, self.hops + 1):
                if hop not in self.sent:
                    self.remote(way, hop).wait_send()


def backward_kernel(n, length, names_in, names_out, *refs):
    ins = dict(zip(names_in, refs))
    outs = dict(zip(names_out, refs[len(names_in) :]))
    (gsum, gpieces, dh, other, peers, nears, fars, come_rows, sums_rows, come_cols, sums_cols, add_sems, local_sems, send_sems, recv_sems, swap_sems, swap_send, swap_recv, gain_send, gain_recv) = refs[
        len(names_in) + len(names_out) :
    ]
    keep_ref, prefix_ref = ins["keep"], ins["prefix"]
    dy, x, gains_w = ins["dy"], ins["x"], ins["gains"]
    wq, wk, wv, wo, wg, wu, wd = (ins[name] for name in ("wq", "wk", "wv", "wo", "wg", "wu", "wd"))
    tokens, width = x.shape
    q_cols, kv_cols, hidden = wq.shape[1], wk.shape[1], wg.shape[1]
    block = width // n
    per = length // ROWS
    repeat = q_cols // kv_cols
    scale = 1.0 / math.sqrt(HEAD_SIZE)
    place = Place(n)
    core = place.core
    barrier = pltpu.get_barrier_semaphore()
    for j in range(1, n):
        pl.semaphore_signal(barrier, inc=1, device_id={"dp": place.at(j)}, device_id_type=MESH)
    for peer in (place.core_peer, place.chip_peer):
        pl.semaphore_signal(barrier, inc=1, device_id={"tensor": peer}, device_id_type=MESH)
    pl.semaphore_wait(barrier, n + 1)

    own_rows = pl.ds(pl.multiple_of(core * length, length), length)
    by_row = Buffers(come_rows, sums_rows, add_sems.at[0])
    by_col = Buffers(come_cols, sums_cols, add_sems.at[1])
    grads = {
        "down": (by_cols(hidden, block), (hidden, block), by_col),
        "gate": (by_rows(block), (block, hidden), by_row),
        "up": (by_rows(block), (block, hidden), by_row),
        "out": (by_cols(q_cols, block), (q_cols, block), by_col),
        "qkv": (by_rows(block), (block, q_cols + 2 * kv_cols), by_row),
    }
    rings = {
        name: Scatter(
            place,
            outs["g_" + name],
            where,
            piece,
            [(outs[f"r_{name}_{way}_first"], outs[f"r_{name}_{way}"]) for way in range(2)],
            buffers,
            send_sems.at[i],
            recv_sems.at[i],
        )
        for i, (name, (where, piece, buffers)) in enumerate(grads.items())
    }
    swaps = []

    def swap(source, target, peer):
        i = len(swaps)
        swaps.append(Swap(source, target, peer, swap_send.at[i], swap_recv.at[i]))
        return swaps[-1].copy

    def act_grads(jobs):
        def body(dy_ref, wd_ref, fa_ref, fb_ref, dg_ref, du_ref):
            which = pl.program_id(0) // per
            df = (dy_ref[...].astype(F32) * keep_ref[which]).astype(BF16)
            for at, size in tiles(hidden):
                cols = slice(at, at + size)
                dm = dot_tb(df, wd_ref[cols, :])
                dg_ref[:, cols] = (dm * fa_ref[:, cols]).astype(BF16)
                du_ref[:, cols] = (dm * fb_ref[:, cols]).astype(BF16)

        pltpu.emit_pipeline(
            with_jobs(jobs, body),
            grid=(tokens // ROWS,),
            in_specs=[spec(ROWS, width), fixed(hidden, width), spec(ROWS, hidden), spec(ROWS, hidden)],
            out_specs=[spec(ROWS, hidden)] * 2,
        )(dy, wd, ins["fa"], ins["fb"], outs["dg"], outs["du"])

    def outer(left, right, target, jobs):
        def body(l_ref, r_ref, o_ref):
            o_ref[...] = dot_ta(l_ref[...], r_ref[...]).astype(BF16)

        cols = right.shape[1]
        pltpu.emit_pipeline(
            with_jobs(jobs, body),
            grid=(width // 256,),
            in_specs=[pl.BlockSpec((tokens, 256), lambda i: (0, i)), fixed(tokens, cols)],
            out_specs=[spec(256, cols)],
        )(left, right, target)

    def exchange(i):
        return Exchange(place, other, peers.at[i], nears.at[i], fars.at[i], swap_sems.at[i])

    in_n2, in_f, in_n1 = exchange(0), exchange(1), exchange(2)

    def back(jobs):
        in_n2.run(
            lambda refs, cols: dot_tb(refs[0][...], refs[2][cols, :]) + dot_tb(refs[1][...], refs[3][cols, :]),
            width, 256, [hidden, hidden], [outs["dg"], outs["du"]], [wg, wu], jobs,
        )

    def add_gain(which, terms):
        gsum[which] += sum(terms[i * 8 : (i + 1) * 8] for i in range(terms.shape[0] // 8))

    def norm_back(d, h, gain, which):
        r = lax.rsqrt(jnp.mean(h * h, axis=-1, keepdims=True) + EPSILON)
        add_gain(which, d * h * r)
        scaled = d * gain
        return r * scaled - h * (r * r * r) * jnp.mean(scaled * h, axis=-1, keepdims=True)

    def hid_grads():
        def body(hid_ref, dy_ref, gains_ref, da_ref):
            gain = gain_row(gains_ref, 1)
            keep = keep_ref[core]

            def chunk(part, row):
                d = in_n2.total(row, CHUNK)
                value = dy_ref[part, :].astype(F32) + norm_back(d, hid_ref[part, :], gain, 1)
                dh[pl.ds(pl.multiple_of(row, CHUNK), CHUNK), :] = value
                da_ref[part, :] = (keep * value).astype(BF16)

            by_chunks(pl.program_id(0), chunk)

        pltpu.emit_pipeline(
            with_jobs(in_n2.arrivals(), body),
            grid=(length // BLOCK,),
            in_specs=[spec(BLOCK, width)] * 2 + [fixed(*gains_w.shape)],
            out_specs=[spec(BLOCK, width)],
        )(ins["hid"], dy.at[own_rows], gains_w, outs["da"].at[own_rows])
        return swap(outs["da"].at[own_rows], outs["da"].at[own_rows], place.core_peer)

    def input_grads():
        def body(x_ref, gains_ref, dx_ref):
            gain = gain_row(gains_ref, 0)

            def chunk(part, row):
                d = in_n1.total(row, CHUNK)
                value = norm_back(d, x_ref[part, :].astype(F32), gain, 0)
                dx_ref[part, :] = (dh[pl.ds(pl.multiple_of(row, CHUNK), CHUNK), :] + value).astype(BF16)

            by_chunks(pl.program_id(0), chunk)

        pltpu.emit_pipeline(
            with_jobs(in_n1.arrivals(), body),
            grid=(length // BLOCK,),
            in_specs=[spec(BLOCK, width), fixed(*gains_w.shape)],
            out_specs=[spec(BLOCK, width)],
        )(x.at[own_rows], gains_w, outs["dx"].at[own_rows])
        return swap(outs["dx"].at[own_rows], outs["dx"].at[own_rows], place.core_peer)

    def results():
        def body(hid_ref, o_ref):
            keep = keep_ref[core]

            def chunk(part, row):
                o_ref[part, :] = (hid_ref[part, :] + keep * in_f.total(row, CHUNK)).astype(BF16)

            by_chunks(pl.program_id(0), chunk)

        pltpu.emit_pipeline(
            with_jobs(in_f.arrivals(), body),
            grid=(length // BLOCK,),
            in_specs=[spec(BLOCK, width)],
            out_specs=[spec(BLOCK, width)],
        )(ins["hid"], outs["output"].at[own_rows])
        return swap(outs["output"].at[own_rows], outs["output"].at[own_rows], place.core_peer)

    def forth(jobs):
        in_f.run(lambda refs, cols: dot(refs[0][...], refs[1][:, cols]), width, 512, [hidden], [ins["m"]], [wd], jobs)

    def out_grad(jobs):
        def body(ob_ref, da_ref, o_ref):
            o_ref[...] = dot_ta(ob_ref[...], da_ref[...]).astype(BF16)

        pltpu.emit_pipeline(
            with_jobs(jobs, body),
            grid=(width // 256,),
            in_specs=[fixed(tokens, q_cols), pl.BlockSpec((tokens, 256), lambda i: (0, i))],
            out_specs=[pl.BlockSpec((q_cols, 256), lambda i: (0, i))],
        )(ins["ob"], outs["da"], outs["g_out"])

    def mixed_grad():
        def body(da_ref, wo_ref, o_ref):
            o_ref[...] = dot_tb(da_ref[...], wo_ref[...]).astype(BF16)

        pltpu.emit_pipeline(
            body, grid=(tokens // ROWS,), in_specs=[spec(ROWS, width), fixed(q_cols, width)], out_specs=[spec(ROWS, q_cols)]
        )(outs["da"], wo, outs["dob"])

    def attend_back(which, jobs):
        seq = pl.ds(which * length, length)

        def heads(dk_sum, dv_sum):
            def body(q_ref, k_ref, v_ref, d_ref, cos_ref, sin_ref, dq_ref, dk_ref, dv_ref):
                head = pl.program_id(0) % repeat
                prefix = prefix_ref[which]
                keys, values = k_ref[...], v_ref[...]

                @pl.when(head == 0)
                def _():
                    dk_sum[...] = jnp.zeros_like(dk_sum)
                    dv_sum[...] = jnp.zeros_like(dv_sum)

                @pl.loop(0, length, step=128)
                def _(at):
                    part = pl.ds(pl.multiple_of(at, 128), 128)
                    queries, grads = q_ref[part, :], d_ref[part, :]
                    s = dot_tb(keys, queries) * scale
                    col = lax.broadcasted_iota(jnp.int32, s.shape, 0)
                    row = lax.broadcasted_iota(jnp.int32, s.shape, 1) + at
                    s = jnp.where((col <= row) | (col < prefix), s, NEGATIVE)
                    e = jnp.exp(s - jnp.max(s, axis=0, keepdims=True))
                    p = e / jnp.sum(e, axis=0, keepdims=True)
                    dp = dot_tb(values, grads)
                    inner = jnp.sum(p * dp, axis=0, keepdims=True)
                    dz = (p * (dp - inner)).astype(BF16)
                    dv_sum[...] += dot(p.astype(BF16), grads)
                    dk_sum[...] += dot(dz, queries)
                    dq = dot_ta(dz, keys) * scale
                    dq_ref[part, :] = turn(dq, cos_ref[part, :], -sin_ref[part, :]).astype(BF16)

                @pl.when(head == repeat - 1)
                def _():
                    dk_ref[...] = turn(dk_sum[...] * scale, cos_ref[...], -sin_ref[...]).astype(BF16)
                    dv_ref[...] = dv_sum[...].astype(BF16)

            one = pl.BlockSpec((length, HEAD_SIZE), lambda h: (0, h))
            shared = pl.BlockSpec((length, HEAD_SIZE), lambda h: (0, h // repeat))
            table = pl.BlockSpec((length, HEAD_SIZE), lambda h: (0, 0))
            dqkv = outs["dqkv"].at[seq]
            pltpu.emit_pipeline(
                with_jobs(jobs, body),
                grid=(q_cols // HEAD_SIZE,),
                in_specs=[one, shared, shared, one, table, table],
                out_specs=[one, shared, shared],
            )(
                ins["q"].at[seq],
                ins["k"].at[seq],
                ins["v"].at[seq],
                outs["dob"].at[seq],
                ins["cos"],
                ins["sin"],
                dqkv.at[:, pl.ds(0, q_cols)],
                dqkv.at[:, pl.ds(q_cols, kv_cols)],
                dqkv.at[:, pl.ds(q_cols + kv_cols, kv_cols)],
            )

        pl.run_scoped(heads, pltpu.VMEM((length, HEAD_SIZE), F32), pltpu.VMEM((length, HEAD_SIZE), F32))

    def back_qkv(jobs):
        def term(refs, cols):
            d_ref, wq_ref, wk_ref, wv_ref = refs
            dq, dk, dv = d_ref[:, :q_cols], d_ref[:, q_cols : q_cols + kv_cols], d_ref[:, q_cols + kv_cols :]
            return dot_tb(dq, wq_ref[cols, :]) + dot_tb(dk, wk_ref[cols, :]) + dot_tb(dv, wv_ref[cols, :])

        in_n1.run(term, width, 256, [q_cols + 2 * kv_cols], [outs["dqkv"]], [wq, wk, wv], jobs)

    def gain_grads():
        for which in range(2):
            row = jnp.sum(gsum[which], axis=0, keepdims=True)
            for j in range(n):
                gpieces[j, which : which + 1, :] = row[:, j * block : (j + 1) * block]
        copy = pltpu.make_async_copy(gpieces, outs["gain_terms"], local_sems.at[0])
        copy.start()
        copy.wait()
        mine = pltpu.make_async_copy(outs["gain_terms"].at[place.me], outs["gain_slots"].at[0], local_sems.at[1])
        mine.start()
        copies = []
        for j in range(1, n):
            copy = pltpu.make_async_remote_copy(
                src_ref=outs["gain_terms"].at[place.at(j)],
                dst_ref=outs["gain_slots"].at[j],
                send_sem=gain_send.at[j],
                recv_sem=gain_recv.at[j],
                device_id={"dp": place.at(j)},
                device_id_type=MESH,
            )
            copy.start()
            copies.append(copy)
        return mine, copies

    plans = {}
    for name, hop in (
        ("down", 2), ("down", 3), ("gate", 2), ("down", 4), ("gate", 3), ("up", 2), ("gate", 4), ("up", 3), ("out", 2),
        ("up", 4), ("qkv", 2), ("out", 3), ("qkv", 3), ("out", 4), ("qkv", 4),
    ):
        plans[name, hop] = rings[name].plan(hop)

    def fetch(name, hop):
        return plans[name, hop][0]

    def emit(name, hop):
        return plans[name, hop][1]

    rings["down"].first()
    gsum[...] = jnp.zeros_like(gsum)
    gpieces[...] = jnp.zeros_like(gpieces)
    act_grads([(3, fetch("down", 2))])
    emit("down", 2)()
    outer(ins["n2"], outs["dg"], outs["g_gate"], [])
    rings["gate"].first()
    back([(1, fetch("down", 3)), (2, emit("down", 3)), (3, fetch("gate", 2))])
    emit("gate", 2)()
    outer(ins["n2"], outs["du"], outs["g_up"], [(5, fetch("down", 4)), (7, emit("down", 4))])
    rings["up"].first()
    forth([])
    fetch("gate", 3)()
    emit("gate", 3)()
    share_da = hid_grads()
    fetch("up", 2)()
    emit("up", 2)()
    share_da.wait_recv()
    mixed_grad()
    out_grad([(4, fetch("gate", 4)), (6, emit("gate", 4))])
    rings["out"].first()
    attend_back(0, [(3, fetch("up", 3))])
    attend_back(1, [(0, emit("up", 3)), (3, fetch("out", 2))])
    emit("out", 2)()
    back_qkv([])
    outer(ins["n1"], outs["dqkv"], outs["g_qkv"], [(3, fetch("up", 4))])
    rings["qkv"].first()
    emit("up", 4)()
    share_out = results()
    fetch("qkv", 2)()
    emit("qkv", 2)()
    fetch("out", 3)()
    emit("out", 3)()
    fetch("qkv", 3)()
    emit("qkv", 3)()
    fetch("out", 4)()
    emit("out", 4)()
    share_dx = input_grads()
    fetch("qkv", 4)()
    emit("qkv", 4)()
    mine, copies = gain_grads()
    share_out.wait_recv()
    share_dx.wait_recv()
    mine.wait()
    for copy in copies:
        copy.wait_recv()
    for ring in rings.values():
        ring.drain()
    for copy in copies:
        copy.wait_send()
    for item in swaps:
        item.copy.wait_send()
    for item in (in_n2, in_f, in_n1):
        item.drain()


def backward(n, length, values):
    shape = jax.ShapeDtypeStruct
    tokens, width = values["x"].shape
    q_cols, kv_cols, hidden = values["wq"].shape[1], values["wk"].shape[1], values["wg"].shape[1]
    block = width // n
    widest = max(hidden, q_cols + 2 * kv_cols)
    outs = {}
    sizes = {
        "down": ((hidden, width), (hidden, block)),
        "gate": ((width, hidden), (block, hidden)),
        "up": ((width, hidden), (block, hidden)),
        "out": ((q_cols, width), (q_cols, block)),
        "qkv": ((width, q_cols + 2 * kv_cols), (block, q_cols + 2 * kv_cols)),
    }
    for name, (whole, piece) in sizes.items():
        outs["g_" + name] = shape(whole, BF16)
        for way in range(2):
            outs[f"r_{name}_{way}_first"] = shape((piece[0] // 2, piece[1]), BF16)
            outs[f"r_{name}_{way}"] = shape((n // 2 - 1,) + piece, BF16)
    outs["dg"] = outs["du"] = shape((tokens, hidden), BF16)
    outs["da"] = outs["dx"] = outs["output"] = shape((tokens, width), BF16)
    outs["dob"] = shape((tokens, q_cols), BF16)
    outs["dqkv"] = shape((tokens, q_cols + 2 * kv_cols), BF16)
    outs["gain_terms"] = outs["gain_slots"] = shape((n, 8, block), F32)
    names_in, names_out = list(values), list(outs)
    results = pl.pallas_call(
        functools.partial(backward_kernel, n, length, names_in, names_out),
        out_shape=list(outs.values()),
        in_specs=[SMEM if name in ("keep", "prefix") else HBM for name in names_in],
        out_specs=[HBM] * len(outs),
        input_output_aliases={names_in.index("g_down"): names_out.index("g_down")},
        scratch_shapes=[
            pltpu.VMEM((2, 8, width), F32),
            pltpu.VMEM((n, 8, block), F32),
            pltpu.VMEM((length, width), F32),
            pltpu.VMEM((length // ROWS, ROWS, width), BF16),
            pltpu.VMEM((3, length // ROWS, ROWS, width), BF16),
            pltpu.VMEM((3, length // ROWS, ROWS, width), BF16),
            pltpu.VMEM((3, length // ROWS, ROWS, width), BF16),
            pltpu.VMEM((2, 2, block, widest), BF16),
            pltpu.VMEM((3, 2, block, widest), BF16),
            pltpu.VMEM((2, 2, widest, block), BF16),
            pltpu.VMEM((3, 2, widest, block), BF16),
            pltpu.SemaphoreType.DMA((2, 3, 2, 2)),
            pltpu.SemaphoreType.DMA((2,)),
            pltpu.SemaphoreType.DMA((5, 2, n // 2)),
            pltpu.SemaphoreType.DMA((5, 2, n // 2)),
            pltpu.SemaphoreType.DMA((3, 4, length // ROWS)),
            pltpu.SemaphoreType.DMA((3,)),
            pltpu.SemaphoreType.DMA((3,)),
            pltpu.SemaphoreType.DMA((n,)),
            pltpu.SemaphoreType.DMA((n,)),
        ],
        compiler_params=pltpu.CompilerParams(collective_id=1, has_side_effects=True, vmem_limit_bytes=60 * 1024 * 1024),
    )(*values.values())
    return dict(zip(names_out, results))


def rotary_tables(length_total):
    half_width = HEAD_SIZE // 2
    frequency = (10000.0 ** (-(np.arange(half_width, dtype=np.float32) * 2.0) / HEAD_SIZE)).astype(np.float32)
    angles = np.arange(length_total, dtype=np.float32)[:, None] * frequency[None, :]
    return (jnp.asarray(np.cos(angles)), jnp.asarray(np.sin(angles)))


def rotate(values, cos_part, sin_part):
    first, second = jnp.split(values, 2, axis=-1)
    return jnp.concatenate(
        [first * cos_part - second * sin_part, first * sin_part + second * cos_part], axis=-1
    )


class Ring:
    def __init__(self, size):
        self.size = size
        self.half = size // 2
        self.order = [2 * p if p < self.half else 2 * (size - 1 - p) + 1 for p in range(size)]
        self.right = [(self.order[p], self.order[(p + 1) % size]) for p in range(size)]
        self.left = [(b, a) for a, b in self.right]

    def place(self):
        me = lax.axis_index("dp")
        odd = me % 2
        return (1 - odd) * (me // 2) + odd * (self.size - 1 - me // 2)

    def owners(self):
        return jnp.asarray(np.array(self.order, np.int32))[(self.place() + np.arange(self.size)) % self.size]

    def gather(self, shard):
        n, m = self.size, self.half
        pieces = [None] * n
        pieces[0] = shard
        from_left, from_right = shard, shard
        for hop in range(1, m):
            from_left = lax.ppermute(from_left, "dp", self.right)
            from_right = lax.ppermute(from_right, "dp", self.left)
            pieces[n - hop] = from_left
            pieces[hop] = from_right
        rows = shard.shape[0] // 2
        top = lax.ppermute(from_left[:rows], "dp", self.right)
        low = lax.ppermute(from_right[rows:], "dp", self.left)
        pieces[m] = jnp.concatenate([top, low], axis=0)
        return pieces

    def scatter(self, parts):
        n, m = self.size, self.half
        rows = parts[0].shape[0] // 2
        kind = BF16
        up = lax.ppermute(parts[m][:rows].astype(kind), "dp", self.right)
        down = lax.ppermute(parts[m][rows:].astype(kind), "dp", self.left)
        for hop in range(m - 1, 0, -1):
            mine_up, mine_down = parts[hop], parts[n - hop]
            if hop == m - 1:
                mine_up = jnp.concatenate([mine_up[:rows] + up.astype(F32), mine_up[rows:]], axis=0)
                mine_down = jnp.concatenate([mine_down[:rows], mine_down[rows:] + down.astype(F32)], axis=0)
            else:
                mine_up = mine_up + up.astype(F32)
                mine_down = mine_down + down.astype(F32)
            up = lax.ppermute(mine_up.astype(kind), "dp", self.right)
            down = lax.ppermute(mine_down.astype(kind), "dp", self.left)
        if m == 1:
            return jnp.concatenate([parts[0][:rows] + up.astype(F32), parts[0][rows:] + down.astype(F32)], axis=0)
        return parts[0] + up.astype(F32) + down.astype(F32)


    def small_scatter(self, sums):
        up = sums[:, self.half]
        for hop in range(self.half - 1, -1, -1):
            up = lax.ppermute(up, "dp", self.right)
            up = up + sums[:, hop]
        if self.size > 2:
            down = sums[:, self.half + 1]
            for hop in range(self.half - 2, -1, -1):
                down = lax.ppermute(down, "dp", self.left)
                if hop:
                    down = down + sums[:, self.size - hop]
            up = up + down
        return up


CORE_PAIRS = [(0, 1), (1, 0), (2, 3), (3, 2)]
CHIP_PAIRS = [(0, 2), (2, 0), (1, 3), (3, 1)]


def swap_core(value):
    return lax.ppermute(value, "tensor", CORE_PAIRS)


def swap_chip(value):
    return lax.ppermute(value, "tensor", CHIP_PAIRS)


def tensor_sum(part):
    near = part[0] + swap_core(part[1].astype(BF16)).astype(F32)
    near = near.astype(BF16)
    return near.astype(F32) + swap_chip(near).astype(F32)


def ring_local(ring, inputs, attention_gain, query_weight, key_matrix, value_matrix, out_weight, feedforward_gain,
          gate_weight, up_weight, down_weight, cotangent, layer_keep, prefix_length):
    n = ring.size
    seqs, length, width = inputs.shape
    block = width // n
    q_cols, kv_cols = query_weight.shape[1], key_matrix.shape[1]
    heads = q_cols // HEAD_SIZE
    kv_heads = kv_cols // HEAD_SIZE
    repeat = heads // kv_heads
    scale = 1.0 / math.sqrt(HEAD_SIZE)
    core = lax.axis_index("tensor") % 2
    owners = ring.owners()

    def arrange(array):
        array = jnp.where(core == 0, array, array[::-1])
        return jnp.concatenate(
            [lax.dynamic_slice_in_dim(array, owners[j] * block, block, axis=2) for j in range(n)], axis=2
        )

    def restore(own, other):
        array = jnp.stack([jnp.where(core == 0, own, other), jnp.where(core == 0, other, own)])
        places = jnp.asarray(np.argsort(np.array(ring.order)).astype(np.int32))
        where = (places - ring.place()) % n
        return jnp.concatenate(
            [lax.dynamic_slice_in_dim(array, where[j] * block, block, axis=2) for j in range(n)], axis=2
        )

    gains = jnp.concatenate([attention_gain, feedforward_gain])
    fill = jnp.zeros((8, q_cols + 2 * kv_cols), BF16)
    fill = lax.dynamic_update_slice(fill, gains[None, :], (0, 0))
    first = jnp.concatenate(
        [jnp.concatenate([query_weight, key_matrix, value_matrix], axis=1), fill], axis=0
    )
    first_pieces = ring.gather(first)
    qkv_w = jnp.concatenate([p[:block] for p in first_pieces], axis=0)
    gain_a = jnp.concatenate([p[block, :block] for p in first_pieces]).astype(F32)
    gain_f = jnp.concatenate([p[block, block : 2 * block] for p in first_pieces]).astype(F32)
    out_w = jnp.concatenate(ring.gather(out_weight), axis=1)
    gate_w = jnp.concatenate(ring.gather(gate_weight), axis=0)
    up_w = jnp.concatenate(ring.gather(up_weight), axis=0)
    down_w = jnp.concatenate(ring.gather(down_weight), axis=1)

    keep = layer_keep.astype(F32)
    keep = jnp.where(core == 0, keep, keep[::-1])
    prefix = jnp.where(core == 0, prefix_length, prefix_length[::-1])
    x = arrange(inputs)
    dy = arrange(cotangent)

    cos_part, sin_part = rotary_tables(length)
    cos_part, sin_part = cos_part[None, :, None, :], sin_part[None, :, None, :]
    position = jnp.arange(length, dtype=jnp.int32)

    rows = x.reshape(seqs * length, width).astype(F32)
    r1 = lax.rsqrt(jnp.mean(rows * rows, axis=-1, keepdims=True) + EPSILON)
    n1 = (rows * r1 * gain_a).astype(BF16)
    qkv = dot(n1, qkv_w)
    q = rotate(qkv[:, :q_cols].reshape(seqs, length, heads, HEAD_SIZE), cos_part, sin_part).astype(BF16)
    k = rotate(qkv[:, q_cols : q_cols + kv_cols].reshape(seqs, length, kv_heads, HEAD_SIZE), cos_part, sin_part).astype(BF16)
    v = qkv[:, q_cols + kv_cols :].astype(BF16).reshape(seqs, length, kv_heads, HEAD_SIZE)
    q = q.reshape(seqs, length, kv_heads, repeat, HEAD_SIZE)
    scores = jnp.einsum("bqgrd,bkgd->bgrqk", q, k, preferred_element_type=F32) * scale
    allowed = (position[None, None, :] <= position[None, :, None]) | (position[None, None, :] < prefix[:, None, None])
    scores = jnp.where(allowed[:, None, None], scores, NEGATIVE)
    exps = jnp.exp(scores - jnp.max(scores, axis=-1, keepdims=True))
    probs = exps / jnp.sum(exps, axis=-1, keepdims=True)
    probs_low = probs.astype(BF16)
    mixed = jnp.einsum("bgrqk,bkgd->bqgrd", probs_low, v, preferred_element_type=F32)
    mixed = mixed.reshape(seqs * length, q_cols).astype(BF16)
    a_own = tensor_sum(dot(mixed, out_w).reshape(seqs, length, width))
    x_own = x[0].astype(F32)
    hid = x_own + keep[0] * a_own
    r2 = lax.rsqrt(jnp.mean(hid * hid, axis=-1, keepdims=True) + EPSILON)
    n2_own = (hid * r2 * gain_f).astype(BF16)
    n2 = jnp.concatenate([n2_own, swap_core(n2_own)], axis=0)

    g = dot(n2, gate_w)
    u = dot(n2, up_w)
    sig = jax.nn.sigmoid(g)
    swish = g * sig
    m = (swish * u).astype(BF16)
    f_own = tensor_sum(dot(m, down_w).reshape(seqs, length, width))
    out_own = (hid + keep[0] * f_own).astype(BF16)
    output = restore(out_own, swap_core(out_own))

    df = (keep[:, None, None] * dy.astype(F32)).astype(BF16).reshape(seqs * length, width)
    grad_down = dot_ta(m, df)
    dm = dot_tb(df, down_w)
    dg = (dm * u * sig * (1.0 + g * (1.0 - sig))).astype(BF16)
    du = (dm * swish).astype(BF16)
    grad_down = ring.scatter([grad_down[:, j * block : (j + 1) * block] for j in range(n)])
    grad_gate = dot_ta(n2, dg)
    grad_gate = ring.scatter([grad_gate[j * block : (j + 1) * block] for j in range(n)])
    grad_up = dot_ta(n2, du)
    grad_up = ring.scatter([grad_up[j * block : (j + 1) * block] for j in range(n)])
    dn2 = tensor_sum((dot_tb(dg, gate_w) + dot_tb(du, up_w)).reshape(seqs, length, width))
    gain_f_sum = jnp.sum(dn2 * hid * r2, axis=0)
    scaled = dn2 * gain_f
    dh = dy[0].astype(F32) + r2 * scaled - hid * (r2 * r2 * r2) * jnp.mean(scaled * hid, axis=-1, keepdims=True)
    da_own = (keep[0] * dh).astype(BF16)
    da = jnp.concatenate([da_own, swap_core(da_own)], axis=0)

    grad_out = dot_ta(mixed, da)
    grad_out = ring.scatter([grad_out[:, j * block : (j + 1) * block] for j in range(n)])
    dmixed = dot_tb(da, out_w).astype(BF16).reshape(seqs, length, kv_heads, repeat, HEAD_SIZE)
    dprobs = jnp.einsum("bqgrd,bkgd->bgrqk", dmixed, v, preferred_element_type=F32)
    dv = jnp.einsum("bgrqk,bqgrd->bkgd", probs_low, dmixed, preferred_element_type=F32).astype(BF16)
    inner = jnp.sum(probs * dprobs, axis=-1, keepdims=True)
    dscores = (probs * (dprobs - inner)).astype(BF16)
    dq = jnp.einsum("bgrqk,bkgd->bqgrd", dscores, k, preferred_element_type=F32) * scale
    dk = jnp.einsum("bgrqk,bqgrd->bkgd", dscores, q, preferred_element_type=F32) * scale
    dq = rotate(dq.reshape(seqs, length, heads, HEAD_SIZE), cos_part, -sin_part).astype(BF16)
    dk = rotate(dk, cos_part, -sin_part).astype(BF16)
    dqkv = jnp.concatenate(
        [d.reshape(seqs * length, -1) for d in (dq, dk, dv)], axis=1
    )
    grad_qkv = dot_ta(n1, dqkv)
    grad_qkv = ring.scatter([grad_qkv[j * block : (j + 1) * block] for j in range(n)])
    dn1 = tensor_sum(dot_tb(dqkv, qkv_w).reshape(seqs, length, width))
    r1_own = r1[:length]
    gain_a_sum = jnp.sum(dn1 * x_own * r1_own, axis=0)
    scaled = dn1 * gain_a
    dx = dh + r1_own * scaled - x_own * (r1_own * r1_own * r1_own) * jnp.mean(scaled * x_own, axis=-1, keepdims=True)
    dx = dx.astype(BF16)
    input_grad = restore(dx, swap_core(dx))

    sums = jnp.stack([gain_a_sum, gain_f_sum]).reshape(2, n, block)
    sums = sums + swap_core(sums)
    gain_grads = ring.small_scatter(sums)
    return (
        output,
        input_grad,
        gain_grads[0],
        grad_qkv[:, :q_cols],
        grad_qkv[:, q_cols : q_cols + kv_cols],
        grad_qkv[:, q_cols + kv_cols :],
        grad_out,
        gain_grads[1],
        grad_gate,
        grad_up,
        grad_down,
    )


def local(ring, inputs, attention_gain, query_weight, key_matrix, value_matrix, out_weight, feedforward_gain,
          gate_weight, up_weight, down_weight, cotangent, layer_keep, prefix_length):
    n = ring.size
    seqs, length, width = inputs.shape
    tokens = seqs * length
    block = width // n
    q_cols, kv_cols = query_weight.shape[1], key_matrix.shape[1]
    cos_part, sin_part = rotary_tables(length)
    cos = jnp.concatenate([cos_part, cos_part], axis=1)
    sin = jnp.concatenate([-sin_part, sin_part], axis=1)
    keep = layer_keep.astype(F32)
    gains = jnp.concatenate([attention_gain[None], feedforward_gain[None], jnp.zeros((14, block), BF16)], axis=0)
    x = inputs.reshape(tokens, width)
    dy = cotangent.reshape(tokens, width)
    names = ("gains", "wq", "wk", "wv", "wo", "wg", "wu", "wd", "n1", "q", "k", "v", "ob", "hid", "n2", "m", "fa", "fb", "g_down")
    values = dict(
        zip(
            names,
            forward(
                n, x, dy, gains, query_weight, key_matrix, value_matrix, out_weight, gate_weight, up_weight, down_weight,
                cos, sin, keep, prefix_length, length,
            ),
        )
    )
    values |= {"x": x, "dy": dy, "cos": cos, "sin": sin, "keep": keep, "prefix": prefix_length}
    outs = backward(n, length, values)
    me = lax.axis_index("dp")

    def total(name, axis):
        own = lax.dynamic_slice_in_dim(outs["g_" + name], me * block, block, axis=axis)
        return own.astype(F32) + outs[f"r_{name}_0"][-1].astype(F32) + outs[f"r_{name}_1"][-1].astype(F32)

    qkv = total("qkv", 0)
    gain_sums = jnp.sum(outs["gain_slots"], axis=0)[:2]
    gain_sums = gain_sums + swap_core(gain_sums)
    return (
        outs["output"].reshape(inputs.shape),
        outs["dx"].reshape(inputs.shape),
        gain_sums[0],
        qkv[:, :q_cols],
        qkv[:, q_cols : q_cols + kv_cols],
        qkv[:, q_cols + kv_cols :],
        total("out", 1),
        gain_sums[1],
        total("gate", 0),
        total("up", 0),
        total("down", 1),
    )


def solution(mesh):
    ring = Ring(mesh.shape["dp"])
    if mesh.shape["tensor"] != 4:
        raise ValueError("tensor axis")
    row, col = P("dp", "tensor"), P("tensor", "dp")
    data = P("dp", None, None)

    def layer(*args):
        block = args[0].shape[2] // ring.size
        return (local if block % 256 == 0 else ring_local)(ring, *args)

    return jax.shard_map(
        layer,
        mesh=mesh,
        in_specs=(data, P("dp"), row, row, row, col, P("dp"), row, row, col, data, P("dp"), P("dp")),
        out_specs=(data, data, P("dp"), row, row, row, col, P("dp"), row, row, col),
        check_vma=False,
    )
```

```python
import functools
import math

import jax
import jax.numpy as jnp
import numpy as np
from jax import lax
from jax.experimental import pallas as pl
from jax.experimental.pallas import tpu as pltpu
from jax.sharding import PartitionSpec as P

HEAD_SIZE = 128
EPSILON = 1e-05
NEGATIVE = -1e30
BF16 = jnp.bfloat16
F32 = jnp.float32
MESH = pl.DeviceIdType.MESH
HBM = pl.BlockSpec(memory_space=pltpu.HBM)
SMEM = pl.BlockSpec(memory_space=pltpu.SMEM)
ROWS = 256


def dot(a, b):
    return jnp.dot(a, b, preferred_element_type=F32)


def dot_ta(a, b):
    return lax.dot_general(a, b, (((0,), (0,)), ((), ())), preferred_element_type=F32)


def dot_tb(a, b):
    return lax.dot_general(a, b, (((1,), (1,)), ((), ())), preferred_element_type=F32)


def spec(rows, cols):
    return pl.BlockSpec((rows, cols), lambda i: (i, 0))


def fixed(*shape):
    return pl.BlockSpec(shape, lambda i: (0,) * len(shape), pipeline_mode=pl.Buffered(1))


def tiles(total, step=256):
    return [(at, min(step, total - at)) for at in range(0, total, step)]


def gain_row(gains_ref, which):
    n = gains_ref.shape[0]
    return jnp.concatenate([gains_ref[j, which : which + 1, :] for j in range(n)], axis=1).astype(F32)


def turn(values, cos, sin):
    return values * cos + pltpu.roll(values, HEAD_SIZE // 2, axis=1) * sin


class Place:
    def __init__(self, n):
        self.n = n
        self.me = lax.axis_index("dp")
        odd = self.me % 2
        self.p = (1 - odd) * (self.me // 2) + odd * (n - 1 - self.me // 2)
        tensor = lax.axis_index("tensor")
        self.core = tensor % 2
        self.core_peer = tensor + 1 - 2 * self.core
        self.chip_peer = (tensor + 2) % 4
        self.right = self.at(1)
        self.left = self.at(-1)

    def at(self, j):
        p = (self.p + j + 2 * self.n) % self.n
        low = p // (self.n // 2)
        return (1 - low) * 2 * p + low * (2 * (self.n - 1 - p) + 1)

    def greet(self):
        barrier = pltpu.get_barrier_semaphore()
        for peer in (self.left, self.right):
            pl.semaphore_signal(barrier, inc=1, device_id={"dp": peer}, device_id_type=MESH)
        for peer in (self.core_peer, self.chip_peer):
            pl.semaphore_signal(barrier, inc=1, device_id={"tensor": peer}, device_id_type=MESH)
        pl.semaphore_wait(barrier, 4)


class Gather:
    def __init__(self, place, shard, whole, where, local_sem, send_sems, recv_sems):
        self.place, self.shard, self.whole, self.where = place, shard, whole, where
        self.send_sems, self.recv_sems = send_sems, recv_sems
        self.hops = place.n // 2
        self.local = pltpu.make_async_copy(shard, where(whole, place.me, None), local_sem)

    def copy(self, way, hop):
        place = self.place
        sign = 1 - 2 * way
        owner = place.at(-sign * (hop - 1))
        half = way if hop == self.hops else None
        target = self.where(self.whole, owner, half)
        if hop > 1:
            source = target
        elif half is None:
            source = self.shard
        else:
            rows = self.shard.shape[0] // 2
            source = self.shard.at[pl.ds(half * rows, rows)]
        return pltpu.make_async_remote_copy(
            src_ref=source,
            dst_ref=target,
            send_sem=self.send_sems.at[way, hop - 1],
            recv_sem=self.recv_sems.at[way, hop - 1],
            device_id={"dp": place.right if way == 0 else place.left},
            device_id_type=MESH,
        )

    def step(self, hop):
        for way in range(2):
            if hop > 1:
                self.copy(way, hop - 1).wait_recv()
            self.copy(way, hop).start()

    def arrived(self):
        self.local.wait()
        for way in range(2):
            self.copy(way, self.hops).wait_recv()

    def drain(self):
        for way in range(2):
            for hop in range(1, self.hops + 1):
                self.copy(way, hop).wait_send()


def by_rows(rows):
    def where(whole, owner, half):
        if half is None:
            return whole.at[pl.ds(pl.multiple_of(owner * rows, rows), rows)]
        return whole.at[pl.ds(pl.multiple_of(owner * rows + half * (rows // 2), rows // 2), rows // 2)]

    return where


def by_cols(rows, cols):
    def where(whole, owner, half):
        at = pl.ds(pl.multiple_of(owner * cols, cols), cols)
        if half is None:
            return whole.at[:, at]
        return whole.at[pl.ds(half * (rows // 2), rows // 2), at]

    return where


def by_slot(whole, owner, half):
    if half is None:
        return whole.at[owner]
    rows = whole.shape[1] // 2
    return whole.at[owner, pl.ds(half * rows, rows)]


class Swap:
    def __init__(self, source, target, peer, send_sem, recv_sem):
        self.copy = pltpu.make_async_remote_copy(
            src_ref=source, dst_ref=target, send_sem=send_sem, recv_sem=recv_sem,
            device_id={"tensor": peer}, device_id_type=MESH,
        )
        self.copy.start()


def with_jobs(jobs, body):
    def both(*refs):
        for step, job in jobs:
            pl.when(pl.program_id(0) == step)(job)
        body(*refs)

    return both


class Exchange:
    def __init__(self, place, other, peer, near, far, sems):
        self.place, self.other, self.peer, self.near, self.far, self.sems = place, other, peer, near, far, sems
        self.per, self.rows = other.shape[0], other.shape[1]

    def core(self, i):
        return pltpu.make_async_remote_copy(
            src_ref=self.other.at[i], dst_ref=self.peer.at[i], send_sem=self.sems.at[0, i], recv_sem=self.sems.at[1, i],
            device_id={"tensor": self.place.core_peer}, device_id_type=MESH,
        )

    def chip(self, i):
        return pltpu.make_async_remote_copy(
            src_ref=self.near.at[i], dst_ref=self.far.at[i], send_sem=self.sems.at[2, i], recv_sem=self.sems.at[3, i],
            device_id={"tensor": self.place.chip_peer}, device_id_type=MESH,
        )

    def run(self, term, width, step, row_cols, row_args, fixed_args, jobs=()):
        per, core = self.per, self.place.core

        def body(*refs):
            s = pl.program_id(0)
            for i in range(per):
                if i:
                    @pl.when(s == i)
                    def _():
                        self.core(i - 1).start()

                @pl.when(s == per + i)
                def _():
                    if i == 0:
                        self.core(per - 1).start()
                    else:
                        self.chip(i - 1).start()
                    self.core(i).wait_recv()

            @pl.when(s < per)
            def _():
                for at, size in tiles(width, step):
                    cols = slice(at, at + size)
                    self.other[s, :, cols] = term(refs, cols).astype(BF16)

            @pl.when(s >= per)
            def _():
                for at, size in tiles(width, step):
                    cols = slice(at, at + size)
                    self.near[s - per, :, cols] = (term(refs, cols) + self.peer[s - per, :, cols].astype(F32)).astype(BF16)

        def block(s):
            return ((1 - core) + (s // per) * (2 * core - 1)) * per + s % per

        pltpu.emit_pipeline(
            with_jobs(jobs, body),
            grid=(2 * per,),
            in_specs=[pl.BlockSpec((self.rows, cols), lambda s: (block(s), 0)) for cols in row_cols]
            + [fixed(*w.shape) for w in fixed_args],
        )(*row_args, *fixed_args)
        self.chip(per - 1).start()
        for i in range(per):
            self.core(i).wait_send()

    def arrivals(self):
        return [(i * (self.rows // BLOCK), self.chip(i).wait_recv) for i in range(self.per)]

    def drain(self):
        for i in range(self.per):
            self.chip(i).wait_send()

    def total(self, at, rows):
        i, part = at // self.rows, pl.ds(pl.multiple_of(at % self.rows, rows), rows)
        return self.near[i, part, :].astype(F32) + self.far[i, part, :].astype(F32)


CHUNK = 16
BLOCK = 128


def by_chunks(step, body):
    @pl.loop(0, BLOCK, step=CHUNK)
    def _(at):
        at = pl.multiple_of(at, CHUNK)
        body(pl.ds(at, CHUNK), step * BLOCK + at)


def forward_kernel(
    n, length, x_hbm, dy_hbm, gains_in, wq_in, wk_in, wv_in, wo_in, wg_in, wu_in, wd_in, cos_hbm, sin_hbm, keep_ref, prefix_ref,
    gains_w, wq, wk, wv, wo, wg, wu, wd, n1_hbm, q_hbm, k_hbm, v_hbm, ob_hbm, hid_hbm, n2_hbm, m_hbm, fa_hbm, fb_hbm, gd_hbm,
    other, peer, near, far, local_sems, send_sems, recv_sems, swap_sems, share_sems,
):
    place = Place(n)
    core = place.core
    place.greet()
    tokens, width = x_hbm.shape
    scale = 1.0 / math.sqrt(HEAD_SIZE)
    half = wd_in.shape[0] // 2
    upper, lower = pl.ds(0, half), pl.ds(half, half)
    arrays = {
        "n": (gains_in, gains_w, by_slot),
        "q": (wq_in, wq, by_rows(wq_in.shape[0])),
        "k": (wk_in, wk, by_rows(wk_in.shape[0])),
        "v": (wv_in, wv, by_rows(wv_in.shape[0])),
        "o": (wo_in, wo, by_cols(*wo_in.shape)),
        "g": (wg_in, wg, by_rows(wg_in.shape[0])),
        "u": (wu_in, wu, by_rows(wu_in.shape[0])),
        "a": (wd_in.at[upper], wd.at[upper], by_cols(half, wd_in.shape[1])),
        "b": (wd_in.at[lower], wd.at[lower], by_cols(half, wd_in.shape[1])),
    }
    rings = {
        name: Gather(place, shard, whole, where, local_sems.at[i], send_sems.at[i], recv_sems.at[i])
        for i, (name, (shard, whole, where)) in enumerate(arrays.items())
    }
    hops = n // 2
    done = {name: 0 for name in rings}

    def go(names):
        for name in names:
            if done[name] < hops:
                done[name] += 1
                rings[name].step(done[name])

    own_rows = pl.ds(pl.multiple_of(core * length, length), length)
    other_rows = pl.ds(pl.multiple_of((1 - core) * length, length), length)

    go("nqkv")
    for name in "nqkvogu":
        rings[name].local.start()
    go("nqkvo")
    go("nqkvo")
    go("nqkvog")
    for name in "nqkv":
        go(name * hops)
        rings[name].arrived()

    def project(x_ref, gains_ref, wq_ref, wk_ref, wv_ref, cos_ref, sin_ref, n1_ref, q_ref, k_ref, v_ref):
        gain = gain_row(gains_ref, 0)

        @pl.loop(0, ROWS, step=32)
        def _(at):
            part = pl.ds(pl.multiple_of(at, 32), 32)
            xf = x_ref[part, :].astype(F32)
            r1 = lax.rsqrt(jnp.mean(xf * xf, axis=-1, keepdims=True) + EPSILON)
            n1_ref[part, :] = (xf * r1 * gain).astype(BF16)

        rows = n1_ref[...]
        cos, sin = cos_ref[...], sin_ref[...]
        for w_ref, o_ref in ((wq_ref, q_ref), (wk_ref, k_ref)):
            for at in range(0, w_ref.shape[1], HEAD_SIZE):
                head = slice(at, at + HEAD_SIZE)
                o_ref[:, head] = turn(dot(rows, w_ref[:, head]), cos, sin).astype(BF16)
        v_ref[...] = dot(rows, wv_ref[...]).astype(BF16)

    q_cols, kv_cols = wq.shape[1], wk.shape[1]
    per = length // ROWS
    turns = pl.BlockSpec((ROWS, HEAD_SIZE), lambda i: (i % per, 0))
    pltpu.emit_pipeline(
        project,
        grid=(tokens // ROWS,),
        in_specs=[spec(ROWS, width), fixed(*gains_w.shape), fixed(*wq.shape), fixed(*wk.shape), fixed(*wv.shape), turns, turns],
        out_specs=[spec(ROWS, width), spec(ROWS, q_cols), spec(ROWS, kv_cols), spec(ROWS, kv_cols)],
    )(x_hbm, gains_w, wq, wk, wv, cos_hbm, sin_hbm, n1_hbm, q_hbm, k_hbm, v_hbm)
    go("ogu")

    repeat = q_cols // kv_cols

    def attend(which, q_ref, k_ref, v_ref, o_ref):
        prefix = prefix_ref[which]
        keys, values = k_ref[...], v_ref[...]

        @pl.loop(0, length, step=128)
        def _(at):
            part = pl.ds(pl.multiple_of(at, 128), 128)
            s = dot_tb(q_ref[part, :], keys) * scale
            row = lax.broadcasted_iota(jnp.int32, s.shape, 0) + at
            col = lax.broadcasted_iota(jnp.int32, s.shape, 1)
            s = jnp.where((col <= row) | (col < prefix), s, NEGATIVE)
            e = jnp.exp(s - jnp.max(s, axis=-1, keepdims=True))
            p = e / jnp.sum(e, axis=-1, keepdims=True)
            o_ref[part, :] = dot(p.astype(BF16), values).astype(BF16)

    for which in range(2):
        seq = pl.ds(which * length, length)
        pltpu.emit_pipeline(
            functools.partial(attend, which),
            grid=(q_cols // HEAD_SIZE,),
            in_specs=[
                pl.BlockSpec((length, HEAD_SIZE), lambda h: (0, h)),
                pl.BlockSpec((length, HEAD_SIZE), lambda h: (0, h // repeat)),
                pl.BlockSpec((length, HEAD_SIZE), lambda h: (0, h // repeat)),
            ],
            out_specs=[pl.BlockSpec((length, HEAD_SIZE), lambda h: (0, h))],
        )(q_hbm.at[seq], k_hbm.at[seq], v_hbm.at[seq], ob_hbm.at[seq])

    go("o" * hops)
    rings["o"].arrived()
    go("g")
    mixed = Exchange(place, other, peer, near, far, swap_sems)
    mixed.run(lambda refs, cols: dot(refs[0][...], refs[1][:, cols]), width, 512, [q_cols], [ob_hbm], [wo])
    for name in "ab":
        rings[name].local.start()
    go("u")
    go("g")
    go("u")

    def residual(x_ref, gains_ref, hid_ref, n2_ref):
        gain = gain_row(gains_ref, 1)
        keep = keep_ref[core]

        def chunk(part, row):
            h = x_ref[part, :].astype(F32) + keep * mixed.total(row, CHUNK)
            hid_ref[part, :] = h
            r2 = lax.rsqrt(jnp.mean(h * h, axis=-1, keepdims=True) + EPSILON)
            n2_ref[part, :] = (h * r2 * gain).astype(BF16)

        by_chunks(pl.program_id(0), chunk)

    pltpu.emit_pipeline(
        with_jobs(mixed.arrivals(), residual),
        grid=(length // BLOCK,),
        in_specs=[spec(BLOCK, width), fixed(*gains_w.shape)],
        out_specs=[spec(BLOCK, width)] * 2,
    )(x_hbm.at[own_rows], gains_w, hid_hbm, n2_hbm.at[own_rows])
    share = Swap(n2_hbm.at[own_rows], n2_hbm.at[own_rows], place.core_peer, share_sems.at[0], share_sems.at[1])
    share.copy.wait_recv()
    go("g" * hops + "u" * hops + "ab")
    rings["g"].arrived()
    rings["u"].arrived()

    hidden = wg.shape[1]

    def during(at, name, hop):
        pl.when(pl.program_id(0) == at)(lambda: rings[name].step(hop))
        done[name] = hop

    def feed(n2_ref, wg_ref, wu_ref, m_ref, fa_ref, fb_ref):
        during(tokens // ROWS - 2, "a", 2)
        during(tokens // ROWS - 1, "b", 2)
        rows = n2_ref[...]
        for at, size in tiles(hidden):
            cols = slice(at, at + size)
            g = dot(rows, wg_ref[:, cols])
            u = dot(rows, wu_ref[:, cols])
            sig = 1.0 / (1.0 + jnp.exp(-g))
            swish = g * sig
            m_ref[:, cols] = (swish * u).astype(BF16)
            fa_ref[:, cols] = u * sig * (1.0 + g * (1.0 - sig))
            fb_ref[:, cols] = swish

    pltpu.emit_pipeline(
        feed,
        grid=(tokens // ROWS,),
        in_specs=[spec(ROWS, width), fixed(*wg.shape), fixed(*wu.shape)],
        out_specs=[spec(ROWS, hidden)] * 3,
    )(n2_hbm, wg, wu, m_hbm, fa_hbm, fb_hbm)

    def down_grad(m_ref, dy_ref, o_ref):
        during(1, "a", 3)
        during(5, "b", 3)
        total = None
        for which in range(2):
            seq = slice(which * length, (which + 1) * length)
            df = (dy_ref[seq, :].astype(F32) * keep_ref[which]).astype(BF16)
            term = dot_ta(m_ref[seq, :], df)
            total = term if total is None else total + term
        o_ref[...] = total.astype(BF16)

    cols = pl.BlockSpec((tokens, 256), lambda i: (0, i))
    pltpu.emit_pipeline(
        down_grad,
        grid=(width // 256,),
        in_specs=[fixed(tokens, hidden), cols],
        out_specs=[pl.BlockSpec((hidden, 256), lambda i: (0, i))],
    )(m_hbm, dy_hbm, gd_hbm)
    for _ in range(hops):
        go("ab")
    rings["a"].arrived()
    rings["b"].arrived()
    for ring in rings.values():
        ring.drain()
    mixed.drain()
    share.copy.wait_send()


def forward(n, x, dy, gains, wq, wk, wv, wo, wg, wu, wd, cos, sin, keep, prefix, length):
    tokens, width = x.shape
    shape = jax.ShapeDtypeStruct
    ff = wg.shape[1]
    outs = [
        shape((n,) + gains.shape, BF16),
        shape((width, wq.shape[1]), BF16),
        shape((width, wk.shape[1]), BF16),
        shape((width, wv.shape[1]), BF16),
        shape((wo.shape[0], width), BF16),
        shape((width, ff), BF16),
        shape((width, ff), BF16),
        shape((ff, width), BF16),
        shape((tokens, width), BF16),
        shape((tokens, wq.shape[1]), BF16),
        shape((tokens, wk.shape[1]), BF16),
        shape((tokens, wv.shape[1]), BF16),
        shape((tokens, wq.shape[1]), BF16),
        shape((length, width), F32),
        shape((tokens, width), BF16),
        shape((tokens, ff), BF16),
        shape((tokens, ff), F32),
        shape((tokens, ff), F32),
        shape((ff, width), BF16),
    ]
    blocks = pltpu.VMEM((length // ROWS, ROWS, width), BF16)
    return pl.pallas_call(
        functools.partial(forward_kernel, n, length),
        out_shape=outs,
        in_specs=[HBM] * 12 + [SMEM] * 2,
        out_specs=[HBM] * len(outs),
        scratch_shapes=[
            blocks,
            blocks,
            blocks,
            blocks,
            pltpu.SemaphoreType.DMA((9,)),
            pltpu.SemaphoreType.DMA((9, 2, n // 2)),
            pltpu.SemaphoreType.DMA((9, 2, n // 2)),
            pltpu.SemaphoreType.DMA((4, length // ROWS)),
            pltpu.SemaphoreType.DMA((2,)),
        ],
        compiler_params=pltpu.CompilerParams(collective_id=0, has_side_effects=True, vmem_limit_bytes=60 * 1024 * 1024),
    )(x, dy, gains, wq, wk, wv, wo, wg, wu, wd, cos, sin, keep, prefix)


class Buffers:
    def __init__(self, arrived, sums, sems):
        self.arrived, self.sums, self.sems = arrived, sums, sems
        self.users = []


class Scatter:
    def __init__(self, place, whole, where, piece, slots, buffers, send_sems, recv_sems):
        self.place, self.whole, self.where, self.piece = place, whole, where, piece
        self.slots, self.buffers = slots, buffers
        self.send_sems, self.recv_sems = send_sems, recv_sems
        self.hops = place.n // 2
        self.turns = {}
        self.sent = set()

    def view(self, way, hop):
        sign = 1 - 2 * way
        owner = self.place.at(sign * (self.hops + 1 - hop))
        return self.where(self.whole, owner, way if hop == 1 else None)

    def slot(self, way, hop):
        first, rest = self.slots[way]
        return first if hop == 1 else rest.at[hop - 2]

    def going(self, way, hop):
        rows, cols = self.piece
        buffers = self.buffers
        return buffers.sums.at[self.turns[hop] % buffers.sums.shape[0], way, pl.ds(0, rows), pl.ds(0, cols)]

    def come(self, way, hop):
        rows, cols = self.piece
        buffers = self.buffers
        rows = rows // 2 if hop == 2 else rows
        return buffers.arrived.at[self.turns[hop] % buffers.arrived.shape[0], way, pl.ds(0, rows), pl.ds(0, cols)]

    def remote(self, way, hop):
        return pltpu.make_async_remote_copy(
            src_ref=self.view(way, hop) if hop == 1 else self.going(way, hop),
            dst_ref=self.slot(way, hop),
            send_sem=self.send_sems.at[way, hop - 1],
            recv_sem=self.recv_sems.at[way, hop - 1],
            device_id={"dp": self.place.right if way == 0 else self.place.left},
            device_id_type=MESH,
        )

    def locals(self, hop):
        sems = self.buffers.sems
        turn = self.turns[hop] % sems.shape[0]
        for way in range(2):
            yield pltpu.make_async_copy(self.slot(way, hop - 1), self.come(way, hop), sems.at[turn, way, 0])
            yield pltpu.make_async_copy(self.view(way, hop), self.going(way, hop), sems.at[turn, way, 1])

    def first(self):
        for way in range(2):
            self.remote(way, 1).start()

    def plan(self, hop):
        users = self.buffers.users
        self.turns[hop] = len(users)
        before = users[-self.buffers.sums.shape[0]] if len(users) >= self.buffers.sums.shape[0] else None
        users.append((self, hop))
        if before:
            before[0].sent.add(before[1])

        def fetch():
            for way in range(2):
                self.remote(way, hop - 1).wait_recv()
                if before:
                    before[0].remote(way, before[1]).wait_send()
            for copy in self.locals(hop):
                copy.start()

        def emit():
            for copy in self.locals(hop):
                copy.wait()
            rows = self.piece[0]
            for way in range(2):
                come, going = self.come(way, hop), self.going(way, hop)
                base = way * (rows // 2) if hop == 2 else 0

                @pl.loop(0, rows // 2 if hop == 2 else rows, step=CHUNK)
                def _(at):
                    at = pl.multiple_of(at, CHUNK)
                    part = pl.ds(pl.multiple_of(base + at, CHUNK), CHUNK)
                    going[part, :] = (going[part, :].astype(F32) + come[pl.ds(at, CHUNK), :].astype(F32)).astype(BF16)

                self.remote(way, hop).start()

        return fetch, emit

    def drain(self):
        for way in range(2):
            self.remote(way, self.hops).wait_recv()
            for hop in range(1, self.hops + 1):
                if hop not in self.sent:
                    self.remote(way, hop).wait_send()


def backward_kernel(n, length, names_in, names_out, *refs):
    ins = dict(zip(names_in, refs))
    outs = dict(zip(names_out, refs[len(names_in) :]))
    (gsum, gpieces, dh, other, peers, nears, fars, come_rows, sums_rows, come_cols, sums_cols, add_sems, local_sems, send_sems, recv_sems, swap_sems, swap_send, swap_recv, gain_send, gain_recv) = refs[
        len(names_in) + len(names_out) :
    ]
    keep_ref, prefix_ref = ins["keep"], ins["prefix"]
    dy, x, gains_w = ins["dy"], ins["x"], ins["gains"]
    wq, wk, wv, wo, wg, wu, wd = (ins[name] for name in ("wq", "wk", "wv", "wo", "wg", "wu", "wd"))
    tokens, width = x.shape
    q_cols, kv_cols, hidden = wq.shape[1], wk.shape[1], wg.shape[1]
    block = width // n
    per = length // ROWS
    repeat = q_cols // kv_cols
    scale = 1.0 / math.sqrt(HEAD_SIZE)
    place = Place(n)
    core = place.core
    barrier = pltpu.get_barrier_semaphore()
    for j in range(1, n):
        pl.semaphore_signal(barrier, inc=1, device_id={"dp": place.at(j)}, device_id_type=MESH)
    for peer in (place.core_peer, place.chip_peer):
        pl.semaphore_signal(barrier, inc=1, device_id={"tensor": peer}, device_id_type=MESH)
    pl.semaphore_wait(barrier, n + 1)

    own_rows = pl.ds(pl.multiple_of(core * length, length), length)
    by_row = Buffers(come_rows, sums_rows, add_sems.at[0])
    by_col = Buffers(come_cols, sums_cols, add_sems.at[1])
    grads = {
        "down": (by_cols(hidden, block), (hidden, block), by_col),
        "gate": (by_rows(block), (block, hidden), by_row),
        "up": (by_rows(block), (block, hidden), by_row),
        "out": (by_cols(q_cols, block), (q_cols, block), by_col),
        "qkv": (by_rows(block), (block, q_cols + 2 * kv_cols), by_row),
    }
    rings = {
        name: Scatter(
            place,
            outs["g_" + name],
            where,
            piece,
            [(outs[f"r_{name}_{way}_first"], outs[f"r_{name}_{way}"]) for way in range(2)],
            buffers,
            send_sems.at[i],
            recv_sems.at[i],
        )
        for i, (name, (where, piece, buffers)) in enumerate(grads.items())
    }
    swaps = []

    def swap(source, target, peer):
        i = len(swaps)
        swaps.append(Swap(source, target, peer, swap_send.at[i], swap_recv.at[i]))
        return swaps[-1].copy

    def act_grads(jobs):
        def body(dy_ref, wd_ref, fa_ref, fb_ref, dg_ref, du_ref):
            which = pl.program_id(0) // per
            df = (dy_ref[...].astype(F32) * keep_ref[which]).astype(BF16)
            for at, size in tiles(hidden):
                cols = slice(at, at + size)
                dm = dot_tb(df, wd_ref[cols, :])
                dg_ref[:, cols] = (dm * fa_ref[:, cols]).astype(BF16)
                du_ref[:, cols] = (dm * fb_ref[:, cols]).astype(BF16)

        pltpu.emit_pipeline(
            with_jobs(jobs, body),
            grid=(tokens // ROWS,),
            in_specs=[spec(ROWS, width), fixed(hidden, width), spec(ROWS, hidden), spec(ROWS, hidden)],
            out_specs=[spec(ROWS, hidden)] * 2,
        )(dy, wd, ins["fa"], ins["fb"], outs["dg"], outs["du"])

    def outer(left, right, target, jobs):
        def body(l_ref, r_ref, o_ref):
            o_ref[...] = dot_ta(l_ref[...], r_ref[...]).astype(BF16)

        cols = right.shape[1]
        pltpu.emit_pipeline(
            with_jobs(jobs, body),
            grid=(width // 256,),
            in_specs=[pl.BlockSpec((tokens, 256), lambda i: (0, i)), fixed(tokens, cols)],
            out_specs=[spec(256, cols)],
        )(left, right, target)

    def exchange(i):
        return Exchange(place, other, peers.at[i], nears.at[i], fars.at[i], swap_sems.at[i])

    in_n2, in_f, in_n1 = exchange(0), exchange(1), exchange(2)

    def back(jobs):
        in_n2.run(
            lambda refs, cols: dot_tb(refs[0][...], refs[2][cols, :]) + dot_tb(refs[1][...], refs[3][cols, :]),
            width, 256, [hidden, hidden], [outs["dg"], outs["du"]], [wg, wu], jobs,
        )

    def add_gain(which, terms):
        gsum[which] += sum(terms[i * 8 : (i + 1) * 8] for i in range(terms.shape[0] // 8))

    def norm_back(d, h, gain, which):
        r = lax.rsqrt(jnp.mean(h * h, axis=-1, keepdims=True) + EPSILON)
        add_gain(which, d * h * r)
        scaled = d * gain
        return r * scaled - h * (r * r * r) * jnp.mean(scaled * h, axis=-1, keepdims=True)

    def hid_grads():
        def body(hid_ref, dy_ref, gains_ref, da_ref):
            gain = gain_row(gains_ref, 1)
            keep = keep_ref[core]

            def chunk(part, row):
                d = in_n2.total(row, CHUNK)
                value = dy_ref[part, :].astype(F32) + norm_back(d, hid_ref[part, :], gain, 1)
                dh[pl.ds(pl.multiple_of(row, CHUNK), CHUNK), :] = value
                da_ref[part, :] = (keep * value).astype(BF16)

            by_chunks(pl.program_id(0), chunk)

        pltpu.emit_pipeline(
            with_jobs(in_n2.arrivals(), body),
            grid=(length // BLOCK,),
            in_specs=[spec(BLOCK, width)] * 2 + [fixed(*gains_w.shape)],
            out_specs=[spec(BLOCK, width)],
        )(ins["hid"], dy.at[own_rows], gains_w, outs["da"].at[own_rows])
        return swap(outs["da"].at[own_rows], outs["da"].at[own_rows], place.core_peer)

    def input_grads():
        def body(x_ref, gains_ref, dx_ref):
            gain = gain_row(gains_ref, 0)

            def chunk(part, row):
                d = in_n1.total(row, CHUNK)
                value = norm_back(d, x_ref[part, :].astype(F32), gain, 0)
                dx_ref[part, :] = (dh[pl.ds(pl.multiple_of(row, CHUNK), CHUNK), :] + value).astype(BF16)

            by_chunks(pl.program_id(0), chunk)

        pltpu.emit_pipeline(
            with_jobs(in_n1.arrivals(), body),
            grid=(length // BLOCK,),
            in_specs=[spec(BLOCK, width), fixed(*gains_w.shape)],
            out_specs=[spec(BLOCK, width)],
        )(x.at[own_rows], gains_w, outs["dx"].at[own_rows])
        return swap(outs["dx"].at[own_rows], outs["dx"].at[own_rows], place.core_peer)

    def results():
        def body(hid_ref, o_ref):
            keep = keep_ref[core]

            def chunk(part, row):
                o_ref[part, :] = (hid_ref[part, :] + keep * in_f.total(row, CHUNK)).astype(BF16)

            by_chunks(pl.program_id(0), chunk)

        pltpu.emit_pipeline(
            with_jobs(in_f.arrivals(), body),
            grid=(length // BLOCK,),
            in_specs=[spec(BLOCK, width)],
            out_specs=[spec(BLOCK, width)],
        )(ins["hid"], outs["output"].at[own_rows])
        return swap(outs["output"].at[own_rows], outs["output"].at[own_rows], place.core_peer)

    def forth(jobs):
        in_f.run(lambda refs, cols: dot(refs[0][...], refs[1][:, cols]), width, 512, [hidden], [ins["m"]], [wd], jobs)

    def out_grad(jobs):
        def body(ob_ref, da_ref, o_ref):
            o_ref[...] = dot_ta(ob_ref[...], da_ref[...]).astype(BF16)

        pltpu.emit_pipeline(
            with_jobs(jobs, body),
            grid=(width // 256,),
            in_specs=[fixed(tokens, q_cols), pl.BlockSpec((tokens, 256), lambda i: (0, i))],
            out_specs=[pl.BlockSpec((q_cols, 256), lambda i: (0, i))],
        )(ins["ob"], outs["da"], outs["g_out"])

    def mixed_grad():
        def body(da_ref, wo_ref, o_ref):
            o_ref[...] = dot_tb(da_ref[...], wo_ref[...]).astype(BF16)

        pltpu.emit_pipeline(
            body, grid=(tokens // ROWS,), in_specs=[spec(ROWS, width), fixed(q_cols, width)], out_specs=[spec(ROWS, q_cols)]
        )(outs["da"], wo, outs["dob"])

    def attend_back(which, jobs):
        seq = pl.ds(which * length, length)

        def heads(dk_sum, dv_sum):
            def body(q_ref, k_ref, v_ref, d_ref, cos_ref, sin_ref, dq_ref, dk_ref, dv_ref):
                head = pl.program_id(0) % repeat
                prefix = prefix_ref[which]
                keys, values = k_ref[...], v_ref[...]

                @pl.when(head == 0)
                def _():
                    dk_sum[...] = jnp.zeros_like(dk_sum)
                    dv_sum[...] = jnp.zeros_like(dv_sum)

                @pl.loop(0, length, step=128)
                def _(at):
                    part = pl.ds(pl.multiple_of(at, 128), 128)
                    queries, grads = q_ref[part, :], d_ref[part, :]
                    s = dot_tb(keys, queries) * scale
                    col = lax.broadcasted_iota(jnp.int32, s.shape, 0)
                    row = lax.broadcasted_iota(jnp.int32, s.shape, 1) + at
                    s = jnp.where((col <= row) | (col < prefix), s, NEGATIVE)
                    e = jnp.exp(s - jnp.max(s, axis=0, keepdims=True))
                    p = e / jnp.sum(e, axis=0, keepdims=True)
                    dp = dot_tb(values, grads)
                    inner = jnp.sum(p * dp, axis=0, keepdims=True)
                    dz = (p * (dp - inner)).astype(BF16)
                    dv_sum[...] += dot(p.astype(BF16), grads)
                    dk_sum[...] += dot(dz, queries)
                    dq = dot_ta(dz, keys) * scale
                    dq_ref[part, :] = turn(dq, cos_ref[part, :], -sin_ref[part, :]).astype(BF16)

                @pl.when(head == repeat - 1)
                def _():
                    dk_ref[...] = turn(dk_sum[...] * scale, cos_ref[...], -sin_ref[...]).astype(BF16)
                    dv_ref[...] = dv_sum[...].astype(BF16)

            one = pl.BlockSpec((length, HEAD_SIZE), lambda h: (0, h))
            shared = pl.BlockSpec((length, HEAD_SIZE), lambda h: (0, h // repeat))
            table = pl.BlockSpec((length, HEAD_SIZE), lambda h: (0, 0))
            dqkv = outs["dqkv"].at[seq]
            pltpu.emit_pipeline(
                with_jobs(jobs, body),
                grid=(q_cols // HEAD_SIZE,),
                in_specs=[one, shared, shared, one, table, table],
                out_specs=[one, shared, shared],
            )(
                ins["q"].at[seq],
                ins["k"].at[seq],
                ins["v"].at[seq],
                outs["dob"].at[seq],
                ins["cos"],
                ins["sin"],
                dqkv.at[:, pl.ds(0, q_cols)],
                dqkv.at[:, pl.ds(q_cols, kv_cols)],
                dqkv.at[:, pl.ds(q_cols + kv_cols, kv_cols)],
            )

        pl.run_scoped(heads, pltpu.VMEM((length, HEAD_SIZE), F32), pltpu.VMEM((length, HEAD_SIZE), F32))

    def back_qkv(jobs):
        def term(refs, cols):
            d_ref, wq_ref, wk_ref, wv_ref = refs
            dq, dk, dv = d_ref[:, :q_cols], d_ref[:, q_cols : q_cols + kv_cols], d_ref[:, q_cols + kv_cols :]
            return dot_tb(dq, wq_ref[cols, :]) + dot_tb(dk, wk_ref[cols, :]) + dot_tb(dv, wv_ref[cols, :])

        in_n1.run(term, width, 256, [q_cols + 2 * kv_cols], [outs["dqkv"]], [wq, wk, wv], jobs)

    def gain_grads():
        for which in range(2):
            row = jnp.sum(gsum[which], axis=0, keepdims=True)
            for j in range(n):
                gpieces[j, which : which + 1, :] = row[:, j * block : (j + 1) * block]
        copy = pltpu.make_async_copy(gpieces, outs["gain_terms"], local_sems.at[0])
        copy.start()
        copy.wait()
        mine = pltpu.make_async_copy(outs["gain_terms"].at[place.me], outs["gain_slots"].at[0], local_sems.at[1])
        mine.start()
        copies = []
        for j in range(1, n):
            copy = pltpu.make_async_remote_copy(
                src_ref=outs["gain_terms"].at[place.at(j)],
                dst_ref=outs["gain_slots"].at[j],
                send_sem=gain_send.at[j],
                recv_sem=gain_recv.at[j],
                device_id={"dp": place.at(j)},
                device_id_type=MESH,
            )
            copy.start()
            copies.append(copy)
        return mine, copies

    plans = {}
    for name, hop in (
        ("down", 2), ("down", 3), ("gate", 2), ("down", 4), ("gate", 3), ("up", 2), ("gate", 4), ("up", 3), ("out", 2),
        ("up", 4), ("out", 3), ("qkv", 2), ("qkv", 3), ("out", 4), ("qkv", 4),
    ):
        plans[name, hop] = rings[name].plan(hop)

    def fetch(name, hop):
        return plans[name, hop][0]

    def emit(name, hop):
        return plans[name, hop][1]

    rings["down"].first()
    gsum[...] = jnp.zeros_like(gsum)
    gpieces[...] = jnp.zeros_like(gpieces)
    act_grads([(2, fetch("down", 2)), (3, emit("down", 2))])
    outer(ins["n2"], outs["dg"], outs["g_gate"], [])
    rings["gate"].first()
    back([(0, fetch("down", 3)), (1, emit("down", 3)), (2, fetch("gate", 2)), (3, emit("gate", 2))])
    outer(ins["n2"], outs["du"], outs["g_up"], [(3, fetch("down", 4)), (5, emit("down", 4))])
    rings["up"].first()
    forth([])
    fetch("gate", 3)()
    emit("gate", 3)()
    share_da = hid_grads()
    fetch("up", 2)()
    emit("up", 2)()
    share_da.wait_recv()
    mixed_grad()
    out_grad([(4, fetch("gate", 4)), (6, emit("gate", 4))])
    rings["out"].first()
    attend_back(0, [(2, fetch("up", 3)), (3, emit("up", 3))])
    attend_back(1, [(3, fetch("out", 2))])
    emit("out", 2)()
    back_qkv([(3, fetch("up", 4))])
    outer(ins["n1"], outs["dqkv"], outs["g_qkv"], [(0, emit("up", 4)), (5, fetch("out", 3))])
    rings["qkv"].first()
    emit("out", 3)()
    share_out = results()
    fetch("qkv", 2)()
    emit("qkv", 2)()
    fetch("qkv", 3)()
    emit("qkv", 3)()
    fetch("out", 4)()
    emit("out", 4)()
    share_dx = input_grads()
    fetch("qkv", 4)()
    emit("qkv", 4)()
    mine, copies = gain_grads()
    share_out.wait_recv()
    share_dx.wait_recv()
    mine.wait()
    for copy in copies:
        copy.wait_recv()
    for ring in rings.values():
        ring.drain()
    for copy in copies:
        copy.wait_send()
    for item in swaps:
        item.copy.wait_send()
    for item in (in_n2, in_f, in_n1):
        item.drain()


def backward(n, length, values):
    shape = jax.ShapeDtypeStruct
    tokens, width = values["x"].shape
    q_cols, kv_cols, hidden = values["wq"].shape[1], values["wk"].shape[1], values["wg"].shape[1]
    block = width // n
    widest = max(hidden, q_cols + 2 * kv_cols)
    outs = {}
    sizes = {
        "down": ((hidden, width), (hidden, block)),
        "gate": ((width, hidden), (block, hidden)),
        "up": ((width, hidden), (block, hidden)),
        "out": ((q_cols, width), (q_cols, block)),
        "qkv": ((width, q_cols + 2 * kv_cols), (block, q_cols + 2 * kv_cols)),
    }
    for name, (whole, piece) in sizes.items():
        outs["g_" + name] = shape(whole, BF16)
        for way in range(2):
            outs[f"r_{name}_{way}_first"] = shape((piece[0] // 2, piece[1]), BF16)
            outs[f"r_{name}_{way}"] = shape((n // 2 - 1,) + piece, BF16)
    outs["dg"] = outs["du"] = shape((tokens, hidden), BF16)
    outs["da"] = outs["dx"] = outs["output"] = shape((tokens, width), BF16)
    outs["dob"] = shape((tokens, q_cols), BF16)
    outs["dqkv"] = shape((tokens, q_cols + 2 * kv_cols), BF16)
    outs["gain_terms"] = outs["gain_slots"] = shape((n, 8, block), F32)
    names_in, names_out = list(values), list(outs)
    results = pl.pallas_call(
        functools.partial(backward_kernel, n, length, names_in, names_out),
        out_shape=list(outs.values()),
        in_specs=[SMEM if name in ("keep", "prefix") else HBM for name in names_in],
        out_specs=[HBM] * len(outs),
        input_output_aliases={names_in.index("g_down"): names_out.index("g_down")},
        scratch_shapes=[
            pltpu.VMEM((2, 8, width), F32),
            pltpu.VMEM((n, 8, block), F32),
            pltpu.VMEM((length, width), F32),
            pltpu.VMEM((length // ROWS, ROWS, width), BF16),
            pltpu.VMEM((3, length // ROWS, ROWS, width), BF16),
            pltpu.VMEM((3, length // ROWS, ROWS, width), BF16),
            pltpu.VMEM((3, length // ROWS, ROWS, width), BF16),
            pltpu.VMEM((2, 2, block, widest), BF16),
            pltpu.VMEM((3, 2, block, widest), BF16),
            pltpu.VMEM((2, 2, widest, block), BF16),
            pltpu.VMEM((3, 2, widest, block), BF16),
            pltpu.SemaphoreType.DMA((2, 3, 2, 2)),
            pltpu.SemaphoreType.DMA((2,)),
            pltpu.SemaphoreType.DMA((5, 2, n // 2)),
            pltpu.SemaphoreType.DMA((5, 2, n // 2)),
            pltpu.SemaphoreType.DMA((3, 4, length // ROWS)),
            pltpu.SemaphoreType.DMA((3,)),
            pltpu.SemaphoreType.DMA((3,)),
            pltpu.SemaphoreType.DMA((n,)),
            pltpu.SemaphoreType.DMA((n,)),
        ],
        compiler_params=pltpu.CompilerParams(collective_id=1, has_side_effects=True, vmem_limit_bytes=60 * 1024 * 1024),
    )(*values.values())
    return dict(zip(names_out, results))


def finish(n, outs, q_cols, kv_cols):
    steps = 8
    shape = jax.ShapeDtypeStruct
    tokens, width = outs["output"].shape
    hidden = outs["g_gate"].shape[1]
    block = width // n
    last = n // 2 - 2

    def copied():
        return pl.BlockSpec((tokens // steps, width), lambda i, me: (i, 0))

    def by_row(cols):
        rows = block // steps
        slot = pl.BlockSpec((None, rows, cols), lambda i, me: (last, i, 0))
        return [pl.BlockSpec((rows, cols), lambda i, me: (me[0] * steps + i, 0)), slot, slot]

    def by_col(rows):
        rows = rows // steps
        slot = pl.BlockSpec((None, rows, block), lambda i, me: (last, i, 0))
        return [pl.BlockSpec((rows, block), lambda i, me: (i, me[0])), slot, slot]

    def result(rows, cols):
        return pl.BlockSpec((rows // steps, cols), lambda i, me: (i, 0))

    def body(me, output, dx, *refs):
        terms, results = refs[:15], refs[15:]
        results[0][...] = output[...]
        results[1][...] = dx[...]
        sums = [sum(ref[...].astype(F32) for ref in terms[3 * i : 3 * i + 3]) for i in range(5)]
        results[2][...] = sums[0][:, :q_cols]
        results[3][...] = sums[0][:, q_cols : q_cols + kv_cols]
        results[4][...] = sums[0][:, q_cols + kv_cols :]
        for i in range(1, 5):
            results[4 + i][...] = sums[i]

    wide = q_cols + 2 * kv_cols
    names = ("qkv", "out", "gate", "up", "down")
    sizes = [(block, q_cols), (block, kv_cols), (block, kv_cols), (q_cols, block), (block, hidden), (block, hidden), (hidden, block)]
    return pl.pallas_call(
        body,
        grid_spec=pltpu.PrefetchScalarGridSpec(
            num_scalar_prefetch=1,
            grid=(steps,),
            in_specs=[copied(), copied()] + by_row(wide) + by_col(q_cols) + by_row(hidden) + by_row(hidden) + by_col(hidden),
            out_specs=[copied(), copied()] + [result(*size) for size in sizes],
        ),
        out_shape=[shape((tokens, width), BF16)] * 2 + [shape(size, F32) for size in sizes],
    )(
        lax.axis_index("dp").astype(jnp.int32).reshape(1),
        outs["output"],
        outs["dx"],
        *[outs[key] for name in names for key in ("g_" + name, f"r_{name}_0", f"r_{name}_1")],
    )


def rotary_tables(length_total):
    half_width = HEAD_SIZE // 2
    frequency = (10000.0 ** (-(np.arange(half_width, dtype=np.float32) * 2.0) / HEAD_SIZE)).astype(np.float32)
    angles = np.arange(length_total, dtype=np.float32)[:, None] * frequency[None, :]
    return (jnp.asarray(np.cos(angles)), jnp.asarray(np.sin(angles)))


def rotate(values, cos_part, sin_part):
    first, second = jnp.split(values, 2, axis=-1)
    return jnp.concatenate(
        [first * cos_part - second * sin_part, first * sin_part + second * cos_part], axis=-1
    )


class Ring:
    def __init__(self, size):
        self.size = size
        self.half = size // 2
        self.order = [2 * p if p < self.half else 2 * (size - 1 - p) + 1 for p in range(size)]
        self.right = [(self.order[p], self.order[(p + 1) % size]) for p in range(size)]
        self.left = [(b, a) for a, b in self.right]

    def place(self):
        me = lax.axis_index("dp")
        odd = me % 2
        return (1 - odd) * (me // 2) + odd * (self.size - 1 - me // 2)

    def owners(self):
        return jnp.asarray(np.array(self.order, np.int32))[(self.place() + np.arange(self.size)) % self.size]

    def gather(self, shard):
        n, m = self.size, self.half
        pieces = [None] * n
        pieces[0] = shard
        from_left, from_right = shard, shard
        for hop in range(1, m):
            from_left = lax.ppermute(from_left, "dp", self.right)
            from_right = lax.ppermute(from_right, "dp", self.left)
            pieces[n - hop] = from_left
            pieces[hop] = from_right
        rows = shard.shape[0] // 2
        top = lax.ppermute(from_left[:rows], "dp", self.right)
        low = lax.ppermute(from_right[rows:], "dp", self.left)
        pieces[m] = jnp.concatenate([top, low], axis=0)
        return pieces

    def scatter(self, parts):
        n, m = self.size, self.half
        rows = parts[0].shape[0] // 2
        kind = BF16
        up = lax.ppermute(parts[m][:rows].astype(kind), "dp", self.right)
        down = lax.ppermute(parts[m][rows:].astype(kind), "dp", self.left)
        for hop in range(m - 1, 0, -1):
            mine_up, mine_down = parts[hop], parts[n - hop]
            if hop == m - 1:
                mine_up = jnp.concatenate([mine_up[:rows] + up.astype(F32), mine_up[rows:]], axis=0)
                mine_down = jnp.concatenate([mine_down[:rows], mine_down[rows:] + down.astype(F32)], axis=0)
            else:
                mine_up = mine_up + up.astype(F32)
                mine_down = mine_down + down.astype(F32)
            up = lax.ppermute(mine_up.astype(kind), "dp", self.right)
            down = lax.ppermute(mine_down.astype(kind), "dp", self.left)
        if m == 1:
            return jnp.concatenate([parts[0][:rows] + up.astype(F32), parts[0][rows:] + down.astype(F32)], axis=0)
        return parts[0] + up.astype(F32) + down.astype(F32)


    def small_scatter(self, sums):
        up = sums[:, self.half]
        for hop in range(self.half - 1, -1, -1):
            up = lax.ppermute(up, "dp", self.right)
            up = up + sums[:, hop]
        if self.size > 2:
            down = sums[:, self.half + 1]
            for hop in range(self.half - 2, -1, -1):
                down = lax.ppermute(down, "dp", self.left)
                if hop:
                    down = down + sums[:, self.size - hop]
            up = up + down
        return up


CORE_PAIRS = [(0, 1), (1, 0), (2, 3), (3, 2)]
CHIP_PAIRS = [(0, 2), (2, 0), (1, 3), (3, 1)]


def swap_core(value):
    return lax.ppermute(value, "tensor", CORE_PAIRS)


def swap_chip(value):
    return lax.ppermute(value, "tensor", CHIP_PAIRS)


def tensor_sum(part):
    near = part[0] + swap_core(part[1].astype(BF16)).astype(F32)
    near = near.astype(BF16)
    return near.astype(F32) + swap_chip(near).astype(F32)


def ring_local(ring, inputs, attention_gain, query_weight, key_matrix, value_matrix, out_weight, feedforward_gain,
          gate_weight, up_weight, down_weight, cotangent, layer_keep, prefix_length):
    n = ring.size
    seqs, length, width = inputs.shape
    block = width // n
    q_cols, kv_cols = query_weight.shape[1], key_matrix.shape[1]
    heads = q_cols // HEAD_SIZE
    kv_heads = kv_cols // HEAD_SIZE
    repeat = heads // kv_heads
    scale = 1.0 / math.sqrt(HEAD_SIZE)
    core = lax.axis_index("tensor") % 2
    owners = ring.owners()

    def arrange(array):
        array = jnp.where(core == 0, array, array[::-1])
        return jnp.concatenate(
            [lax.dynamic_slice_in_dim(array, owners[j] * block, block, axis=2) for j in range(n)], axis=2
        )

    def restore(own, other):
        array = jnp.stack([jnp.where(core == 0, own, other), jnp.where(core == 0, other, own)])
        places = jnp.asarray(np.argsort(np.array(ring.order)).astype(np.int32))
        where = (places - ring.place()) % n
        return jnp.concatenate(
            [lax.dynamic_slice_in_dim(array, where[j] * block, block, axis=2) for j in range(n)], axis=2
        )

    gains = jnp.concatenate([attention_gain, feedforward_gain])
    fill = jnp.zeros((8, q_cols + 2 * kv_cols), BF16)
    fill = lax.dynamic_update_slice(fill, gains[None, :], (0, 0))
    first = jnp.concatenate(
        [jnp.concatenate([query_weight, key_matrix, value_matrix], axis=1), fill], axis=0
    )
    first_pieces = ring.gather(first)
    qkv_w = jnp.concatenate([p[:block] for p in first_pieces], axis=0)
    gain_a = jnp.concatenate([p[block, :block] for p in first_pieces]).astype(F32)
    gain_f = jnp.concatenate([p[block, block : 2 * block] for p in first_pieces]).astype(F32)
    out_w = jnp.concatenate(ring.gather(out_weight), axis=1)
    gate_w = jnp.concatenate(ring.gather(gate_weight), axis=0)
    up_w = jnp.concatenate(ring.gather(up_weight), axis=0)
    down_w = jnp.concatenate(ring.gather(down_weight), axis=1)

    keep = layer_keep.astype(F32)
    keep = jnp.where(core == 0, keep, keep[::-1])
    prefix = jnp.where(core == 0, prefix_length, prefix_length[::-1])
    x = arrange(inputs)
    dy = arrange(cotangent)

    cos_part, sin_part = rotary_tables(length)
    cos_part, sin_part = cos_part[None, :, None, :], sin_part[None, :, None, :]
    position = jnp.arange(length, dtype=jnp.int32)

    rows = x.reshape(seqs * length, width).astype(F32)
    r1 = lax.rsqrt(jnp.mean(rows * rows, axis=-1, keepdims=True) + EPSILON)
    n1 = (rows * r1 * gain_a).astype(BF16)
    qkv = dot(n1, qkv_w)
    q = rotate(qkv[:, :q_cols].reshape(seqs, length, heads, HEAD_SIZE), cos_part, sin_part).astype(BF16)
    k = rotate(qkv[:, q_cols : q_cols + kv_cols].reshape(seqs, length, kv_heads, HEAD_SIZE), cos_part, sin_part).astype(BF16)
    v = qkv[:, q_cols + kv_cols :].astype(BF16).reshape(seqs, length, kv_heads, HEAD_SIZE)
    q = q.reshape(seqs, length, kv_heads, repeat, HEAD_SIZE)
    scores = jnp.einsum("bqgrd,bkgd->bgrqk", q, k, preferred_element_type=F32) * scale
    allowed = (position[None, None, :] <= position[None, :, None]) | (position[None, None, :] < prefix[:, None, None])
    scores = jnp.where(allowed[:, None, None], scores, NEGATIVE)
    exps = jnp.exp(scores - jnp.max(scores, axis=-1, keepdims=True))
    probs = exps / jnp.sum(exps, axis=-1, keepdims=True)
    probs_low = probs.astype(BF16)
    mixed = jnp.einsum("bgrqk,bkgd->bqgrd", probs_low, v, preferred_element_type=F32)
    mixed = mixed.reshape(seqs * length, q_cols).astype(BF16)
    a_own = tensor_sum(dot(mixed, out_w).reshape(seqs, length, width))
    x_own = x[0].astype(F32)
    hid = x_own + keep[0] * a_own
    r2 = lax.rsqrt(jnp.mean(hid * hid, axis=-1, keepdims=True) + EPSILON)
    n2_own = (hid * r2 * gain_f).astype(BF16)
    n2 = jnp.concatenate([n2_own, swap_core(n2_own)], axis=0)

    g = dot(n2, gate_w)
    u = dot(n2, up_w)
    sig = jax.nn.sigmoid(g)
    swish = g * sig
    m = (swish * u).astype(BF16)
    f_own = tensor_sum(dot(m, down_w).reshape(seqs, length, width))
    out_own = (hid + keep[0] * f_own).astype(BF16)
    output = restore(out_own, swap_core(out_own))

    df = (keep[:, None, None] * dy.astype(F32)).astype(BF16).reshape(seqs * length, width)
    grad_down = dot_ta(m, df)
    dm = dot_tb(df, down_w)
    dg = (dm * u * sig * (1.0 + g * (1.0 - sig))).astype(BF16)
    du = (dm * swish).astype(BF16)
    grad_down = ring.scatter([grad_down[:, j * block : (j + 1) * block] for j in range(n)])
    grad_gate = dot_ta(n2, dg)
    grad_gate = ring.scatter([grad_gate[j * block : (j + 1) * block] for j in range(n)])
    grad_up = dot_ta(n2, du)
    grad_up = ring.scatter([grad_up[j * block : (j + 1) * block] for j in range(n)])
    dn2 = tensor_sum((dot_tb(dg, gate_w) + dot_tb(du, up_w)).reshape(seqs, length, width))
    gain_f_sum = jnp.sum(dn2 * hid * r2, axis=0)
    scaled = dn2 * gain_f
    dh = dy[0].astype(F32) + r2 * scaled - hid * (r2 * r2 * r2) * jnp.mean(scaled * hid, axis=-1, keepdims=True)
    da_own = (keep[0] * dh).astype(BF16)
    da = jnp.concatenate([da_own, swap_core(da_own)], axis=0)

    grad_out = dot_ta(mixed, da)
    grad_out = ring.scatter([grad_out[:, j * block : (j + 1) * block] for j in range(n)])
    dmixed = dot_tb(da, out_w).astype(BF16).reshape(seqs, length, kv_heads, repeat, HEAD_SIZE)
    dprobs = jnp.einsum("bqgrd,bkgd->bgrqk", dmixed, v, preferred_element_type=F32)
    dv = jnp.einsum("bgrqk,bqgrd->bkgd", probs_low, dmixed, preferred_element_type=F32).astype(BF16)
    inner = jnp.sum(probs * dprobs, axis=-1, keepdims=True)
    dscores = (probs * (dprobs - inner)).astype(BF16)
    dq = jnp.einsum("bgrqk,bkgd->bqgrd", dscores, k, preferred_element_type=F32) * scale
    dk = jnp.einsum("bgrqk,bqgrd->bkgd", dscores, q, preferred_element_type=F32) * scale
    dq = rotate(dq.reshape(seqs, length, heads, HEAD_SIZE), cos_part, -sin_part).astype(BF16)
    dk = rotate(dk, cos_part, -sin_part).astype(BF16)
    dqkv = jnp.concatenate(
        [d.reshape(seqs * length, -1) for d in (dq, dk, dv)], axis=1
    )
    grad_qkv = dot_ta(n1, dqkv)
    grad_qkv = ring.scatter([grad_qkv[j * block : (j + 1) * block] for j in range(n)])
    dn1 = tensor_sum(dot_tb(dqkv, qkv_w).reshape(seqs, length, width))
    r1_own = r1[:length]
    gain_a_sum = jnp.sum(dn1 * x_own * r1_own, axis=0)
    scaled = dn1 * gain_a
    dx = dh + r1_own * scaled - x_own * (r1_own * r1_own * r1_own) * jnp.mean(scaled * x_own, axis=-1, keepdims=True)
    dx = dx.astype(BF16)
    input_grad = restore(dx, swap_core(dx))

    sums = jnp.stack([gain_a_sum, gain_f_sum]).reshape(2, n, block)
    sums = sums + swap_core(sums)
    gain_grads = ring.small_scatter(sums)
    return (
        output,
        input_grad,
        gain_grads[0],
        grad_qkv[:, :q_cols],
        grad_qkv[:, q_cols : q_cols + kv_cols],
        grad_qkv[:, q_cols + kv_cols :],
        grad_out,
        gain_grads[1],
        grad_gate,
        grad_up,
        grad_down,
    )


def local(ring, inputs, attention_gain, query_weight, key_matrix, value_matrix, out_weight, feedforward_gain,
          gate_weight, up_weight, down_weight, cotangent, layer_keep, prefix_length):
    n = ring.size
    seqs, length, width = inputs.shape
    tokens = seqs * length
    block = width // n
    q_cols, kv_cols = query_weight.shape[1], key_matrix.shape[1]
    cos_part, sin_part = rotary_tables(length)
    cos = jnp.concatenate([cos_part, cos_part], axis=1)
    sin = jnp.concatenate([-sin_part, sin_part], axis=1)
    keep = layer_keep.astype(F32)
    gains = jnp.concatenate([attention_gain[None], feedforward_gain[None], jnp.zeros((14, block), BF16)], axis=0)
    x = inputs.reshape(tokens, width)
    dy = cotangent.reshape(tokens, width)
    names = ("gains", "wq", "wk", "wv", "wo", "wg", "wu", "wd", "n1", "q", "k", "v", "ob", "hid", "n2", "m", "fa", "fb", "g_down")
    values = dict(
        zip(
            names,
            forward(
                n, x, dy, gains, query_weight, key_matrix, value_matrix, out_weight, gate_weight, up_weight, down_weight,
                cos, sin, keep, prefix_length, length,
            ),
        )
    )
    values |= {"x": x, "dy": dy, "cos": cos, "sin": sin, "keep": keep, "prefix": prefix_length}
    outs = backward(n, length, values)
    gain_sums = jnp.sum(outs["gain_slots"], axis=0)[:2]
    gain_sums = gain_sums + swap_core(gain_sums)
    output, dx, g_query, g_key, g_value, g_out, g_gate, g_up, g_down = finish(n, outs, query_weight.shape[1], key_matrix.shape[1])
    return (
        output.reshape(inputs.shape),
        dx.reshape(inputs.shape),
        gain_sums[0],
        g_query,
        g_key,
        g_value,
        g_out,
        gain_sums[1],
        g_gate,
        g_up,
        g_down,
    )


def solution(mesh):
    ring = Ring(mesh.shape["dp"])
    if mesh.shape["tensor"] != 4:
        raise ValueError("tensor axis")
    row, col = P("dp", "tensor"), P("tensor", "dp")
    data = P("dp", None, None)

    def layer(*args):
        block = args[0].shape[2] // ring.size
        return (local if block % 256 == 0 else ring_local)(ring, *args)

    return jax.shard_map(
        layer,
        mesh=mesh,
        in_specs=(data, P("dp"), row, row, row, col, P("dp"), row, row, col, data, P("dp"), P("dp")),
        out_specs=(data, data, P("dp"), row, row, row, col, P("dp"), row, row, col),
        check_vma=False,
    )
```

```python
import functools
import math

import jax
import jax.numpy as jnp
import numpy as np
from jax import lax
from jax.experimental import pallas as pl
from jax.experimental.pallas import tpu as pltpu
from jax.sharding import PartitionSpec as P

HEAD_SIZE = 128
EPSILON = 1e-05
NEGATIVE = -1e30
BF16 = jnp.bfloat16
F32 = jnp.float32
MESH = pl.DeviceIdType.MESH
HBM = pl.BlockSpec(memory_space=pltpu.HBM)
SMEM = pl.BlockSpec(memory_space=pltpu.SMEM)
ROWS = 256


def dot(a, b):
    return jnp.dot(a, b, preferred_element_type=F32)


def dot_ta(a, b):
    return lax.dot_general(a, b, (((0,), (0,)), ((), ())), preferred_element_type=F32)


def dot_tb(a, b):
    return lax.dot_general(a, b, (((1,), (1,)), ((), ())), preferred_element_type=F32)


def spec(rows, cols):
    return pl.BlockSpec((rows, cols), lambda i: (i, 0))


def fixed(*shape):
    return pl.BlockSpec(shape, lambda i: (0,) * len(shape), pipeline_mode=pl.Buffered(1))


def tiles(total, step=256):
    return [(at, min(step, total - at)) for at in range(0, total, step)]


def gain_row(gains_ref, which):
    n = gains_ref.shape[0]
    return jnp.concatenate([gains_ref[j, which : which + 1, :] for j in range(n)], axis=1).astype(F32)


def turn(values, cos, sin):
    return values * cos + pltpu.roll(values, HEAD_SIZE // 2, axis=1) * sin


class Place:
    def __init__(self, n):
        self.n = n
        self.me = lax.axis_index("dp")
        odd = self.me % 2
        self.p = (1 - odd) * (self.me // 2) + odd * (n - 1 - self.me // 2)
        tensor = lax.axis_index("tensor")
        self.core = tensor % 2
        self.core_peer = tensor + 1 - 2 * self.core
        self.chip_peer = (tensor + 2) % 4
        self.right = self.at(1)
        self.left = self.at(-1)

    def at(self, j):
        p = (self.p + j + 2 * self.n) % self.n
        low = p // (self.n // 2)
        return (1 - low) * 2 * p + low * (2 * (self.n - 1 - p) + 1)

    def greet(self):
        barrier = pltpu.get_barrier_semaphore()
        for peer in (self.left, self.right):
            pl.semaphore_signal(barrier, inc=1, device_id={"dp": peer}, device_id_type=MESH)
        for peer in (self.core_peer, self.chip_peer):
            pl.semaphore_signal(barrier, inc=1, device_id={"tensor": peer}, device_id_type=MESH)
        pl.semaphore_wait(barrier, 4)


class Gather:
    def __init__(self, place, shard, whole, where, local_sem, send_sems, recv_sems):
        self.place, self.shard, self.whole, self.where = place, shard, whole, where
        self.send_sems, self.recv_sems = send_sems, recv_sems
        self.hops = place.n // 2
        self.local = pltpu.make_async_copy(shard, where(whole, place.me, None), local_sem)

    def copy(self, way, hop):
        place = self.place
        sign = 1 - 2 * way
        owner = place.at(-sign * (hop - 1))
        half = way if hop == self.hops else None
        target = self.where(self.whole, owner, half)
        if hop > 1:
            source = target
        elif half is None:
            source = self.shard
        else:
            rows = self.shard.shape[0] // 2
            source = self.shard.at[pl.ds(half * rows, rows)]
        return pltpu.make_async_remote_copy(
            src_ref=source,
            dst_ref=target,
            send_sem=self.send_sems.at[way, hop - 1],
            recv_sem=self.recv_sems.at[way, hop - 1],
            device_id={"dp": place.right if way == 0 else place.left},
            device_id_type=MESH,
        )

    def step(self, hop):
        for way in range(2):
            if hop > 1:
                self.copy(way, hop - 1).wait_recv()
            self.copy(way, hop).start()

    def arrived(self):
        self.local.wait()
        for way in range(2):
            self.copy(way, self.hops).wait_recv()

    def drain(self):
        for way in range(2):
            for hop in range(1, self.hops + 1):
                self.copy(way, hop).wait_send()


def by_rows(rows):
    def where(whole, owner, half):
        if half is None:
            return whole.at[pl.ds(pl.multiple_of(owner * rows, rows), rows)]
        return whole.at[pl.ds(pl.multiple_of(owner * rows + half * (rows // 2), rows // 2), rows // 2)]

    return where


def by_cols(rows, cols):
    def where(whole, owner, half):
        at = pl.ds(pl.multiple_of(owner * cols, cols), cols)
        if half is None:
            return whole.at[:, at]
        return whole.at[pl.ds(half * (rows // 2), rows // 2), at]

    return where


def by_slot(whole, owner, half):
    if half is None:
        return whole.at[owner]
    rows = whole.shape[1] // 2
    return whole.at[owner, pl.ds(half * rows, rows)]


class Swap:
    def __init__(self, source, target, peer, send_sem, recv_sem):
        self.copy = pltpu.make_async_remote_copy(
            src_ref=source, dst_ref=target, send_sem=send_sem, recv_sem=recv_sem,
            device_id={"tensor": peer}, device_id_type=MESH,
        )
        self.copy.start()


def with_jobs(jobs, body):
    def both(*refs):
        for step, job in jobs:
            pl.when(pl.program_id(0) == step)(job)
        body(*refs)

    return both


class Exchange:
    def __init__(self, place, other, peer, near, far, sems):
        self.place, self.other, self.peer, self.near, self.far, self.sems = place, other, peer, near, far, sems
        self.per, self.rows = other.shape[0], other.shape[1]

    def core(self, i):
        return pltpu.make_async_remote_copy(
            src_ref=self.other.at[i], dst_ref=self.peer.at[i], send_sem=self.sems.at[0, i], recv_sem=self.sems.at[1, i],
            device_id={"tensor": self.place.core_peer}, device_id_type=MESH,
        )

    def chip(self, i):
        return pltpu.make_async_remote_copy(
            src_ref=self.near.at[i], dst_ref=self.far.at[i], send_sem=self.sems.at[2, i], recv_sem=self.sems.at[3, i],
            device_id={"tensor": self.place.chip_peer}, device_id_type=MESH,
        )

    def run(self, term, width, step, row_cols, row_args, fixed_args, jobs=()):
        per, core = self.per, self.place.core

        def body(*refs):
            s = pl.program_id(0)
            for i in range(per):
                if i:
                    @pl.when(s == i)
                    def _():
                        self.core(i - 1).start()

                @pl.when(s == per + i)
                def _():
                    if i == 0:
                        self.core(per - 1).start()
                    else:
                        self.chip(i - 1).start()
                    self.core(i).wait_recv()

            @pl.when(s < per)
            def _():
                for at, size in tiles(width, step):
                    cols = slice(at, at + size)
                    self.other[s, :, cols] = term(refs, cols).astype(BF16)

            @pl.when(s >= per)
            def _():
                for at, size in tiles(width, step):
                    cols = slice(at, at + size)
                    self.near[s - per, :, cols] = (term(refs, cols) + self.peer[s - per, :, cols].astype(F32)).astype(BF16)

        def block(s):
            return ((1 - core) + (s // per) * (2 * core - 1)) * per + s % per

        pltpu.emit_pipeline(
            with_jobs(jobs, body),
            grid=(2 * per,),
            in_specs=[pl.BlockSpec((self.rows, cols), lambda s: (block(s), 0)) for cols in row_cols]
            + [fixed(*w.shape) for w in fixed_args],
        )(*row_args, *fixed_args)
        self.chip(per - 1).start()
        for i in range(per):
            self.core(i).wait_send()

    def arrivals(self):
        return [(i * (self.rows // BLOCK), self.chip(i).wait_recv) for i in range(self.per)]

    def drain(self):
        for i in range(self.per):
            self.chip(i).wait_send()

    def total(self, at, rows):
        i, part = at // self.rows, pl.ds(pl.multiple_of(at % self.rows, rows), rows)
        return self.near[i, part, :].astype(F32) + self.far[i, part, :].astype(F32)


CHUNK = 16
BLOCK = 128


def by_chunks(step, body):
    @pl.loop(0, BLOCK, step=CHUNK)
    def _(at):
        at = pl.multiple_of(at, CHUNK)
        body(pl.ds(at, CHUNK), step * BLOCK + at)


def forward_kernel(
    n, length, x_hbm, dy_hbm, gains_in, wq_in, wk_in, wv_in, wo_in, wg_in, wu_in, wd_in, cos_hbm, sin_hbm, keep_ref, prefix_ref,
    gains_w, wq, wk, wv, wo, wg, wu, wd, n1_hbm, q_hbm, k_hbm, v_hbm, ob_hbm, hid_hbm, n2_hbm, m_hbm, fa_hbm, fb_hbm, gd_hbm,
    other, peer, near, far, local_sems, send_sems, recv_sems, swap_sems, share_sems,
):
    place = Place(n)
    core = place.core
    place.greet()
    tokens, width = x_hbm.shape
    scale = 1.0 / math.sqrt(HEAD_SIZE)
    half = wd_in.shape[0] // 2
    upper, lower = pl.ds(0, half), pl.ds(half, half)
    arrays = {
        "n": (gains_in, gains_w, by_slot),
        "q": (wq_in, wq, by_rows(wq_in.shape[0])),
        "k": (wk_in, wk, by_rows(wk_in.shape[0])),
        "v": (wv_in, wv, by_rows(wv_in.shape[0])),
        "o": (wo_in, wo, by_cols(*wo_in.shape)),
        "g": (wg_in, wg, by_rows(wg_in.shape[0])),
        "u": (wu_in, wu, by_rows(wu_in.shape[0])),
        "a": (wd_in.at[upper], wd.at[upper], by_cols(half, wd_in.shape[1])),
        "b": (wd_in.at[lower], wd.at[lower], by_cols(half, wd_in.shape[1])),
    }
    rings = {
        name: Gather(place, shard, whole, where, local_sems.at[i], send_sems.at[i], recv_sems.at[i])
        for i, (name, (shard, whole, where)) in enumerate(arrays.items())
    }
    hops = n // 2
    done = {name: 0 for name in rings}

    def go(names):
        for name in names:
            if done[name] < hops:
                done[name] += 1
                rings[name].step(done[name])

    own_rows = pl.ds(pl.multiple_of(core * length, length), length)
    other_rows = pl.ds(pl.multiple_of((1 - core) * length, length), length)

    go("nqkv")
    for name in "nqkvogu":
        rings[name].local.start()
    go("nqkvo")
    go("nqkvo")
    go("nqkvog")
    for name in "nqkv":
        go(name * hops)
        rings[name].arrived()

    def project(x_ref, gains_ref, wq_ref, wk_ref, wv_ref, cos_ref, sin_ref, n1_ref, q_ref, k_ref, v_ref):
        gain = gain_row(gains_ref, 0)

        @pl.loop(0, ROWS, step=32)
        def _(at):
            part = pl.ds(pl.multiple_of(at, 32), 32)
            xf = x_ref[part, :].astype(F32)
            r1 = lax.rsqrt(jnp.mean(xf * xf, axis=-1, keepdims=True) + EPSILON)
            n1_ref[part, :] = (xf * r1 * gain).astype(BF16)

        rows = n1_ref[...]
        cos, sin = cos_ref[...], sin_ref[...]
        for w_ref, o_ref in ((wq_ref, q_ref), (wk_ref, k_ref)):
            for at in range(0, w_ref.shape[1], HEAD_SIZE):
                head = slice(at, at + HEAD_SIZE)
                o_ref[:, head] = turn(dot(rows, w_ref[:, head]), cos, sin).astype(BF16)
        v_ref[...] = dot(rows, wv_ref[...]).astype(BF16)

    q_cols, kv_cols = wq.shape[1], wk.shape[1]
    per = length // ROWS
    turns = pl.BlockSpec((ROWS, HEAD_SIZE), lambda i: (i % per, 0))
    pltpu.emit_pipeline(
        project,
        grid=(tokens // ROWS,),
        in_specs=[spec(ROWS, width), fixed(*gains_w.shape), fixed(*wq.shape), fixed(*wk.shape), fixed(*wv.shape), turns, turns],
        out_specs=[spec(ROWS, width), spec(ROWS, q_cols), spec(ROWS, kv_cols), spec(ROWS, kv_cols)],
    )(x_hbm, gains_w, wq, wk, wv, cos_hbm, sin_hbm, n1_hbm, q_hbm, k_hbm, v_hbm)
    go("ogu")

    repeat = q_cols // kv_cols

    def attend(which, q_ref, k_ref, v_ref, o_ref):
        prefix = prefix_ref[which]
        keys, values = k_ref[...], v_ref[...]

        @pl.loop(0, length, step=128)
        def _(at):
            part = pl.ds(pl.multiple_of(at, 128), 128)
            s = dot_tb(q_ref[part, :], keys) * scale
            row = lax.broadcasted_iota(jnp.int32, s.shape, 0) + at
            col = lax.broadcasted_iota(jnp.int32, s.shape, 1)
            s = jnp.where((col <= row) | (col < prefix), s, NEGATIVE)
            e = jnp.exp(s - jnp.max(s, axis=-1, keepdims=True))
            p = e / jnp.sum(e, axis=-1, keepdims=True)
            o_ref[part, :] = dot(p.astype(BF16), values).astype(BF16)

    for which in range(2):
        seq = pl.ds(which * length, length)
        pltpu.emit_pipeline(
            functools.partial(attend, which),
            grid=(q_cols // HEAD_SIZE,),
            in_specs=[
                pl.BlockSpec((length, HEAD_SIZE), lambda h: (0, h)),
                pl.BlockSpec((length, HEAD_SIZE), lambda h: (0, h // repeat)),
                pl.BlockSpec((length, HEAD_SIZE), lambda h: (0, h // repeat)),
            ],
            out_specs=[pl.BlockSpec((length, HEAD_SIZE), lambda h: (0, h))],
        )(q_hbm.at[seq], k_hbm.at[seq], v_hbm.at[seq], ob_hbm.at[seq])

    go("o" * hops)
    rings["o"].arrived()
    go("g")
    mixed = Exchange(place, other, peer, near, far, swap_sems)
    mixed.run(lambda refs, cols: dot(refs[0][...], refs[1][:, cols]), width, 512, [q_cols], [ob_hbm], [wo])
    for name in "ab":
        rings[name].local.start()
    go("u")
    go("g")
    go("u")

    def residual(x_ref, gains_ref, hid_ref, n2_ref):
        gain = gain_row(gains_ref, 1)
        keep = keep_ref[core]

        def chunk(part, row):
            h = x_ref[part, :].astype(F32) + keep * mixed.total(row, CHUNK)
            hid_ref[part, :] = h
            r2 = lax.rsqrt(jnp.mean(h * h, axis=-1, keepdims=True) + EPSILON)
            n2_ref[part, :] = (h * r2 * gain).astype(BF16)

        by_chunks(pl.program_id(0), chunk)

    pltpu.emit_pipeline(
        with_jobs(mixed.arrivals(), residual),
        grid=(length // BLOCK,),
        in_specs=[spec(BLOCK, width), fixed(*gains_w.shape)],
        out_specs=[spec(BLOCK, width)] * 2,
    )(x_hbm.at[own_rows], gains_w, hid_hbm, n2_hbm.at[own_rows])
    share = Swap(n2_hbm.at[own_rows], n2_hbm.at[own_rows], place.core_peer, share_sems.at[0], share_sems.at[1])
    share.copy.wait_recv()
    go("g" * hops + "u" * hops + "ab")
    rings["g"].arrived()
    rings["u"].arrived()

    hidden = wg.shape[1]

    def during(at, name, hop):
        pl.when(pl.program_id(0) == at)(lambda: rings[name].step(hop))
        done[name] = hop

    def feed(n2_ref, wg_ref, wu_ref, m_ref, fa_ref, fb_ref):
        during(tokens // ROWS - 2, "a", 2)
        during(tokens // ROWS - 1, "b", 2)
        rows = n2_ref[...]
        for at, size in tiles(hidden):
            cols = slice(at, at + size)
            g = dot(rows, wg_ref[:, cols])
            u = dot(rows, wu_ref[:, cols])
            sig = 1.0 / (1.0 + jnp.exp(-g))
            swish = g * sig
            m_ref[:, cols] = (swish * u).astype(BF16)
            fa_ref[:, cols] = u * sig * (1.0 + g * (1.0 - sig))
            fb_ref[:, cols] = swish

    pltpu.emit_pipeline(
        feed,
        grid=(tokens // ROWS,),
        in_specs=[spec(ROWS, width), fixed(*wg.shape), fixed(*wu.shape)],
        out_specs=[spec(ROWS, hidden)] * 3,
    )(n2_hbm, wg, wu, m_hbm, fa_hbm, fb_hbm)

    def down_grad(m_ref, dy_ref, o_ref):
        during(1, "a", 3)
        during(5, "b", 3)
        total = None
        for which in range(2):
            seq = slice(which * length, (which + 1) * length)
            df = (dy_ref[seq, :].astype(F32) * keep_ref[which]).astype(BF16)
            term = dot_ta(m_ref[seq, :], df)
            total = term if total is None else total + term
        o_ref[...] = total.astype(BF16)

    cols = pl.BlockSpec((tokens, 256), lambda i: (0, i))
    pltpu.emit_pipeline(
        down_grad,
        grid=(width // 256,),
        in_specs=[fixed(tokens, hidden), cols],
        out_specs=[pl.BlockSpec((hidden, 256), lambda i: (0, i))],
    )(m_hbm, dy_hbm, gd_hbm)
    for _ in range(hops):
        go("ab")
    rings["a"].arrived()
    rings["b"].arrived()
    for ring in rings.values():
        ring.drain()
    mixed.drain()
    share.copy.wait_send()


def forward(n, x, dy, gains, wq, wk, wv, wo, wg, wu, wd, cos, sin, keep, prefix, length):
    tokens, width = x.shape
    shape = jax.ShapeDtypeStruct
    ff = wg.shape[1]
    outs = [
        shape((n,) + gains.shape, BF16),
        shape((width, wq.shape[1]), BF16),
        shape((width, wk.shape[1]), BF16),
        shape((width, wv.shape[1]), BF16),
        shape((wo.shape[0], width), BF16),
        shape((width, ff), BF16),
        shape((width, ff), BF16),
        shape((ff, width), BF16),
        shape((tokens, width), BF16),
        shape((tokens, wq.shape[1]), BF16),
        shape((tokens, wk.shape[1]), BF16),
        shape((tokens, wv.shape[1]), BF16),
        shape((tokens, wq.shape[1]), BF16),
        shape((length, width), F32),
        shape((tokens, width), BF16),
        shape((tokens, ff), BF16),
        shape((tokens, ff), F32),
        shape((tokens, ff), F32),
        shape((ff, width), BF16),
    ]
    blocks = pltpu.VMEM((length // ROWS, ROWS, width), BF16)
    return pl.pallas_call(
        functools.partial(forward_kernel, n, length),
        out_shape=outs,
        in_specs=[HBM] * 12 + [SMEM] * 2,
        out_specs=[HBM] * len(outs),
        scratch_shapes=[
            blocks,
            blocks,
            blocks,
            blocks,
            pltpu.SemaphoreType.DMA((9,)),
            pltpu.SemaphoreType.DMA((9, 2, n // 2)),
            pltpu.SemaphoreType.DMA((9, 2, n // 2)),
            pltpu.SemaphoreType.DMA((4, length // ROWS)),
            pltpu.SemaphoreType.DMA((2,)),
        ],
        compiler_params=pltpu.CompilerParams(collective_id=0, has_side_effects=True, vmem_limit_bytes=60 * 1024 * 1024),
    )(x, dy, gains, wq, wk, wv, wo, wg, wu, wd, cos, sin, keep, prefix)


class Buffers:
    def __init__(self, arrived, sums, sems):
        self.arrived, self.sums, self.sems = arrived, sums, sems
        self.users = []


class Scatter:
    def __init__(self, place, whole, where, piece, slots, buffers, send_sems, recv_sems, inner=None):
        self.place, self.whole, self.where, self.piece = place, whole, where, piece
        self.slots, self.buffers, self.inner = slots, buffers, inner
        self.send_sems, self.recv_sems = send_sems, recv_sems
        self.hops = place.n // 2
        self.turns = {}
        self.sent = set()

    def view(self, way, hop):
        sign = 1 - 2 * way
        owner = self.place.at(sign * (self.hops + 1 - hop))
        return self.where(self.whole, owner, way if hop == 1 else None)

    def slot(self, way, hop):
        if self.inner and hop < self.hops:
            first, rest = self.inner
            return first.at[way] if hop == 1 else rest.at[way, hop - 2]
        first, rest = self.slots[way]
        return first if hop == 1 else rest.at[hop - 2]

    def going(self, way, hop):
        rows, cols = self.piece
        buffers = self.buffers
        return buffers.sums.at[self.turns[hop] % buffers.sums.shape[0], way, pl.ds(0, rows), pl.ds(0, cols)]

    def come(self, way, hop):
        if self.inner:
            return self.slot(way, hop - 1)
        rows, cols = self.piece
        buffers = self.buffers
        rows = rows // 2 if hop == 2 else rows
        return buffers.arrived.at[self.turns[hop] % buffers.arrived.shape[0], way, pl.ds(0, rows), pl.ds(0, cols)]

    def remote(self, way, hop):
        return pltpu.make_async_remote_copy(
            src_ref=self.view(way, hop) if hop == 1 else self.going(way, hop),
            dst_ref=self.slot(way, hop),
            send_sem=self.send_sems.at[way, hop - 1],
            recv_sem=self.recv_sems.at[way, hop - 1],
            device_id={"dp": self.place.right if way == 0 else self.place.left},
            device_id_type=MESH,
        )

    def locals(self, hop):
        sems = self.buffers.sems
        turn = self.turns[hop] % sems.shape[0]
        for way in range(2):
            if not self.inner:
                yield pltpu.make_async_copy(self.slot(way, hop - 1), self.come(way, hop), sems.at[turn, way, 0])
            yield pltpu.make_async_copy(self.view(way, hop), self.going(way, hop), sems.at[turn, way, 1])

    def first(self):
        for way in range(2):
            self.remote(way, 1).start()

    def plan(self, hop):
        users = self.buffers.users
        self.turns[hop] = len(users)
        before = users[-self.buffers.sums.shape[0]] if len(users) >= self.buffers.sums.shape[0] else None
        users.append((self, hop))
        if before:
            before[0].sent.add(before[1])

        def fetch():
            for way in range(2):
                if not self.inner:
                    self.remote(way, hop - 1).wait_recv()
                if before:
                    before[0].remote(way, before[1]).wait_send()
            for copy in self.locals(hop):
                copy.start()

        def emit():
            for copy in self.locals(hop):
                copy.wait()
            rows = self.piece[0]
            for way in range(2):
                if self.inner:
                    self.remote(way, hop - 1).wait_recv()
                come, going = self.come(way, hop), self.going(way, hop)
                base = way * (rows // 2) if hop == 2 else 0

                @pl.loop(0, rows // 2 if hop == 2 else rows, step=CHUNK)
                def _(at):
                    at = pl.multiple_of(at, CHUNK)
                    part = pl.ds(pl.multiple_of(base + at, CHUNK), CHUNK)
                    going[part, :] = (going[part, :].astype(F32) + come[pl.ds(at, CHUNK), :].astype(F32)).astype(BF16)

                self.remote(way, hop).start()

        return fetch, emit

    def drain(self):
        for way in range(2):
            self.remote(way, self.hops).wait_recv()
            for hop in range(1, self.hops + 1):
                if hop not in self.sent:
                    self.remote(way, hop).wait_send()


def backward_kernel(n, length, names_in, names_out, *refs):
    ins = dict(zip(names_in, refs))
    outs = dict(zip(names_out, refs[len(names_in) :]))
    (gsum, gpieces, dh, other, peers, nears, fars, come_rows, sums_rows, come_cols, sums_cols, qkv_first, qkv_rest, add_sems, local_sems, send_sems, recv_sems, swap_sems, swap_send, swap_recv, gain_send, gain_recv) = refs[
        len(names_in) + len(names_out) :
    ]
    keep_ref, prefix_ref = ins["keep"], ins["prefix"]
    dy, x, gains_w = ins["dy"], ins["x"], ins["gains"]
    wq, wk, wv, wo, wg, wu, wd = (ins[name] for name in ("wq", "wk", "wv", "wo", "wg", "wu", "wd"))
    tokens, width = x.shape
    q_cols, kv_cols, hidden = wq.shape[1], wk.shape[1], wg.shape[1]
    block = width // n
    per = length // ROWS
    repeat = q_cols // kv_cols
    scale = 1.0 / math.sqrt(HEAD_SIZE)
    place = Place(n)
    core = place.core
    barrier = pltpu.get_barrier_semaphore()
    for j in range(1, n):
        pl.semaphore_signal(barrier, inc=1, device_id={"dp": place.at(j)}, device_id_type=MESH)
    for peer in (place.core_peer, place.chip_peer):
        pl.semaphore_signal(barrier, inc=1, device_id={"tensor": peer}, device_id_type=MESH)
    pl.semaphore_wait(barrier, n + 1)

    own_rows = pl.ds(pl.multiple_of(core * length, length), length)
    by_row = Buffers(come_rows, sums_rows, add_sems.at[0])
    by_col = Buffers(come_cols, sums_cols, add_sems.at[1])
    grads = {
        "down": (by_cols(hidden, block), (hidden, block), by_col),
        "gate": (by_rows(block), (block, hidden), by_row),
        "up": (by_rows(block), (block, hidden), by_row),
        "out": (by_cols(q_cols, block), (q_cols, block), by_col),
        "qkv": (by_rows(block), (block, q_cols + 2 * kv_cols), by_row),
    }
    rings = {
        name: Scatter(
            place,
            outs["g_" + name],
            where,
            piece,
            [(outs[f"r_{name}_{way}_first"], outs[f"r_{name}_{way}"]) for way in range(2)],
            buffers,
            send_sems.at[i],
            recv_sems.at[i],
            (qkv_first, qkv_rest) if name == "qkv" else None,
        )
        for i, (name, (where, piece, buffers)) in enumerate(grads.items())
    }
    swaps = []

    def swap(source, target, peer):
        i = len(swaps)
        swaps.append(Swap(source, target, peer, swap_send.at[i], swap_recv.at[i]))
        return swaps[-1].copy

    def act_grads(jobs):
        def body(dy_ref, wd_ref, fa_ref, fb_ref, dg_ref, du_ref):
            which = pl.program_id(0) // per
            df = (dy_ref[...].astype(F32) * keep_ref[which]).astype(BF16)
            for at, size in tiles(hidden):
                cols = slice(at, at + size)
                dm = dot_tb(df, wd_ref[cols, :])
                dg_ref[:, cols] = (dm * fa_ref[:, cols]).astype(BF16)
                du_ref[:, cols] = (dm * fb_ref[:, cols]).astype(BF16)

        pltpu.emit_pipeline(
            with_jobs(jobs, body),
            grid=(tokens // ROWS,),
            in_specs=[spec(ROWS, width), fixed(hidden, width), spec(ROWS, hidden), spec(ROWS, hidden)],
            out_specs=[spec(ROWS, hidden)] * 2,
        )(dy, wd, ins["fa"], ins["fb"], outs["dg"], outs["du"])

    def outer(left, right, target, jobs):
        def body(l_ref, r_ref, o_ref):
            o_ref[...] = dot_ta(l_ref[...], r_ref[...]).astype(BF16)

        cols = right.shape[1]
        pltpu.emit_pipeline(
            with_jobs(jobs, body),
            grid=(width // 256,),
            in_specs=[pl.BlockSpec((tokens, 256), lambda i: (0, i)), fixed(tokens, cols)],
            out_specs=[spec(256, cols)],
        )(left, right, target)

    def exchange(i):
        return Exchange(place, other, peers.at[i], nears.at[i], fars.at[i], swap_sems.at[i])

    in_n2, in_f, in_n1 = exchange(0), exchange(1), exchange(2)

    def back(jobs):
        in_n2.run(
            lambda refs, cols: dot_tb(refs[0][...], refs[2][cols, :]) + dot_tb(refs[1][...], refs[3][cols, :]),
            width, 256, [hidden, hidden], [outs["dg"], outs["du"]], [wg, wu], jobs,
        )

    def add_gain(which, terms):
        gsum[which] += sum(terms[i * 8 : (i + 1) * 8] for i in range(terms.shape[0] // 8))

    def norm_back(d, h, gain, which):
        r = lax.rsqrt(jnp.mean(h * h, axis=-1, keepdims=True) + EPSILON)
        add_gain(which, d * h * r)
        scaled = d * gain
        return r * scaled - h * (r * r * r) * jnp.mean(scaled * h, axis=-1, keepdims=True)

    def hid_grads():
        def body(hid_ref, dy_ref, gains_ref, da_ref):
            gain = gain_row(gains_ref, 1)
            keep = keep_ref[core]

            def chunk(part, row):
                d = in_n2.total(row, CHUNK)
                value = dy_ref[part, :].astype(F32) + norm_back(d, hid_ref[part, :], gain, 1)
                dh[pl.ds(pl.multiple_of(row, CHUNK), CHUNK), :] = value
                da_ref[part, :] = (keep * value).astype(BF16)

            by_chunks(pl.program_id(0), chunk)

        pltpu.emit_pipeline(
            with_jobs(in_n2.arrivals(), body),
            grid=(length // BLOCK,),
            in_specs=[spec(BLOCK, width)] * 2 + [fixed(*gains_w.shape)],
            out_specs=[spec(BLOCK, width)],
        )(ins["hid"], dy.at[own_rows], gains_w, outs["da"].at[own_rows])
        return swap(outs["da"].at[own_rows], outs["da"].at[own_rows], place.core_peer)

    def input_grads():
        def body(x_ref, gains_ref, dx_ref):
            gain = gain_row(gains_ref, 0)

            def chunk(part, row):
                d = in_n1.total(row, CHUNK)
                value = norm_back(d, x_ref[part, :].astype(F32), gain, 0)
                dx_ref[part, :] = (dh[pl.ds(pl.multiple_of(row, CHUNK), CHUNK), :] + value).astype(BF16)

            by_chunks(pl.program_id(0), chunk)

        pltpu.emit_pipeline(
            with_jobs(in_n1.arrivals(), body),
            grid=(length // BLOCK,),
            in_specs=[spec(BLOCK, width), fixed(*gains_w.shape)],
            out_specs=[spec(BLOCK, width)],
        )(x.at[own_rows], gains_w, outs["dx"].at[own_rows])
        return swap(outs["dx"].at[own_rows], outs["dx"].at[own_rows], place.core_peer)

    def results():
        def body(hid_ref, o_ref):
            keep = keep_ref[core]

            def chunk(part, row):
                o_ref[part, :] = (hid_ref[part, :] + keep * in_f.total(row, CHUNK)).astype(BF16)

            by_chunks(pl.program_id(0), chunk)

        pltpu.emit_pipeline(
            with_jobs(in_f.arrivals(), body),
            grid=(length // BLOCK,),
            in_specs=[spec(BLOCK, width)],
            out_specs=[spec(BLOCK, width)],
        )(ins["hid"], outs["output"].at[own_rows])
        return swap(outs["output"].at[own_rows], outs["output"].at[own_rows], place.core_peer)

    def forth(jobs):
        in_f.run(lambda refs, cols: dot(refs[0][...], refs[1][:, cols]), width, 512, [hidden], [ins["m"]], [wd], jobs)

    def out_grad(jobs):
        def body(ob_ref, da_ref, o_ref):
            o_ref[...] = dot_ta(ob_ref[...], da_ref[...]).astype(BF16)

        pltpu.emit_pipeline(
            with_jobs(jobs, body),
            grid=(width // 256,),
            in_specs=[fixed(tokens, q_cols), pl.BlockSpec((tokens, 256), lambda i: (0, i))],
            out_specs=[pl.BlockSpec((q_cols, 256), lambda i: (0, i))],
        )(ins["ob"], outs["da"], outs["g_out"])

    def mixed_grad():
        def body(da_ref, wo_ref, o_ref):
            o_ref[...] = dot_tb(da_ref[...], wo_ref[...]).astype(BF16)

        pltpu.emit_pipeline(
            body, grid=(tokens // ROWS,), in_specs=[spec(ROWS, width), fixed(q_cols, width)], out_specs=[spec(ROWS, q_cols)]
        )(outs["da"], wo, outs["dob"])

    def attend_back(which, jobs):
        seq = pl.ds(which * length, length)

        def heads(dk_sum, dv_sum):
            def body(q_ref, k_ref, v_ref, d_ref, cos_ref, sin_ref, dq_ref, dk_ref, dv_ref):
                head = pl.program_id(0) % repeat
                prefix = prefix_ref[which]
                keys, values = k_ref[...], v_ref[...]

                @pl.when(head == 0)
                def _():
                    dk_sum[...] = jnp.zeros_like(dk_sum)
                    dv_sum[...] = jnp.zeros_like(dv_sum)

                @pl.loop(0, length, step=128)
                def _(at):
                    part = pl.ds(pl.multiple_of(at, 128), 128)
                    queries, grads = q_ref[part, :], d_ref[part, :]
                    s = dot_tb(keys, queries) * scale
                    col = lax.broadcasted_iota(jnp.int32, s.shape, 0)
                    row = lax.broadcasted_iota(jnp.int32, s.shape, 1) + at
                    s = jnp.where((col <= row) | (col < prefix), s, NEGATIVE)
                    e = jnp.exp(s - jnp.max(s, axis=0, keepdims=True))
                    p = e / jnp.sum(e, axis=0, keepdims=True)
                    dp = dot_tb(values, grads)
                    inner = jnp.sum(p * dp, axis=0, keepdims=True)
                    dz = (p * (dp - inner)).astype(BF16)
                    dv_sum[...] += dot(p.astype(BF16), grads)
                    dk_sum[...] += dot(dz, queries)
                    dq = dot_ta(dz, keys) * scale
                    dq_ref[part, :] = turn(dq, cos_ref[part, :], -sin_ref[part, :]).astype(BF16)

                @pl.when(head == repeat - 1)
                def _():
                    dk_ref[...] = turn(dk_sum[...] * scale, cos_ref[...], -sin_ref[...]).astype(BF16)
                    dv_ref[...] = dv_sum[...].astype(BF16)

            one = pl.BlockSpec((length, HEAD_SIZE), lambda h: (0, h))
            shared = pl.BlockSpec((length, HEAD_SIZE), lambda h: (0, h // repeat))
            table = pl.BlockSpec((length, HEAD_SIZE), lambda h: (0, 0))
            dqkv = outs["dqkv"].at[seq]
            pltpu.emit_pipeline(
                with_jobs(jobs, body),
                grid=(q_cols // HEAD_SIZE,),
                in_specs=[one, shared, shared, one, table, table],
                out_specs=[one, shared, shared],
            )(
                ins["q"].at[seq],
                ins["k"].at[seq],
                ins["v"].at[seq],
                outs["dob"].at[seq],
                ins["cos"],
                ins["sin"],
                dqkv.at[:, pl.ds(0, q_cols)],
                dqkv.at[:, pl.ds(q_cols, kv_cols)],
                dqkv.at[:, pl.ds(q_cols + kv_cols, kv_cols)],
            )

        pl.run_scoped(heads, pltpu.VMEM((length, HEAD_SIZE), F32), pltpu.VMEM((length, HEAD_SIZE), F32))

    def back_qkv(jobs):
        def term(refs, cols):
            d_ref, wq_ref, wk_ref, wv_ref = refs
            dq, dk, dv = d_ref[:, :q_cols], d_ref[:, q_cols : q_cols + kv_cols], d_ref[:, q_cols + kv_cols :]
            return dot_tb(dq, wq_ref[cols, :]) + dot_tb(dk, wk_ref[cols, :]) + dot_tb(dv, wv_ref[cols, :])

        in_n1.run(term, width, 256, [q_cols + 2 * kv_cols], [outs["dqkv"]], [wq, wk, wv], jobs)

    def gain_grads():
        for which in range(2):
            row = jnp.sum(gsum[which], axis=0, keepdims=True)
            for j in range(n):
                gpieces[j, which : which + 1, :] = row[:, j * block : (j + 1) * block]
        copy = pltpu.make_async_copy(gpieces, outs["gain_terms"], local_sems.at[0])
        copy.start()
        copy.wait()
        mine = pltpu.make_async_copy(outs["gain_terms"].at[place.me], outs["gain_slots"].at[0], local_sems.at[1])
        mine.start()
        copies = []
        for j in range(1, n):
            copy = pltpu.make_async_remote_copy(
                src_ref=outs["gain_terms"].at[place.at(j)],
                dst_ref=outs["gain_slots"].at[j],
                send_sem=gain_send.at[j],
                recv_sem=gain_recv.at[j],
                device_id={"dp": place.at(j)},
                device_id_type=MESH,
            )
            copy.start()
            copies.append(copy)
        return mine, copies

    plans = {}
    for name, hop in (
        ("down", 2), ("down", 3), ("gate", 2), ("down", 4), ("gate", 3), ("up", 2), ("gate", 4), ("up", 3), ("out", 2),
        ("up", 4), ("out", 3), ("qkv", 2), ("qkv", 3), ("out", 4), ("qkv", 4),
    ):
        plans[name, hop] = rings[name].plan(hop)

    def fetch(name, hop):
        return plans[name, hop][0]

    def emit(name, hop):
        return plans[name, hop][1]

    rings["down"].first()
    gsum[...] = jnp.zeros_like(gsum)
    gpieces[...] = jnp.zeros_like(gpieces)
    act_grads([(2, fetch("down", 2)), (3, emit("down", 2))])
    outer(ins["n2"], outs["dg"], outs["g_gate"], [])
    rings["gate"].first()
    back([(0, fetch("down", 3)), (1, emit("down", 3)), (2, fetch("gate", 2)), (3, emit("gate", 2))])
    outer(ins["n2"], outs["du"], outs["g_up"], [(3, fetch("down", 4)), (5, emit("down", 4))])
    rings["up"].first()
    forth([])
    fetch("gate", 3)()
    emit("gate", 3)()
    share_da = hid_grads()
    fetch("up", 2)()
    emit("up", 2)()
    share_da.wait_recv()
    mixed_grad()
    out_grad([(4, fetch("gate", 4)), (6, emit("gate", 4))])
    rings["out"].first()
    attend_back(0, [(2, fetch("up", 3)), (3, emit("up", 3))])
    attend_back(1, [(3, fetch("out", 2))])
    emit("out", 2)()
    back_qkv([(3, fetch("up", 4))])
    outer(ins["n1"], outs["dqkv"], outs["g_qkv"], [(0, emit("up", 4)), (5, fetch("out", 3))])
    rings["qkv"].first()
    emit("out", 3)()
    fetch("qkv", 2)()
    share_out = results()
    emit("qkv", 2)()
    fetch("qkv", 3)()
    emit("qkv", 3)()
    fetch("out", 4)()
    emit("out", 4)()
    fetch("qkv", 4)()
    share_dx = input_grads()
    emit("qkv", 4)()
    mine, copies = gain_grads()
    share_out.wait_recv()
    share_dx.wait_recv()
    mine.wait()
    for copy in copies:
        copy.wait_recv()
    for ring in rings.values():
        ring.drain()
    for copy in copies:
        copy.wait_send()
    for item in swaps:
        item.copy.wait_send()
    for item in (in_n2, in_f, in_n1):
        item.drain()


def backward(n, length, values):
    shape = jax.ShapeDtypeStruct
    tokens, width = values["x"].shape
    q_cols, kv_cols, hidden = values["wq"].shape[1], values["wk"].shape[1], values["wg"].shape[1]
    block = width // n
    widest = max(hidden, q_cols + 2 * kv_cols)
    outs = {}
    sizes = {
        "down": ((hidden, width), (hidden, block)),
        "gate": ((width, hidden), (block, hidden)),
        "up": ((width, hidden), (block, hidden)),
        "out": ((q_cols, width), (q_cols, block)),
        "qkv": ((width, q_cols + 2 * kv_cols), (block, q_cols + 2 * kv_cols)),
    }
    for name, (whole, piece) in sizes.items():
        outs["g_" + name] = shape(whole, BF16)
        for way in range(2):
            outs[f"r_{name}_{way}_first"] = shape((piece[0] // 2, piece[1]), BF16)
            outs[f"r_{name}_{way}"] = shape((n // 2 - 1,) + piece, BF16)
    outs["dg"] = outs["du"] = shape((tokens, hidden), BF16)
    outs["da"] = outs["dx"] = outs["output"] = shape((tokens, width), BF16)
    outs["dob"] = shape((tokens, q_cols), BF16)
    outs["dqkv"] = shape((tokens, q_cols + 2 * kv_cols), BF16)
    outs["gain_terms"] = outs["gain_slots"] = shape((n, 8, block), F32)
    names_in, names_out = list(values), list(outs)
    results = pl.pallas_call(
        functools.partial(backward_kernel, n, length, names_in, names_out),
        out_shape=list(outs.values()),
        in_specs=[SMEM if name in ("keep", "prefix") else HBM for name in names_in],
        out_specs=[HBM] * len(outs),
        input_output_aliases={names_in.index("g_down"): names_out.index("g_down")},
        scratch_shapes=[
            pltpu.VMEM((2, 8, width), F32),
            pltpu.VMEM((n, 8, block), F32),
            pltpu.VMEM((length, width), F32),
            pltpu.VMEM((length // ROWS, ROWS, width), BF16),
            pltpu.VMEM((3, length // ROWS, ROWS, width), BF16),
            pltpu.VMEM((3, length // ROWS, ROWS, width), BF16),
            pltpu.VMEM((3, length // ROWS, ROWS, width), BF16),
            pltpu.VMEM((2, 2, block, widest), BF16),
            pltpu.VMEM((3, 2, block, widest), BF16),
            pltpu.VMEM((2, 2, widest, block), BF16),
            pltpu.VMEM((3, 2, widest, block), BF16),
            pltpu.VMEM((2, block // 2, q_cols + 2 * kv_cols), BF16),
            pltpu.VMEM((2, n // 2 - 2, block, q_cols + 2 * kv_cols), BF16),
            pltpu.SemaphoreType.DMA((2, 3, 2, 2)),
            pltpu.SemaphoreType.DMA((2,)),
            pltpu.SemaphoreType.DMA((5, 2, n // 2)),
            pltpu.SemaphoreType.DMA((5, 2, n // 2)),
            pltpu.SemaphoreType.DMA((3, 4, length // ROWS)),
            pltpu.SemaphoreType.DMA((3,)),
            pltpu.SemaphoreType.DMA((3,)),
            pltpu.SemaphoreType.DMA((n,)),
            pltpu.SemaphoreType.DMA((n,)),
        ],
        compiler_params=pltpu.CompilerParams(collective_id=1, has_side_effects=True, vmem_limit_bytes=60 * 1024 * 1024),
    )(*values.values())
    return dict(zip(names_out, results))


def finish(n, outs, q_cols, kv_cols):
    steps = 8
    shape = jax.ShapeDtypeStruct
    tokens, width = outs["output"].shape
    hidden = outs["g_gate"].shape[1]
    block = width // n
    last = n // 2 - 2

    def copied():
        return pl.BlockSpec((tokens // steps, width), lambda i, me: (i, 0))

    def by_row(cols):
        rows = block // steps
        slot = pl.BlockSpec((None, rows, cols), lambda i, me: (last, i, 0))
        return [pl.BlockSpec((rows, cols), lambda i, me: (me[0] * steps + i, 0)), slot, slot]

    def by_col(rows):
        rows = rows // steps
        slot = pl.BlockSpec((None, rows, block), lambda i, me: (last, i, 0))
        return [pl.BlockSpec((rows, block), lambda i, me: (i, me[0])), slot, slot]

    def result(rows, cols):
        return pl.BlockSpec((rows // steps, cols), lambda i, me: (i, 0))

    def body(me, output, dx, *refs):
        terms, results = refs[:15], refs[15:]
        results[0][...] = output[...]
        results[1][...] = dx[...]
        sums = [sum(ref[...].astype(F32) for ref in terms[3 * i : 3 * i + 3]) for i in range(5)]
        results[2][...] = sums[0][:, :q_cols]
        results[3][...] = sums[0][:, q_cols : q_cols + kv_cols]
        results[4][...] = sums[0][:, q_cols + kv_cols :]
        for i in range(1, 5):
            results[4 + i][...] = sums[i]

    wide = q_cols + 2 * kv_cols
    names = ("qkv", "out", "gate", "up", "down")
    sizes = [(block, q_cols), (block, kv_cols), (block, kv_cols), (q_cols, block), (block, hidden), (block, hidden), (hidden, block)]
    return pl.pallas_call(
        body,
        grid_spec=pltpu.PrefetchScalarGridSpec(
            num_scalar_prefetch=1,
            grid=(steps,),
            in_specs=[copied(), copied()] + by_row(wide) + by_col(q_cols) + by_row(hidden) + by_row(hidden) + by_col(hidden),
            out_specs=[copied(), copied()] + [result(*size) for size in sizes],
        ),
        out_shape=[shape((tokens, width), BF16)] * 2 + [shape(size, F32) for size in sizes],
    )(
        lax.axis_index("dp").astype(jnp.int32).reshape(1),
        outs["output"],
        outs["dx"],
        *[outs[key] for name in names for key in ("g_" + name, f"r_{name}_0", f"r_{name}_1")],
    )


def rotary_tables(length_total):
    half_width = HEAD_SIZE // 2
    frequency = (10000.0 ** (-(np.arange(half_width, dtype=np.float32) * 2.0) / HEAD_SIZE)).astype(np.float32)
    angles = np.arange(length_total, dtype=np.float32)[:, None] * frequency[None, :]
    return (jnp.asarray(np.cos(angles)), jnp.asarray(np.sin(angles)))


def rotate(values, cos_part, sin_part):
    first, second = jnp.split(values, 2, axis=-1)
    return jnp.concatenate(
        [first * cos_part - second * sin_part, first * sin_part + second * cos_part], axis=-1
    )


class Ring:
    def __init__(self, size):
        self.size = size
        self.half = size // 2
        self.order = [2 * p if p < self.half else 2 * (size - 1 - p) + 1 for p in range(size)]
        self.right = [(self.order[p], self.order[(p + 1) % size]) for p in range(size)]
        self.left = [(b, a) for a, b in self.right]

    def place(self):
        me = lax.axis_index("dp")
        odd = me % 2
        return (1 - odd) * (me // 2) + odd * (self.size - 1 - me // 2)

    def owners(self):
        return jnp.asarray(np.array(self.order, np.int32))[(self.place() + np.arange(self.size)) % self.size]

    def gather(self, shard):
        n, m = self.size, self.half
        pieces = [None] * n
        pieces[0] = shard
        from_left, from_right = shard, shard
        for hop in range(1, m):
            from_left = lax.ppermute(from_left, "dp", self.right)
            from_right = lax.ppermute(from_right, "dp", self.left)
            pieces[n - hop] = from_left
            pieces[hop] = from_right
        rows = shard.shape[0] // 2
        top = lax.ppermute(from_left[:rows], "dp", self.right)
        low = lax.ppermute(from_right[rows:], "dp", self.left)
        pieces[m] = jnp.concatenate([top, low], axis=0)
        return pieces

    def scatter(self, parts):
        n, m = self.size, self.half
        rows = parts[0].shape[0] // 2
        kind = BF16
        up = lax.ppermute(parts[m][:rows].astype(kind), "dp", self.right)
        down = lax.ppermute(parts[m][rows:].astype(kind), "dp", self.left)
        for hop in range(m - 1, 0, -1):
            mine_up, mine_down = parts[hop], parts[n - hop]
            if hop == m - 1:
                mine_up = jnp.concatenate([mine_up[:rows] + up.astype(F32), mine_up[rows:]], axis=0)
                mine_down = jnp.concatenate([mine_down[:rows], mine_down[rows:] + down.astype(F32)], axis=0)
            else:
                mine_up = mine_up + up.astype(F32)
                mine_down = mine_down + down.astype(F32)
            up = lax.ppermute(mine_up.astype(kind), "dp", self.right)
            down = lax.ppermute(mine_down.astype(kind), "dp", self.left)
        if m == 1:
            return jnp.concatenate([parts[0][:rows] + up.astype(F32), parts[0][rows:] + down.astype(F32)], axis=0)
        return parts[0] + up.astype(F32) + down.astype(F32)


    def small_scatter(self, sums):
        up = sums[:, self.half]
        for hop in range(self.half - 1, -1, -1):
            up = lax.ppermute(up, "dp", self.right)
            up = up + sums[:, hop]
        if self.size > 2:
            down = sums[:, self.half + 1]
            for hop in range(self.half - 2, -1, -1):
                down = lax.ppermute(down, "dp", self.left)
                if hop:
                    down = down + sums[:, self.size - hop]
            up = up + down
        return up


CORE_PAIRS = [(0, 1), (1, 0), (2, 3), (3, 2)]
CHIP_PAIRS = [(0, 2), (2, 0), (1, 3), (3, 1)]


def swap_core(value):
    return lax.ppermute(value, "tensor", CORE_PAIRS)


def swap_chip(value):
    return lax.ppermute(value, "tensor", CHIP_PAIRS)


def tensor_sum(part):
    near = part[0] + swap_core(part[1].astype(BF16)).astype(F32)
    near = near.astype(BF16)
    return near.astype(F32) + swap_chip(near).astype(F32)


def ring_local(ring, inputs, attention_gain, query_weight, key_matrix, value_matrix, out_weight, feedforward_gain,
          gate_weight, up_weight, down_weight, cotangent, layer_keep, prefix_length):
    n = ring.size
    seqs, length, width = inputs.shape
    block = width // n
    q_cols, kv_cols = query_weight.shape[1], key_matrix.shape[1]
    heads = q_cols // HEAD_SIZE
    kv_heads = kv_cols // HEAD_SIZE
    repeat = heads // kv_heads
    scale = 1.0 / math.sqrt(HEAD_SIZE)
    core = lax.axis_index("tensor") % 2
    owners = ring.owners()

    def arrange(array):
        array = jnp.where(core == 0, array, array[::-1])
        return jnp.concatenate(
            [lax.dynamic_slice_in_dim(array, owners[j] * block, block, axis=2) for j in range(n)], axis=2
        )

    def restore(own, other):
        array = jnp.stack([jnp.where(core == 0, own, other), jnp.where(core == 0, other, own)])
        places = jnp.asarray(np.argsort(np.array(ring.order)).astype(np.int32))
        where = (places - ring.place()) % n
        return jnp.concatenate(
            [lax.dynamic_slice_in_dim(array, where[j] * block, block, axis=2) for j in range(n)], axis=2
        )

    gains = jnp.concatenate([attention_gain, feedforward_gain])
    fill = jnp.zeros((8, q_cols + 2 * kv_cols), BF16)
    fill = lax.dynamic_update_slice(fill, gains[None, :], (0, 0))
    first = jnp.concatenate(
        [jnp.concatenate([query_weight, key_matrix, value_matrix], axis=1), fill], axis=0
    )
    first_pieces = ring.gather(first)
    qkv_w = jnp.concatenate([p[:block] for p in first_pieces], axis=0)
    gain_a = jnp.concatenate([p[block, :block] for p in first_pieces]).astype(F32)
    gain_f = jnp.concatenate([p[block, block : 2 * block] for p in first_pieces]).astype(F32)
    out_w = jnp.concatenate(ring.gather(out_weight), axis=1)
    gate_w = jnp.concatenate(ring.gather(gate_weight), axis=0)
    up_w = jnp.concatenate(ring.gather(up_weight), axis=0)
    down_w = jnp.concatenate(ring.gather(down_weight), axis=1)

    keep = layer_keep.astype(F32)
    keep = jnp.where(core == 0, keep, keep[::-1])
    prefix = jnp.where(core == 0, prefix_length, prefix_length[::-1])
    x = arrange(inputs)
    dy = arrange(cotangent)

    cos_part, sin_part = rotary_tables(length)
    cos_part, sin_part = cos_part[None, :, None, :], sin_part[None, :, None, :]
    position = jnp.arange(length, dtype=jnp.int32)

    rows = x.reshape(seqs * length, width).astype(F32)
    r1 = lax.rsqrt(jnp.mean(rows * rows, axis=-1, keepdims=True) + EPSILON)
    n1 = (rows * r1 * gain_a).astype(BF16)
    qkv = dot(n1, qkv_w)
    q = rotate(qkv[:, :q_cols].reshape(seqs, length, heads, HEAD_SIZE), cos_part, sin_part).astype(BF16)
    k = rotate(qkv[:, q_cols : q_cols + kv_cols].reshape(seqs, length, kv_heads, HEAD_SIZE), cos_part, sin_part).astype(BF16)
    v = qkv[:, q_cols + kv_cols :].astype(BF16).reshape(seqs, length, kv_heads, HEAD_SIZE)
    q = q.reshape(seqs, length, kv_heads, repeat, HEAD_SIZE)
    scores = jnp.einsum("bqgrd,bkgd->bgrqk", q, k, preferred_element_type=F32) * scale
    allowed = (position[None, None, :] <= position[None, :, None]) | (position[None, None, :] < prefix[:, None, None])
    scores = jnp.where(allowed[:, None, None], scores, NEGATIVE)
    exps = jnp.exp(scores - jnp.max(scores, axis=-1, keepdims=True))
    probs = exps / jnp.sum(exps, axis=-1, keepdims=True)
    probs_low = probs.astype(BF16)
    mixed = jnp.einsum("bgrqk,bkgd->bqgrd", probs_low, v, preferred_element_type=F32)
    mixed = mixed.reshape(seqs * length, q_cols).astype(BF16)
    a_own = tensor_sum(dot(mixed, out_w).reshape(seqs, length, width))
    x_own = x[0].astype(F32)
    hid = x_own + keep[0] * a_own
    r2 = lax.rsqrt(jnp.mean(hid * hid, axis=-1, keepdims=True) + EPSILON)
    n2_own = (hid * r2 * gain_f).astype(BF16)
    n2 = jnp.concatenate([n2_own, swap_core(n2_own)], axis=0)

    g = dot(n2, gate_w)
    u = dot(n2, up_w)
    sig = jax.nn.sigmoid(g)
    swish = g * sig
    m = (swish * u).astype(BF16)
    f_own = tensor_sum(dot(m, down_w).reshape(seqs, length, width))
    out_own = (hid + keep[0] * f_own).astype(BF16)
    output = restore(out_own, swap_core(out_own))

    df = (keep[:, None, None] * dy.astype(F32)).astype(BF16).reshape(seqs * length, width)
    grad_down = dot_ta(m, df)
    dm = dot_tb(df, down_w)
    dg = (dm * u * sig * (1.0 + g * (1.0 - sig))).astype(BF16)
    du = (dm * swish).astype(BF16)
    grad_down = ring.scatter([grad_down[:, j * block : (j + 1) * block] for j in range(n)])
    grad_gate = dot_ta(n2, dg)
    grad_gate = ring.scatter([grad_gate[j * block : (j + 1) * block] for j in range(n)])
    grad_up = dot_ta(n2, du)
    grad_up = ring.scatter([grad_up[j * block : (j + 1) * block] for j in range(n)])
    dn2 = tensor_sum((dot_tb(dg, gate_w) + dot_tb(du, up_w)).reshape(seqs, length, width))
    gain_f_sum = jnp.sum(dn2 * hid * r2, axis=0)
    scaled = dn2 * gain_f
    dh = dy[0].astype(F32) + r2 * scaled - hid * (r2 * r2 * r2) * jnp.mean(scaled * hid, axis=-1, keepdims=True)
    da_own = (keep[0] * dh).astype(BF16)
    da = jnp.concatenate([da_own, swap_core(da_own)], axis=0)

    grad_out = dot_ta(mixed, da)
    grad_out = ring.scatter([grad_out[:, j * block : (j + 1) * block] for j in range(n)])
    dmixed = dot_tb(da, out_w).astype(BF16).reshape(seqs, length, kv_heads, repeat, HEAD_SIZE)
    dprobs = jnp.einsum("bqgrd,bkgd->bgrqk", dmixed, v, preferred_element_type=F32)
    dv = jnp.einsum("bgrqk,bqgrd->bkgd", probs_low, dmixed, preferred_element_type=F32).astype(BF16)
    inner = jnp.sum(probs * dprobs, axis=-1, keepdims=True)
    dscores = (probs * (dprobs - inner)).astype(BF16)
    dq = jnp.einsum("bgrqk,bkgd->bqgrd", dscores, k, preferred_element_type=F32) * scale
    dk = jnp.einsum("bgrqk,bqgrd->bkgd", dscores, q, preferred_element_type=F32) * scale
    dq = rotate(dq.reshape(seqs, length, heads, HEAD_SIZE), cos_part, -sin_part).astype(BF16)
    dk = rotate(dk, cos_part, -sin_part).astype(BF16)
    dqkv = jnp.concatenate(
        [d.reshape(seqs * length, -1) for d in (dq, dk, dv)], axis=1
    )
    grad_qkv = dot_ta(n1, dqkv)
    grad_qkv = ring.scatter([grad_qkv[j * block : (j + 1) * block] for j in range(n)])
    dn1 = tensor_sum(dot_tb(dqkv, qkv_w).reshape(seqs, length, width))
    r1_own = r1[:length]
    gain_a_sum = jnp.sum(dn1 * x_own * r1_own, axis=0)
    scaled = dn1 * gain_a
    dx = dh + r1_own * scaled - x_own * (r1_own * r1_own * r1_own) * jnp.mean(scaled * x_own, axis=-1, keepdims=True)
    dx = dx.astype(BF16)
    input_grad = restore(dx, swap_core(dx))

    sums = jnp.stack([gain_a_sum, gain_f_sum]).reshape(2, n, block)
    sums = sums + swap_core(sums)
    gain_grads = ring.small_scatter(sums)
    return (
        output,
        input_grad,
        gain_grads[0],
        grad_qkv[:, :q_cols],
        grad_qkv[:, q_cols : q_cols + kv_cols],
        grad_qkv[:, q_cols + kv_cols :],
        grad_out,
        gain_grads[1],
        grad_gate,
        grad_up,
        grad_down,
    )


def local(ring, inputs, attention_gain, query_weight, key_matrix, value_matrix, out_weight, feedforward_gain,
          gate_weight, up_weight, down_weight, cotangent, layer_keep, prefix_length):
    n = ring.size
    seqs, length, width = inputs.shape
    tokens = seqs * length
    block = width // n
    q_cols, kv_cols = query_weight.shape[1], key_matrix.shape[1]
    cos_part, sin_part = rotary_tables(length)
    cos = jnp.concatenate([cos_part, cos_part], axis=1)
    sin = jnp.concatenate([-sin_part, sin_part], axis=1)
    keep = layer_keep.astype(F32)
    gains = jnp.concatenate([attention_gain[None], feedforward_gain[None], jnp.zeros((14, block), BF16)], axis=0)
    x = inputs.reshape(tokens, width)
    dy = cotangent.reshape(tokens, width)
    names = ("gains", "wq", "wk", "wv", "wo", "wg", "wu", "wd", "n1", "q", "k", "v", "ob", "hid", "n2", "m", "fa", "fb", "g_down")
    values = dict(
        zip(
            names,
            forward(
                n, x, dy, gains, query_weight, key_matrix, value_matrix, out_weight, gate_weight, up_weight, down_weight,
                cos, sin, keep, prefix_length, length,
            ),
        )
    )
    values |= {"x": x, "dy": dy, "cos": cos, "sin": sin, "keep": keep, "prefix": prefix_length}
    outs = backward(n, length, values)
    gain_sums = jnp.sum(outs["gain_slots"], axis=0)[:2]
    gain_sums = gain_sums + swap_core(gain_sums)
    output, dx, g_query, g_key, g_value, g_out, g_gate, g_up, g_down = finish(n, outs, query_weight.shape[1], key_matrix.shape[1])
    return (
        output.reshape(inputs.shape),
        dx.reshape(inputs.shape),
        gain_sums[0],
        g_query,
        g_key,
        g_value,
        g_out,
        gain_sums[1],
        g_gate,
        g_up,
        g_down,
    )


def solution(mesh):
    ring = Ring(mesh.shape["dp"])
    if mesh.shape["tensor"] != 4:
        raise ValueError("tensor axis")
    row, col = P("dp", "tensor"), P("tensor", "dp")
    data = P("dp", None, None)

    def layer(*args):
        block = args[0].shape[2] // ring.size
        return (local if block % 256 == 0 else ring_local)(ring, *args)

    return jax.shard_map(
        layer,
        mesh=mesh,
        in_specs=(data, P("dp"), row, row, row, col, P("dp"), row, row, col, data, P("dp"), P("dp")),
        out_specs=(data, data, P("dp"), row, row, row, col, P("dp"), row, row, col),
        check_vma=False,
    )
```

```python
import functools
import math

import jax
import jax.numpy as jnp
import numpy as np
from jax import lax
from jax.experimental import pallas as pl
from jax.experimental.pallas import tpu as pltpu
from jax.sharding import PartitionSpec as P

HEAD_SIZE = 128
EPSILON = 1e-05
NEGATIVE = -1e30
BF16 = jnp.bfloat16
F32 = jnp.float32
MESH = pl.DeviceIdType.MESH
HBM = pl.BlockSpec(memory_space=pltpu.HBM)
SMEM = pl.BlockSpec(memory_space=pltpu.SMEM)
ROWS = 256


def dot(a, b):
    return jnp.dot(a, b, preferred_element_type=F32)


def dot_ta(a, b):
    return lax.dot_general(a, b, (((0,), (0,)), ((), ())), preferred_element_type=F32)


def dot_tb(a, b):
    return lax.dot_general(a, b, (((1,), (1,)), ((), ())), preferred_element_type=F32)


def spec(rows, cols):
    return pl.BlockSpec((rows, cols), lambda i: (i, 0))


def fixed(*shape):
    return pl.BlockSpec(shape, lambda i: (0,) * len(shape), pipeline_mode=pl.Buffered(1))


def tiles(total, step=256):
    return [(at, min(step, total - at)) for at in range(0, total, step)]


def gain_row(gains_ref, which):
    n = gains_ref.shape[0]
    return jnp.concatenate([gains_ref[j, which : which + 1, :] for j in range(n)], axis=1).astype(F32)


def turn(values, cos, sin):
    return values * cos + pltpu.roll(values, HEAD_SIZE // 2, axis=1) * sin


class Place:
    def __init__(self, n):
        self.n = n
        self.me = lax.axis_index("dp")
        odd = self.me % 2
        self.p = (1 - odd) * (self.me // 2) + odd * (n - 1 - self.me // 2)
        tensor = lax.axis_index("tensor")
        self.core = tensor % 2
        self.core_peer = tensor + 1 - 2 * self.core
        self.chip_peer = (tensor + 2) % 4
        self.right = self.at(1)
        self.left = self.at(-1)

    def at(self, j):
        p = (self.p + j + 2 * self.n) % self.n
        low = p // (self.n // 2)
        return (1 - low) * 2 * p + low * (2 * (self.n - 1 - p) + 1)

    def greet(self):
        barrier = pltpu.get_barrier_semaphore()
        for peer in (self.left, self.right):
            pl.semaphore_signal(barrier, inc=1, device_id={"dp": peer}, device_id_type=MESH)
        for peer in (self.core_peer, self.chip_peer):
            pl.semaphore_signal(barrier, inc=1, device_id={"tensor": peer}, device_id_type=MESH)
        pl.semaphore_wait(barrier, 4)


class Gather:
    def __init__(self, place, shard, whole, where, local_sem, send_sems, recv_sems):
        self.place, self.shard, self.whole, self.where = place, shard, whole, where
        self.send_sems, self.recv_sems = send_sems, recv_sems
        self.hops = place.n // 2
        self.local = pltpu.make_async_copy(shard, where(whole, place.me, None), local_sem)

    def copy(self, way, hop):
        place = self.place
        sign = 1 - 2 * way
        owner = place.at(-sign * (hop - 1))
        half = way if hop == self.hops else None
        target = self.where(self.whole, owner, half)
        if hop > 1:
            source = target
        elif half is None:
            source = self.shard
        else:
            rows = self.shard.shape[0] // 2
            source = self.shard.at[pl.ds(half * rows, rows)]
        return pltpu.make_async_remote_copy(
            src_ref=source,
            dst_ref=target,
            send_sem=self.send_sems.at[way, hop - 1],
            recv_sem=self.recv_sems.at[way, hop - 1],
            device_id={"dp": place.right if way == 0 else place.left},
            device_id_type=MESH,
        )

    def step(self, hop):
        for way in range(2):
            if hop > 1:
                self.copy(way, hop - 1).wait_recv()
            self.copy(way, hop).start()

    def arrived(self):
        self.local.wait()
        for way in range(2):
            self.copy(way, self.hops).wait_recv()

    def drain(self):
        for way in range(2):
            for hop in range(1, self.hops + 1):
                self.copy(way, hop).wait_send()


def by_rows(rows):
    def where(whole, owner, half):
        if half is None:
            return whole.at[pl.ds(pl.multiple_of(owner * rows, rows), rows)]
        return whole.at[pl.ds(pl.multiple_of(owner * rows + half * (rows // 2), rows // 2), rows // 2)]

    return where


def by_cols(rows, cols):
    def where(whole, owner, half):
        at = pl.ds(pl.multiple_of(owner * cols, cols), cols)
        if half is None:
            return whole.at[:, at]
        return whole.at[pl.ds(half * (rows // 2), rows // 2), at]

    return where


def by_slot(whole, owner, half):
    if half is None:
        return whole.at[owner]
    rows = whole.shape[1] // 2
    return whole.at[owner, pl.ds(half * rows, rows)]


class Swap:
    def __init__(self, source, target, peer, send_sem, recv_sem):
        self.copy = pltpu.make_async_remote_copy(
            src_ref=source, dst_ref=target, send_sem=send_sem, recv_sem=recv_sem,
            device_id={"tensor": peer}, device_id_type=MESH,
        )
        self.copy.start()


def with_jobs(jobs, body):
    def both(*refs):
        for step, job in jobs:
            pl.when(pl.program_id(0) == step)(job)
        body(*refs)

    return both


class Exchange:
    def __init__(self, place, other, peer, near, far, sems):
        self.place, self.other, self.peer, self.near, self.far, self.sems = place, other, peer, near, far, sems
        self.per, self.rows = other.shape[0], other.shape[1]

    def core(self, i):
        return pltpu.make_async_remote_copy(
            src_ref=self.other.at[i], dst_ref=self.peer.at[i], send_sem=self.sems.at[0, i], recv_sem=self.sems.at[1, i],
            device_id={"tensor": self.place.core_peer}, device_id_type=MESH,
        )

    def chip(self, i):
        return pltpu.make_async_remote_copy(
            src_ref=self.near.at[i], dst_ref=self.far.at[i], send_sem=self.sems.at[2, i], recv_sem=self.sems.at[3, i],
            device_id={"tensor": self.place.chip_peer}, device_id_type=MESH,
        )

    def run(self, term, width, step, row_cols, row_args, fixed_args, jobs=()):
        per, core = self.per, self.place.core

        def body(*refs):
            s = pl.program_id(0)
            for i in range(per):
                if i:
                    @pl.when(s == i)
                    def _():
                        self.core(i - 1).start()

                @pl.when(s == per + i)
                def _():
                    if i == 0:
                        self.core(per - 1).start()
                    else:
                        self.chip(i - 1).start()
                    self.core(i).wait_recv()

            @pl.when(s < per)
            def _():
                for at, size in tiles(width, step):
                    cols = slice(at, at + size)
                    self.other[s, :, cols] = term(refs, cols).astype(BF16)

            @pl.when(s >= per)
            def _():
                for at, size in tiles(width, step):
                    cols = slice(at, at + size)
                    self.near[s - per, :, cols] = (term(refs, cols) + self.peer[s - per, :, cols].astype(F32)).astype(BF16)

        def block(s):
            return ((1 - core) + (s // per) * (2 * core - 1)) * per + s % per

        pltpu.emit_pipeline(
            with_jobs(jobs, body),
            grid=(2 * per,),
            in_specs=[pl.BlockSpec((self.rows, cols), lambda s: (block(s), 0)) for cols in row_cols]
            + [fixed(*w.shape) for w in fixed_args],
        )(*row_args, *fixed_args)
        self.chip(per - 1).start()
        for i in range(per):
            self.core(i).wait_send()

    def arrivals(self):
        return [(i * (self.rows // BLOCK), self.chip(i).wait_recv) for i in range(self.per)]

    def drain(self):
        for i in range(self.per):
            self.chip(i).wait_send()

    def total(self, at, rows):
        i, part = at // self.rows, pl.ds(pl.multiple_of(at % self.rows, rows), rows)
        return self.near[i, part, :].astype(F32) + self.far[i, part, :].astype(F32)


CHUNK = 16
BLOCK = 128


def by_chunks(step, body):
    @pl.loop(0, BLOCK, step=CHUNK)
    def _(at):
        at = pl.multiple_of(at, CHUNK)
        body(pl.ds(at, CHUNK), step * BLOCK + at)


def forward_kernel(
    n, length, x_hbm, dy_hbm, gains_in, wq_in, wk_in, wv_in, wo_in, wg_in, wu_in, wd_in, cos_hbm, sin_hbm, keep_ref, prefix_ref,
    gains_w, wq, wk, wv, wo, wg, wu, wd, n1_hbm, q_hbm, k_hbm, v_hbm, ob_hbm, hid_hbm, n2_hbm, m_hbm, fa_hbm, fb_hbm, gd_hbm,
    other, peer, near, far, local_sems, send_sems, recv_sems, swap_sems, share_sems,
):
    place = Place(n)
    core = place.core
    place.greet()
    tokens, width = x_hbm.shape
    scale = 1.0 / math.sqrt(HEAD_SIZE)
    half = wd_in.shape[0] // 2
    upper, lower = pl.ds(0, half), pl.ds(half, half)
    arrays = {
        "n": (gains_in, gains_w, by_slot),
        "q": (wq_in, wq, by_rows(wq_in.shape[0])),
        "k": (wk_in, wk, by_rows(wk_in.shape[0])),
        "v": (wv_in, wv, by_rows(wv_in.shape[0])),
        "o": (wo_in, wo, by_cols(*wo_in.shape)),
        "g": (wg_in, wg, by_rows(wg_in.shape[0])),
        "u": (wu_in, wu, by_rows(wu_in.shape[0])),
        "a": (wd_in.at[upper], wd.at[upper], by_cols(half, wd_in.shape[1])),
        "b": (wd_in.at[lower], wd.at[lower], by_cols(half, wd_in.shape[1])),
    }
    rings = {
        name: Gather(place, shard, whole, where, local_sems.at[i], send_sems.at[i], recv_sems.at[i])
        for i, (name, (shard, whole, where)) in enumerate(arrays.items())
    }
    hops = n // 2
    done = {name: 0 for name in rings}

    def go(names):
        for name in names:
            if done[name] < hops:
                done[name] += 1
                rings[name].step(done[name])

    own_rows = pl.ds(pl.multiple_of(core * length, length), length)
    other_rows = pl.ds(pl.multiple_of((1 - core) * length, length), length)

    go("nqkv")
    for name in "nqkvogu":
        rings[name].local.start()
    go("nqkvo")
    go("nqkvo")
    go("nqkvog")
    for name in "nqkv":
        go(name * hops)
        rings[name].arrived()

    def project(x_ref, gains_ref, wq_ref, wk_ref, wv_ref, cos_ref, sin_ref, n1_ref, q_ref, k_ref, v_ref):
        gain = gain_row(gains_ref, 0)

        @pl.loop(0, ROWS, step=32)
        def _(at):
            part = pl.ds(pl.multiple_of(at, 32), 32)
            xf = x_ref[part, :].astype(F32)
            r1 = lax.rsqrt(jnp.mean(xf * xf, axis=-1, keepdims=True) + EPSILON)
            n1_ref[part, :] = (xf * r1 * gain).astype(BF16)

        rows = n1_ref[...]
        cos, sin = cos_ref[...], sin_ref[...]
        for w_ref, o_ref in ((wq_ref, q_ref), (wk_ref, k_ref)):
            for at in range(0, w_ref.shape[1], HEAD_SIZE):
                head = slice(at, at + HEAD_SIZE)
                o_ref[:, head] = turn(dot(rows, w_ref[:, head]), cos, sin).astype(BF16)
        v_ref[...] = dot(rows, wv_ref[...]).astype(BF16)

    q_cols, kv_cols = wq.shape[1], wk.shape[1]
    per = length // ROWS
    turns = pl.BlockSpec((ROWS, HEAD_SIZE), lambda i: (i % per, 0))
    pltpu.emit_pipeline(
        project,
        grid=(tokens // ROWS,),
        in_specs=[spec(ROWS, width), fixed(*gains_w.shape), fixed(*wq.shape), fixed(*wk.shape), fixed(*wv.shape), turns, turns],
        out_specs=[spec(ROWS, width), spec(ROWS, q_cols), spec(ROWS, kv_cols), spec(ROWS, kv_cols)],
    )(x_hbm, gains_w, wq, wk, wv, cos_hbm, sin_hbm, n1_hbm, q_hbm, k_hbm, v_hbm)
    go("ogu")

    repeat = q_cols // kv_cols

    def attend(which, q_ref, k_ref, v_ref, o_ref):
        prefix = prefix_ref[which]
        keys, values = k_ref[...], v_ref[...]

        @pl.loop(0, length, step=128)
        def _(at):
            part = pl.ds(pl.multiple_of(at, 128), 128)
            s = dot_tb(q_ref[part, :], keys) * scale
            row = lax.broadcasted_iota(jnp.int32, s.shape, 0) + at
            col = lax.broadcasted_iota(jnp.int32, s.shape, 1)
            s = jnp.where((col <= row) | (col < prefix), s, NEGATIVE)
            e = jnp.exp(s - jnp.max(s, axis=-1, keepdims=True))
            p = e / jnp.sum(e, axis=-1, keepdims=True)
            o_ref[part, :] = dot(p.astype(BF16), values).astype(BF16)

    for which in range(2):
        seq = pl.ds(which * length, length)
        pltpu.emit_pipeline(
            functools.partial(attend, which),
            grid=(q_cols // HEAD_SIZE,),
            in_specs=[
                pl.BlockSpec((length, HEAD_SIZE), lambda h: (0, h)),
                pl.BlockSpec((length, HEAD_SIZE), lambda h: (0, h // repeat)),
                pl.BlockSpec((length, HEAD_SIZE), lambda h: (0, h // repeat)),
            ],
            out_specs=[pl.BlockSpec((length, HEAD_SIZE), lambda h: (0, h))],
        )(q_hbm.at[seq], k_hbm.at[seq], v_hbm.at[seq], ob_hbm.at[seq])

    go("o" * hops)
    rings["o"].arrived()
    go("g")
    mixed = Exchange(place, other, peer, near, far, swap_sems)
    mixed.run(lambda refs, cols: dot(refs[0][...], refs[1][:, cols]), width, 512, [q_cols], [ob_hbm], [wo])
    for name in "ab":
        rings[name].local.start()
    go("u")
    go("g")
    go("u")

    def residual(x_ref, gains_ref, hid_ref, n2_ref):
        gain = gain_row(gains_ref, 1)
        keep = keep_ref[core]

        def chunk(part, row):
            h = x_ref[part, :].astype(F32) + keep * mixed.total(row, CHUNK)
            hid_ref[part, :] = h
            r2 = lax.rsqrt(jnp.mean(h * h, axis=-1, keepdims=True) + EPSILON)
            n2_ref[part, :] = (h * r2 * gain).astype(BF16)

        by_chunks(pl.program_id(0), chunk)

    pltpu.emit_pipeline(
        with_jobs(mixed.arrivals(), residual),
        grid=(length // BLOCK,),
        in_specs=[spec(BLOCK, width), fixed(*gains_w.shape)],
        out_specs=[spec(BLOCK, width)] * 2,
    )(x_hbm.at[own_rows], gains_w, hid_hbm, n2_hbm.at[own_rows])
    share = Swap(n2_hbm.at[own_rows], n2_hbm.at[own_rows], place.core_peer, share_sems.at[0], share_sems.at[1])
    share.copy.wait_recv()
    go("g" * hops + "u" * hops + "ab")
    rings["g"].arrived()
    rings["u"].arrived()

    hidden = wg.shape[1]

    def during(at, name, hop):
        pl.when(pl.program_id(0) == at)(lambda: rings[name].step(hop))
        done[name] = hop

    def feed(n2_ref, wg_ref, wu_ref, m_ref, fa_ref, fb_ref):
        during(tokens // ROWS - 2, "a", 2)
        during(tokens // ROWS - 1, "b", 2)
        rows = n2_ref[...]
        for at, size in tiles(hidden):
            cols = slice(at, at + size)
            g = dot(rows, wg_ref[:, cols])
            u = dot(rows, wu_ref[:, cols])
            sig = 1.0 / (1.0 + jnp.exp(-g))
            swish = g * sig
            m_ref[:, cols] = (swish * u).astype(BF16)
            fa_ref[:, cols] = u * sig * (1.0 + g * (1.0 - sig))
            fb_ref[:, cols] = swish

    pltpu.emit_pipeline(
        feed,
        grid=(tokens // ROWS,),
        in_specs=[spec(ROWS, width), fixed(*wg.shape), fixed(*wu.shape)],
        out_specs=[spec(ROWS, hidden)] * 3,
    )(n2_hbm, wg, wu, m_hbm, fa_hbm, fb_hbm)

    def down_grad(m_ref, dy_ref, o_ref):
        during(0, "a", 3)
        during(4, "b", 3)
        total = None
        for which in range(2):
            seq = slice(which * length, (which + 1) * length)
            df = (dy_ref[seq, :].astype(F32) * keep_ref[which]).astype(BF16)
            term = dot_ta(m_ref[seq, :], df)
            total = term if total is None else total + term
        o_ref[...] = total.astype(BF16)

    cols = pl.BlockSpec((tokens, 256), lambda i: (0, i))
    pltpu.emit_pipeline(
        down_grad,
        grid=(width // 256,),
        in_specs=[fixed(tokens, hidden), cols],
        out_specs=[pl.BlockSpec((hidden, 256), lambda i: (0, i))],
    )(m_hbm, dy_hbm, gd_hbm)
    for _ in range(hops):
        go("ab")
    rings["a"].arrived()
    rings["b"].arrived()
    for ring in rings.values():
        ring.drain()
    mixed.drain()
    share.copy.wait_send()


def forward(n, x, dy, gains, wq, wk, wv, wo, wg, wu, wd, cos, sin, keep, prefix, length):
    tokens, width = x.shape
    shape = jax.ShapeDtypeStruct
    ff = wg.shape[1]
    outs = [
        shape((n,) + gains.shape, BF16),
        shape((width, wq.shape[1]), BF16),
        shape((width, wk.shape[1]), BF16),
        shape((width, wv.shape[1]), BF16),
        shape((wo.shape[0], width), BF16),
        shape((width, ff), BF16),
        shape((width, ff), BF16),
        shape((ff, width), BF16),
        shape((tokens, width), BF16),
        shape((tokens, wq.shape[1]), BF16),
        shape((tokens, wk.shape[1]), BF16),
        shape((tokens, wv.shape[1]), BF16),
        shape((tokens, wq.shape[1]), BF16),
        shape((length, width), F32),
        shape((tokens, width), BF16),
        shape((tokens, ff), BF16),
        shape((tokens, ff), F32),
        shape((tokens, ff), F32),
        shape((ff, width), BF16),
    ]
    blocks = pltpu.VMEM((length // ROWS, ROWS, width), BF16)
    return pl.pallas_call(
        functools.partial(forward_kernel, n, length),
        out_shape=outs,
        in_specs=[HBM] * 12 + [SMEM] * 2,
        out_specs=[HBM] * len(outs),
        scratch_shapes=[
            blocks,
            blocks,
            blocks,
            blocks,
            pltpu.SemaphoreType.DMA((9,)),
            pltpu.SemaphoreType.DMA((9, 2, n // 2)),
            pltpu.SemaphoreType.DMA((9, 2, n // 2)),
            pltpu.SemaphoreType.DMA((4, length // ROWS)),
            pltpu.SemaphoreType.DMA((2,)),
        ],
        compiler_params=pltpu.CompilerParams(collective_id=0, has_side_effects=True, vmem_limit_bytes=60 * 1024 * 1024),
    )(x, dy, gains, wq, wk, wv, wo, wg, wu, wd, cos, sin, keep, prefix)


class Buffers:
    def __init__(self, arrived, sums, sems):
        self.arrived, self.sums, self.sems = arrived, sums, sems
        self.users = []


class Scatter:
    def __init__(self, place, whole, where, piece, slots, buffers, send_sems, recv_sems, inner=None):
        self.place, self.whole, self.where, self.piece = place, whole, where, piece
        self.slots, self.buffers, self.inner = slots, buffers, inner
        self.send_sems, self.recv_sems = send_sems, recv_sems
        self.hops = place.n // 2
        self.turns = {}
        self.sent = set()

    def view(self, way, hop):
        sign = 1 - 2 * way
        owner = self.place.at(sign * (self.hops + 1 - hop))
        return self.where(self.whole, owner, way if hop == 1 else None)

    def slot(self, way, hop):
        if self.inner and hop < self.hops:
            first, rest = self.inner
            return first.at[way] if hop == 1 else rest.at[way, hop - 2]
        first, rest = self.slots[way]
        return first if hop == 1 else rest.at[hop - 2]

    def going(self, way, hop):
        rows, cols = self.piece
        buffers = self.buffers
        return buffers.sums.at[self.turns[hop] % buffers.sums.shape[0], way, pl.ds(0, rows), pl.ds(0, cols)]

    def come(self, way, hop):
        if self.inner:
            return self.slot(way, hop - 1)
        rows, cols = self.piece
        buffers = self.buffers
        rows = rows // 2 if hop == 2 else rows
        return buffers.arrived.at[self.turns[hop] % buffers.arrived.shape[0], way, pl.ds(0, rows), pl.ds(0, cols)]

    def remote(self, way, hop):
        return pltpu.make_async_remote_copy(
            src_ref=self.view(way, hop) if hop == 1 else self.going(way, hop),
            dst_ref=self.slot(way, hop),
            send_sem=self.send_sems.at[way, hop - 1],
            recv_sem=self.recv_sems.at[way, hop - 1],
            device_id={"dp": self.place.right if way == 0 else self.place.left},
            device_id_type=MESH,
        )

    def locals(self, hop):
        sems = self.buffers.sems
        turn = self.turns[hop] % sems.shape[0]
        for way in range(2):
            if not self.inner:
                yield pltpu.make_async_copy(self.slot(way, hop - 1), self.come(way, hop), sems.at[turn, way, 0])
            yield pltpu.make_async_copy(self.view(way, hop), self.going(way, hop), sems.at[turn, way, 1])

    def first(self):
        for way in range(2):
            self.remote(way, 1).start()

    def plan(self, hop):
        users = self.buffers.users
        self.turns[hop] = len(users)
        before = users[-self.buffers.sums.shape[0]] if len(users) >= self.buffers.sums.shape[0] else None
        users.append((self, hop))
        if before:
            before[0].sent.add(before[1])

        def fetch():
            for way in range(2):
                if not self.inner:
                    self.remote(way, hop - 1).wait_recv()
                if before:
                    before[0].remote(way, before[1]).wait_send()
            for copy in self.locals(hop):
                copy.start()

        def emit():
            for copy in self.locals(hop):
                copy.wait()
            rows = self.piece[0]
            for way in range(2):
                if self.inner:
                    self.remote(way, hop - 1).wait_recv()
                come, going = self.come(way, hop), self.going(way, hop)
                base = way * (rows // 2) if hop == 2 else 0

                @pl.loop(0, rows // 2 if hop == 2 else rows, step=CHUNK)
                def _(at):
                    at = pl.multiple_of(at, CHUNK)
                    part = pl.ds(pl.multiple_of(base + at, CHUNK), CHUNK)
                    going[part, :] = (going[part, :].astype(F32) + come[pl.ds(at, CHUNK), :].astype(F32)).astype(BF16)

                self.remote(way, hop).start()

        return fetch, emit

    def drain(self):
        for way in range(2):
            self.remote(way, self.hops).wait_recv()
            for hop in range(1, self.hops + 1):
                if hop not in self.sent:
                    self.remote(way, hop).wait_send()


def backward_kernel(n, length, names_in, names_out, *refs):
    ins = dict(zip(names_in, refs))
    outs = dict(zip(names_out, refs[len(names_in) :]))
    (gsum, gpieces, dh, other, peers, nears, fars, come_rows, sums_rows, come_cols, sums_cols, qkv_first, qkv_rest, add_sems, local_sems, send_sems, recv_sems, swap_sems, swap_send, swap_recv, gain_send, gain_recv) = refs[
        len(names_in) + len(names_out) :
    ]
    keep_ref, prefix_ref = ins["keep"], ins["prefix"]
    dy, x, gains_w = ins["dy"], ins["x"], ins["gains"]
    wq, wk, wv, wo, wg, wu, wd = (ins[name] for name in ("wq", "wk", "wv", "wo", "wg", "wu", "wd"))
    tokens, width = x.shape
    q_cols, kv_cols, hidden = wq.shape[1], wk.shape[1], wg.shape[1]
    block = width // n
    per = length // ROWS
    repeat = q_cols // kv_cols
    scale = 1.0 / math.sqrt(HEAD_SIZE)
    place = Place(n)
    core = place.core
    barrier = pltpu.get_barrier_semaphore()
    for j in range(1, n):
        pl.semaphore_signal(barrier, inc=1, device_id={"dp": place.at(j)}, device_id_type=MESH)
    for peer in (place.core_peer, place.chip_peer):
        pl.semaphore_signal(barrier, inc=1, device_id={"tensor": peer}, device_id_type=MESH)
    pl.semaphore_wait(barrier, n + 1)

    own_rows = pl.ds(pl.multiple_of(core * length, length), length)
    by_row = Buffers(come_rows, sums_rows, add_sems.at[0])
    by_col = Buffers(come_cols, sums_cols, add_sems.at[1])
    grads = {
        "down": (by_cols(hidden, block), (hidden, block), by_col),
        "gate": (by_rows(block), (block, hidden), by_row),
        "up": (by_rows(block), (block, hidden), by_row),
        "out": (by_cols(q_cols, block), (q_cols, block), by_col),
        "qkv": (by_rows(block), (block, q_cols + 2 * kv_cols), by_row),
    }
    rings = {
        name: Scatter(
            place,
            outs["g_" + name],
            where,
            piece,
            [(outs[f"r_{name}_{way}_first"], outs[f"r_{name}_{way}"]) for way in range(2)],
            buffers,
            send_sems.at[i],
            recv_sems.at[i],
            (qkv_first, qkv_rest) if name == "qkv" else None,
        )
        for i, (name, (where, piece, buffers)) in enumerate(grads.items())
    }
    swaps = []

    def swap(source, target, peer):
        i = len(swaps)
        swaps.append(Swap(source, target, peer, swap_send.at[i], swap_recv.at[i]))
        return swaps[-1].copy

    def act_grads(jobs):
        def body(dy_ref, wd_ref, fa_ref, fb_ref, dg_ref, du_ref):
            which = pl.program_id(0) // per
            df = (dy_ref[...].astype(F32) * keep_ref[which]).astype(BF16)
            for at, size in tiles(hidden):
                cols = slice(at, at + size)
                dm = dot_tb(df, wd_ref[cols, :])
                dg_ref[:, cols] = (dm * fa_ref[:, cols]).astype(BF16)
                du_ref[:, cols] = (dm * fb_ref[:, cols]).astype(BF16)

        pltpu.emit_pipeline(
            with_jobs(jobs, body),
            grid=(tokens // ROWS,),
            in_specs=[spec(ROWS, width), fixed(hidden, width), spec(ROWS, hidden), spec(ROWS, hidden)],
            out_specs=[spec(ROWS, hidden)] * 2,
        )(dy, wd, ins["fa"], ins["fb"], outs["dg"], outs["du"])

    def outer(left, right, target, jobs):
        def body(l_ref, r_ref, o_ref):
            o_ref[...] = dot_ta(l_ref[...], r_ref[...]).astype(BF16)

        cols = right.shape[1]
        pltpu.emit_pipeline(
            with_jobs(jobs, body),
            grid=(width // 256,),
            in_specs=[pl.BlockSpec((tokens, 256), lambda i: (0, i)), fixed(tokens, cols)],
            out_specs=[spec(256, cols)],
        )(left, right, target)

    def exchange(i):
        return Exchange(place, other, peers.at[i], nears.at[i], fars.at[i], swap_sems.at[i])

    in_n2, in_f, in_n1 = exchange(0), exchange(1), exchange(2)

    def back(jobs):
        in_n2.run(
            lambda refs, cols: dot_tb(refs[0][...], refs[2][cols, :]) + dot_tb(refs[1][...], refs[3][cols, :]),
            width, 256, [hidden, hidden], [outs["dg"], outs["du"]], [wg, wu], jobs,
        )

    def add_gain(which, terms):
        gsum[which] += sum(terms[i * 8 : (i + 1) * 8] for i in range(terms.shape[0] // 8))

    def norm_back(d, h, gain, which):
        r = lax.rsqrt(jnp.mean(h * h, axis=-1, keepdims=True) + EPSILON)
        add_gain(which, d * h * r)
        scaled = d * gain
        return r * scaled - h * (r * r * r) * jnp.mean(scaled * h, axis=-1, keepdims=True)

    def hid_grads():
        def body(hid_ref, dy_ref, gains_ref, da_ref):
            gain = gain_row(gains_ref, 1)
            keep = keep_ref[core]

            def chunk(part, row):
                d = in_n2.total(row, CHUNK)
                value = dy_ref[part, :].astype(F32) + norm_back(d, hid_ref[part, :], gain, 1)
                dh[pl.ds(pl.multiple_of(row, CHUNK), CHUNK), :] = value
                da_ref[part, :] = (keep * value).astype(BF16)

            by_chunks(pl.program_id(0), chunk)

        pltpu.emit_pipeline(
            with_jobs(in_n2.arrivals(), body),
            grid=(length // BLOCK,),
            in_specs=[spec(BLOCK, width)] * 2 + [fixed(*gains_w.shape)],
            out_specs=[spec(BLOCK, width)],
        )(ins["hid"], dy.at[own_rows], gains_w, outs["da"].at[own_rows])
        return swap(outs["da"].at[own_rows], outs["da"].at[own_rows], place.core_peer)

    def input_grads():
        def body(x_ref, gains_ref, dx_ref):
            gain = gain_row(gains_ref, 0)

            def chunk(part, row):
                d = in_n1.total(row, CHUNK)
                value = norm_back(d, x_ref[part, :].astype(F32), gain, 0)
                dx_ref[part, :] = (dh[pl.ds(pl.multiple_of(row, CHUNK), CHUNK), :] + value).astype(BF16)

            by_chunks(pl.program_id(0), chunk)

        pltpu.emit_pipeline(
            with_jobs(in_n1.arrivals(), body),
            grid=(length // BLOCK,),
            in_specs=[spec(BLOCK, width), fixed(*gains_w.shape)],
            out_specs=[spec(BLOCK, width)],
        )(x.at[own_rows], gains_w, outs["dx"].at[own_rows])
        return swap(outs["dx"].at[own_rows], outs["dx"].at[own_rows], place.core_peer)

    def results():
        def body(hid_ref, o_ref):
            keep = keep_ref[core]

            def chunk(part, row):
                o_ref[part, :] = (hid_ref[part, :] + keep * in_f.total(row, CHUNK)).astype(BF16)

            by_chunks(pl.program_id(0), chunk)

        pltpu.emit_pipeline(
            with_jobs(in_f.arrivals(), body),
            grid=(length // BLOCK,),
            in_specs=[spec(BLOCK, width)],
            out_specs=[spec(BLOCK, width)],
        )(ins["hid"], outs["output"].at[own_rows])
        return swap(outs["output"].at[own_rows], outs["output"].at[own_rows], place.core_peer)

    def forth(jobs):
        in_f.run(lambda refs, cols: dot(refs[0][...], refs[1][:, cols]), width, 512, [hidden], [ins["m"]], [wd], jobs)

    def out_grad(jobs):
        def body(ob_ref, da_ref, o_ref):
            o_ref[...] = dot_ta(ob_ref[...], da_ref[...]).astype(BF16)

        pltpu.emit_pipeline(
            with_jobs(jobs, body),
            grid=(width // 256,),
            in_specs=[fixed(tokens, q_cols), pl.BlockSpec((tokens, 256), lambda i: (0, i))],
            out_specs=[pl.BlockSpec((q_cols, 256), lambda i: (0, i))],
        )(ins["ob"], outs["da"], outs["g_out"])

    def mixed_grad():
        def body(da_ref, wo_ref, o_ref):
            o_ref[...] = dot_tb(da_ref[...], wo_ref[...]).astype(BF16)

        pltpu.emit_pipeline(
            body, grid=(tokens // ROWS,), in_specs=[spec(ROWS, width), fixed(q_cols, width)], out_specs=[spec(ROWS, q_cols)]
        )(outs["da"], wo, outs["dob"])

    def attend_back(which, jobs):
        seq = pl.ds(which * length, length)

        def heads(dk_sum, dv_sum):
            def body(q_ref, k_ref, v_ref, d_ref, cos_ref, sin_ref, dq_ref, dk_ref, dv_ref):
                head = pl.program_id(0) % repeat
                prefix = prefix_ref[which]
                keys, values = k_ref[...], v_ref[...]

                @pl.when(head == 0)
                def _():
                    dk_sum[...] = jnp.zeros_like(dk_sum)
                    dv_sum[...] = jnp.zeros_like(dv_sum)

                @pl.loop(0, length, step=128)
                def _(at):
                    part = pl.ds(pl.multiple_of(at, 128), 128)
                    queries, grads = q_ref[part, :], d_ref[part, :]
                    s = dot_tb(keys, queries) * scale
                    col = lax.broadcasted_iota(jnp.int32, s.shape, 0)
                    row = lax.broadcasted_iota(jnp.int32, s.shape, 1) + at
                    s = jnp.where((col <= row) | (col < prefix), s, NEGATIVE)
                    e = jnp.exp(s - jnp.max(s, axis=0, keepdims=True))
                    p = e / jnp.sum(e, axis=0, keepdims=True)
                    dp = dot_tb(values, grads)
                    inner = jnp.sum(p * dp, axis=0, keepdims=True)
                    dz = (p * (dp - inner)).astype(BF16)
                    dv_sum[...] += dot(p.astype(BF16), grads)
                    dk_sum[...] += dot(dz, queries)
                    dq = dot_ta(dz, keys) * scale
                    dq_ref[part, :] = turn(dq, cos_ref[part, :], -sin_ref[part, :]).astype(BF16)

                @pl.when(head == repeat - 1)
                def _():
                    dk_ref[...] = turn(dk_sum[...] * scale, cos_ref[...], -sin_ref[...]).astype(BF16)
                    dv_ref[...] = dv_sum[...].astype(BF16)

            one = pl.BlockSpec((length, HEAD_SIZE), lambda h: (0, h))
            shared = pl.BlockSpec((length, HEAD_SIZE), lambda h: (0, h // repeat))
            table = pl.BlockSpec((length, HEAD_SIZE), lambda h: (0, 0))
            dqkv = outs["dqkv"].at[seq]
            pltpu.emit_pipeline(
                with_jobs(jobs, body),
                grid=(q_cols // HEAD_SIZE,),
                in_specs=[one, shared, shared, one, table, table],
                out_specs=[one, shared, shared],
            )(
                ins["q"].at[seq],
                ins["k"].at[seq],
                ins["v"].at[seq],
                outs["dob"].at[seq],
                ins["cos"],
                ins["sin"],
                dqkv.at[:, pl.ds(0, q_cols)],
                dqkv.at[:, pl.ds(q_cols, kv_cols)],
                dqkv.at[:, pl.ds(q_cols + kv_cols, kv_cols)],
            )

        pl.run_scoped(heads, pltpu.VMEM((length, HEAD_SIZE), F32), pltpu.VMEM((length, HEAD_SIZE), F32))

    def back_qkv(jobs):
        def term(refs, cols):
            d_ref, wq_ref, wk_ref, wv_ref = refs
            dq, dk, dv = d_ref[:, :q_cols], d_ref[:, q_cols : q_cols + kv_cols], d_ref[:, q_cols + kv_cols :]
            return dot_tb(dq, wq_ref[cols, :]) + dot_tb(dk, wk_ref[cols, :]) + dot_tb(dv, wv_ref[cols, :])

        in_n1.run(term, width, 256, [q_cols + 2 * kv_cols], [outs["dqkv"]], [wq, wk, wv], jobs)

    def gain_grads():
        for which in range(2):
            row = jnp.sum(gsum[which], axis=0, keepdims=True)
            for j in range(n):
                gpieces[j, which : which + 1, :] = row[:, j * block : (j + 1) * block]
        copy = pltpu.make_async_copy(gpieces, outs["gain_terms"], local_sems.at[0])
        copy.start()
        copy.wait()
        mine = pltpu.make_async_copy(outs["gain_terms"].at[place.me], outs["gain_slots"].at[0], local_sems.at[1])
        mine.start()
        copies = []
        for j in range(1, n):
            copy = pltpu.make_async_remote_copy(
                src_ref=outs["gain_terms"].at[place.at(j)],
                dst_ref=outs["gain_slots"].at[j],
                send_sem=gain_send.at[j],
                recv_sem=gain_recv.at[j],
                device_id={"dp": place.at(j)},
                device_id_type=MESH,
            )
            copy.start()
            copies.append(copy)
        return mine, copies

    plans = {}
    for name, hop in (
        ("down", 2), ("down", 3), ("gate", 2), ("down", 4), ("gate", 3), ("up", 2), ("gate", 4), ("up", 3), ("out", 2),
        ("up", 4), ("out", 3), ("qkv", 2), ("qkv", 3), ("out", 4), ("qkv", 4),
    ):
        plans[name, hop] = rings[name].plan(hop)

    def fetch(name, hop):
        return plans[name, hop][0]

    def emit(name, hop):
        return plans[name, hop][1]

    rings["down"].first()
    gsum[...] = jnp.zeros_like(gsum)
    gpieces[...] = jnp.zeros_like(gpieces)
    act_grads([(2, fetch("down", 2)), (3, emit("down", 2))])
    outer(ins["n2"], outs["dg"], outs["g_gate"], [])
    rings["gate"].first()
    back([(0, fetch("down", 3)), (1, emit("down", 3)), (2, fetch("gate", 2)), (3, emit("gate", 2))])
    outer(ins["n2"], outs["du"], outs["g_up"], [(3, fetch("down", 4)), (5, emit("down", 4))])
    rings["up"].first()
    forth([])
    fetch("gate", 3)()
    emit("gate", 3)()
    share_da = hid_grads()
    fetch("up", 2)()
    emit("up", 2)()
    share_da.wait_recv()
    mixed_grad()
    out_grad([(4, fetch("gate", 4)), (6, emit("gate", 4))])
    rings["out"].first()
    attend_back(0, [(2, fetch("up", 3)), (3, emit("up", 3))])
    attend_back(1, [(3, fetch("out", 2))])
    emit("out", 2)()
    back_qkv([(3, fetch("up", 4))])
    outer(ins["n1"], outs["dqkv"], outs["g_qkv"], [(0, emit("up", 4)), (5, fetch("out", 3))])
    rings["qkv"].first()
    emit("out", 3)()
    fetch("qkv", 2)()
    share_out = results()
    emit("qkv", 2)()
    fetch("qkv", 3)()
    emit("qkv", 3)()
    fetch("out", 4)()
    emit("out", 4)()
    fetch("qkv", 4)()
    share_dx = input_grads()
    emit("qkv", 4)()
    mine, copies = gain_grads()
    share_out.wait_recv()
    share_dx.wait_recv()
    mine.wait()
    for copy in copies:
        copy.wait_recv()
    for ring in rings.values():
        ring.drain()
    for copy in copies:
        copy.wait_send()
    for item in swaps:
        item.copy.wait_send()
    for item in (in_n2, in_f, in_n1):
        item.drain()


def backward(n, length, values):
    shape = jax.ShapeDtypeStruct
    tokens, width = values["x"].shape
    q_cols, kv_cols, hidden = values["wq"].shape[1], values["wk"].shape[1], values["wg"].shape[1]
    block = width // n
    widest = max(hidden, q_cols + 2 * kv_cols)
    outs = {}
    sizes = {
        "down": ((hidden, width), (hidden, block)),
        "gate": ((width, hidden), (block, hidden)),
        "up": ((width, hidden), (block, hidden)),
        "out": ((q_cols, width), (q_cols, block)),
        "qkv": ((width, q_cols + 2 * kv_cols), (block, q_cols + 2 * kv_cols)),
    }
    for name, (whole, piece) in sizes.items():
        outs["g_" + name] = shape(whole, BF16)
        for way in range(2):
            outs[f"r_{name}_{way}_first"] = shape((piece[0] // 2, piece[1]), BF16)
            outs[f"r_{name}_{way}"] = shape((n // 2 - 1,) + piece, BF16)
    outs["dg"] = outs["du"] = shape((tokens, hidden), BF16)
    outs["da"] = outs["dx"] = outs["output"] = shape((tokens, width), BF16)
    outs["dob"] = shape((tokens, q_cols), BF16)
    outs["dqkv"] = shape((tokens, q_cols + 2 * kv_cols), BF16)
    outs["gain_terms"] = outs["gain_slots"] = shape((n, 8, block), F32)
    names_in, names_out = list(values), list(outs)
    results = pl.pallas_call(
        functools.partial(backward_kernel, n, length, names_in, names_out),
        out_shape=list(outs.values()),
        in_specs=[SMEM if name in ("keep", "prefix") else HBM for name in names_in],
        out_specs=[HBM] * len(outs),
        input_output_aliases={names_in.index("g_down"): names_out.index("g_down")},
        scratch_shapes=[
            pltpu.VMEM((2, 8, width), F32),
            pltpu.VMEM((n, 8, block), F32),
            pltpu.VMEM((length, width), F32),
            pltpu.VMEM((length // ROWS, ROWS, width), BF16),
            pltpu.VMEM((3, length // ROWS, ROWS, width), BF16),
            pltpu.VMEM((3, length // ROWS, ROWS, width), BF16),
            pltpu.VMEM((3, length // ROWS, ROWS, width), BF16),
            pltpu.VMEM((2, 2, block, widest), BF16),
            pltpu.VMEM((3, 2, block, widest), BF16),
            pltpu.VMEM((2, 2, widest, block), BF16),
            pltpu.VMEM((3, 2, widest, block), BF16),
            pltpu.VMEM((2, block // 2, q_cols + 2 * kv_cols), BF16),
            pltpu.VMEM((2, n // 2 - 2, block, q_cols + 2 * kv_cols), BF16),
            pltpu.SemaphoreType.DMA((2, 3, 2, 2)),
            pltpu.SemaphoreType.DMA((2,)),
            pltpu.SemaphoreType.DMA((5, 2, n // 2)),
            pltpu.SemaphoreType.DMA((5, 2, n // 2)),
            pltpu.SemaphoreType.DMA((3, 4, length // ROWS)),
            pltpu.SemaphoreType.DMA((3,)),
            pltpu.SemaphoreType.DMA((3,)),
            pltpu.SemaphoreType.DMA((n,)),
            pltpu.SemaphoreType.DMA((n,)),
        ],
        compiler_params=pltpu.CompilerParams(collective_id=1, has_side_effects=True, vmem_limit_bytes=60 * 1024 * 1024),
    )(*values.values())
    return dict(zip(names_out, results))


def finish(n, outs, q_cols, kv_cols):
    steps = 8
    shape = jax.ShapeDtypeStruct
    tokens, width = outs["output"].shape
    hidden = outs["g_gate"].shape[1]
    block = width // n
    last = n // 2 - 2

    def copied():
        return pl.BlockSpec((tokens // steps, width), lambda i, me: (i, 0))

    def by_row(cols):
        rows = block // steps
        slot = pl.BlockSpec((None, rows, cols), lambda i, me: (last, i, 0))
        return [pl.BlockSpec((rows, cols), lambda i, me: (me[0] * steps + i, 0)), slot, slot]

    def by_col(rows):
        rows = rows // steps
        slot = pl.BlockSpec((None, rows, block), lambda i, me: (last, i, 0))
        return [pl.BlockSpec((rows, block), lambda i, me: (i, me[0])), slot, slot]

    def result(rows, cols):
        return pl.BlockSpec((rows // steps, cols), lambda i, me: (i, 0))

    def body(me, output, dx, *refs):
        terms, results = refs[:15], refs[15:]
        results[0][...] = output[...]
        results[1][...] = dx[...]
        sums = [sum(ref[...].astype(F32) for ref in terms[3 * i : 3 * i + 3]) for i in range(5)]
        results[2][...] = sums[0][:, :q_cols]
        results[3][...] = sums[0][:, q_cols : q_cols + kv_cols]
        results[4][...] = sums[0][:, q_cols + kv_cols :]
        for i in range(1, 5):
            results[4 + i][...] = sums[i]

    wide = q_cols + 2 * kv_cols
    names = ("qkv", "out", "gate", "up", "down")
    sizes = [(block, q_cols), (block, kv_cols), (block, kv_cols), (q_cols, block), (block, hidden), (block, hidden), (hidden, block)]
    return pl.pallas_call(
        body,
        grid_spec=pltpu.PrefetchScalarGridSpec(
            num_scalar_prefetch=1,
            grid=(steps,),
            in_specs=[copied(), copied()] + by_row(wide) + by_col(q_cols) + by_row(hidden) + by_row(hidden) + by_col(hidden),
            out_specs=[copied(), copied()] + [result(*size) for size in sizes],
        ),
        out_shape=[shape((tokens, width), BF16)] * 2 + [shape(size, F32) for size in sizes],
    )(
        lax.axis_index("dp").astype(jnp.int32).reshape(1),
        outs["output"],
        outs["dx"],
        *[outs[key] for name in names for key in ("g_" + name, f"r_{name}_0", f"r_{name}_1")],
    )


def rotary_tables(length_total):
    half_width = HEAD_SIZE // 2
    frequency = (10000.0 ** (-(np.arange(half_width, dtype=np.float32) * 2.0) / HEAD_SIZE)).astype(np.float32)
    angles = np.arange(length_total, dtype=np.float32)[:, None] * frequency[None, :]
    return (jnp.asarray(np.cos(angles)), jnp.asarray(np.sin(angles)))


def rotate(values, cos_part, sin_part):
    first, second = jnp.split(values, 2, axis=-1)
    return jnp.concatenate(
        [first * cos_part - second * sin_part, first * sin_part + second * cos_part], axis=-1
    )


class Ring:
    def __init__(self, size):
        self.size = size
        self.half = size // 2
        self.order = [2 * p if p < self.half else 2 * (size - 1 - p) + 1 for p in range(size)]
        self.right = [(self.order[p], self.order[(p + 1) % size]) for p in range(size)]
        self.left = [(b, a) for a, b in self.right]

    def place(self):
        me = lax.axis_index("dp")
        odd = me % 2
        return (1 - odd) * (me // 2) + odd * (self.size - 1 - me // 2)

    def owners(self):
        return jnp.asarray(np.array(self.order, np.int32))[(self.place() + np.arange(self.size)) % self.size]

    def gather(self, shard):
        n, m = self.size, self.half
        pieces = [None] * n
        pieces[0] = shard
        from_left, from_right = shard, shard
        for hop in range(1, m):
            from_left = lax.ppermute(from_left, "dp", self.right)
            from_right = lax.ppermute(from_right, "dp", self.left)
            pieces[n - hop] = from_left
            pieces[hop] = from_right
        rows = shard.shape[0] // 2
        top = lax.ppermute(from_left[:rows], "dp", self.right)
        low = lax.ppermute(from_right[rows:], "dp", self.left)
        pieces[m] = jnp.concatenate([top, low], axis=0)
        return pieces

    def scatter(self, parts):
        n, m = self.size, self.half
        rows = parts[0].shape[0] // 2
        kind = BF16
        up = lax.ppermute(parts[m][:rows].astype(kind), "dp", self.right)
        down = lax.ppermute(parts[m][rows:].astype(kind), "dp", self.left)
        for hop in range(m - 1, 0, -1):
            mine_up, mine_down = parts[hop], parts[n - hop]
            if hop == m - 1:
                mine_up = jnp.concatenate([mine_up[:rows] + up.astype(F32), mine_up[rows:]], axis=0)
                mine_down = jnp.concatenate([mine_down[:rows], mine_down[rows:] + down.astype(F32)], axis=0)
            else:
                mine_up = mine_up + up.astype(F32)
                mine_down = mine_down + down.astype(F32)
            up = lax.ppermute(mine_up.astype(kind), "dp", self.right)
            down = lax.ppermute(mine_down.astype(kind), "dp", self.left)
        if m == 1:
            return jnp.concatenate([parts[0][:rows] + up.astype(F32), parts[0][rows:] + down.astype(F32)], axis=0)
        return parts[0] + up.astype(F32) + down.astype(F32)


    def small_scatter(self, sums):
        up = sums[:, self.half]
        for hop in range(self.half - 1, -1, -1):
            up = lax.ppermute(up, "dp", self.right)
            up = up + sums[:, hop]
        if self.size > 2:
            down = sums[:, self.half + 1]
            for hop in range(self.half - 2, -1, -1):
                down = lax.ppermute(down, "dp", self.left)
                if hop:
                    down = down + sums[:, self.size - hop]
            up = up + down
        return up


CORE_PAIRS = [(0, 1), (1, 0), (2, 3), (3, 2)]
CHIP_PAIRS = [(0, 2), (2, 0), (1, 3), (3, 1)]


def swap_core(value):
    return lax.ppermute(value, "tensor", CORE_PAIRS)


def swap_chip(value):
    return lax.ppermute(value, "tensor", CHIP_PAIRS)


def tensor_sum(part):
    near = part[0] + swap_core(part[1].astype(BF16)).astype(F32)
    near = near.astype(BF16)
    return near.astype(F32) + swap_chip(near).astype(F32)


def ring_local(ring, inputs, attention_gain, query_weight, key_matrix, value_matrix, out_weight, feedforward_gain,
          gate_weight, up_weight, down_weight, cotangent, layer_keep, prefix_length):
    n = ring.size
    seqs, length, width = inputs.shape
    block = width // n
    q_cols, kv_cols = query_weight.shape[1], key_matrix.shape[1]
    heads = q_cols // HEAD_SIZE
    kv_heads = kv_cols // HEAD_SIZE
    repeat = heads // kv_heads
    scale = 1.0 / math.sqrt(HEAD_SIZE)
    core = lax.axis_index("tensor") % 2
    owners = ring.owners()

    def arrange(array):
        array = jnp.where(core == 0, array, array[::-1])
        return jnp.concatenate(
            [lax.dynamic_slice_in_dim(array, owners[j] * block, block, axis=2) for j in range(n)], axis=2
        )

    def restore(own, other):
        array = jnp.stack([jnp.where(core == 0, own, other), jnp.where(core == 0, other, own)])
        places = jnp.asarray(np.argsort(np.array(ring.order)).astype(np.int32))
        where = (places - ring.place()) % n
        return jnp.concatenate(
            [lax.dynamic_slice_in_dim(array, where[j] * block, block, axis=2) for j in range(n)], axis=2
        )

    gains = jnp.concatenate([attention_gain, feedforward_gain])
    fill = jnp.zeros((8, q_cols + 2 * kv_cols), BF16)
    fill = lax.dynamic_update_slice(fill, gains[None, :], (0, 0))
    first = jnp.concatenate(
        [jnp.concatenate([query_weight, key_matrix, value_matrix], axis=1), fill], axis=0
    )
    first_pieces = ring.gather(first)
    qkv_w = jnp.concatenate([p[:block] for p in first_pieces], axis=0)
    gain_a = jnp.concatenate([p[block, :block] for p in first_pieces]).astype(F32)
    gain_f = jnp.concatenate([p[block, block : 2 * block] for p in first_pieces]).astype(F32)
    out_w = jnp.concatenate(ring.gather(out_weight), axis=1)
    gate_w = jnp.concatenate(ring.gather(gate_weight), axis=0)
    up_w = jnp.concatenate(ring.gather(up_weight), axis=0)
    down_w = jnp.concatenate(ring.gather(down_weight), axis=1)

    keep = layer_keep.astype(F32)
    keep = jnp.where(core == 0, keep, keep[::-1])
    prefix = jnp.where(core == 0, prefix_length, prefix_length[::-1])
    x = arrange(inputs)
    dy = arrange(cotangent)

    cos_part, sin_part = rotary_tables(length)
    cos_part, sin_part = cos_part[None, :, None, :], sin_part[None, :, None, :]
    position = jnp.arange(length, dtype=jnp.int32)

    rows = x.reshape(seqs * length, width).astype(F32)
    r1 = lax.rsqrt(jnp.mean(rows * rows, axis=-1, keepdims=True) + EPSILON)
    n1 = (rows * r1 * gain_a).astype(BF16)
    qkv = dot(n1, qkv_w)
    q = rotate(qkv[:, :q_cols].reshape(seqs, length, heads, HEAD_SIZE), cos_part, sin_part).astype(BF16)
    k = rotate(qkv[:, q_cols : q_cols + kv_cols].reshape(seqs, length, kv_heads, HEAD_SIZE), cos_part, sin_part).astype(BF16)
    v = qkv[:, q_cols + kv_cols :].astype(BF16).reshape(seqs, length, kv_heads, HEAD_SIZE)
    q = q.reshape(seqs, length, kv_heads, repeat, HEAD_SIZE)
    scores = jnp.einsum("bqgrd,bkgd->bgrqk", q, k, preferred_element_type=F32) * scale
    allowed = (position[None, None, :] <= position[None, :, None]) | (position[None, None, :] < prefix[:, None, None])
    scores = jnp.where(allowed[:, None, None], scores, NEGATIVE)
    exps = jnp.exp(scores - jnp.max(scores, axis=-1, keepdims=True))
    probs = exps / jnp.sum(exps, axis=-1, keepdims=True)
    probs_low = probs.astype(BF16)
    mixed = jnp.einsum("bgrqk,bkgd->bqgrd", probs_low, v, preferred_element_type=F32)
    mixed = mixed.reshape(seqs * length, q_cols).astype(BF16)
    a_own = tensor_sum(dot(mixed, out_w).reshape(seqs, length, width))
    x_own = x[0].astype(F32)
    hid = x_own + keep[0] * a_own
    r2 = lax.rsqrt(jnp.mean(hid * hid, axis=-1, keepdims=True) + EPSILON)
    n2_own = (hid * r2 * gain_f).astype(BF16)
    n2 = jnp.concatenate([n2_own, swap_core(n2_own)], axis=0)

    g = dot(n2, gate_w)
    u = dot(n2, up_w)
    sig = jax.nn.sigmoid(g)
    swish = g * sig
    m = (swish * u).astype(BF16)
    f_own = tensor_sum(dot(m, down_w).reshape(seqs, length, width))
    out_own = (hid + keep[0] * f_own).astype(BF16)
    output = restore(out_own, swap_core(out_own))

    df = (keep[:, None, None] * dy.astype(F32)).astype(BF16).reshape(seqs * length, width)
    grad_down = dot_ta(m, df)
    dm = dot_tb(df, down_w)
    dg = (dm * u * sig * (1.0 + g * (1.0 - sig))).astype(BF16)
    du = (dm * swish).astype(BF16)
    grad_down = ring.scatter([grad_down[:, j * block : (j + 1) * block] for j in range(n)])
    grad_gate = dot_ta(n2, dg)
    grad_gate = ring.scatter([grad_gate[j * block : (j + 1) * block] for j in range(n)])
    grad_up = dot_ta(n2, du)
    grad_up = ring.scatter([grad_up[j * block : (j + 1) * block] for j in range(n)])
    dn2 = tensor_sum((dot_tb(dg, gate_w) + dot_tb(du, up_w)).reshape(seqs, length, width))
    gain_f_sum = jnp.sum(dn2 * hid * r2, axis=0)
    scaled = dn2 * gain_f
    dh = dy[0].astype(F32) + r2 * scaled - hid * (r2 * r2 * r2) * jnp.mean(scaled * hid, axis=-1, keepdims=True)
    da_own = (keep[0] * dh).astype(BF16)
    da = jnp.concatenate([da_own, swap_core(da_own)], axis=0)

    grad_out = dot_ta(mixed, da)
    grad_out = ring.scatter([grad_out[:, j * block : (j + 1) * block] for j in range(n)])
    dmixed = dot_tb(da, out_w).astype(BF16).reshape(seqs, length, kv_heads, repeat, HEAD_SIZE)
    dprobs = jnp.einsum("bqgrd,bkgd->bgrqk", dmixed, v, preferred_element_type=F32)
    dv = jnp.einsum("bgrqk,bqgrd->bkgd", probs_low, dmixed, preferred_element_type=F32).astype(BF16)
    inner = jnp.sum(probs * dprobs, axis=-1, keepdims=True)
    dscores = (probs * (dprobs - inner)).astype(BF16)
    dq = jnp.einsum("bgrqk,bkgd->bqgrd", dscores, k, preferred_element_type=F32) * scale
    dk = jnp.einsum("bgrqk,bqgrd->bkgd", dscores, q, preferred_element_type=F32) * scale
    dq = rotate(dq.reshape(seqs, length, heads, HEAD_SIZE), cos_part, -sin_part).astype(BF16)
    dk = rotate(dk, cos_part, -sin_part).astype(BF16)
    dqkv = jnp.concatenate(
        [d.reshape(seqs * length, -1) for d in (dq, dk, dv)], axis=1
    )
    grad_qkv = dot_ta(n1, dqkv)
    grad_qkv = ring.scatter([grad_qkv[j * block : (j + 1) * block] for j in range(n)])
    dn1 = tensor_sum(dot_tb(dqkv, qkv_w).reshape(seqs, length, width))
    r1_own = r1[:length]
    gain_a_sum = jnp.sum(dn1 * x_own * r1_own, axis=0)
    scaled = dn1 * gain_a
    dx = dh + r1_own * scaled - x_own * (r1_own * r1_own * r1_own) * jnp.mean(scaled * x_own, axis=-1, keepdims=True)
    dx = dx.astype(BF16)
    input_grad = restore(dx, swap_core(dx))

    sums = jnp.stack([gain_a_sum, gain_f_sum]).reshape(2, n, block)
    sums = sums + swap_core(sums)
    gain_grads = ring.small_scatter(sums)
    return (
        output,
        input_grad,
        gain_grads[0],
        grad_qkv[:, :q_cols],
        grad_qkv[:, q_cols : q_cols + kv_cols],
        grad_qkv[:, q_cols + kv_cols :],
        grad_out,
        gain_grads[1],
        grad_gate,
        grad_up,
        grad_down,
    )


def local(ring, inputs, attention_gain, query_weight, key_matrix, value_matrix, out_weight, feedforward_gain,
          gate_weight, up_weight, down_weight, cotangent, layer_keep, prefix_length):
    n = ring.size
    seqs, length, width = inputs.shape
    tokens = seqs * length
    block = width // n
    q_cols, kv_cols = query_weight.shape[1], key_matrix.shape[1]
    cos_part, sin_part = rotary_tables(length)
    cos = jnp.concatenate([cos_part, cos_part], axis=1)
    sin = jnp.concatenate([-sin_part, sin_part], axis=1)
    keep = layer_keep.astype(F32)
    gains = jnp.concatenate([attention_gain[None], feedforward_gain[None], jnp.zeros((14, block), BF16)], axis=0)
    x = inputs.reshape(tokens, width)
    dy = cotangent.reshape(tokens, width)
    names = ("gains", "wq", "wk", "wv", "wo", "wg", "wu", "wd", "n1", "q", "k", "v", "ob", "hid", "n2", "m", "fa", "fb", "g_down")
    values = dict(
        zip(
            names,
            forward(
                n, x, dy, gains, query_weight, key_matrix, value_matrix, out_weight, gate_weight, up_weight, down_weight,
                cos, sin, keep, prefix_length, length,
            ),
        )
    )
    values |= {"x": x, "dy": dy, "cos": cos, "sin": sin, "keep": keep, "prefix": prefix_length}
    outs = backward(n, length, values)
    gain_sums = jnp.sum(outs["gain_slots"], axis=0)[:2]
    gain_sums = gain_sums + swap_core(gain_sums)
    output, dx, g_query, g_key, g_value, g_out, g_gate, g_up, g_down = finish(n, outs, query_weight.shape[1], key_matrix.shape[1])
    return (
        output.reshape(inputs.shape),
        dx.reshape(inputs.shape),
        gain_sums[0],
        g_query,
        g_key,
        g_value,
        g_out,
        gain_sums[1],
        g_gate,
        g_up,
        g_down,
    )


def solution(mesh):
    ring = Ring(mesh.shape["dp"])
    if mesh.shape["tensor"] != 4:
        raise ValueError("tensor axis")
    row, col = P("dp", "tensor"), P("tensor", "dp")
    data = P("dp", None, None)

    def layer(*args):
        block = args[0].shape[2] // ring.size
        return (local if block % 256 == 0 else ring_local)(ring, *args)

    return jax.shard_map(
        layer,
        mesh=mesh,
        in_specs=(data, P("dp"), row, row, row, col, P("dp"), row, row, col, data, P("dp"), P("dp")),
        out_specs=(data, data, P("dp"), row, row, row, col, P("dp"), row, row, col),
        check_vma=False,
    )
```
